32 devices in a mesh: fsdp: 16 (over z, y, x), seq: 2 (over core).
Axes of the slice: x: 2, y: 2, z: 4, core: 2. Of those that a mesh axis runs over, the one named last changes fastest.
Arguments:
- hidden_in: bfloat16 [16, 512, 768], P('fsdp', 'seq'), may hold values from -6 to 6
- query_weight: bfloat16 [768, 768], P(('fsdp', 'seq')), may hold values from -0.21875 to 0.21875
- query_bias: bfloat16 [768], P(('fsdp', 'seq')), may hold values from -3 to 3
- key_weight: bfloat16 [768, 768], P(('fsdp', 'seq')), may hold values from -0.21875 to 0.21875
- value_weight: bfloat16 [768, 768], P(('fsdp', 'seq')), may hold values from -0.21875 to 0.21875
- value_bias: bfloat16 [768], P(('fsdp', 'seq')), may hold values from -3 to 3
- output_weight: bfloat16 [768, 768], P(('fsdp', 'seq')), may hold values from -0.625 to 0.625
- output_bias: bfloat16 [768], P(('fsdp', 'seq')), may hold values from -3 to 3
- first_gain: bfloat16 [768], P(('fsdp', 'seq')), may hold values from 0.5 to 1.5
- first_shift: bfloat16 [768], P(('fsdp', 'seq')), may hold values from -3 to 3
- inner_weight: bfloat16 [768, 3072], P(('fsdp', 'seq')), may hold values from -0.21875 to 0.21875
- inner_bias: bfloat16 [3072], P(('fsdp', 'seq')), may hold values from -3 to 3
- outer_weight: bfloat16 [3072, 768], P(('fsdp', 'seq')), may hold values from -0.109375 to 0.109375
- outer_bias: bfloat16 [768], P(('fsdp', 'seq')), may hold values from -3 to 3
- second_gain: bfloat16 [768], P(('fsdp', 'seq')), may hold values from 0.5 to 1.5
- second_shift: bfloat16 [768], P(('fsdp', 'seq')), may hold values from -3 to 3
- relative_table: bfloat16 [512, 768], P(None, ('fsdp', 'seq')), may hold values from -6 to 6
- segments: int32 [16, 512], P('fsdp'), may hold values from 0 to 15, never falling along the last dimension, each value on 1 to 256 neighbouring positions
- buckets: int32 [1023], replicated, may hold values from 0 to 511
- predicted: int32 [16, 512], P('fsdp', 'seq'), may hold values 0 or 1
- labels: int32 [16, 512], P('fsdp', 'seq'), may hold values 0 or 1
- cotangent: bfloat16 [16, 512, 768], P('fsdp', 'seq'), may hold values from -6 to 6
Outputs:
- result: bfloat16 [16, 512, 768], P('fsdp', 'seq')
- input_grad: bfloat16 [16, 512, 768], P('fsdp', 'seq')
- query_weight_grad: float32 [768, 768], P(('fsdp', 'seq'))
- query_bias_grad: float32 [768], P(('fsdp', 'seq'))
- key_weight_grad: float32 [768, 768], P(('fsdp', 'seq'))
- value_weight_grad: float32 [768, 768], P(('fsdp', 'seq'))
- value_bias_grad: float32 [768], P(('fsdp', 'seq'))
- output_weight_grad: float32 [768, 768], P(('fsdp', 'seq'))
- output_bias_grad: float32 [768], P(('fsdp', 'seq'))
- first_gain_grad: float32 [768], P(('fsdp', 'seq'))
- first_shift_grad: float32 [768], P(('fsdp', 'seq'))
- inner_weight_grad: float32 [768, 3072], P(('fsdp', 'seq'))
- inner_bias_grad: float32 [3072], P(('fsdp', 'seq'))
- outer_weight_grad: float32 [3072, 768], P(('fsdp', 'seq'))
- outer_bias_grad: float32 [768], P(('fsdp', 'seq'))
- second_gain_grad: float32 [768], P(('fsdp', 'seq'))
- second_shift_grad: float32 [768], P(('fsdp', 'seq'))
- relative_table_grad: float32 [512, 768], P(None, ('fsdp', 'seq'))
- correct_count: int32 [], replicated
The draws below stay inside these ranges and needn't reach their ends.
Inputs may be any that keep to these rules, and one draw needn't show every extreme that they name: `segments`: segment numbers never fall along a row; a document has at most 256 tokens. `buckets`: entry d is the bucket of relative distance d - 511.
All inputs are finite; a program needn't handle non-finite values. No bound on the sum of `predicted` or of `labels` on one device may be relied on, other than what follows from the above.
Results may differ from the reference program's by a relative error of at most 0.015.
Values may be sent and summed in bfloat16 or wider, within the bound.
A program may use at most 192 MiB of HBM per device.

```python
import math
import jax
import jax.numpy as jnp
import numpy as np
from jax import lax

D = 768
HEADS = 12
HEAD = 64
FF = 3072
BUCKETS = 256
LENGTH = 512
ROWS = 16


def with_ends(values, key, least, high):
    place = [jax.random.randint(jax.random.fold_in(key, axis), (), 0, length) for axis, length in enumerate(values.shape)]
    main_axis = values.shape.index(max(values.shape))
    beside = place[:main_axis] + [(place[main_axis] + 1) % values.shape[main_axis]] + place[main_axis + 1:]
    return values.at[tuple(place)].set(least).at[tuple(beside)].set(high)


def level_of(stream_key, shape, cuts, least, largest):
    def one(dim, blocks):
        heights = jax.random.uniform(jax.random.fold_in(jax.random.fold_in(stream_key, 6), dim), (blocks,), jnp.float32, least / len(cuts), largest / len(cuts))
        return jnp.repeat(jnp.exp(heights), shape[dim] // blocks).reshape((-1,) + (1,) * (len(shape) - dim - 1))

    level = one(*cuts[0])
    for cut in cuts[1:]:
        level = level * one(*cut)
    return level


def profile(amount, total, bound, skew):
    weights = [(1 << 20) // math.isqrt(rank ** skew) + 1 for rank in range(2, amount + 1)]
    spare, counts = total - bound - (amount - 1), [1] * (amount - 1)
    while spare > 0:
        movable = [i for i in range(amount - 1) if counts[i] < bound]
        pool, budget = sum([weights[i] for i in movable]), spare
        for i in movable:
            extra = min(bound - counts[i], max(1, budget * weights[i] // pool), spare)
            counts[i] = counts[i] + extra
            spare = spare - extra
    return np.array([bound] + counts)


def ragged_sizes(stream_key, amount, total, bound, slope):
    if amount == 2:
        one = jax.random.randint(stream_key, (), max(1, total - bound), min(bound, total - 1) + 1)
        return jnp.stack([one, total - one])
    sizes = jnp.asarray(profile(amount, total, bound, slope), jnp.int32)
    couples = (amount - 1) // 2
    source_of, sink = sizes[1:1 + 2 * couples:2], sizes[2:2 + 2 * couples:2]
    slack = jnp.minimum(source_of - 1, bound - sink)
    moved = jax.random.randint(jax.random.fold_in(stream_key, 1), (couples,), 0, 1 << 20) % (slack + 1)
    sizes = sizes.at[1:1 + 2 * couples:2].set(source_of - moved).at[2:2 + 2 * couples:2].set(sink + moved)
    return sizes[jax.random.permutation(jax.random.fold_in(stream_key, 2), amount)]


def normal_values(key, extent, spread, limit, cuts=(), kind=jnp.bfloat16):
    factor_of = level_of(key, extent, cuts, -0.22, 0.18) if cuts else 1.0
    array = jax.random.normal(key, extent, jnp.float32) * spread * factor_of
    return jnp.minimum(jnp.maximum(array, -limit), limit).astype(kind)


def setup_inputs(seed: int = 0) -> dict:
    arg_keys = jax.random.split(jax.random.key(seed), 23)
    return {
        "hidden_in": normal_values(arg_keys[0], (ROWS, LENGTH, D), 1.0, 6.0, ((0, 16), (1, 2))),
        "query_weight": normal_values(arg_keys[1], (D, D), D ** -0.5, 0.21875, ((0, 32),)),
        "query_bias": normal_values(arg_keys[2], (D,), 0.5, 3.0, ((0, 32),)),
        "key_weight": normal_values(arg_keys[3], (D, D), D ** -0.5, 0.21875, ((0, 32),)),
        "value_weight": normal_values(arg_keys[4], (D, D), D ** -0.5, 0.21875, ((0, 32),)),
        "value_bias": normal_values(arg_keys[5], (D,), 0.5, 3.0, ((0, 32),)),
        "output_weight": normal_values(arg_keys[6], (D, D), (D // 8) ** -0.5, 0.625, ((0, 32),)),
        "output_bias": normal_values(arg_keys[7], (D,), 0.5, 3.0, ((0, 32),)),
        "first_gain": jnp.clip(1.0 + 0.1 * jax.random.normal(arg_keys[8], (D,), jnp.float32), 0.5, 1.5).astype(jnp.bfloat16),
        "first_shift": normal_values(arg_keys[9], (D,), 0.5, 3.0, ((0, 32),)),
        "inner_weight": normal_values(arg_keys[10], (D, FF), D ** -0.5, 0.21875, ((0, 32),)),
        "inner_bias": normal_values(arg_keys[11], (FF,), 0.5, 3.0, ((0, 32),)),
        "outer_weight": normal_values(arg_keys[12], (FF, D), FF ** -0.5, 0.109375, ((0, 32),)),
        "outer_bias": normal_values(arg_keys[13], (D,), 0.5, 3.0, ((0, 32),)),
        "second_gain": jnp.clip(1.0 + 0.1 * jax.random.normal(arg_keys[14], (D,), jnp.float32), 0.5, 1.5).astype(jnp.bfloat16),
        "second_shift": normal_values(arg_keys[15], (D,), 0.5, 3.0, ((0, 32),)),
        "relative_table": normal_values(arg_keys[16], (2 * BUCKETS, D), 1.0, 6.0, ((1, 32),)),
        "segments": jax.vmap(lambda own: jnp.searchsorted(jnp.cumsum(ragged_sizes(own, 16, LENGTH, LENGTH // 2, 2)), jnp.arange(LENGTH), side="right"))(jax.random.split(arg_keys[17], ROWS)).reshape((ROWS, LENGTH)).astype(jnp.int32),
        "buckets": with_ends(jax.random.randint(arg_keys[18], (2 * LENGTH - 1,), 0, 2 * BUCKETS), jax.random.fold_in(arg_keys[18], 1), 0, (2 * BUCKETS) - 1).astype(jnp.int32),
        "predicted": with_ends((jax.random.randint(arg_keys[19], (ROWS, LENGTH), 0, 4) < 1).astype(jnp.int32), jax.random.fold_in(arg_keys[19], 1), 0, 1),
        "labels": with_ends((jax.random.randint(arg_keys[20], (ROWS, LENGTH), 0, 20) < 3).astype(jnp.int32), jax.random.fold_in(arg_keys[20], 1), 0, 1),
        "cotangent": normal_values(arg_keys[21], (ROWS, LENGTH, D), 1.0, 6.0, ((0, 16), (1, 2))),
    }


@jax.custom_vjp
def low(v):
    return lax.optimization_barrier(v.astype(jnp.bfloat16)).astype(jnp.float32)

@jax.custom_vjp
def low_back(v):
    return v

def low_keep(v):
    return (low(v), None)

def low_pass(kept, grad):
    return (grad,)

def back_keep(v):
    return (v, None)

def back_low(kept, grad):
    return (low(grad),)
low.defvjp(low_keep, low_pass)
low_back.defvjp(back_keep, back_low)
EPSILON = 1e-07
NEGATIVE = -1e+30

def product(spec, left, right):
    return jnp.einsum(spec, left, right, precision=lax.Precision.HIGHEST)

def layer_norm(values, gain, shift):
    average = lax.optimization_barrier(jnp.mean(values, axis=-1, keepdims=True))
    centred = values - average
    variance = lax.optimization_barrier(jnp.mean(centred * centred, axis=-1, keepdims=True))
    return centred * lax.rsqrt(variance + EPSILON) * gain + shift

def reference(hidden_in, query_weight, query_bias, key_weight, value_weight, value_bias, output_weight, output_bias, first_gain, first_shift, inner_weight, inner_bias, outer_weight, outer_bias, second_gain, second_shift, relative_table, segments, buckets, predicted, labels, cotangent):
    group_rows = math.gcd(ROWS, 4)
    score_scale = (3.0 * HEAD) ** (-0.5)
    positions = jnp.arange(LENGTH, dtype=jnp.int32)
    distance_index = (positions[:, None] - positions[None, :] + (LENGTH - 1)).astype(jnp.int32)

    def forward(tokens_in, query_w, query_b, key_w, value_w, value_b, output_w, output_b, gain_one, shift_one, inner_w, inner_b, outer_w, outer_b, gain_two, shift_two, table_in):
        key_rel = low(product('pd,de->pe', table_in, key_w))
        query_rel = low(product('pd,de->pe', table_in, query_w) + query_b)
        bucket_keys = key_rel[buckets].reshape(2 * LENGTH - 1, HEADS, HEAD)
        bucket_queries = query_rel[buckets].reshape(2 * LENGTH - 1, HEADS, HEAD)

        def row_block(carry, pieces):
            rows_in, doc_ids = pieces
            queries = low(low_back(product('gtd,de->gte', rows_in, query_w) + query_b)).reshape(group_rows, LENGTH, HEADS, HEAD)
            keys_here = low(low_back(product('gtd,de->gte', rows_in, key_w))).reshape(group_rows, LENGTH, HEADS, HEAD)
            values_here = low(low_back(product('gtd,de->gte', rows_in, value_w) + value_b)).reshape(group_rows, LENGTH, HEADS, HEAD)
            content = product('gihe,gjhe->ghij', queries, keys_here)
            near_scores = product('gihe,dhe->ghid', queries, bucket_keys)
            far_scores = product('gjhe,dhe->ghjd', keys_here, bucket_queries)
            index_full = jnp.broadcast_to(distance_index, (group_rows, HEADS, LENGTH, LENGTH))
            to_position = jnp.take_along_axis(near_scores, index_full, axis=3)
            from_position = jnp.swapaxes(jnp.take_along_axis(far_scores, index_full, axis=3), 2, 3)
            summed = low_back(content + to_position + from_position)
            same_doc = (doc_ids[:, :, None] == doc_ids[:, None, :])[:, None]
            masked = jnp.where(same_doc, summed * score_scale, NEGATIVE)
            probability = jax.nn.softmax(masked, axis=-1)
            context = product('ghij,gjhe->gihe', low(probability), values_here).reshape(group_rows, LENGTH, HEADS * HEAD)
            context = low(low_back(context))
            attention_out = low_back(product('gte,ed->gtd', context, output_w) + output_b)
            first_out = layer_norm(rows_in + attention_out, gain_one, shift_one)
            inner_pre = low_back(product('gtd,df->gtf', low(first_out), inner_w) + inner_b)
            activated = low(low_back(jax.nn.gelu(inner_pre, approximate=False)))
            outer_out = low_back(product('gtf,fd->gtd', activated, outer_w) + outer_b)
            return (carry, layer_norm(first_out + outer_out, gain_two, shift_two))
        stacked_in = tokens_in.reshape(ROWS // group_rows, group_rows, LENGTH, D)
        stacked_ids = segments.reshape(ROWS // group_rows, group_rows, LENGTH)
        _, stacked = lax.scan(jax.checkpoint(row_block), jnp.zeros((), jnp.float32), (stacked_in, stacked_ids))
        return stacked.reshape(ROWS, LENGTH, D)
    params = tuple((array_in.astype(jnp.float32) for array_in in (hidden_in, query_weight, query_bias, key_weight, value_weight, value_bias, output_weight, output_bias, first_gain, first_shift, inner_weight, inner_bias, outer_weight, outer_bias, second_gain, second_shift, relative_table)))
    result, pullback = jax.vjp(forward, *params)
    gradients = pullback(cotangent.astype(jnp.float32))
    correct_count = jnp.sum((predicted == labels).astype(jnp.int32))
    return (result.astype(jnp.bfloat16), gradients[0].astype(jnp.bfloat16), gradients[1], gradients[2], gradients[3], gradients[4], gradients[5], gradients[6], gradients[7], gradients[8], gradients[9], gradients[10], gradients[11], gradients[12], gradients[13], gradients[14], gradients[15], gradients[16], correct_count)
```

```python
from functools import partial

import jax
import jax.numpy as jnp
import numpy as np
from jax import lax
from jax.experimental import pallas as pl
from jax.experimental.pallas import tpu as pltpu
from jax.sharding import PartitionSpec as P

HEAD = 64


EPSILON = 1e-07
NEGATIVE = -1e30


def matmul(spec, left, right):
    return jnp.einsum(spec, left, right, preferred_element_type=jnp.float32)


def precise(spec, left, right):
    return jnp.einsum(spec, left, right, precision=lax.Precision.HIGHEST)


def skew_rows(scores_in, offset, columns):
    leading = scores_in.shape[:-2]
    row_count = scores_in.shape[-2]
    breadth = scores_in.shape[-1]
    flattened = scores_in.reshape(leading + (row_count * breadth,))
    flattened = jnp.concatenate(
        [flattened, jnp.zeros(leading + (2 * breadth,), scores_in.dtype)], axis=-1
    )
    selected = lax.dynamic_slice_in_dim(flattened, offset, row_count * (breadth - 1), len(leading))
    return selected.reshape(leading + (row_count, breadth - 1))[..., :columns]


def unskew_rows(values, offset, breadth):
    leading = values.shape[:-2]
    row_count = values.shape[-2]
    columns = values.shape[-1]
    padded = jnp.concatenate(
        [values, jnp.zeros(leading + (row_count, breadth - 1 - columns), values.dtype)], axis=-1
    )
    flattened = padded.reshape(leading + (row_count * (breadth - 1),))
    zero_room = jnp.zeros(leading + (row_count * breadth + 2 * breadth,), values.dtype)
    placed = lax.dynamic_update_slice_in_dim(zero_room, flattened, offset, len(leading))
    return placed[..., : row_count * breadth].reshape(leading + (row_count, breadth))


def layer_norm(values, gain, shift):
    average = jnp.mean(values, axis=-1, keepdims=True)
    centred = values - average
    variance = jnp.mean(centred * centred, axis=-1, keepdims=True)
    inverse = lax.rsqrt(variance + EPSILON)
    normed = centred * inverse
    return (normed * gain + shift, normed, inverse)


def norm_backward(upstream, normed, inverse, gain):
    scaled_up = upstream * gain
    first_mean = jnp.mean(scaled_up, axis=-1, keepdims=True)
    second_mean = jnp.mean(scaled_up * normed, axis=-1, keepdims=True)
    grad_in = inverse * (scaled_up - first_mean - normed * second_mean)
    return (grad_in, jnp.sum(upstream * normed, axis=0), jnp.sum(upstream, axis=0))


def shards(
    hidden_in,
    query_weight,
    query_bias,
    key_weight,
    value_weight,
    value_bias,
    output_weight,
    output_bias,
    first_gain,
    first_shift,
    inner_weight,
    inner_bias,
    outer_weight,
    outer_bias,
    second_gain,
    second_shift,
    relative_table,
    segments,
    buckets,
    predicted,
    labels,
    cotangent,
):
    row_count, window, model_width = hidden_in.shape
    length = segments.shape[1]
    distances = 2 * length - 1
    span = window + length - 1
    pair_width = 2 * HEAD
    pair_count = model_width // pair_width
    score_scale = (3.0 * HEAD) ** (-0.5)
    window_start = lax.axis_index("seq") * window
    near_start = length - window - window_start
    token_count = row_count * window
    attention_set = (
        lax.all_gather(query_weight, ("fsdp", "seq"), axis=0, tiled=True),
        lax.all_gather(query_bias, ("fsdp", "seq"), axis=0, tiled=True),
        lax.all_gather(key_weight, ("fsdp", "seq"), axis=0, tiled=True),
        lax.all_gather(value_weight, ("fsdp", "seq"), axis=0, tiled=True),
        lax.all_gather(value_bias, ("fsdp", "seq"), axis=0, tiled=True),
        lax.all_gather(output_weight, ("fsdp", "seq"), axis=0, tiled=True),
        lax.all_gather(output_bias, ("fsdp", "seq"), axis=0, tiled=True),
        lax.all_gather(first_gain, ("fsdp", "seq"), axis=0, tiled=True),
        lax.all_gather(first_shift, ("fsdp", "seq"), axis=0, tiled=True),
        lax.all_gather(relative_table, ("fsdp", "seq"), axis=1, tiled=True),
    )
    feed_set = (
        lax.all_gather(inner_weight, ("fsdp", "seq"), axis=0, tiled=True),
        lax.all_gather(inner_bias, ("fsdp", "seq"), axis=0, tiled=True),
        lax.all_gather(outer_weight, ("fsdp", "seq"), axis=0, tiled=True),
        lax.all_gather(outer_bias, ("fsdp", "seq"), axis=0, tiled=True),
        lax.all_gather(second_gain, ("fsdp", "seq"), axis=0, tiled=True),
        lax.all_gather(second_shift, ("fsdp", "seq"), axis=0, tiled=True),
    )
    (
        query_matrix,
        query_offset,
        key_matrix,
        value_matrix,
        value_offset,
        output_matrix,
        output_offset,
        gain_first,
        shift_first,
        table_full,
    ) = attention_set
    inner_matrix, inner_offset, outer_matrix, outer_offset, gain_second, shift_second = feed_set
    tokens = hidden_in.reshape(token_count, model_width)
    queries = (
        (matmul("td,de->te", tokens, query_matrix) + query_offset.astype(jnp.float32))
        .astype(jnp.bfloat16)
        .reshape(row_count, window, model_width)
    )
    keys_own = (
        matmul("td,de->te", tokens, key_matrix)
        .astype(jnp.bfloat16)
        .reshape(row_count, window, model_width)
    )
    values_own = (
        (matmul("td,de->te", tokens, value_matrix) + value_offset.astype(jnp.float32))
        .astype(jnp.bfloat16)
        .reshape(row_count, window, model_width)
    )
    keys_all, values_all = (
        lax.all_gather(keys_own, "seq", axis=1, tiled=True),
        lax.all_gather(values_own, "seq", axis=1, tiled=True),
    )
    key_rel = matmul("pd,de->pe", table_full, key_matrix).astype(jnp.bfloat16)
    query_rel = (
        matmul("pd,de->pe", table_full, query_matrix) + query_offset.astype(jnp.float32)
    ).astype(jnp.bfloat16)
    reversed_buckets = buckets[::-1]
    table_rows = table_full.shape[0]
    one_hot = (
        reversed_buckets[:, None] == jnp.arange(table_rows, dtype=jnp.int32)[None, :]
    ).astype(jnp.bfloat16)
    bucket_keys = matmul("dp,pe->de", one_hot, key_rel).astype(jnp.bfloat16)
    bucket_queries = matmul("dp,pe->de", one_hot, query_rel).astype(jnp.bfloat16)
    near_keys = lax.dynamic_slice_in_dim(bucket_keys, near_start, span, 0)
    far_queries = lax.dynamic_slice_in_dim(bucket_queries, window_start, span, 0)
    segment_own = lax.dynamic_slice_in_dim(segments, window_start, window, 1)
    same_doc = (segment_own[:, :, None] == segments[:, None, :])[:, None]

    def pair_scores(pair_index):
        column = pair_index * pair_width
        query_pair = lax.dynamic_slice_in_dim(queries, column, pair_width, 2).reshape(
            row_count, window, 2, HEAD
        )
        key_pair = lax.dynamic_slice_in_dim(keys_all, column, pair_width, 2).reshape(
            row_count, length, 2, HEAD
        )
        value_pair = lax.dynamic_slice_in_dim(values_all, column, pair_width, 2).reshape(
            row_count, length, 2, HEAD
        )
        bucketkeys = lax.dynamic_slice_in_dim(near_keys, column, pair_width, 1).reshape(
            span, 2, HEAD
        )
        bucketqueries = lax.dynamic_slice_in_dim(far_queries, column, pair_width, 1).reshape(
            span, 2, HEAD
        )
        content = matmul("rihe,rjhe->rhij", query_pair, key_pair)
        near_scores = matmul("rihe,dhe->rhid", query_pair, bucketkeys)
        far_scores = matmul("rjhe,dhe->rhjd", key_pair, bucketqueries)
        to_position = skew_rows(near_scores, window - 1, length)
        from_position = jnp.swapaxes(skew_rows(far_scores, length - 1, window), 2, 3)
        summed = content + to_position + from_position
        masked = jnp.where(same_doc, summed * score_scale, NEGATIVE)
        return (masked, query_pair, key_pair, value_pair, bucketkeys, bucketqueries)

    def attend_pair(pair_index):
        masked, query_pair, key_pair, value_pair, bucketkeys, bucketqueries = pair_scores(
            pair_index
        )
        highest = jnp.max(masked, axis=-1, keepdims=True)
        expsum = jnp.exp(masked - highest)
        totals = jnp.sum(expsum, axis=-1, keepdims=True)
        weights_soft = (expsum / totals).astype(jnp.bfloat16)
        context_pair = matmul("rhij,rjhe->rihe", weights_soft, value_pair).astype(jnp.bfloat16)
        return (
            context_pair.reshape(row_count, window, pair_width),
            (highest + jnp.log(totals))[..., 0],
        )

    context_parts, log_totals = lax.map(attend_pair, jnp.arange(pair_count, dtype=jnp.int32))
    context = jnp.moveaxis(context_parts, 0, 2).reshape(token_count, model_width)
    attention_out = matmul("te,ed->td", context, output_matrix) + output_offset.astype(jnp.float32)
    residual_one = tokens.astype(jnp.float32) + attention_out
    first_out, first_normed, first_inverse = layer_norm(
        residual_one, gain_first.astype(jnp.float32), shift_first.astype(jnp.float32)
    )
    first_low = first_out.astype(jnp.bfloat16)
    inner_pre = matmul("td,df->tf", first_low, inner_matrix) + inner_offset.astype(jnp.float32)
    activated = jax.nn.gelu(inner_pre, approximate=False).astype(jnp.bfloat16)
    outer_out = matmul("tf,fd->td", activated, outer_matrix) + outer_offset.astype(jnp.float32)
    final_out, final_normed, final_inverse = layer_norm(
        first_out + outer_out, gain_second.astype(jnp.float32), shift_second.astype(jnp.float32)
    )
    result = final_out.astype(jnp.bfloat16).reshape(row_count, window, model_width)
    correct_count = lax.psum(jnp.sum((predicted == labels).astype(jnp.int32)), ("fsdp", "seq"))
    regathered = attention_set + feed_set
    (
        query_back,
        query_offset_back,
        key_back,
        value_back,
        value_offset_back,
        output_back,
        output_offset_back,
        gain_first_back,
        shift_first_back,
        table_back,
        inner_back,
        inner_offset_back,
        outer_back,
        outer_offset_back,
        gain_second_back,
        shift_second_back,
    ) = regathered
    upstream = cotangent.reshape(token_count, model_width).astype(jnp.float32)
    grad_sum2, grad_gain2, grad_shift2 = norm_backward(
        upstream, final_normed, final_inverse, gain_second_back.astype(jnp.float32)
    )
    grad_outer = grad_sum2.astype(jnp.bfloat16)
    outer_bias_part = jnp.sum(grad_outer.astype(jnp.float32), axis=0)
    outer_weight_part = matmul("tf,td->fd", activated, grad_outer)
    grad_act = matmul("td,fd->tf", grad_outer, outer_back).astype(jnp.bfloat16)
    _, gelu_back = jax.vjp(partial(jax.nn.gelu, approximate=False), inner_pre)
    grad_inner = gelu_back(grad_act.astype(jnp.float32))[0].astype(jnp.bfloat16)
    inner_bias_part = jnp.sum(grad_inner.astype(jnp.float32), axis=0)
    inner_weight_part = matmul("td,tf->df", first_low, grad_inner)
    grad_first = matmul("tf,df->td", grad_inner, inner_back) + grad_sum2
    feed_grads = (
        lax.psum_scatter(inner_weight_part, ("fsdp", "seq"), scatter_dimension=0, tiled=True),
        lax.psum_scatter(inner_bias_part, ("fsdp", "seq"), scatter_dimension=0, tiled=True),
        lax.psum_scatter(outer_weight_part, ("fsdp", "seq"), scatter_dimension=0, tiled=True),
        lax.psum_scatter(outer_bias_part, ("fsdp", "seq"), scatter_dimension=0, tiled=True),
        lax.psum_scatter(grad_gain2, ("fsdp", "seq"), scatter_dimension=0, tiled=True),
        lax.psum_scatter(grad_shift2, ("fsdp", "seq"), scatter_dimension=0, tiled=True),
    )
    grad_sum1, grad_gain1, grad_shift1 = norm_backward(
        grad_first, first_normed, first_inverse, gain_first_back.astype(jnp.float32)
    )
    grad_attention = grad_sum1.astype(jnp.bfloat16)
    output_bias_part = jnp.sum(grad_attention.astype(jnp.float32), axis=0)
    output_weight_part = matmul("te,td->ed", context, grad_attention)
    grad_context = (
        matmul("td,ed->te", grad_attention, output_back)
        .astype(jnp.bfloat16)
        .reshape(row_count, window, model_width)
    )

    def attend_back(pieces):
        pair_index, log_total = pieces
        masked, query_pair, key_pair, value_pair, bucketkeys, bucketqueries = pair_scores(
            pair_index
        )
        probability = jnp.exp(masked - log_total[..., None])
        grad_context_pair = lax.dynamic_slice_in_dim(
            grad_context, pair_index * pair_width, pair_width, 2
        ).reshape(row_count, window, 2, HEAD)
        grad_soft = matmul("rihe,rjhe->rhij", grad_context_pair, value_pair)
        grad_scores = probability * (
            grad_soft - jnp.sum(probability * grad_soft, axis=-1, keepdims=True)
        )
        grad_low = (grad_scores * score_scale).astype(jnp.bfloat16)
        grad_value = matmul("rhij,rihe->rjhe", probability.astype(jnp.bfloat16), grad_context_pair)
        grad_near = unskew_rows(grad_low, window - 1, span)
        grad_far = unskew_rows(jnp.swapaxes(grad_low, 2, 3), length - 1, span)
        grad_query = matmul("rhij,rjhe->rihe", grad_low, key_pair) + matmul(
            "rhid,dhe->rihe", grad_near, bucketkeys
        )
        grad_key = matmul("rhij,rihe->rjhe", grad_low, query_pair) + matmul(
            "rhjd,dhe->rjhe", grad_far, bucketqueries
        )
        grad_bkeys = matmul("rhid,rihe->dhe", grad_near, query_pair)
        grad_bqueries = matmul("rhjd,rjhe->dhe", grad_far, key_pair)
        return (
            grad_query.reshape(row_count, window, pair_width),
            grad_key.reshape(row_count, length, pair_width),
            grad_value.reshape(row_count, length, pair_width),
            grad_bkeys.reshape(span, pair_width),
            grad_bqueries.reshape(span, pair_width),
        )

    query_parts, key_parts, value_parts, bkey_parts, bquery_parts = lax.map(
        attend_back, (jnp.arange(pair_count, dtype=jnp.int32), log_totals)
    )
    grad_query_all = jnp.moveaxis(query_parts, 0, 2).reshape(token_count, model_width)
    grad_key_all = jnp.moveaxis(key_parts, 0, 2).reshape(row_count, length, model_width)
    grad_value_all = jnp.moveaxis(value_parts, 0, 2).reshape(row_count, length, model_width)
    near_grads = jnp.moveaxis(bkey_parts, 0, 1).reshape(span, model_width)
    far_grads = jnp.moveaxis(bquery_parts, 0, 1).reshape(span, model_width)
    grad_bucket_keys = lax.dynamic_update_slice_in_dim(
        jnp.zeros((distances, model_width), jnp.float32), near_grads, near_start, 0
    )
    grad_bucket_queries = lax.dynamic_update_slice_in_dim(
        jnp.zeros((distances, model_width), jnp.float32), far_grads, window_start, 0
    )
    key_grads, value_grads = (
        lax.psum_scatter(
            grad_key_all.astype(jnp.bfloat16), "seq", scatter_dimension=1, tiled=True
        ).astype(jnp.float32),
        lax.psum_scatter(
            grad_value_all.astype(jnp.bfloat16), "seq", scatter_dimension=1, tiled=True
        ).astype(jnp.float32),
    )
    query_low = grad_query_all.astype(jnp.bfloat16)
    key_low = key_grads.reshape(token_count, model_width).astype(jnp.bfloat16)
    value_low = value_grads.reshape(token_count, model_width).astype(jnp.bfloat16)
    grad_key_rel = jax.ops.segment_sum(grad_bucket_keys, reversed_buckets, num_segments=table_rows)
    grad_query_rel = jax.ops.segment_sum(
        grad_bucket_queries, reversed_buckets, num_segments=table_rows
    )
    query_token_part = matmul("td,te->de", tokens, query_low)
    query_bias_token = jnp.sum(query_low.astype(jnp.float32), axis=0)
    key_token_part = matmul("td,te->de", tokens, key_low)
    value_weight_part = matmul("td,te->de", tokens, value_low)
    value_bias_part = jnp.sum(value_low.astype(jnp.float32), axis=0)
    grad_input = (
        grad_sum1
        + matmul("te,de->td", query_low, query_back)
        + matmul("te,de->td", key_low, key_back)
        + matmul("te,de->td", value_low, value_back)
    )
    input_grad = grad_input.astype(jnp.bfloat16).reshape(row_count, window, model_width)
    key_rel_total, query_rel_total = lax.psum((grad_key_rel, grad_query_rel), ("fsdp", "seq"))
    attention_grads = (
        lax.psum_scatter(query_token_part, ("fsdp", "seq"), scatter_dimension=0, tiled=True),
        lax.psum_scatter(query_bias_token, ("fsdp", "seq"), scatter_dimension=0, tiled=True),
        lax.psum_scatter(key_token_part, ("fsdp", "seq"), scatter_dimension=0, tiled=True),
        lax.psum_scatter(value_weight_part, ("fsdp", "seq"), scatter_dimension=0, tiled=True),
        lax.psum_scatter(value_bias_part, ("fsdp", "seq"), scatter_dimension=0, tiled=True),
        lax.psum_scatter(output_weight_part, ("fsdp", "seq"), scatter_dimension=0, tiled=True),
        lax.psum_scatter(output_bias_part, ("fsdp", "seq"), scatter_dimension=0, tiled=True),
        lax.psum_scatter(grad_gain1, ("fsdp", "seq"), scatter_dimension=0, tiled=True),
        lax.psum_scatter(grad_shift1, ("fsdp", "seq"), scatter_dimension=0, tiled=True),
    )
    shard_rows = query_weight.shape[0]
    shard_start = lax.axis_index(("fsdp", "seq")) * shard_rows
    table_shard = relative_table.astype(jnp.float32)
    query_weight_grad = attention_grads[0] + precise("pd,pe->de", table_shard, query_rel_total)
    key_weight_grad = attention_grads[2] + precise("pd,pe->de", table_shard, key_rel_total)
    query_bias_grad = attention_grads[1] + jnp.sum(
        lax.dynamic_slice_in_dim(query_rel_total, shard_start, shard_rows, 1), axis=0
    )
    relative_table_grad = precise(
        "pe,de->pd", query_rel_total, query_weight.astype(jnp.float32)
    ) + precise("pe,de->pd", key_rel_total, key_weight.astype(jnp.float32))
    return (
        result,
        input_grad,
        query_weight_grad,
        query_bias_grad,
        key_weight_grad,
        attention_grads[3],
        attention_grads[4],
        attention_grads[5],
        attention_grads[6],
        attention_grads[7],
        attention_grads[8],
        feed_grads[0],
        feed_grads[1],
        feed_grads[2],
        feed_grads[3],
        feed_grads[4],
        feed_grads[5],
        relative_table_grad,
        correct_count,
    )


MESH = pl.DeviceIdType.MESH
F32 = jnp.float32
BF16 = jnp.bfloat16


def dot(left, right, left_dim=1, right_dim=0):
    return lax.dot_general(
        left, right, (((left_dim,), (right_dim,)), ((), ())), preferred_element_type=F32
    )


def low(value):
    return value.astype(BF16)


class Route:
    def __init__(self):
        chip = lax.axis_index("fsdp")
        self.core = lax.axis_index("seq")
        self.other = 1 - self.core
        self.chip = chip
        self.x = chip % 2
        self.y = (chip // 2) % 2
        self.z = chip // 4
        self.plane = chip % 4
        self.plane_x = self.plane + 1 - 2 * self.x
        self.plane_y = self.plane + 2 - 4 * self.y
        self.partner = (chip, self.other)
        self.at_x = (self.z * 4 + self.plane_x, self.core)
        self.at_y = (self.z * 4 + self.plane_y, self.core)

    def at_line(self, line):
        return (line * 4 + self.plane, self.core)

    def ahead(self, step):
        return (self.z + step) % LINE

    def behind(self, step):
        return (self.z + LINE - step) % LINE


def remote(source, target, send_sem, recv_sem, device):
    return pltpu.make_async_remote_copy(
        source, target, send_sem, recv_sem, device_id=device, device_id_type=MESH
    )


class Gather:
    def __init__(self, route, arrays, send, recv):
        self.r, self.arrays, self.send, self.recv = route, arrays, send, recv

    def copy(self, which, kind, send_at, recv_at, line, plane, device):
        block = self.arrays[which].at[line, plane]
        return remote(
            block,
            block,
            self.send.at[which, kind, send_at],
            self.recv.at[which, kind, recv_at],
            device,
        )

    def along_line(self, step):
        r = self.r
        return [
            self.copy(i, 0, step, r.z, r.z, r.plane, r.at_line(r.ahead(step)))
            for i in range(len(self.arrays))
        ]

    def to_sides(self, line):
        r = self.r
        return [
            self.copy(i, kind, line, line, line, r.plane, device)
            for i in range(len(self.arrays))
            for kind, device in ((1, r.at_x), (2, r.at_y))
        ]

    def to_corner(self, line):
        r = self.r
        return [
            self.copy(
                i,
                3,
                line,
                line,
                line,
                r.plane_y if i == 1 else r.plane_x,
                r.at_x if i == 1 else r.at_y,
            )
            for i in range(len(self.arrays))
        ]

    def start(self):
        for step in range(1, LINE):
            for copy in self.along_line(step):
                copy.start()
        for copy in self.to_sides(self.r.z):
            copy.start()

    def got_line(self, step):
        r = self.r
        line = r.behind(step)
        for i in range(len(self.arrays)):
            self.copy(i, 0, step, line, line, r.plane, r.at_line(line)).wait_recv()

    def got_sides(self, line):
        r = self.r
        for i in range(len(self.arrays)):
            self.copy(i, 1, line, line, line, r.plane_x, r.at_x).wait_recv()
            self.copy(i, 2, line, line, line, r.plane_y, r.at_y).wait_recv()

    def got_corner(self, line):
        r = self.r
        for i in range(len(self.arrays)):
            self.copy(i, 3, line, line, line, 3 - r.plane, r.at_y).wait_recv()

    def turn(self, step):
        self.got_line(step)
        for copy in self.to_sides(self.r.behind(step)):
            copy.start()
        self.corner(step - 1)

    def corner(self, step):
        line = self.r.behind(step) if step else self.r.z
        self.got_sides(line)
        for copy in self.to_corner(line):
            copy.start()

    def finish(self):
        for line in range(LINE):
            self.got_corner(line)

    def sent(self):
        for step in range(1, LINE):
            for copy in self.along_line(step):
                copy.wait_send()
        for line in range(LINE):
            for copy in self.to_sides(line) + self.to_corner(line):
                copy.wait_send()


class Scatter:
    def __init__(self, route, arrays, first, second, last, send, recv):
        self.r, self.arrays = route, arrays
        self.first, self.second, self.last = first, second, last
        self.send, self.recv = send, recv

    def side(self, i, k):
        r = self.r
        return (1 - r.x) + 2 * k if i == 0 else 2 * (1 - r.y) + k

    def kept(self, i, k):
        r = self.r
        return r.x + 2 * k if i == 0 else 2 * r.y + k

    def step_one(self, line, which=(0, 1)):
        r = self.r
        return [
            remote(
                self.arrays[i].at[line, self.side(i, k)],
                self.first[i].at[line, k],
                self.send.at[i, k, line],
                self.recv.at[i, k, line],
                r.at_x if i == 0 else r.at_y,
            )
            for i in which
            for k in (0, 1)
        ]

    def step_two(self, line):
        r = self.r
        return [
            remote(
                self.arrays[i].at[line, r.plane_y if i == 0 else r.plane_x],
                self.second[i].at[line],
                self.send.at[i, 2, line],
                self.recv.at[i, 2, line],
                r.at_y if i == 0 else r.at_x,
            )
            for i in (0, 1)
        ]

    def step_line(self, step):
        r = self.r
        line = r.ahead(step)
        return [
            remote(
                self.arrays[i].at[line, r.plane],
                self.last[i].at[r.z],
                self.send.at[i, 3, step],
                self.recv.at[i, 3, r.z],
                r.at_line(line),
            )
            for i in (0, 1)
        ]

    def one(self, step, which=(0, 1)):
        for copy in self.step_one(self.r.ahead(step), which):
            copy.start()

    def two(self, step):
        line = self.r.ahead(step)
        for copy in self.step_one(line):
            copy.wait_recv()
        for i in (0, 1):
            for k in (0, 1):
                at = self.arrays[i].at[line, self.kept(i, k)]
                at[...] = low(at[...].astype(F32) + self.first[i][line, k].astype(F32))
        for copy in self.step_two(line):
            copy.start()

    def three(self, step, last=False):
        line = self.r.ahead(step)
        for copy in self.step_two(line):
            copy.wait_recv()
        for i in (0, 1):
            at = self.arrays[i].at[line, self.r.plane]
            at[...] = low(at[...].astype(F32) + self.second[i][line].astype(F32))
        if not last:
            for copy in self.step_line(step):
                copy.start()

    def total(self, i):
        r = self.r
        value = self.arrays[i][r.z, r.plane].astype(F32)
        for step in range(1, LINE):
            value = value + self.last[i][r.behind(step)].astype(F32)
        return value

    def finish(self):
        r = self.r
        for step in range(1, LINE):
            line = r.behind(step)
            for i in (0, 1):
                remote(
                    self.arrays[i].at[line, r.plane],
                    self.last[i].at[line],
                    self.send.at[i, 3, step],
                    self.recv.at[i, 3, line],
                    r.at_line(line),
                ).wait_recv()

    def sent(self):
        for line in range(LINE):
            for copy in self.step_one(line) + self.step_two(line):
                copy.wait_send()
        for step in range(1, LINE):
            for copy in self.step_line(step):
                copy.wait_send()


def loop(count, body):
    def step(index, carry):
        body(index)
        return carry

    lax.fori_loop(0, count, step, 0)


def aligned(index, size):
    return pl.ds(pl.multiple_of(index * size, size), size)


def erf_parts(value):
    tail = lax.erf(value * np.float32(0.5**0.5))
    half = 0.5 * (1.0 + tail)
    density = jnp.exp(value * value * -0.5) * np.float32((2.0 * np.pi) ** -0.5)
    return value * half, half + value * density


def norm(values, gain, shift):
    average = jnp.mean(values, axis=-1, keepdims=True)
    centred = values - average
    variance = jnp.mean(centred * centred, axis=-1, keepdims=True)
    inverse = lax.rsqrt(variance + EPSILON)
    normed = centred * inverse
    return normed * gain + shift, normed, inverse


def norm_pull(upstream, normed, inverse, gain):
    scaled_up = upstream * gain
    first_mean = jnp.mean(scaled_up, axis=-1, keepdims=True)
    second_mean = jnp.mean(scaled_up * normed, axis=-1, keepdims=True)
    return inverse * (scaled_up - first_mean - normed * second_mean)


def layer_kernel(names, *refs):
    b = dict(zip(names, refs))
    at = type("Refs", (), b)
    r = Route()
    core, other = r.core, r.other
    own_rows = aligned(core, 256)
    other_rows = aligned(other, 256)
    score_scale = np.float32((3.0 * HEAD) ** (-0.5))

    barrier = pltpu.get_barrier_semaphore()
    friends = [r.partner, r.at_x, r.at_y] + [r.at_line(r.ahead(k)) for k in range(1, LINE)]
    for device in friends:
        pl.semaphore_signal(barrier, inc=1, device_id=device, device_id_type=MESH)

    waiting = []

    def swap(slot, source, target):
        copy = remote(source, target, at.swap_send.at[slot], at.swap_recv.at[slot], r.partner)
        copy.start()
        waiting.append(copy)
        return copy

    gather_one = Gather(r, (at.gat_a, at.gat_b, at.gat_s), at.ga_send, at.ga_recv)
    gather_two = Gather(r, (at.gat_1, at.gat_2), at.gf_send, at.gf_recv)

    at.sums[...] = jnp.zeros_like(at.sums)
    right = (at.predicted[...] == at.labels[...]).astype(F32)
    at.sums[10:11, :] = jnp.broadcast_to(jnp.sum(right, axis=1, keepdims=True), (1, 768))
    pl.semaphore_wait(barrier, len(friends))

    half = aligned(other, 384)
    arrive = [
        swap(0, at.key_w.at[:, half], at.come_a.at[:, pl.ds(0, 384)]),
        swap(1, at.value_w.at[:, half], at.come_a.at[:, pl.ds(384, 384)]),
        swap(2, at.query_w.at[:, half], at.come_b.at[:, pl.ds(0, 384)]),
        swap(3, at.output_w.at[:, half], at.come_b.at[:, pl.ds(384, 384)]),
        swap(4, at.table_t.at[:, aligned(other, 256)], at.come_b.at[:, pl.ds(768, 256)]),
        swap(5, at.small, at.come_s),
    ]
    come_inner = swap(6, at.inner_w.at[other], at.come_1)
    come_x = swap(7, at.hidden, at.x_all.at[own_rows])
    place_x = pltpu.make_async_copy(at.hidden, at.x_all.at[own_rows], at.here.at[0])
    place_x.start()
    place_2 = pltpu.make_async_copy(at.outer_w, at.gat_2.at[r.z, r.plane], at.here.at[1])
    place_2.start()
    for copy in arrive:
        copy.wait_recv()

    def stack(mine, came):
        mine, came = mine.astype(F32), came.astype(F32)
        upper = jnp.where(core == 0, mine, came)
        lower = jnp.where(core == 0, came, mine)
        return low(jnp.concatenate([upper, lower], axis=0))

    mine_half = aligned(core, 384)
    at.gat_a[r.z, r.plane, :, 0:384] = stack(at.key_w[:, mine_half], at.come_a[:, 0:384])
    at.gat_a[r.z, r.plane, :, 384:768] = stack(at.value_w[:, mine_half], at.come_a[:, 384:768])
    at.gat_b[r.z, r.plane, :, 0:384] = stack(at.query_w[:, mine_half], at.come_b[:, 0:384])
    at.gat_b[r.z, r.plane, :, 384:768] = stack(at.output_w[:, mine_half], at.come_b[:, 384:768])
    at.gat_b[r.z, r.plane, :, 768:1024] = stack(
        at.table_t[:, aligned(core, 256)], at.come_b[:, 768:1024]
    )
    at.gat_s[r.z, r.plane, core] = at.small[...]
    at.gat_s[r.z, r.plane, other] = at.come_s[...]
    gather_one.start()
    come_inner.wait_recv()
    at.gat_1[r.z, r.plane] = stack(at.inner_w[core], at.come_1[...])
    place_2.wait()
    place_x.wait()
    come_x.wait_recv()
    at.x_turned[...] = at.x_all[...].T
    columns = lax.broadcasted_iota(jnp.int32, (512, 512), 1)
    at.one_hot[...] = low((at.bucket_col[...] == columns).astype(F32))
    flip_i = lax.broadcasted_iota(jnp.int32, (128, 128), 0)
    flip_j = lax.broadcasted_iota(jnp.int32, (128, 128), 1)
    at.flip[...] = low((flip_i + flip_j == 127).astype(F32))
    for table in (at.near_rows, at.far_rows):
        table[0:256, :] = jnp.zeros((256, 384), BF16)
        table[768:1024, :] = jnp.zeros((256, 384), BF16)
    for step in range(1, LINE):
        gather_one.turn(step)
    gather_one.corner(LINE - 1)
    gather_two.start()
    gather_one.finish()

    out_mine = at.gat_b.at[:, :, :, pl.ds(384, 384)]
    table_mine = at.gat_b.at[:, :, :, pl.ds(768, 256)]
    come_table = swap(8, table_mine, at.table_all.at[core])
    come_out = swap(9, out_mine, at.out_all.at[core])
    place_table = pltpu.make_async_copy(table_mine, at.table_all.at[core], at.here.at[0])
    place_table.start()
    place_out = pltpu.make_async_copy(out_mine, at.out_all.at[core], at.here.at[1])
    place_out.start()

    for line in range(LINE):
        for plane in range(4):
            chip = line * 4 + plane
            for which in range(2):
                device = 2 * chip + which
                tile = at.gat_s[line, plane, which].astype(F32)
                at.vectors[:, 24 * device : 24 * device + 24] = tile[0:8, 0:24]
            tile = at.gat_s[line, plane, core].astype(F32)
            at.inner_bias[0:1, 96 * chip : 96 * chip + 96] = tile[8:9, 0:96]

    def rows(value):
        return value.reshape(768, value.shape[-1])

    vector_half = aligned(core, 384)
    query_bias = at.vectors[0:1, vector_half]
    value_bias = at.vectors[1:2, vector_half]
    at.kvq[:, 0:384] = low(dot(at.x_all[...], rows(at.gat_a[:, :, :, 0:384])))
    at.kvq[:, 384:768] = low(dot(at.x_all[...], rows(at.gat_a[:, :, :, 384:768])) + value_bias)
    at.kvq[:, 768:1152] = low(dot(at.x_all[...], rows(at.gat_b[:, :, :, 0:384])) + query_bias)
    place_table.wait()
    come_table.wait_recv()
    for part in range(2):
        piece = pl.ds(256 * part, 256)
        table = rows(at.table_all[part])
        at.key_rel[piece, :] = low(dot(table, rows(at.gat_a[:, :, :, 0:384]), 0, 0))
        at.query_rel[piece, :] = low(dot(table, rows(at.gat_b[:, :, :, 0:384]), 0, 0) + query_bias)
    at.near_rows[256:768, :] = low(dot(at.one_hot[...], at.key_rel[...]))
    at.far_rows[256:768, :] = low(dot(at.one_hot[...], at.query_rel[...]))

    gather_two.turn(1)

    lanes = lax.broadcasted_iota(jnp.int32, (1, 128), 1) // HEAD
    no_score = np.float32(NEGATIVE)

    def forward_head(head):
        pair = aligned(head // 2, 128)
        key_lanes = pl.ds(pl.multiple_of((head // 2) * 128, 128), 128)
        value_lanes = pl.ds(pl.multiple_of(384 + (head // 2) * 128, 128), 128)
        query_lanes = pl.ds(pl.multiple_of(768 + (head // 2) * 128, 128), 128)
        mine = lanes == head % 2
        only = low(mine.astype(F32))
        keys = at.kvq[:, key_lanes]
        values = at.kvq[:, value_lanes]
        for block in range(4):
            piece = pl.ds(128 * block, 128)
            shifted = dot(
                at.kvq[piece, key_lanes] * only, at.far_rows[pl.ds(384 - 128 * block, 640), pair], 1, 1
            )
            at.far_scores[piece, :] = pltpu.roll(shifted, 0, 1, stride=1, stride_axis=0)[:, 128:640]
        for block in range(4):
            piece = pl.ds(128 * block, 128)
            queries = at.kvq[piece, query_lanes] * only
            shifted = dot(queries, at.near_rows[pl.ds(384 - 128 * block, 640), pair], 1, 1)
            summed = (
                dot(queries, keys, 1, 1)
                + pltpu.roll(shifted, 0, 1, stride=1, stride_axis=0)[:, 128:640]
                + at.far_scores[:, piece].T
            )
            masked = jnp.where(
                at.segment_col[piece, :] == at.segment_row[...], summed * score_scale, no_score
            )
            highest = jnp.max(masked, axis=-1, keepdims=True)
            expsum = jnp.exp(masked - highest)
            soft = expsum / jnp.sum(expsum, axis=-1, keepdims=True)
            at.soft[head, piece, :] = soft
            context = dot(low(soft), values)
            here = at.context.at[core, piece, pair]
            here[...] = low(jnp.where(mine, context, here[...].astype(F32)))

    def forward_pair(index):
        loop(2, lambda which: forward_head(2 * index + which))
        remote(
            at.context.at[core, :, aligned(index, 128)],
            at.context.at[core, :, aligned(index, 128)],
            at.context_send.at[index],
            at.context_recv.at[index],
            r.partner,
        ).start()

    loop(3, forward_pair)
    gather_two.turn(2)
    place_out.wait()
    come_out.wait_recv()
    for index in range(3):
        remote(
            at.context.at[other, :, pl.ds(128 * index, 128)],
            at.context.at[other, :, pl.ds(128 * index, 128)],
            at.context_send.at[index],
            at.context_recv.at[index],
            r.partner,
        ).wait_recv()

    def vector(index):
        return at.vectors[index : index + 1, :]

    for part in range(2):
        piece = pl.ds(384 * part, 384)
        weight = rows(at.out_all[part])
        at.wide[:, piece] = dot(at.context[0, own_rows, :], weight[0:384]) + dot(
            at.context[1, own_rows, :], weight[384:768]
        )

    def first_norm(index):
        piece = aligned(index, 64)
        token_rows = pl.ds(pl.multiple_of(core * 256 + index * 64, 64), 64)
        residual = at.x_all[token_rows, :].astype(F32) + at.wide[piece, :] + vector(2)
        out, normed, inverse = norm(residual, vector(3), vector(4))
        at.first_out[piece, :] = out
        at.first_normed[piece, :] = normed
        at.first_inverse[piece, :] = jnp.broadcast_to(inverse, (64, 128))
        at.first_low[token_rows, :] = low(out)

    loop(4, first_norm)
    come_first = swap(10, at.first_low.at[own_rows], at.first_low.at[own_rows])
    gather_two.turn(3)
    come_first.wait_recv()
    at.first_turned[...] = at.first_low[...].T
    gather_two.corner(LINE - 1)
    gather_two.finish()

    def inner_units(index):
        piece = aligned(index, 256)
        pre = dot(at.first_low[...], rows(at.gat_1[:, :, :, piece])) + at.inner_bias[0:1, piece]
        value, slope = erf_parts(pre)
        at.active[:, piece] = low(value)
        at.slope[:, piece] = slope

    loop(6, inner_units)

    def outer_half(rows_at, out):
        for part in range(3):
            piece = pl.ds(256 * part, 256)
            out[:, piece] = dot(
                at.active[rows_at, :], at.gat_2[:, :, :, piece].reshape(1536, 256)
            )

    outer_half(other_rows, at.part_send)
    come_outer = swap(11, at.part_send, at.part_recv)
    outer_half(own_rows, at.wide)
    come_outer.wait_recv()

    def second_norm(index):
        piece = aligned(index, 64)
        token_rows = pl.ds(pl.multiple_of(core * 256 + index * 64, 64), 64)
        total = at.first_out[piece, :] + at.wide[piece, :] + at.part_recv[piece, :] + vector(5)
        out, normed, inverse = norm(total, vector(6), vector(7))
        at.result[piece, :] = low(out)
        upstream = at.cotangent[piece, :].astype(F32)
        grad = norm_pull(upstream, normed, inverse, vector(6))
        at.grad_sum[piece, :] = grad
        rounded = low(grad)
        at.grad_outer[token_rows, :] = rounded
        at.sums[5:6, :] += jnp.sum(rounded.astype(F32), axis=0, keepdims=True)
        at.sums[6:7, :] += jnp.sum(upstream * normed, axis=0, keepdims=True)
        at.sums[7:8, :] += jnp.sum(upstream, axis=0, keepdims=True)

    loop(4, second_norm)
    come_grad = swap(12, at.grad_outer.at[own_rows], at.grad_outer.at[own_rows])
    scatter_two = Scatter(
        r, (at.grad_1, at.grad_2), (at.one_1, at.one_2), (at.two_1, at.two_2),
        (at.last_1, at.last_2), at.sf_send, at.sf_recv,
    )
    scatter_one = Scatter(
        r, (at.grad_a, at.grad_b), (at.one_a, at.one_b), (at.two_a, at.two_b),
        (at.last_a, at.last_b), at.sa_send, at.sa_recv,
    )
    come_grad.wait_recv()

    def outer_weight(index):
        units = aligned(index, 384)
        grad = dot(at.active[:, units], at.grad_outer[...], 0, 0)
        at.grad_2[index] = low(grad).reshape(4, 96, 768)

    loop(4, outer_weight)
    for step in (1, 2, 3, 0):
        scatter_two.one(step, (1,))

    def inner_grad(index):
        units = aligned(index, 384)
        grad = low(dot(at.grad_outer[...], at.gat_2[index].reshape(384, 768), 1, 1))
        pre = low(grad.astype(F32) * at.slope[:, units])
        at.grad_pre[:, units] = pre
        at.bias_inner[0:1, units] = jnp.sum(pre.astype(F32), axis=0, keepdims=True)
        at.grad_1[:, :, :, units] = low(dot(at.first_turned[...], pre)).reshape(LINE, 4, 48, 384)

    loop(4, inner_grad)
    for step in (1, 2, 3, 0):
        scatter_two.one(step, (0,))
    at.sums[8:9, :] = at.bias_inner[0:1, 0:768]
    at.sums[9:10, :] = at.bias_inner[0:1, 768:1536]

    def first_half(rows_at, out):
        for part in range(2):
            weight = at.gat_1[2 * part : 2 * part + 2].reshape(384, 1536)
            out[:, 384 * part : 384 * part + 384] = dot(at.grad_pre[rows_at, :], weight, 1, 1)

    first_half(other_rows, at.part_send2)
    come_grad_first = swap(13, at.part_send2, at.part_recv2)
    first_half(own_rows, at.wide)
    come_grad_first.wait_recv()

    def first_norm_back(index):
        piece = aligned(index, 64)
        token_rows = pl.ds(pl.multiple_of(core * 256 + index * 64, 64), 64)
        upstream = at.wide[piece, :] + at.part_recv2[piece, :] + at.grad_sum[piece, :]
        normed = at.first_normed[piece, :]
        grad = norm_pull(upstream, normed, at.first_inverse[piece, 0:1], vector(3))
        at.grad_sum[piece, :] = grad
        rounded = low(grad)
        at.grad_att[token_rows, :] = rounded
        at.sums[2:3, :] += jnp.sum(rounded.astype(F32), axis=0, keepdims=True)
        at.sums[3:4, :] += jnp.sum(upstream * normed, axis=0, keepdims=True)
        at.sums[4:5, :] += jnp.sum(upstream, axis=0, keepdims=True)

    loop(4, first_norm_back)
    come_att = swap(14, at.grad_att.at[own_rows], at.grad_att.at[own_rows])
    come_att.wait_recv()
    scatter_two.two(1)
    out_rows = pl.ds(pl.multiple_of(2 * core, 2), 2)
    weight_0 = at.out_all[0, out_rows].reshape(384, 384)
    weight_1 = at.out_all[1, out_rows].reshape(384, 384)
    at.grad_context[...] = low(
        dot(at.grad_att[:, 0:384], weight_0, 1, 1) + dot(at.grad_att[:, 384:768], weight_1, 1, 1)
    )
    for part in range(2):
        grad = dot(at.context[part], at.grad_att[:, aligned(core, 384)], 0, 0)
        at.grad_b[2 * part : 2 * part + 2, :, :, 384:768] = low(grad).reshape(2, 4, 48, 384)
    scatter_two.two(2)

    at.near_grad[...] = jnp.zeros_like(at.near_grad)
    at.far_grad[...] = jnp.zeros_like(at.far_grad)
    room = jnp.zeros((128, 128), BF16)

    def spread(flipped):
        return pltpu.roll(jnp.concatenate([flipped, room], axis=1), 1, 1, stride=1, stride_axis=0)

    def backward_head(head):
        pair = aligned(head // 2, 128)
        key_lanes = pl.ds(pl.multiple_of((head // 2) * 128, 128), 128)
        value_lanes = pl.ds(pl.multiple_of(384 + (head // 2) * 128, 128), 128)
        query_lanes = pl.ds(pl.multiple_of(768 + (head // 2) * 128, 128), 128)
        mine = lanes == head % 2
        only = low(mine.astype(F32))
        flip = at.flip[...]
        keys = at.kvq[:, key_lanes]
        queries = at.kvq[:, query_lanes]
        values = at.kvq[:, value_lanes]

        def merge(here, value):
            here[...] = low(jnp.where(mine, value, here[...].astype(F32)))

        for block in range(4):
            piece = pl.ds(128 * block, 128)
            window = pl.ds(384 - 128 * block, 640)
            soft = at.soft[head, piece, :]
            grad_soft = dot(at.grad_context[piece, pair] * only, values, 1, 1)
            inner = jnp.sum(soft * grad_soft, axis=-1, keepdims=True)
            grad_low = low(soft * (grad_soft - inner) * score_scale)
            at.grad_low[piece, :] = grad_low
            flipped = low(dot(flip, grad_low))
            near = spread(flipped)
            grad = low(dot(flipped, keys) + dot(near, at.near_rows[window, pair]))
            merge(at.grad_kvq.at[piece, query_lanes], dot(flip, grad))
            back = low(dot(flip, at.kvq[piece, query_lanes] * only))
            at.near_grad[window, pair] += dot(near, back, 0, 0)
        grad_context = at.grad_context[:, pair]
        for block in range(4):
            piece = pl.ds(128 * block, 128)
            window = pl.ds(384 - 128 * block, 640)
            flipped = low(dot(flip, at.grad_low[:, piece], 1, 1))
            far = spread(flipped)
            grad = low(dot(flipped, queries) + dot(far, at.far_rows[window, pair]))
            merge(at.grad_kvq.at[piece, key_lanes], dot(flip, grad))
            back = low(dot(flip, at.kvq[piece, key_lanes] * only))
            at.far_grad[window, pair] += dot(far, back, 0, 0)
            weights = low(at.soft[head, :, piece])
            merge(at.grad_kvq.at[piece, value_lanes], dot(weights, grad_context, 0, 0))

    def backward_pair(index):
        loop(2, lambda which: backward_head(2 * index + which))
        scatter_two.three(index + 1)

        @pl.when(index < 2)
        def _():
            scatter_two.two(index + 3)

    loop(3, backward_pair)
    scatter_two.three(0, True)

    grad_key_rel = dot(at.one_hot[...], low(at.near_grad[256:768, :]), 0, 0)
    grad_query_rel = dot(at.one_hot[...], low(at.far_grad[256:768, :]), 0, 0)
    at.key_rel[...] = low(grad_key_rel)
    at.query_rel[...] = low(grad_query_rel)

    def token_weight(kvq_at):
        return dot(at.x_turned[...], at.grad_kvq[:, kvq_at : kvq_at + 384])

    def table_weight(rel):
        return dot(rows(at.table_all[0]), rel[0:256, :]) + dot(rows(at.table_all[1]), rel[256:512, :])

    def shape_weight(value):
        return low(value).reshape(LINE, 4, 48, value.shape[-1])

    def table_half(which):
        piece = aligned(which, 256)
        return dot(rows(at.gat_b[:, :, :, 0:384]), at.query_rel[piece, :], 1, 1) + dot(
            rows(at.gat_a[:, :, :, 0:384]), at.key_rel[piece, :], 1, 1
        )

    at.table_send[...] = shape_weight(table_half(other))
    come_part = swap(15, at.table_send, at.table_recv)
    at.grad_a[:, :, :, 0:384] = shape_weight(token_weight(0) + table_weight(at.key_rel))
    at.grad_a[:, :, :, 384:768] = shape_weight(token_weight(384))
    for step in (1, 2, 3, 0):
        scatter_one.one(step, (0,))
    at.grad_b[:, :, :, 0:384] = shape_weight(token_weight(768) + table_weight(at.query_rel))
    own_table = table_half(core)
    come_part.wait_recv()
    at.grad_b[:, :, :, 768:1024] = shape_weight(own_table + rows(at.table_recv[...]).astype(F32))
    for step in (1, 2, 3, 0):
        scatter_one.one(step, (1,))

    at.sums[0:1, vector_half] = jnp.sum(
        at.grad_kvq[:, 768:1152].astype(F32), axis=0, keepdims=True
    ) + jnp.sum(at.far_grad[256:768, :], axis=0, keepdims=True)
    at.sums[1:2, vector_half] = jnp.sum(
        at.grad_kvq[:, 384:768].astype(F32), axis=0, keepdims=True
    )

    def exchange(stage, source, device):
        return remote(
            source, at.sums_come.at[stage], at.sums_send.at[stage], at.sums_recv.at[stage], device
        )

    stage_copies = [exchange(0, at.sums, r.partner)]
    stage_copies[0].start()

    def input_half(rows_at, out):
        for part in range(2):
            weight_a = at.gat_a[2 * part : 2 * part + 2].reshape(384, 768)
            weight_b = at.gat_b[2 * part : 2 * part + 2, :, :, 0:384].reshape(384, 384)
            out[:, 384 * part : 384 * part + 384] = dot(
                at.grad_kvq[rows_at, 0:768], weight_a, 1, 1
            ) + dot(at.grad_kvq[rows_at, 768:1152], weight_b, 1, 1)

    come_outer.wait_send()
    input_half(other_rows, at.part_send)
    come_input = swap(16, at.part_send, at.part_recv)

    stage_copies[0].wait_recv()
    lines = lax.broadcasted_iota(jnp.int32, (16, 1), 0)
    shared = jnp.where((lines == 8) | (lines == 9), 0.0, at.sums_come[0])
    at.sums_step[0] = at.sums[...] + shared
    stage_copies.append(exchange(1, at.sums_step.at[0], r.at_x))
    stage_copies[1].start()
    scatter_one.two(1)
    input_half(own_rows, at.wide)
    scatter_one.two(2)
    stage_copies[1].wait_recv()
    at.sums_step[1] = at.sums_step[0] + at.sums_come[1]
    stage_copies.append(exchange(2, at.sums_step.at[1], r.at_y))
    stage_copies[2].start()
    scatter_one.three(1)
    scatter_one.two(3)
    come_input.wait_recv()
    at.input_grad[...] = low(at.grad_sum[...] + at.wide[...] + at.part_recv[...])

    scatter_two.finish()
    at.d_outer[...] = scatter_two.total(1)
    inner_total = scatter_two.total(0)
    at.give_1[...] = inner_total.reshape(2, 24, 1536)
    swap(17, at.give_1.at[other], at.d_inner.at[core])
    at.d_inner[core] = at.give_1[core]

    scatter_one.three(2)
    scatter_one.two(0)
    stage_copies[2].wait_recv()
    at.sums_step[2] = at.sums_step[1] + at.sums_come[2]
    for step in range(1, LINE):
        copy = exchange(2 + step, at.sums_step.at[2], r.at_line(r.ahead(step)))
        copy.start()
        stage_copies.append(copy)
    scatter_one.three(3)
    scatter_one.three(0, True)
    for copy in stage_copies[3:]:
        copy.wait_recv()
    at.vector_grads[...] = (
        at.sums_step[2] + at.sums_come[3] + at.sums_come[4] + at.sums_come[5]
    )
    scatter_one.finish()
    at.give_a[...] = scatter_one.total(0).reshape(2, 24, 768)
    at.give_b[...] = scatter_one.total(1).reshape(2, 24, 1024)
    outs = (
        (at.give_a, 0, 384, at.d_key),
        (at.give_a, 384, 384, at.d_value),
        (at.give_b, 0, 384, at.d_query),
        (at.give_b, 384, 384, at.d_output),
        (at.give_b, 768, 256, at.d_table),
    )
    for slot, (give, start, width, out) in enumerate(outs):
        swap(18 + slot, give.at[other, :, pl.ds(start, width)], out.at[:, aligned(core, width)])
        out[:, aligned(core, width)] = give[core, :, start : start + width]
    for copy in waiting[17:]:
        copy.wait_recv()
    for copy in waiting:
        if copy is not come_outer:
            copy.wait_send()
    for copy in stage_copies:
        copy.wait_send()
    for index in range(3):
        remote(
            at.context.at[core, :, pl.ds(128 * index, 128)],
            at.context.at[core, :, pl.ds(128 * index, 128)],
            at.context_send.at[index],
            at.context_recv.at[index],
            r.partner,
        ).wait_send()
    for user in (gather_one, gather_two, scatter_two, scatter_one):
        user.sent()


OUTPUTS = dict(
    result=((256, 768), BF16),
    input_grad=((256, 768), BF16),
    d_query=((24, 768), F32),
    d_key=((24, 768), F32),
    d_value=((24, 768), F32),
    d_output=((24, 768), F32),
    d_table=((24, 512), F32),
    d_inner=((2, 24, 1536), F32),
    d_outer=((96, 768), F32),
    vector_grads=((16, 768), F32),
)
LINE = 4
BLOCKS = (LINE, 4, 48)
SCRATCH = dict(
    come_a=((24, 768), BF16),
    come_b=((24, 1024), BF16),
    come_s=((16, 128), BF16),
    come_1=((24, 1536), BF16),
    gat_a=(BLOCKS + (768,), BF16),
    gat_b=(BLOCKS + (1024,), BF16),
    gat_s=((LINE, 4, 2, 16, 128), BF16),
    gat_1=(BLOCKS + (1536,), BF16),
    gat_2=((LINE, 4, 96, 768), BF16),
    x_all=((512, 768), BF16),
    x_turned=((768, 512), BF16),
    one_hot=((512, 512), BF16),
    flip=((128, 128), BF16),
    near_rows=((1024, 384), BF16),
    far_rows=((1024, 384), BF16),
    near_grad=((1024, 384), F32),
    far_grad=((1024, 384), F32),
    key_rel=((512, 384), BF16),
    query_rel=((512, 384), BF16),
    table_all=((2,) + BLOCKS + (256,), BF16),
    out_all=((2,) + BLOCKS + (384,), BF16),
    vectors=((8, 768), F32),
    inner_bias=((8, 1536), F32),
    bias_inner=((8, 1536), F32),
    kvq=((512, 1152), BF16),
    grad_kvq=((512, 1152), BF16),
    far_scores=((512, 512), F32),
    grad_low=((512, 512), BF16),
    soft=((6, 512, 512), F32),
    context=((2, 512, 384), BF16),
    grad_context=((512, 384), BF16),
    wide=((256, 768), F32),
    first_out=((256, 768), F32),
    first_normed=((256, 768), F32),
    first_inverse=((256, 128), F32),
    first_low=((512, 768), BF16),
    first_turned=((768, 512), BF16),
    active=((512, 1536), BF16),
    slope=((512, 1536), F32),
    grad_pre=((512, 1536), BF16),
    part_send=((256, 768), F32),
    part_recv=((256, 768), F32),
    part_send2=((256, 768), F32),
    part_recv2=((256, 768), F32),
    grad_sum=((256, 768), F32),
    grad_outer=((512, 768), BF16),
    grad_att=((512, 768), BF16),
    table_send=(BLOCKS + (256,), BF16),
    table_recv=(BLOCKS + (256,), BF16),
    sums=((16, 768), F32),
    sums_step=((3, 16, 768), F32),
    sums_come=((6, 16, 768), F32),
    grad_1=(BLOCKS + (1536,), BF16),
    grad_2=((LINE, 4, 96, 768), BF16),
    one_1=((LINE, 2, 48, 1536), BF16),
    one_2=((LINE, 2, 96, 768), BF16),
    two_1=((LINE, 48, 1536), BF16),
    two_2=((LINE, 96, 768), BF16),
    last_1=((LINE, 48, 1536), BF16),
    last_2=((LINE, 96, 768), BF16),
    grad_a=(BLOCKS + (768,), BF16),
    grad_b=(BLOCKS + (1024,), BF16),
    one_a=((LINE, 2, 48, 768), BF16),
    one_b=((LINE, 2, 48, 1024), BF16),
    two_a=((LINE, 48, 768), BF16),
    two_b=((LINE, 48, 1024), BF16),
    last_a=((LINE, 48, 768), BF16),
    last_b=((LINE, 48, 1024), BF16),
    give_1=((2, 24, 1536), F32),
    give_a=((2, 24, 768), F32),
    give_b=((2, 24, 1024), F32),
)
SEMAPHORES = dict(
    swap_send=(23,),
    swap_recv=(23,),
    here=(2,),
    context_send=(3,),
    context_recv=(3,),
    ga_send=(3, 4, LINE),
    ga_recv=(3, 4, LINE),
    gf_send=(2, 4, LINE),
    gf_recv=(2, 4, LINE),
    sf_send=(2, 4, LINE),
    sf_recv=(2, 4, LINE),
    sa_send=(2, 4, LINE),
    sa_recv=(2, 4, LINE),
    sums_send=(6,),
    sums_recv=(6,),
)


def block_shards(
    hidden_in,
    query_weight,
    query_bias,
    key_weight,
    value_weight,
    value_bias,
    output_weight,
    output_bias,
    first_gain,
    first_shift,
    inner_weight,
    inner_bias,
    outer_weight,
    outer_bias,
    second_gain,
    second_shift,
    relative_table,
    segments,
    buckets,
    predicted,
    labels,
    cotangent,
):
    chips = 4 * LINE
    units = outer_weight.shape[0]
    inner_pair = (
        inner_weight.reshape(24, chips, 2, units).transpose(2, 0, 1, 3).reshape(2, 24, chips * units)
    )
    vectors = jnp.stack(
        [
            query_bias,
            value_bias,
            output_bias,
            first_gain,
            first_shift,
            outer_bias,
            second_gain,
            second_shift,
        ]
    )
    small = jnp.zeros((16, 128), BF16)
    small = small.at[0:8, 0:24].set(vectors).at[8, 0:units].set(inner_bias)
    inputs = dict(
        hidden=hidden_in[0],
        query_w=query_weight,
        key_w=key_weight,
        value_w=value_weight,
        output_w=output_weight,
        table_t=relative_table.T,
        inner_w=inner_pair,
        outer_w=outer_weight,
        small=small,
        segment_row=segments,
        segment_col=segments.reshape(512, 1),
        bucket_col=buckets[256:768][::-1].reshape(512, 1),
        predicted=predicted,
        labels=labels,
        cotangent=cotangent[0],
    )
    names = tuple(inputs) + tuple(OUTPUTS) + tuple(SCRATCH) + tuple(SEMAPHORES)
    vmem = pl.BlockSpec(memory_space=pltpu.VMEM)
    outs = pl.pallas_call(
        partial(layer_kernel, names),
        name="layer",
        out_shape=tuple(jax.ShapeDtypeStruct(*out) for out in OUTPUTS.values()),
        in_specs=[vmem] * len(inputs),
        out_specs=(vmem,) * len(OUTPUTS),
        scratch_shapes=[pltpu.VMEM(*spec) for spec in SCRATCH.values()]
        + [pltpu.SemaphoreType.DMA(shape) for shape in SEMAPHORES.values()],
        compiler_params=pltpu.CompilerParams(
            collective_id=0, has_side_effects=True, vmem_limit_bytes=67043328
        ),
    )(*inputs.values())
    got = type("Outs", (), dict(zip(OUTPUTS, outs)))
    chip = lax.axis_index("fsdp")
    core = lax.axis_index("seq")
    sums = got.vector_grads
    own = lax.dynamic_slice(sums, (0, (2 * chip + core) * 24), (8, 24))
    inner_bias_grad = lax.dynamic_slice(sums[8:10].reshape(1536), (chip * units,), (units,))
    d_inner = (
        got.d_inner.reshape(2, 24, chips, units).transpose(1, 2, 0, 3).reshape(24, 2 * chips * units)
    )
    return (
        got.result[None],
        got.input_grad[None],
        got.d_query,
        own[0],
        got.d_key,
        got.d_value,
        own[1],
        got.d_output,
        own[2],
        own[3],
        own[4],
        d_inner,
        inner_bias_grad,
        got.d_outer,
        own[5],
        own[6],
        own[7],
        got.d_table.T,
        sums[10, 0].astype(jnp.int32),
    )


def fits(mesh):
    return mesh.shape["fsdp"] == 4 * LINE and mesh.shape["seq"] == 2


def solution(mesh):
    return jax.shard_map(
        block_shards if fits(mesh) else shards,
        mesh=mesh,
        in_specs=(
            P("fsdp", "seq", None),
            P(("fsdp", "seq"), None),
            P(("fsdp", "seq")),
            P(("fsdp", "seq"), None),
            P(("fsdp", "seq"), None),
            P(("fsdp", "seq")),
            P(("fsdp", "seq"), None),
            P(("fsdp", "seq")),
            P(("fsdp", "seq")),
            P(("fsdp", "seq")),
            P(("fsdp", "seq"), None),
            P(("fsdp", "seq")),
            P(("fsdp", "seq"), None),
            P(("fsdp", "seq")),
            P(("fsdp", "seq")),
            P(("fsdp", "seq")),
            P(None, ("fsdp", "seq")),
            P("fsdp", None),
            P(),
            P("fsdp", "seq"),
            P("fsdp", "seq"),
            P("fsdp", "seq", None),
        ),
        out_specs=(
            P("fsdp", "seq", None),
            P("fsdp", "seq", None),
            P(("fsdp", "seq"), None),
            P(("fsdp", "seq")),
            P(("fsdp", "seq"), None),
            P(("fsdp", "seq"), None),
            P(("fsdp", "seq")),
            P(("fsdp", "seq"), None),
            P(("fsdp", "seq")),
            P(("fsdp", "seq")),
            P(("fsdp", "seq")),
            P(("fsdp", "seq"), None),
            P(("fsdp", "seq")),
            P(("fsdp", "seq"), None),
            P(("fsdp", "seq")),
            P(("fsdp", "seq")),
            P(("fsdp", "seq")),
            P(None, ("fsdp", "seq")),
            P(),
        ),
        check_vma=False,
    )
```

```python
from functools import partial

import jax
import jax.numpy as jnp
import numpy as np
from jax import lax
from jax.experimental import pallas as pl
from jax.experimental.pallas import tpu as pltpu
from jax.sharding import PartitionSpec as P

HEAD = 64


EPSILON = 1e-07
NEGATIVE = -1e30


def matmul(spec, left, right):
    return jnp.einsum(spec, left, right, preferred_element_type=jnp.float32)


def precise(spec, left, right):
    return jnp.einsum(spec, left, right, precision=lax.Precision.HIGHEST)


def skew_rows(scores_in, offset, columns):
    leading = scores_in.shape[:-2]
    row_count = scores_in.shape[-2]
    breadth = scores_in.shape[-1]
    flattened = scores_in.reshape(leading + (row_count * breadth,))
    flattened = jnp.concatenate(
        [flattened, jnp.zeros(leading + (2 * breadth,), scores_in.dtype)], axis=-1
    )
    selected = lax.dynamic_slice_in_dim(flattened, offset, row_count * (breadth - 1), len(leading))
    return selected.reshape(leading + (row_count, breadth - 1))[..., :columns]


def unskew_rows(values, offset, breadth):
    leading = values.shape[:-2]
    row_count = values.shape[-2]
    columns = values.shape[-1]
    padded = jnp.concatenate(
        [values, jnp.zeros(leading + (row_count, breadth - 1 - columns), values.dtype)], axis=-1
    )
    flattened = padded.reshape(leading + (row_count * (breadth - 1),))
    zero_room = jnp.zeros(leading + (row_count * breadth + 2 * breadth,), values.dtype)
    placed = lax.dynamic_update_slice_in_dim(zero_room, flattened, offset, len(leading))
    return placed[..., : row_count * breadth].reshape(leading + (row_count, breadth))


def layer_norm(values, gain, shift):
    average = jnp.mean(values, axis=-1, keepdims=True)
    centred = values - average
    variance = jnp.mean(centred * centred, axis=-1, keepdims=True)
    inverse = lax.rsqrt(variance + EPSILON)
    normed = centred * inverse
    return (normed * gain + shift, normed, inverse)


def norm_backward(upstream, normed, inverse, gain):
    scaled_up = upstream * gain
    first_mean = jnp.mean(scaled_up, axis=-1, keepdims=True)
    second_mean = jnp.mean(scaled_up * normed, axis=-1, keepdims=True)
    grad_in = inverse * (scaled_up - first_mean - normed * second_mean)
    return (grad_in, jnp.sum(upstream * normed, axis=0), jnp.sum(upstream, axis=0))


def shards(
    hidden_in,
    query_weight,
    query_bias,
    key_weight,
    value_weight,
    value_bias,
    output_weight,
    output_bias,
    first_gain,
    first_shift,
    inner_weight,
    inner_bias,
    outer_weight,
    outer_bias,
    second_gain,
    second_shift,
    relative_table,
    segments,
    buckets,
    predicted,
    labels,
    cotangent,
):
    row_count, window, model_width = hidden_in.shape
    length = segments.shape[1]
    distances = 2 * length - 1
    span = window + length - 1
    pair_width = 2 * HEAD
    pair_count = model_width // pair_width
    score_scale = (3.0 * HEAD) ** (-0.5)
    window_start = lax.axis_index("seq") * window
    near_start = length - window - window_start
    token_count = row_count * window
    attention_set = (
        lax.all_gather(query_weight, ("fsdp", "seq"), axis=0, tiled=True),
        lax.all_gather(query_bias, ("fsdp", "seq"), axis=0, tiled=True),
        lax.all_gather(key_weight, ("fsdp", "seq"), axis=0, tiled=True),
        lax.all_gather(value_weight, ("fsdp", "seq"), axis=0, tiled=True),
        lax.all_gather(value_bias, ("fsdp", "seq"), axis=0, tiled=True),
        lax.all_gather(output_weight, ("fsdp", "seq"), axis=0, tiled=True),
        lax.all_gather(output_bias, ("fsdp", "seq"), axis=0, tiled=True),
        lax.all_gather(first_gain, ("fsdp", "seq"), axis=0, tiled=True),
        lax.all_gather(first_shift, ("fsdp", "seq"), axis=0, tiled=True),
        lax.all_gather(relative_table, ("fsdp", "seq"), axis=1, tiled=True),
    )
    feed_set = (
        lax.all_gather(inner_weight, ("fsdp", "seq"), axis=0, tiled=True),
        lax.all_gather(inner_bias, ("fsdp", "seq"), axis=0, tiled=True),
        lax.all_gather(outer_weight, ("fsdp", "seq"), axis=0, tiled=True),
        lax.all_gather(outer_bias, ("fsdp", "seq"), axis=0, tiled=True),
        lax.all_gather(second_gain, ("fsdp", "seq"), axis=0, tiled=True),
        lax.all_gather(second_shift, ("fsdp", "seq"), axis=0, tiled=True),
    )
    (
        query_matrix,
        query_offset,
        key_matrix,
        value_matrix,
        value_offset,
        output_matrix,
        output_offset,
        gain_first,
        shift_first,
        table_full,
    ) = attention_set
    inner_matrix, inner_offset, outer_matrix, outer_offset, gain_second, shift_second = feed_set
    tokens = hidden_in.reshape(token_count, model_width)
    queries = (
        (matmul("td,de->te", tokens, query_matrix) + query_offset.astype(jnp.float32))
        .astype(jnp.bfloat16)
        .reshape(row_count, window, model_width)
    )
    keys_own = (
        matmul("td,de->te", tokens, key_matrix)
        .astype(jnp.bfloat16)
        .reshape(row_count, window, model_width)
    )
    values_own = (
        (matmul("td,de->te", tokens, value_matrix) + value_offset.astype(jnp.float32))
        .astype(jnp.bfloat16)
        .reshape(row_count, window, model_width)
    )
    keys_all, values_all = (
        lax.all_gather(keys_own, "seq", axis=1, tiled=True),
        lax.all_gather(values_own, "seq", axis=1, tiled=True),
    )
    key_rel = matmul("pd,de->pe", table_full, key_matrix).astype(jnp.bfloat16)
    query_rel = (
        matmul("pd,de->pe", table_full, query_matrix) + query_offset.astype(jnp.float32)
    ).astype(jnp.bfloat16)
    reversed_buckets = buckets[::-1]
    table_rows = table_full.shape[0]
    one_hot = (
        reversed_buckets[:, None] == jnp.arange(table_rows, dtype=jnp.int32)[None, :]
    ).astype(jnp.bfloat16)
    bucket_keys = matmul("dp,pe->de", one_hot, key_rel).astype(jnp.bfloat16)
    bucket_queries = matmul("dp,pe->de", one_hot, query_rel).astype(jnp.bfloat16)
    near_keys = lax.dynamic_slice_in_dim(bucket_keys, near_start, span, 0)
    far_queries = lax.dynamic_slice_in_dim(bucket_queries, window_start, span, 0)
    segment_own = lax.dynamic_slice_in_dim(segments, window_start, window, 1)
    same_doc = (segment_own[:, :, None] == segments[:, None, :])[:, None]

    def pair_scores(pair_index):
        column = pair_index * pair_width
        query_pair = lax.dynamic_slice_in_dim(queries, column, pair_width, 2).reshape(
            row_count, window, 2, HEAD
        )
        key_pair = lax.dynamic_slice_in_dim(keys_all, column, pair_width, 2).reshape(
            row_count, length, 2, HEAD
        )
        value_pair = lax.dynamic_slice_in_dim(values_all, column, pair_width, 2).reshape(
            row_count, length, 2, HEAD
        )
        bucketkeys = lax.dynamic_slice_in_dim(near_keys, column, pair_width, 1).reshape(
            span, 2, HEAD
        )
        bucketqueries = lax.dynamic_slice_in_dim(far_queries, column, pair_width, 1).reshape(
            span, 2, HEAD
        )
        content = matmul("rihe,rjhe->rhij", query_pair, key_pair)
        near_scores = matmul("rihe,dhe->rhid", query_pair, bucketkeys)
        far_scores = matmul("rjhe,dhe->rhjd", key_pair, bucketqueries)
        to_position = skew_rows(near_scores, window - 1, length)
        from_position = jnp.swapaxes(skew_rows(far_scores, length - 1, window), 2, 3)
        summed = content + to_position + from_position
        masked = jnp.where(same_doc, summed * score_scale, NEGATIVE)
        return (masked, query_pair, key_pair, value_pair, bucketkeys, bucketqueries)

    def attend_pair(pair_index):
        masked, query_pair, key_pair, value_pair, bucketkeys, bucketqueries = pair_scores(
            pair_index
        )
        highest = jnp.max(masked, axis=-1, keepdims=True)
        expsum = jnp.exp(masked - highest)
        totals = jnp.sum(expsum, axis=-1, keepdims=True)
        weights_soft = (expsum / totals).astype(jnp.bfloat16)
        context_pair = matmul("rhij,rjhe->rihe", weights_soft, value_pair).astype(jnp.bfloat16)
        return (
            context_pair.reshape(row_count, window, pair_width),
            (highest + jnp.log(totals))[..., 0],
        )

    context_parts, log_totals = lax.map(attend_pair, jnp.arange(pair_count, dtype=jnp.int32))
    context = jnp.moveaxis(context_parts, 0, 2).reshape(token_count, model_width)
    attention_out = matmul("te,ed->td", context, output_matrix) + output_offset.astype(jnp.float32)
    residual_one = tokens.astype(jnp.float32) + attention_out
    first_out, first_normed, first_inverse = layer_norm(
        residual_one, gain_first.astype(jnp.float32), shift_first.astype(jnp.float32)
    )
    first_low = first_out.astype(jnp.bfloat16)
    inner_pre = matmul("td,df->tf", first_low, inner_matrix) + inner_offset.astype(jnp.float32)
    activated = jax.nn.gelu(inner_pre, approximate=False).astype(jnp.bfloat16)
    outer_out = matmul("tf,fd->td", activated, outer_matrix) + outer_offset.astype(jnp.float32)
    final_out, final_normed, final_inverse = layer_norm(
        first_out + outer_out, gain_second.astype(jnp.float32), shift_second.astype(jnp.float32)
    )
    result = final_out.astype(jnp.bfloat16).reshape(row_count, window, model_width)
    correct_count = lax.psum(jnp.sum((predicted == labels).astype(jnp.int32)), ("fsdp", "seq"))
    regathered = attention_set + feed_set
    (
        query_back,
        query_offset_back,
        key_back,
        value_back,
        value_offset_back,
        output_back,
        output_offset_back,
        gain_first_back,
        shift_first_back,
        table_back,
        inner_back,
        inner_offset_back,
        outer_back,
        outer_offset_back,
        gain_second_back,
        shift_second_back,
    ) = regathered
    upstream = cotangent.reshape(token_count, model_width).astype(jnp.float32)
    grad_sum2, grad_gain2, grad_shift2 = norm_backward(
        upstream, final_normed, final_inverse, gain_second_back.astype(jnp.float32)
    )
    grad_outer = grad_sum2.astype(jnp.bfloat16)
    outer_bias_part = jnp.sum(grad_outer.astype(jnp.float32), axis=0)
    outer_weight_part = matmul("tf,td->fd", activated, grad_outer)
    grad_act = matmul("td,fd->tf", grad_outer, outer_back).astype(jnp.bfloat16)
    _, gelu_back = jax.vjp(partial(jax.nn.gelu, approximate=False), inner_pre)
    grad_inner = gelu_back(grad_act.astype(jnp.float32))[0].astype(jnp.bfloat16)
    inner_bias_part = jnp.sum(grad_inner.astype(jnp.float32), axis=0)
    inner_weight_part = matmul("td,tf->df", first_low, grad_inner)
    grad_first = matmul("tf,df->td", grad_inner, inner_back) + grad_sum2
    feed_grads = (
        lax.psum_scatter(inner_weight_part, ("fsdp", "seq"), scatter_dimension=0, tiled=True),
        lax.psum_scatter(inner_bias_part, ("fsdp", "seq"), scatter_dimension=0, tiled=True),
        lax.psum_scatter(outer_weight_part, ("fsdp", "seq"), scatter_dimension=0, tiled=True),
        lax.psum_scatter(outer_bias_part, ("fsdp", "seq"), scatter_dimension=0, tiled=True),
        lax.psum_scatter(grad_gain2, ("fsdp", "seq"), scatter_dimension=0, tiled=True),
        lax.psum_scatter(grad_shift2, ("fsdp", "seq"), scatter_dimension=0, tiled=True),
    )
    grad_sum1, grad_gain1, grad_shift1 = norm_backward(
        grad_first, first_normed, first_inverse, gain_first_back.astype(jnp.float32)
    )
    grad_attention = grad_sum1.astype(jnp.bfloat16)
    output_bias_part = jnp.sum(grad_attention.astype(jnp.float32), axis=0)
    output_weight_part = matmul("te,td->ed", context, grad_attention)
    grad_context = (
        matmul("td,ed->te", grad_attention, output_back)
        .astype(jnp.bfloat16)
        .reshape(row_count, window, model_width)
    )

    def attend_back(pieces):
        pair_index, log_total = pieces
        masked, query_pair, key_pair, value_pair, bucketkeys, bucketqueries = pair_scores(
            pair_index
        )
        probability = jnp.exp(masked - log_total[..., None])
        grad_context_pair = lax.dynamic_slice_in_dim(
            grad_context, pair_index * pair_width, pair_width, 2
        ).reshape(row_count, window, 2, HEAD)
        grad_soft = matmul("rihe,rjhe->rhij", grad_context_pair, value_pair)
        grad_scores = probability * (
            grad_soft - jnp.sum(probability * grad_soft, axis=-1, keepdims=True)
        )
        grad_low = (grad_scores * score_scale).astype(jnp.bfloat16)
        grad_value = matmul("rhij,rihe->rjhe", probability.astype(jnp.bfloat16), grad_context_pair)
        grad_near = unskew_rows(grad_low, window - 1, span)
        grad_far = unskew_rows(jnp.swapaxes(grad_low, 2, 3), length - 1, span)
        grad_query = matmul("rhij,rjhe->rihe", grad_low, key_pair) + matmul(
            "rhid,dhe->rihe", grad_near, bucketkeys
        )
        grad_key = matmul("rhij,rihe->rjhe", grad_low, query_pair) + matmul(
            "rhjd,dhe->rjhe", grad_far, bucketqueries
        )
        grad_bkeys = matmul("rhid,rihe->dhe", grad_near, query_pair)
        grad_bqueries = matmul("rhjd,rjhe->dhe", grad_far, key_pair)
        return (
            grad_query.reshape(row_count, window, pair_width),
            grad_key.reshape(row_count, length, pair_width),
            grad_value.reshape(row_count, length, pair_width),
            grad_bkeys.reshape(span, pair_width),
            grad_bqueries.reshape(span, pair_width),
        )

    query_parts, key_parts, value_parts, bkey_parts, bquery_parts = lax.map(
        attend_back, (jnp.arange(pair_count, dtype=jnp.int32), log_totals)
    )
    grad_query_all = jnp.moveaxis(query_parts, 0, 2).reshape(token_count, model_width)
    grad_key_all = jnp.moveaxis(key_parts, 0, 2).reshape(row_count, length, model_width)
    grad_value_all = jnp.moveaxis(value_parts, 0, 2).reshape(row_count, length, model_width)
    near_grads = jnp.moveaxis(bkey_parts, 0, 1).reshape(span, model_width)
    far_grads = jnp.moveaxis(bquery_parts, 0, 1).reshape(span, model_width)
    grad_bucket_keys = lax.dynamic_update_slice_in_dim(
        jnp.zeros((distances, model_width), jnp.float32), near_grads, near_start, 0
    )
    grad_bucket_queries = lax.dynamic_update_slice_in_dim(
        jnp.zeros((distances, model_width), jnp.float32), far_grads, window_start, 0
    )
    key_grads, value_grads = (
        lax.psum_scatter(
            grad_key_all.astype(jnp.bfloat16), "seq", scatter_dimension=1, tiled=True
        ).astype(jnp.float32),
        lax.psum_scatter(
            grad_value_all.astype(jnp.bfloat16), "seq", scatter_dimension=1, tiled=True
        ).astype(jnp.float32),
    )
    query_low = grad_query_all.astype(jnp.bfloat16)
    key_low = key_grads.reshape(token_count, model_width).astype(jnp.bfloat16)
    value_low = value_grads.reshape(token_count, model_width).astype(jnp.bfloat16)
    grad_key_rel = jax.ops.segment_sum(grad_bucket_keys, reversed_buckets, num_segments=table_rows)
    grad_query_rel = jax.ops.segment_sum(
        grad_bucket_queries, reversed_buckets, num_segments=table_rows
    )
    query_token_part = matmul("td,te->de", tokens, query_low)
    query_bias_token = jnp.sum(query_low.astype(jnp.float32), axis=0)
    key_token_part = matmul("td,te->de", tokens, key_low)
    value_weight_part = matmul("td,te->de", tokens, value_low)
    value_bias_part = jnp.sum(value_low.astype(jnp.float32), axis=0)
    grad_input = (
        grad_sum1
        + matmul("te,de->td", query_low, query_back)
        + matmul("te,de->td", key_low, key_back)
        + matmul("te,de->td", value_low, value_back)
    )
    input_grad = grad_input.astype(jnp.bfloat16).reshape(row_count, window, model_width)
    key_rel_total, query_rel_total = lax.psum((grad_key_rel, grad_query_rel), ("fsdp", "seq"))
    attention_grads = (
        lax.psum_scatter(query_token_part, ("fsdp", "seq"), scatter_dimension=0, tiled=True),
        lax.psum_scatter(query_bias_token, ("fsdp", "seq"), scatter_dimension=0, tiled=True),
        lax.psum_scatter(key_token_part, ("fsdp", "seq"), scatter_dimension=0, tiled=True),
        lax.psum_scatter(value_weight_part, ("fsdp", "seq"), scatter_dimension=0, tiled=True),
        lax.psum_scatter(value_bias_part, ("fsdp", "seq"), scatter_dimension=0, tiled=True),
        lax.psum_scatter(output_weight_part, ("fsdp", "seq"), scatter_dimension=0, tiled=True),
        lax.psum_scatter(output_bias_part, ("fsdp", "seq"), scatter_dimension=0, tiled=True),
        lax.psum_scatter(grad_gain1, ("fsdp", "seq"), scatter_dimension=0, tiled=True),
        lax.psum_scatter(grad_shift1, ("fsdp", "seq"), scatter_dimension=0, tiled=True),
    )
    shard_rows = query_weight.shape[0]
    shard_start = lax.axis_index(("fsdp", "seq")) * shard_rows
    table_shard = relative_table.astype(jnp.float32)
    query_weight_grad = attention_grads[0] + precise("pd,pe->de", table_shard, query_rel_total)
    key_weight_grad = attention_grads[2] + precise("pd,pe->de", table_shard, key_rel_total)
    query_bias_grad = attention_grads[1] + jnp.sum(
        lax.dynamic_slice_in_dim(query_rel_total, shard_start, shard_rows, 1), axis=0
    )
    relative_table_grad = precise(
        "pe,de->pd", query_rel_total, query_weight.astype(jnp.float32)
    ) + precise("pe,de->pd", key_rel_total, key_weight.astype(jnp.float32))
    return (
        result,
        input_grad,
        query_weight_grad,
        query_bias_grad,
        key_weight_grad,
        attention_grads[3],
        attention_grads[4],
        attention_grads[5],
        attention_grads[6],
        attention_grads[7],
        attention_grads[8],
        feed_grads[0],
        feed_grads[1],
        feed_grads[2],
        feed_grads[3],
        feed_grads[4],
        feed_grads[5],
        relative_table_grad,
        correct_count,
    )


MESH = pl.DeviceIdType.MESH
F32 = jnp.float32
BF16 = jnp.bfloat16


def dot(left, right, left_dim=1, right_dim=0):
    return lax.dot_general(
        left, right, (((left_dim,), (right_dim,)), ((), ())), preferred_element_type=F32
    )


def low(value):
    return value.astype(BF16)


class Route:
    def __init__(self):
        chip = lax.axis_index("fsdp")
        self.core = lax.axis_index("seq")
        self.other = 1 - self.core
        self.chip = chip
        self.x = chip % 2
        self.y = (chip // 2) % 2
        self.z = chip // 4
        self.plane = chip % 4
        self.plane_x = self.plane + 1 - 2 * self.x
        self.plane_y = self.plane + 2 - 4 * self.y
        self.partner = (chip, self.other)
        self.at_x = (self.z * 4 + self.plane_x, self.core)
        self.at_y = (self.z * 4 + self.plane_y, self.core)

    def at_line(self, line):
        return (line * 4 + self.plane, self.core)

    def ahead(self, step):
        return (self.z + step) % LINE

    def behind(self, step):
        return (self.z + LINE - step) % LINE


def remote(source, target, send_sem, recv_sem, device):
    return pltpu.make_async_remote_copy(
        source, target, send_sem, recv_sem, device_id=device, device_id_type=MESH
    )


class Gather:
    def __init__(self, route, arrays, send, recv):
        self.r, self.arrays, self.send, self.recv = route, arrays, send, recv

    def copy(self, which, kind, send_at, recv_at, line, plane, device):
        block = self.arrays[which].at[line, plane]
        return remote(
            block,
            block,
            self.send.at[which, kind, send_at],
            self.recv.at[which, kind, recv_at],
            device,
        )

    def along_line(self, step):
        r = self.r
        return [
            self.copy(i, 0, step, r.z, r.z, r.plane, r.at_line(r.ahead(step)))
            for i in range(len(self.arrays))
        ]

    def to_sides(self, line):
        r = self.r
        return [
            self.copy(i, kind, line, line, line, r.plane, device)
            for i in range(len(self.arrays))
            for kind, device in ((1, r.at_x), (2, r.at_y))
        ]

    def to_corner(self, line):
        r = self.r
        return [
            self.copy(
                i,
                3,
                line,
                line,
                line,
                r.plane_y if i == 1 else r.plane_x,
                r.at_x if i == 1 else r.at_y,
            )
            for i in range(len(self.arrays))
        ]

    def start(self):
        for step in range(1, LINE):
            for copy in self.along_line(step):
                copy.start()
        for copy in self.to_sides(self.r.z):
            copy.start()

    def got_line(self, step):
        r = self.r
        line = r.behind(step)
        for i in range(len(self.arrays)):
            self.copy(i, 0, step, line, line, r.plane, r.at_line(line)).wait_recv()

    def got_sides(self, line):
        r = self.r
        for i in range(len(self.arrays)):
            self.copy(i, 1, line, line, line, r.plane_x, r.at_x).wait_recv()
            self.copy(i, 2, line, line, line, r.plane_y, r.at_y).wait_recv()

    def got_corner(self, line):
        r = self.r
        for i in range(len(self.arrays)):
            self.copy(i, 3, line, line, line, 3 - r.plane, r.at_y).wait_recv()

    def turn(self, step):
        self.got_line(step)
        for copy in self.to_sides(self.r.behind(step)):
            copy.start()
        self.corner(step - 1)

    def corner(self, step):
        line = self.r.behind(step) if step else self.r.z
        self.got_sides(line)
        for copy in self.to_corner(line):
            copy.start()

    def finish(self):
        for line in range(LINE):
            self.got_corner(line)

    def sent(self):
        for step in range(1, LINE):
            for copy in self.along_line(step):
                copy.wait_send()
        for line in range(LINE):
            for copy in self.to_sides(line) + self.to_corner(line):
                copy.wait_send()


class Scatter:
    def __init__(self, route, arrays, first, second, last, send, recv):
        self.r, self.arrays = route, arrays
        self.first, self.second, self.last = first, second, last
        self.send, self.recv = send, recv

    def side(self, i, k):
        r = self.r
        return (1 - r.x) + 2 * k if i == 0 else 2 * (1 - r.y) + k

    def kept(self, i, k):
        r = self.r
        return r.x + 2 * k if i == 0 else 2 * r.y + k

    def step_one(self, line, which=(0, 1)):
        r = self.r
        return [
            remote(
                self.arrays[i].at[line, self.side(i, k)],
                self.first[i].at[line, k],
                self.send.at[i, k, line],
                self.recv.at[i, k, line],
                r.at_x if i == 0 else r.at_y,
            )
            for i in which
            for k in (0, 1)
        ]

    def step_two(self, line):
        r = self.r
        return [
            remote(
                self.arrays[i].at[line, r.plane_y if i == 0 else r.plane_x],
                self.second[i].at[line],
                self.send.at[i, 2, line],
                self.recv.at[i, 2, line],
                r.at_y if i == 0 else r.at_x,
            )
            for i in (0, 1)
        ]

    def step_line(self, step):
        r = self.r
        line = r.ahead(step)
        return [
            remote(
                self.arrays[i].at[line, r.plane],
                self.last[i].at[r.z],
                self.send.at[i, 3, step],
                self.recv.at[i, 3, r.z],
                r.at_line(line),
            )
            for i in (0, 1)
        ]

    def one(self, step, which=(0, 1)):
        for copy in self.step_one(self.r.ahead(step), which):
            copy.start()

    def two(self, step):
        line = self.r.ahead(step)
        for copy in self.step_one(line):
            copy.wait_recv()
        for i in (0, 1):
            for k in (0, 1):
                at = self.arrays[i].at[line, self.kept(i, k)]
                at[...] = low(at[...].astype(F32) + self.first[i][line, k].astype(F32))
        for copy in self.step_two(line):
            copy.start()

    def three(self, step, last=False):
        line = self.r.ahead(step)
        for copy in self.step_two(line):
            copy.wait_recv()
        for i in (0, 1):
            at = self.arrays[i].at[line, self.r.plane]
            at[...] = low(at[...].astype(F32) + self.second[i][line].astype(F32))
        if not last:
            for copy in self.step_line(step):
                copy.start()

    def total(self, i):
        r = self.r
        value = self.arrays[i][r.z, r.plane].astype(F32)
        for step in range(1, LINE):
            value = value + self.last[i][r.behind(step)].astype(F32)
        return value

    def finish(self):
        r = self.r
        for step in range(1, LINE):
            line = r.behind(step)
            for i in (0, 1):
                remote(
                    self.arrays[i].at[line, r.plane],
                    self.last[i].at[line],
                    self.send.at[i, 3, step],
                    self.recv.at[i, 3, line],
                    r.at_line(line),
                ).wait_recv()

    def sent(self):
        for line in range(LINE):
            for copy in self.step_one(line) + self.step_two(line):
                copy.wait_send()
        for step in range(1, LINE):
            for copy in self.step_line(step):
                copy.wait_send()


def loop(count, body):
    def step(index, carry):
        body(index)
        return carry

    lax.fori_loop(0, count, step, 0)


def aligned(index, size):
    return pl.ds(pl.multiple_of(index * size, size), size)


def erf_parts(value):
    tail = lax.erf(value * np.float32(0.5**0.5))
    half = 0.5 * (1.0 + tail)
    density = jnp.exp(value * value * -0.5) * np.float32((2.0 * np.pi) ** -0.5)
    return value * half, half + value * density


def norm(values, gain, shift):
    average = jnp.mean(values, axis=-1, keepdims=True)
    centred = values - average
    variance = jnp.mean(centred * centred, axis=-1, keepdims=True)
    inverse = lax.rsqrt(variance + EPSILON)
    normed = centred * inverse
    return normed * gain + shift, normed, inverse


def norm_pull(upstream, normed, inverse, gain):
    scaled_up = upstream * gain
    first_mean = jnp.mean(scaled_up, axis=-1, keepdims=True)
    second_mean = jnp.mean(scaled_up * normed, axis=-1, keepdims=True)
    return inverse * (scaled_up - first_mean - normed * second_mean)


def layer_kernel(names, *refs):
    b = dict(zip(names, refs))
    at = type("Refs", (), b)
    r = Route()
    core, other = r.core, r.other
    own_rows = aligned(core, 256)
    other_rows = aligned(other, 256)
    score_scale = np.float32((3.0 * HEAD) ** (-0.5))

    barrier = pltpu.get_barrier_semaphore()
    friends = [r.partner, r.at_x, r.at_y] + [r.at_line(r.ahead(k)) for k in range(1, LINE)]
    for device in friends:
        pl.semaphore_signal(barrier, inc=1, device_id=device, device_id_type=MESH)

    waiting = []

    def swap(slot, source, target):
        copy = remote(source, target, at.swap_send.at[slot], at.swap_recv.at[slot], r.partner)
        copy.start()
        waiting.append(copy)
        return copy

    gather_one = Gather(r, (at.gat_a, at.gat_b, at.gat_s), at.ga_send, at.ga_recv)
    gather_two = Gather(r, (at.gat_1, at.gat_2), at.gf_send, at.gf_recv)

    at.sums[...] = jnp.zeros_like(at.sums)
    at.small_wide[...] = jnp.zeros_like(at.small_wide)
    small_rows = (
        at.query_b, at.value_b, at.output_b, at.gain_1, at.shift_1, at.outer_b, at.gain_2, at.shift_2,
        at.inner_b,
    )
    for index, row in enumerate(small_rows):
        at.small_wide[index : index + 1, 0 : row.shape[1]] = row[...].astype(F32)
    at.small[...] = low(at.small_wide[...])
    right = (at.predicted[...] == at.labels[...]).astype(F32)
    at.sums[10:11, :] = jnp.broadcast_to(jnp.sum(right, axis=1, keepdims=True), (1, 768))
    pl.semaphore_wait(barrier, len(friends))

    half = aligned(other, 384)
    arrive = [
        swap(0, at.key_w.at[:, half], at.come_a.at[:, pl.ds(0, 384)]),
        swap(1, at.value_w.at[:, half], at.come_a.at[:, pl.ds(384, 384)]),
        swap(2, at.query_w.at[:, half], at.come_b.at[:, pl.ds(0, 384)]),
        swap(3, at.output_w.at[:, half], at.come_b.at[:, pl.ds(384, 384)]),
        swap(4, at.table_t.at[:, aligned(other, 256)], at.come_b.at[:, pl.ds(768, 256)]),
        swap(5, at.small, at.come_s),
    ]
    come_x = swap(7, at.hidden, at.x_all.at[own_rows])
    place_x = pltpu.make_async_copy(at.hidden, at.x_all.at[own_rows], at.here.at[0])
    place_x.start()
    place_2 = pltpu.make_async_copy(at.outer_w, at.gat_2.at[r.z, r.plane], at.here.at[1])
    place_2.start()
    for copy in arrive:
        copy.wait_recv()

    def stack(mine, came):
        mine, came = mine.astype(F32), came.astype(F32)
        upper = jnp.where(core == 0, mine, came)
        lower = jnp.where(core == 0, came, mine)
        return low(jnp.concatenate([upper, lower], axis=0))

    mine_half = aligned(core, 384)
    at.gat_a[r.z, r.plane, :, 0:384] = stack(at.key_w[:, mine_half], at.come_a[:, 0:384])
    at.gat_a[r.z, r.plane, :, 384:768] = stack(at.value_w[:, mine_half], at.come_a[:, 384:768])
    at.gat_b[r.z, r.plane, :, 0:384] = stack(at.query_w[:, mine_half], at.come_b[:, 0:384])
    at.gat_b[r.z, r.plane, :, 384:768] = stack(at.output_w[:, mine_half], at.come_b[:, 384:768])
    at.gat_b[r.z, r.plane, :, 768:1024] = stack(
        at.table_t[:, aligned(core, 256)], at.come_b[:, 768:1024]
    )
    at.gat_s[r.z, r.plane, core] = at.small[...]
    at.gat_s[r.z, r.plane, other] = at.come_s[...]
    gather_one.start()
    for chip in range(4 * LINE):
        for which in range(2):
            device = 2 * chip + which
            at.inner_pair[which, :, 96 * chip : 96 * chip + 96] = at.inner_w[
                :, 96 * device : 96 * device + 96
            ]
    come_inner = swap(6, at.inner_pair.at[other], at.come_1)
    come_inner.wait_recv()
    at.gat_1[r.z, r.plane] = stack(at.inner_pair[core], at.come_1[...])
    place_2.wait()
    place_x.wait()
    come_x.wait_recv()
    at.x_turned[...] = at.x_all[...].T
    wide_i = lax.broadcasted_iota(jnp.int32, (512, 512), 0)
    wide_j = lax.broadcasted_iota(jnp.int32, (512, 512), 1)
    used = low((at.buckets[0:1, 256:768] == wide_i).astype(F32))
    at.one_hot[...] = low(dot(used, low((wide_i + wide_j == 511).astype(F32))))
    segment_wide = jnp.broadcast_to(at.segments[...].astype(F32), (128, 512))
    at.segment_row[...] = segment_wide[0:8]
    at.segment_col[...] = segment_wide.T
    flip_i = lax.broadcasted_iota(jnp.int32, (128, 128), 0)
    flip_j = lax.broadcasted_iota(jnp.int32, (128, 128), 1)
    at.flip[...] = low((flip_i + flip_j == 127).astype(F32))
    for table in (at.near_rows, at.far_rows):
        table[0:256, :] = jnp.zeros((256, 384), BF16)
        table[768:1024, :] = jnp.zeros((256, 384), BF16)
    for step in range(1, LINE):
        gather_one.turn(step)
    gather_one.corner(LINE - 1)
    gather_two.start()
    gather_one.finish()

    out_mine = at.gat_b.at[:, :, :, pl.ds(384, 384)]
    table_mine = at.gat_b.at[:, :, :, pl.ds(768, 256)]
    come_table = swap(8, table_mine, at.table_all.at[core])
    come_out = swap(9, out_mine, at.out_all.at[core])
    place_table = pltpu.make_async_copy(table_mine, at.table_all.at[core], at.here.at[0])
    place_table.start()
    place_out = pltpu.make_async_copy(out_mine, at.out_all.at[core], at.here.at[1])
    place_out.start()

    for line in range(LINE):
        for plane in range(4):
            chip = line * 4 + plane
            for which in range(2):
                device = 2 * chip + which
                tile = at.gat_s[line, plane, which].astype(F32)
                at.vectors[:, 24 * device : 24 * device + 24] = tile[0:8, 0:24]
            tile = at.gat_s[line, plane, core].astype(F32)
            at.inner_bias[0:1, 96 * chip : 96 * chip + 96] = tile[8:9, 0:96]

    def rows(value):
        return value.reshape(768, value.shape[-1])

    vector_half = aligned(core, 384)
    query_bias = at.vectors[0:1, vector_half]
    value_bias = at.vectors[1:2, vector_half]
    at.kvq[:, 0:384] = low(dot(at.x_all[...], rows(at.gat_a[:, :, :, 0:384])))
    at.kvq[:, 384:768] = low(dot(at.x_all[...], rows(at.gat_a[:, :, :, 384:768])) + value_bias)
    at.kvq[:, 768:1152] = low(dot(at.x_all[...], rows(at.gat_b[:, :, :, 0:384])) + query_bias)
    place_table.wait()
    come_table.wait_recv()
    for part in range(2):
        piece = pl.ds(256 * part, 256)
        table = rows(at.table_all[part])
        at.key_rel[piece, :] = low(dot(table, rows(at.gat_a[:, :, :, 0:384]), 0, 0))
        at.query_rel[piece, :] = low(dot(table, rows(at.gat_b[:, :, :, 0:384]), 0, 0) + query_bias)
    at.near_rows[256:768, :] = low(dot(at.one_hot[...], at.key_rel[...], 0, 0))
    at.far_rows[256:768, :] = low(dot(at.one_hot[...], at.query_rel[...], 0, 0))

    gather_two.turn(1)

    lanes = lax.broadcasted_iota(jnp.int32, (1, 128), 1) // HEAD
    no_score = np.float32(NEGATIVE)

    def forward_head(head):
        pair = aligned(head // 2, 128)
        key_lanes = pl.ds(pl.multiple_of((head // 2) * 128, 128), 128)
        value_lanes = pl.ds(pl.multiple_of(384 + (head // 2) * 128, 128), 128)
        query_lanes = pl.ds(pl.multiple_of(768 + (head // 2) * 128, 128), 128)
        mine = lanes == head % 2
        only = low(mine.astype(F32))
        keys = at.kvq[:, key_lanes]
        values = at.kvq[:, value_lanes]
        for block in range(4):
            piece = pl.ds(128 * block, 128)
            shifted = dot(
                at.kvq[piece, key_lanes] * only, at.far_rows[pl.ds(384 - 128 * block, 640), pair], 1, 1
            )
            at.far_scores[piece, :] = pltpu.roll(shifted, 0, 1, stride=1, stride_axis=0)[:, 128:640]
        for block in range(4):
            piece = pl.ds(128 * block, 128)
            queries = at.kvq[piece, query_lanes] * only
            shifted = dot(queries, at.near_rows[pl.ds(384 - 128 * block, 640), pair], 1, 1)
            summed = (
                dot(queries, keys, 1, 1)
                + pltpu.roll(shifted, 0, 1, stride=1, stride_axis=0)[:, 128:640]
                + at.far_scores[:, piece].T
            )
            masked = jnp.where(
                at.segment_col[piece, 0:1] == at.segment_row[0:1, :], summed * score_scale, no_score
            )
            highest = jnp.max(masked, axis=-1, keepdims=True)
            expsum = jnp.exp(masked - highest)
            soft = expsum / jnp.sum(expsum, axis=-1, keepdims=True)
            at.soft[head, piece, :] = soft
            context = dot(low(soft), values)
            here = at.context.at[core, piece, pair]
            here[...] = low(jnp.where(mine, context, here[...].astype(F32)))

    def forward_pair(index):
        loop(2, lambda which: forward_head(2 * index + which))
        remote(
            at.context.at[core, :, aligned(index, 128)],
            at.context.at[core, :, aligned(index, 128)],
            at.context_send.at[index],
            at.context_recv.at[index],
            r.partner,
        ).start()

    loop(3, forward_pair)
    gather_two.turn(2)
    place_out.wait()
    come_out.wait_recv()
    for index in range(3):
        remote(
            at.context.at[other, :, pl.ds(128 * index, 128)],
            at.context.at[other, :, pl.ds(128 * index, 128)],
            at.context_send.at[index],
            at.context_recv.at[index],
            r.partner,
        ).wait_recv()

    def vector(index):
        return at.vectors[index : index + 1, :]

    for part in range(2):
        piece = pl.ds(384 * part, 384)
        weight = rows(at.out_all[part])
        at.wide[:, piece] = dot(at.context[0, own_rows, :], weight[0:384]) + dot(
            at.context[1, own_rows, :], weight[384:768]
        )

    def first_norm(index):
        piece = aligned(index, 64)
        token_rows = pl.ds(pl.multiple_of(core * 256 + index * 64, 64), 64)
        residual = at.x_all[token_rows, :].astype(F32) + at.wide[piece, :] + vector(2)
        out, normed, inverse = norm(residual, vector(3), vector(4))
        at.first_out[piece, :] = out
        at.first_normed[piece, :] = normed
        at.first_inverse[piece, :] = jnp.broadcast_to(inverse, (64, 128))
        at.first_low[token_rows, :] = low(out)

    loop(4, first_norm)
    come_first = swap(10, at.first_low.at[own_rows], at.first_low.at[own_rows])
    gather_two.turn(3)
    come_first.wait_recv()
    at.first_turned[...] = at.first_low[...].T
    gather_two.corner(LINE - 1)
    gather_two.finish()

    def inner_units(index):
        piece = aligned(index, 256)
        pre = dot(at.first_low[...], rows(at.gat_1[:, :, :, piece])) + at.inner_bias[0:1, piece]
        value, slope = erf_parts(pre)
        at.active[:, piece] = low(value)
        at.slope[:, piece] = slope

    loop(6, inner_units)

    def outer_half(rows_at, out):
        for part in range(3):
            piece = pl.ds(256 * part, 256)
            out[:, piece] = dot(
                at.active[rows_at, :], at.gat_2[:, :, :, piece].reshape(1536, 256)
            )

    outer_half(other_rows, at.part_send)
    come_outer = swap(11, at.part_send, at.part_recv)
    outer_half(own_rows, at.wide)
    come_outer.wait_recv()

    def second_norm(index):
        piece = aligned(index, 64)
        token_rows = pl.ds(pl.multiple_of(core * 256 + index * 64, 64), 64)
        total = at.first_out[piece, :] + at.wide[piece, :] + at.part_recv[piece, :] + vector(5)
        out, normed, inverse = norm(total, vector(6), vector(7))
        at.result[piece, :] = low(out)
        upstream = at.cotangent[piece, :].astype(F32)
        grad = norm_pull(upstream, normed, inverse, vector(6))
        at.grad_sum[piece, :] = grad
        rounded = low(grad)
        at.grad_outer[token_rows, :] = rounded
        at.sums[5:6, :] += jnp.sum(rounded.astype(F32), axis=0, keepdims=True)
        at.sums[6:7, :] += jnp.sum(upstream * normed, axis=0, keepdims=True)
        at.sums[7:8, :] += jnp.sum(upstream, axis=0, keepdims=True)

    loop(4, second_norm)
    come_grad = swap(12, at.grad_outer.at[own_rows], at.grad_outer.at[own_rows])
    scatter_two = Scatter(
        r, (at.grad_1, at.grad_2), (at.one_1, at.one_2), (at.two_1, at.two_2),
        (at.last_1, at.last_2), at.sf_send, at.sf_recv,
    )
    scatter_one = Scatter(
        r, (at.grad_a, at.grad_b), (at.one_a, at.one_b), (at.two_a, at.two_b),
        (at.last_a, at.last_b), at.sa_send, at.sa_recv,
    )
    come_grad.wait_recv()

    def outer_weight(index):
        units = aligned(index, 384)
        grad = dot(at.active[:, units], at.grad_outer[...], 0, 0)
        at.grad_2[index] = low(grad).reshape(4, 96, 768)

    loop(4, outer_weight)
    for step in (1, 2, 3, 0):
        scatter_two.one(step, (1,))

    def inner_grad(index):
        units = aligned(index, 384)
        grad = low(dot(at.grad_outer[...], at.gat_2[index].reshape(384, 768), 1, 1))
        pre = low(grad.astype(F32) * at.slope[:, units])
        at.grad_pre[:, units] = pre
        at.bias_inner[0:1, units] = jnp.sum(pre.astype(F32), axis=0, keepdims=True)
        at.grad_1[:, :, :, units] = low(dot(at.first_turned[...], pre)).reshape(LINE, 4, 48, 384)

    loop(4, inner_grad)
    for step in (1, 2, 3, 0):
        scatter_two.one(step, (0,))
    at.sums[8:9, :] = at.bias_inner[0:1, 0:768]
    at.sums[9:10, :] = at.bias_inner[0:1, 768:1536]

    def first_half(rows_at, out):
        for part in range(2):
            weight = at.gat_1[2 * part : 2 * part + 2].reshape(384, 1536)
            out[:, 384 * part : 384 * part + 384] = dot(at.grad_pre[rows_at, :], weight, 1, 1)

    first_half(other_rows, at.part_send2)
    come_grad_first = swap(13, at.part_send2, at.part_recv2)
    first_half(own_rows, at.wide)
    come_grad_first.wait_recv()

    def first_norm_back(index):
        piece = aligned(index, 64)
        token_rows = pl.ds(pl.multiple_of(core * 256 + index * 64, 64), 64)
        upstream = at.wide[piece, :] + at.part_recv2[piece, :] + at.grad_sum[piece, :]
        normed = at.first_normed[piece, :]
        grad = norm_pull(upstream, normed, at.first_inverse[piece, 0:1], vector(3))
        at.grad_sum[piece, :] = grad
        rounded = low(grad)
        at.grad_att[token_rows, :] = rounded
        at.sums[2:3, :] += jnp.sum(rounded.astype(F32), axis=0, keepdims=True)
        at.sums[3:4, :] += jnp.sum(upstream * normed, axis=0, keepdims=True)
        at.sums[4:5, :] += jnp.sum(upstream, axis=0, keepdims=True)

    loop(4, first_norm_back)
    come_att = swap(14, at.grad_att.at[own_rows], at.grad_att.at[own_rows])
    come_att.wait_recv()
    scatter_two.two(1)
    out_rows = pl.ds(pl.multiple_of(2 * core, 2), 2)
    weight_0 = at.out_all[0, out_rows].reshape(384, 384)
    weight_1 = at.out_all[1, out_rows].reshape(384, 384)
    at.grad_context[...] = low(
        dot(at.grad_att[:, 0:384], weight_0, 1, 1) + dot(at.grad_att[:, 384:768], weight_1, 1, 1)
    )
    for part in range(2):
        grad = dot(at.context[part], at.grad_att[:, aligned(core, 384)], 0, 0)
        at.grad_b[2 * part : 2 * part + 2, :, :, 384:768] = low(grad).reshape(2, 4, 48, 384)
    scatter_two.two(2)

    at.near_grad[...] = jnp.zeros_like(at.near_grad)
    at.far_grad[...] = jnp.zeros_like(at.far_grad)
    room = jnp.zeros((128, 128), BF16)

    def spread(flipped):
        return pltpu.roll(jnp.concatenate([flipped, room], axis=1), 1, 1, stride=1, stride_axis=0)

    def backward_head(head):
        pair = aligned(head // 2, 128)
        key_lanes = pl.ds(pl.multiple_of((head // 2) * 128, 128), 128)
        value_lanes = pl.ds(pl.multiple_of(384 + (head // 2) * 128, 128), 128)
        query_lanes = pl.ds(pl.multiple_of(768 + (head // 2) * 128, 128), 128)
        mine = lanes == head % 2
        only = low(mine.astype(F32))
        flip = at.flip[...]
        keys = at.kvq[:, key_lanes]
        queries = at.kvq[:, query_lanes]
        values = at.kvq[:, value_lanes]

        def merge(here, value):
            here[...] = low(jnp.where(mine, value, here[...].astype(F32)))

        for block in range(4):
            piece = pl.ds(128 * block, 128)
            window = pl.ds(384 - 128 * block, 640)
            soft = at.soft[head, piece, :]
            grad_soft = dot(at.grad_context[piece, pair] * only, values, 1, 1)
            inner = jnp.sum(soft * grad_soft, axis=-1, keepdims=True)
            grad_low = low(soft * (grad_soft - inner) * score_scale)
            at.grad_low[piece, :] = grad_low
            flipped = low(dot(flip, grad_low))
            near = spread(flipped)
            grad = low(dot(flipped, keys) + dot(near, at.near_rows[window, pair]))
            merge(at.grad_kvq.at[piece, query_lanes], dot(flip, grad))
            back = low(dot(flip, at.kvq[piece, query_lanes] * only))
            at.near_grad[window, pair] += dot(near, back, 0, 0)
        grad_context = at.grad_context[:, pair]
        for block in range(4):
            piece = pl.ds(128 * block, 128)
            window = pl.ds(384 - 128 * block, 640)
            flipped = low(dot(flip, at.grad_low[:, piece], 1, 1))
            far = spread(flipped)
            grad = low(dot(flipped, queries) + dot(far, at.far_rows[window, pair]))
            merge(at.grad_kvq.at[piece, key_lanes], dot(flip, grad))
            back = low(dot(flip, at.kvq[piece, key_lanes] * only))
            at.far_grad[window, pair] += dot(far, back, 0, 0)
            weights = low(at.soft[head, :, piece])
            merge(at.grad_kvq.at[piece, value_lanes], dot(weights, grad_context, 0, 0))

    def backward_pair(index):
        loop(2, lambda which: backward_head(2 * index + which))
        scatter_two.three(index + 1)

        @pl.when(index < 2)
        def _():
            scatter_two.two(index + 3)

    loop(3, backward_pair)
    scatter_two.three(0, True)

    grad_key_rel = dot(at.one_hot[...], low(at.near_grad[256:768, :]))
    grad_query_rel = dot(at.one_hot[...], low(at.far_grad[256:768, :]))
    at.key_rel[...] = low(grad_key_rel)
    at.query_rel[...] = low(grad_query_rel)

    def token_weight(kvq_at):
        return dot(at.x_turned[...], at.grad_kvq[:, kvq_at : kvq_at + 384])

    def table_weight(rel):
        return dot(rows(at.table_all[0]), rel[0:256, :]) + dot(rows(at.table_all[1]), rel[256:512, :])

    def shape_weight(value):
        return low(value).reshape(LINE, 4, 48, value.shape[-1])

    def table_half(which):
        piece = aligned(which, 256)
        return dot(rows(at.gat_b[:, :, :, 0:384]), at.query_rel[piece, :], 1, 1) + dot(
            rows(at.gat_a[:, :, :, 0:384]), at.key_rel[piece, :], 1, 1
        )

    at.table_send[...] = shape_weight(table_half(other))
    come_part = swap(15, at.table_send, at.table_recv)
    at.grad_a[:, :, :, 0:384] = shape_weight(token_weight(0) + table_weight(at.key_rel))
    at.grad_a[:, :, :, 384:768] = shape_weight(token_weight(384))
    for step in (1, 2, 3, 0):
        scatter_one.one(step, (0,))
    at.grad_b[:, :, :, 0:384] = shape_weight(token_weight(768) + table_weight(at.query_rel))
    own_table = table_half(core)
    come_part.wait_recv()
    at.grad_b[:, :, :, 768:1024] = shape_weight(own_table + rows(at.table_recv[...]).astype(F32))
    for step in (1, 2, 3, 0):
        scatter_one.one(step, (1,))

    at.sums[0:1, vector_half] = jnp.sum(
        at.grad_kvq[:, 768:1152].astype(F32), axis=0, keepdims=True
    ) + jnp.sum(at.far_grad[256:768, :], axis=0, keepdims=True)
    at.sums[1:2, vector_half] = jnp.sum(
        at.grad_kvq[:, 384:768].astype(F32), axis=0, keepdims=True
    )

    def exchange(stage, source, device):
        return remote(
            source, at.sums_come.at[stage], at.sums_send.at[stage], at.sums_recv.at[stage], device
        )

    stage_copies = [exchange(0, at.sums, r.partner)]
    stage_copies[0].start()

    def input_half(rows_at, out):
        for part in range(2):
            weight_a = at.gat_a[2 * part : 2 * part + 2].reshape(384, 768)
            weight_b = at.gat_b[2 * part : 2 * part + 2, :, :, 0:384].reshape(384, 384)
            out[:, 384 * part : 384 * part + 384] = dot(
                at.grad_kvq[rows_at, 0:768], weight_a, 1, 1
            ) + dot(at.grad_kvq[rows_at, 768:1152], weight_b, 1, 1)

    come_outer.wait_send()
    input_half(other_rows, at.part_send)
    come_input = swap(16, at.part_send, at.part_recv)

    stage_copies[0].wait_recv()
    lines = lax.broadcasted_iota(jnp.int32, (16, 1), 0)
    shared = jnp.where((lines == 8) | (lines == 9), 0.0, at.sums_come[0])
    at.sums_step[0] = at.sums[...] + shared
    stage_copies.append(exchange(1, at.sums_step.at[0], r.at_x))
    stage_copies[1].start()
    scatter_one.two(1)
    input_half(own_rows, at.wide)
    scatter_one.two(2)
    stage_copies[1].wait_recv()
    at.sums_step[1] = at.sums_step[0] + at.sums_come[1]
    stage_copies.append(exchange(2, at.sums_step.at[1], r.at_y))
    stage_copies[2].start()
    scatter_one.three(1)
    scatter_one.two(3)
    come_input.wait_recv()
    at.input_grad[...] = low(at.grad_sum[...] + at.wide[...] + at.part_recv[...])

    scatter_two.finish()
    at.d_outer[...] = scatter_two.total(1)
    inner_total = scatter_two.total(0)
    at.give_1[...] = inner_total.reshape(2, 24, 1536)
    swap(17, at.give_1.at[other], at.d_inner.at[core])
    at.d_inner[core] = at.give_1[core]

    scatter_one.three(2)
    scatter_one.two(0)
    stage_copies[2].wait_recv()
    at.sums_step[2] = at.sums_step[1] + at.sums_come[2]
    for step in range(1, LINE):
        copy = exchange(2 + step, at.sums_step.at[2], r.at_line(r.ahead(step)))
        copy.start()
        stage_copies.append(copy)
    scatter_one.three(3)
    scatter_one.three(0, True)
    for copy in stage_copies[3:]:
        copy.wait_recv()
    at.vector_grads[...] = (
        at.sums_step[2] + at.sums_come[3] + at.sums_come[4] + at.sums_come[5]
    )
    scatter_one.finish()
    at.give_a[...] = scatter_one.total(0).reshape(2, 24, 768)
    at.give_b[...] = scatter_one.total(1).reshape(2, 24, 1024)
    outs = (
        (at.give_a, 0, 384, at.d_key),
        (at.give_a, 384, 384, at.d_value),
        (at.give_b, 0, 384, at.d_query),
        (at.give_b, 384, 384, at.d_output),
        (at.give_b, 768, 256, at.d_table),
    )
    for slot, (give, start, width, out) in enumerate(outs):
        swap(18 + slot, give.at[other, :, pl.ds(start, width)], out.at[:, aligned(core, width)])
        out[:, aligned(core, width)] = give[core, :, start : start + width]
    for copy in waiting[17:]:
        copy.wait_recv()
    for copy in waiting:
        if copy is not come_outer:
            copy.wait_send()
    for copy in stage_copies:
        copy.wait_send()
    for index in range(3):
        remote(
            at.context.at[core, :, pl.ds(128 * index, 128)],
            at.context.at[core, :, pl.ds(128 * index, 128)],
            at.context_send.at[index],
            at.context_recv.at[index],
            r.partner,
        ).wait_send()
    for user in (gather_one, gather_two, scatter_two, scatter_one):
        user.sent()


def finish_kernel(names, *refs):
    at = type("Refs", (), dict(zip(names, refs)))
    chip, core = lax.axis_index("fsdp"), lax.axis_index("seq")
    at.result_out[...] = at.result[...]
    at.input_grad_out[...] = at.input_grad[...]
    at.query_w_out[...] = at.d_query[...]
    at.key_w_out[...] = at.d_key[...]
    at.value_w_out[...] = at.d_value[...]
    at.output_w_out[...] = at.d_output[...]
    at.table_out[...] = at.d_table[...]
    at.outer_w_out[...] = at.d_outer[...]
    for group in range(4 * LINE):
        for which in range(2):
            device = 2 * group + which
            at.inner_w_out[:, 96 * device : 96 * device + 96] = at.d_inner[
                which, :, 96 * group : 96 * group + 96
            ]
    sums = at.vector_grads[...]
    own = pltpu.roll(sums, (768 - 24 * (2 * chip + core)) % 768, 1)
    small_outs = (
        at.query_b_out, at.value_b_out, at.output_b_out, at.gain_1_out, at.shift_1_out,
        at.outer_b_out, at.gain_2_out, at.shift_2_out,
    )
    for index, out in enumerate(small_outs):
        out[...] = own[index : index + 1, 0:24]
    units = jnp.where(chip < 2 * LINE, sums[8:9], sums[9:10])
    units = jnp.broadcast_to(units, (8, 768))
    at.inner_b_out[...] = pltpu.roll(units, (768 - 96 * (chip % (2 * LINE))) % 768, 1)[0:1, 0:96]
    at.count_out[...] = sums[10:11, 0:1].astype(jnp.int32)


OUTPUTS = dict(
    result=((256, 768), BF16),
    input_grad=((256, 768), BF16),
    d_query=((24, 768), F32),
    d_key=((24, 768), F32),
    d_value=((24, 768), F32),
    d_output=((24, 768), F32),
    d_table=((24, 512), F32),
    d_inner=((2, 24, 1536), F32),
    d_outer=((96, 768), F32),
    vector_grads=((16, 768), F32),
)
FINALS = dict(
    result_out=((256, 768), BF16),
    input_grad_out=((256, 768), BF16),
    query_w_out=((24, 768), F32),
    key_w_out=((24, 768), F32),
    value_w_out=((24, 768), F32),
    output_w_out=((24, 768), F32),
    table_out=((24, 512), F32),
    inner_w_out=((24, 3072), F32),
    outer_w_out=((96, 768), F32),
    query_b_out=((1, 24), F32),
    value_b_out=((1, 24), F32),
    output_b_out=((1, 24), F32),
    gain_1_out=((1, 24), F32),
    shift_1_out=((1, 24), F32),
    outer_b_out=((1, 24), F32),
    gain_2_out=((1, 24), F32),
    shift_2_out=((1, 24), F32),
    inner_b_out=((1, 96), F32),
    count_out=((1, 1), jnp.int32),
)
LINE = 4
BLOCKS = (LINE, 4, 48)
SCRATCH = dict(
    small_wide=((16, 128), F32),
    small=((16, 128), BF16),
    inner_pair=((2, 24, 1536), BF16),
    segment_row=((8, 512), F32),
    segment_col=((512, 128), F32),
    come_a=((24, 768), BF16),
    come_b=((24, 1024), BF16),
    come_s=((16, 128), BF16),
    come_1=((24, 1536), BF16),
    gat_a=(BLOCKS + (768,), BF16),
    gat_b=(BLOCKS + (1024,), BF16),
    gat_s=((LINE, 4, 2, 16, 128), BF16),
    gat_1=(BLOCKS + (1536,), BF16),
    gat_2=((LINE, 4, 96, 768), BF16),
    x_all=((512, 768), BF16),
    x_turned=((768, 512), BF16),
    one_hot=((512, 512), BF16),
    flip=((128, 128), BF16),
    near_rows=((1024, 384), BF16),
    far_rows=((1024, 384), BF16),
    near_grad=((1024, 384), F32),
    far_grad=((1024, 384), F32),
    key_rel=((512, 384), BF16),
    query_rel=((512, 384), BF16),
    table_all=((2,) + BLOCKS + (256,), BF16),
    out_all=((2,) + BLOCKS + (384,), BF16),
    vectors=((8, 768), F32),
    inner_bias=((8, 1536), F32),
    bias_inner=((8, 1536), F32),
    kvq=((512, 1152), BF16),
    grad_kvq=((512, 1152), BF16),
    far_scores=((512, 512), F32),
    grad_low=((512, 512), BF16),
    soft=((6, 512, 512), F32),
    context=((2, 512, 384), BF16),
    grad_context=((512, 384), BF16),
    wide=((256, 768), F32),
    first_out=((256, 768), F32),
    first_normed=((256, 768), F32),
    first_inverse=((256, 128), F32),
    first_low=((512, 768), BF16),
    first_turned=((768, 512), BF16),
    active=((512, 1536), BF16),
    slope=((512, 1536), F32),
    grad_pre=((512, 1536), BF16),
    part_send=((256, 768), F32),
    part_recv=((256, 768), F32),
    part_send2=((256, 768), F32),
    part_recv2=((256, 768), F32),
    grad_sum=((256, 768), F32),
    grad_outer=((512, 768), BF16),
    grad_att=((512, 768), BF16),
    table_send=(BLOCKS + (256,), BF16),
    table_recv=(BLOCKS + (256,), BF16),
    sums=((16, 768), F32),
    sums_step=((3, 16, 768), F32),
    sums_come=((6, 16, 768), F32),
    grad_1=(BLOCKS + (1536,), BF16),
    grad_2=((LINE, 4, 96, 768), BF16),
    one_1=((LINE, 2, 48, 1536), BF16),
    one_2=((LINE, 2, 96, 768), BF16),
    two_1=((LINE, 48, 1536), BF16),
    two_2=((LINE, 96, 768), BF16),
    last_1=((LINE, 48, 1536), BF16),
    last_2=((LINE, 96, 768), BF16),
    grad_a=(BLOCKS + (768,), BF16),
    grad_b=(BLOCKS + (1024,), BF16),
    one_a=((LINE, 2, 48, 768), BF16),
    one_b=((LINE, 2, 48, 1024), BF16),
    two_a=((LINE, 48, 768), BF16),
    two_b=((LINE, 48, 1024), BF16),
    last_a=((LINE, 48, 768), BF16),
    last_b=((LINE, 48, 1024), BF16),
    give_1=((2, 24, 1536), F32),
    give_a=((2, 24, 768), F32),
    give_b=((2, 24, 1024), F32),
)
SEMAPHORES = dict(
    swap_send=(23,),
    swap_recv=(23,),
    here=(2,),
    context_send=(3,),
    context_recv=(3,),
    ga_send=(3, 4, LINE),
    ga_recv=(3, 4, LINE),
    gf_send=(2, 4, LINE),
    gf_recv=(2, 4, LINE),
    sf_send=(2, 4, LINE),
    sf_recv=(2, 4, LINE),
    sa_send=(2, 4, LINE),
    sa_recv=(2, 4, LINE),
    sums_send=(6,),
    sums_recv=(6,),
)


def block_shards(
    hidden_in,
    query_weight,
    query_bias,
    key_weight,
    value_weight,
    value_bias,
    output_weight,
    output_bias,
    first_gain,
    first_shift,
    inner_weight,
    inner_bias,
    outer_weight,
    outer_bias,
    second_gain,
    second_shift,
    relative_table,
    segments,
    buckets,
    predicted,
    labels,
    cotangent,
):
    inputs = dict(
        hidden=hidden_in[0],
        query_w=query_weight,
        key_w=key_weight,
        value_w=value_weight,
        output_w=output_weight,
        table_t=relative_table.T,
        inner_w=inner_weight,
        outer_w=outer_weight,
        query_b=query_bias[None],
        value_b=value_bias[None],
        output_b=output_bias[None],
        gain_1=first_gain[None],
        shift_1=first_shift[None],
        outer_b=outer_bias[None],
        gain_2=second_gain[None],
        shift_2=second_shift[None],
        inner_b=inner_bias[None],
        segments=segments,
        buckets=buckets[None],
        predicted=predicted,
        labels=labels,
        cotangent=cotangent[0],
    )
    names = tuple(inputs) + tuple(OUTPUTS) + tuple(SCRATCH) + tuple(SEMAPHORES)
    vmem = pl.BlockSpec(memory_space=pltpu.VMEM)
    outs = pl.pallas_call(
        partial(layer_kernel, names),
        name="layer",
        out_shape=tuple(jax.ShapeDtypeStruct(*out) for out in OUTPUTS.values()),
        in_specs=[vmem] * len(inputs),
        out_specs=(vmem,) * len(OUTPUTS),
        scratch_shapes=[pltpu.VMEM(*spec) for spec in SCRATCH.values()]
        + [pltpu.SemaphoreType.DMA(shape) for shape in SEMAPHORES.values()],
        compiler_params=pltpu.CompilerParams(
            collective_id=0, has_side_effects=True, vmem_limit_bytes=67043328
        ),
    )(*inputs.values())
    finals = pl.pallas_call(
        partial(finish_kernel, tuple(OUTPUTS) + tuple(FINALS)),
        name="finish",
        out_shape=tuple(jax.ShapeDtypeStruct(*out) for out in FINALS.values()),
        in_specs=[vmem] * len(OUTPUTS),
        out_specs=(vmem,) * len(FINALS),
    )(*outs)
    got = type("Outs", (), dict(zip(FINALS, finals)))
    return (
        got.result_out[None],
        got.input_grad_out[None],
        got.query_w_out,
        got.query_b_out[0],
        got.key_w_out,
        got.value_w_out,
        got.value_b_out[0],
        got.output_w_out,
        got.output_b_out[0],
        got.gain_1_out[0],
        got.shift_1_out[0],
        got.inner_w_out,
        got.inner_b_out[0],
        got.outer_w_out,
        got.outer_b_out[0],
        got.gain_2_out[0],
        got.shift_2_out[0],
        got.table_out.T,
        got.count_out[0, 0],
    )


def fits(mesh):
    return mesh.shape["fsdp"] == 4 * LINE and mesh.shape["seq"] == 2


def solution(mesh):
    return jax.shard_map(
        block_shards if fits(mesh) else shards,
        mesh=mesh,
        in_specs=(
            P("fsdp", "seq", None),
            P(("fsdp", "seq"), None),
            P(("fsdp", "seq")),
            P(("fsdp", "seq"), None),
            P(("fsdp", "seq"), None),
            P(("fsdp", "seq")),
            P(("fsdp", "seq"), None),
            P(("fsdp", "seq")),
            P(("fsdp", "seq")),
            P(("fsdp", "seq")),
            P(("fsdp", "seq"), None),
            P(("fsdp", "seq")),
            P(("fsdp", "seq"), None),
            P(("fsdp", "seq")),
            P(("fsdp", "seq")),
            P(("fsdp", "seq")),
            P(None, ("fsdp", "seq")),
            P("fsdp", None),
            P(),
            P("fsdp", "seq"),
            P("fsdp", "seq"),
            P("fsdp", "seq", None),
        ),
        out_specs=(
            P("fsdp", "seq", None),
            P("fsdp", "seq", None),
            P(("fsdp", "seq"), None),
            P(("fsdp", "seq")),
            P(("fsdp", "seq"), None),
            P(("fsdp", "seq"), None),
            P(("fsdp", "seq")),
            P(("fsdp", "seq"), None),
            P(("fsdp", "seq")),
            P(("fsdp", "seq")),
            P(("fsdp", "seq")),
            P(("fsdp", "seq"), None),
            P(("fsdp", "seq")),
            P(("fsdp", "seq"), None),
            P(("fsdp", "seq")),
            P(("fsdp", "seq")),
            P(("fsdp", "seq")),
            P(None, ("fsdp", "seq")),
            P(),
        ),
        check_vma=False,
    )
```

```python
from functools import partial

import jax
import jax.numpy as jnp
import numpy as np
from jax import lax
from jax.experimental import pallas as pl
from jax.experimental.pallas import tpu as pltpu
from jax.sharding import PartitionSpec as P

HEAD = 64


EPSILON = 1e-07
NEGATIVE = -1e30


def matmul(spec, left, right):
    return jnp.einsum(spec, left, right, preferred_element_type=jnp.float32)


def precise(spec, left, right):
    return jnp.einsum(spec, left, right, precision=lax.Precision.HIGHEST)


def skew_rows(scores_in, offset, columns):
    leading = scores_in.shape[:-2]
    row_count = scores_in.shape[-2]
    breadth = scores_in.shape[-1]
    flattened = scores_in.reshape(leading + (row_count * breadth,))
    flattened = jnp.concatenate(
        [flattened, jnp.zeros(leading + (2 * breadth,), scores_in.dtype)], axis=-1
    )
    selected = lax.dynamic_slice_in_dim(flattened, offset, row_count * (breadth - 1), len(leading))
    return selected.reshape(leading + (row_count, breadth - 1))[..., :columns]


def unskew_rows(values, offset, breadth):
    leading = values.shape[:-2]
    row_count = values.shape[-2]
    columns = values.shape[-1]
    padded = jnp.concatenate(
        [values, jnp.zeros(leading + (row_count, breadth - 1 - columns), values.dtype)], axis=-1
    )
    flattened = padded.reshape(leading + (row_count * (breadth - 1),))
    zero_room = jnp.zeros(leading + (row_count * breadth + 2 * breadth,), values.dtype)
    placed = lax.dynamic_update_slice_in_dim(zero_room, flattened, offset, len(leading))
    return placed[..., : row_count * breadth].reshape(leading + (row_count, breadth))


def layer_norm(values, gain, shift):
    average = jnp.mean(values, axis=-1, keepdims=True)
    centred = values - average
    variance = jnp.mean(centred * centred, axis=-1, keepdims=True)
    inverse = lax.rsqrt(variance + EPSILON)
    normed = centred * inverse
    return (normed * gain + shift, normed, inverse)


def norm_backward(upstream, normed, inverse, gain):
    scaled_up = upstream * gain
    first_mean = jnp.mean(scaled_up, axis=-1, keepdims=True)
    second_mean = jnp.mean(scaled_up * normed, axis=-1, keepdims=True)
    grad_in = inverse * (scaled_up - first_mean - normed * second_mean)
    return (grad_in, jnp.sum(upstream * normed, axis=0), jnp.sum(upstream, axis=0))


def shards(
    hidden_in,
    query_weight,
    query_bias,
    key_weight,
    value_weight,
    value_bias,
    output_weight,
    output_bias,
    first_gain,
    first_shift,
    inner_weight,
    inner_bias,
    outer_weight,
    outer_bias,
    second_gain,
    second_shift,
    relative_table,
    segments,
    buckets,
    predicted,
    labels,
    cotangent,
):
    row_count, window, model_width = hidden_in.shape
    length = segments.shape[1]
    distances = 2 * length - 1
    span = window + length - 1
    pair_width = 2 * HEAD
    pair_count = model_width // pair_width
    score_scale = (3.0 * HEAD) ** (-0.5)
    window_start = lax.axis_index("seq") * window
    near_start = length - window - window_start
    token_count = row_count * window
    attention_set = (
        lax.all_gather(query_weight, ("fsdp", "seq"), axis=0, tiled=True),
        lax.all_gather(query_bias, ("fsdp", "seq"), axis=0, tiled=True),
        lax.all_gather(key_weight, ("fsdp", "seq"), axis=0, tiled=True),
        lax.all_gather(value_weight, ("fsdp", "seq"), axis=0, tiled=True),
        lax.all_gather(value_bias, ("fsdp", "seq"), axis=0, tiled=True),
        lax.all_gather(output_weight, ("fsdp", "seq"), axis=0, tiled=True),
        lax.all_gather(output_bias, ("fsdp", "seq"), axis=0, tiled=True),
        lax.all_gather(first_gain, ("fsdp", "seq"), axis=0, tiled=True),
        lax.all_gather(first_shift, ("fsdp", "seq"), axis=0, tiled=True),
        lax.all_gather(relative_table, ("fsdp", "seq"), axis=1, tiled=True),
    )
    feed_set = (
        lax.all_gather(inner_weight, ("fsdp", "seq"), axis=0, tiled=True),
        lax.all_gather(inner_bias, ("fsdp", "seq"), axis=0, tiled=True),
        lax.all_gather(outer_weight, ("fsdp", "seq"), axis=0, tiled=True),
        lax.all_gather(outer_bias, ("fsdp", "seq"), axis=0, tiled=True),
        lax.all_gather(second_gain, ("fsdp", "seq"), axis=0, tiled=True),
        lax.all_gather(second_shift, ("fsdp", "seq"), axis=0, tiled=True),
    )
    (
        query_matrix,
        query_offset,
        key_matrix,
        value_matrix,
        value_offset,
        output_matrix,
        output_offset,
        gain_first,
        shift_first,
        table_full,
    ) = attention_set
    inner_matrix, inner_offset, outer_matrix, outer_offset, gain_second, shift_second = feed_set
    tokens = hidden_in.reshape(token_count, model_width)
    queries = (
        (matmul("td,de->te", tokens, query_matrix) + query_offset.astype(jnp.float32))
        .astype(jnp.bfloat16)
        .reshape(row_count, window, model_width)
    )
    keys_own = (
        matmul("td,de->te", tokens, key_matrix)
        .astype(jnp.bfloat16)
        .reshape(row_count, window, model_width)
    )
    values_own = (
        (matmul("td,de->te", tokens, value_matrix) + value_offset.astype(jnp.float32))
        .astype(jnp.bfloat16)
        .reshape(row_count, window, model_width)
    )
    keys_all, values_all = (
        lax.all_gather(keys_own, "seq", axis=1, tiled=True),
        lax.all_gather(values_own, "seq", axis=1, tiled=True),
    )
    key_rel = matmul("pd,de->pe", table_full, key_matrix).astype(jnp.bfloat16)
    query_rel = (
        matmul("pd,de->pe", table_full, query_matrix) + query_offset.astype(jnp.float32)
    ).astype(jnp.bfloat16)
    reversed_buckets = buckets[::-1]
    table_rows = table_full.shape[0]
    one_hot = (
        reversed_buckets[:, None] == jnp.arange(table_rows, dtype=jnp.int32)[None, :]
    ).astype(jnp.bfloat16)
    bucket_keys = matmul("dp,pe->de", one_hot, key_rel).astype(jnp.bfloat16)
    bucket_queries = matmul("dp,pe->de", one_hot, query_rel).astype(jnp.bfloat16)
    near_keys = lax.dynamic_slice_in_dim(bucket_keys, near_start, span, 0)
    far_queries = lax.dynamic_slice_in_dim(bucket_queries, window_start, span, 0)
    segment_own = lax.dynamic_slice_in_dim(segments, window_start, window, 1)
    same_doc = (segment_own[:, :, None] == segments[:, None, :])[:, None]

    def pair_scores(pair_index):
        column = pair_index * pair_width
        query_pair = lax.dynamic_slice_in_dim(queries, column, pair_width, 2).reshape(
            row_count, window, 2, HEAD
        )
        key_pair = lax.dynamic_slice_in_dim(keys_all, column, pair_width, 2).reshape(
            row_count, length, 2, HEAD
        )
        value_pair = lax.dynamic_slice_in_dim(values_all, column, pair_width, 2).reshape(
            row_count, length, 2, HEAD
        )
        bucketkeys = lax.dynamic_slice_in_dim(near_keys, column, pair_width, 1).reshape(
            span, 2, HEAD
        )
        bucketqueries = lax.dynamic_slice_in_dim(far_queries, column, pair_width, 1).reshape(
            span, 2, HEAD
        )
        content = matmul("rihe,rjhe->rhij", query_pair, key_pair)
        near_scores = matmul("rihe,dhe->rhid", query_pair, bucketkeys)
        far_scores = matmul("rjhe,dhe->rhjd", key_pair, bucketqueries)
        to_position = skew_rows(near_scores, window - 1, length)
        from_position = jnp.swapaxes(skew_rows(far_scores, length - 1, window), 2, 3)
        summed = content + to_position + from_position
        masked = jnp.where(same_doc, summed * score_scale, NEGATIVE)
        return (masked, query_pair, key_pair, value_pair, bucketkeys, bucketqueries)

    def attend_pair(pair_index):
        masked, query_pair, key_pair, value_pair, bucketkeys, bucketqueries = pair_scores(
            pair_index
        )
        highest = jnp.max(masked, axis=-1, keepdims=True)
        expsum = jnp.exp(masked - highest)
        totals = jnp.sum(expsum, axis=-1, keepdims=True)
        weights_soft = (expsum / totals).astype(jnp.bfloat16)
        context_pair = matmul("rhij,rjhe->rihe", weights_soft, value_pair).astype(jnp.bfloat16)
        return (
            context_pair.reshape(row_count, window, pair_width),
            (highest + jnp.log(totals))[..., 0],
        )

    context_parts, log_totals = lax.map(attend_pair, jnp.arange(pair_count, dtype=jnp.int32))
    context = jnp.moveaxis(context_parts, 0, 2).reshape(token_count, model_width)
    attention_out = matmul("te,ed->td", context, output_matrix) + output_offset.astype(jnp.float32)
    residual_one = tokens.astype(jnp.float32) + attention_out
    first_out, first_normed, first_inverse = layer_norm(
        residual_one, gain_first.astype(jnp.float32), shift_first.astype(jnp.float32)
    )
    first_low = first_out.astype(jnp.bfloat16)
    inner_pre = matmul("td,df->tf", first_low, inner_matrix) + inner_offset.astype(jnp.float32)
    activated = jax.nn.gelu(inner_pre, approximate=False).astype(jnp.bfloat16)
    outer_out = matmul("tf,fd->td", activated, outer_matrix) + outer_offset.astype(jnp.float32)
    final_out, final_normed, final_inverse = layer_norm(
        first_out + outer_out, gain_second.astype(jnp.float32), shift_second.astype(jnp.float32)
    )
    result = final_out.astype(jnp.bfloat16).reshape(row_count, window, model_width)
    correct_count = lax.psum(jnp.sum((predicted == labels).astype(jnp.int32)), ("fsdp", "seq"))
    regathered = attention_set + feed_set
    (
        query_back,
        query_offset_back,
        key_back,
        value_back,
        value_offset_back,
        output_back,
        output_offset_back,
        gain_first_back,
        shift_first_back,
        table_back,
        inner_back,
        inner_offset_back,
        outer_back,
        outer_offset_back,
        gain_second_back,
        shift_second_back,
    ) = regathered
    upstream = cotangent.reshape(token_count, model_width).astype(jnp.float32)
    grad_sum2, grad_gain2, grad_shift2 = norm_backward(
        upstream, final_normed, final_inverse, gain_second_back.astype(jnp.float32)
    )
    grad_outer = grad_sum2.astype(jnp.bfloat16)
    outer_bias_part = jnp.sum(grad_outer.astype(jnp.float32), axis=0)
    outer_weight_part = matmul("tf,td->fd", activated, grad_outer)
    grad_act = matmul("td,fd->tf", grad_outer, outer_back).astype(jnp.bfloat16)
    _, gelu_back = jax.vjp(partial(jax.nn.gelu, approximate=False), inner_pre)
    grad_inner = gelu_back(grad_act.astype(jnp.float32))[0].astype(jnp.bfloat16)
    inner_bias_part = jnp.sum(grad_inner.astype(jnp.float32), axis=0)
    inner_weight_part = matmul("td,tf->df", first_low, grad_inner)
    grad_first = matmul("tf,df->td", grad_inner, inner_back) + grad_sum2
    feed_grads = (
        lax.psum_scatter(inner_weight_part, ("fsdp", "seq"), scatter_dimension=0, tiled=True),
        lax.psum_scatter(inner_bias_part, ("fsdp", "seq"), scatter_dimension=0, tiled=True),
        lax.psum_scatter(outer_weight_part, ("fsdp", "seq"), scatter_dimension=0, tiled=True),
        lax.psum_scatter(outer_bias_part, ("fsdp", "seq"), scatter_dimension=0, tiled=True),
        lax.psum_scatter(grad_gain2, ("fsdp", "seq"), scatter_dimension=0, tiled=True),
        lax.psum_scatter(grad_shift2, ("fsdp", "seq"), scatter_dimension=0, tiled=True),
    )
    grad_sum1, grad_gain1, grad_shift1 = norm_backward(
        grad_first, first_normed, first_inverse, gain_first_back.astype(jnp.float32)
    )
    grad_attention = grad_sum1.astype(jnp.bfloat16)
    output_bias_part = jnp.sum(grad_attention.astype(jnp.float32), axis=0)
    output_weight_part = matmul("te,td->ed", context, grad_attention)
    grad_context = (
        matmul("td,ed->te", grad_attention, output_back)
        .astype(jnp.bfloat16)
        .reshape(row_count, window, model_width)
    )

    def attend_back(pieces):
        pair_index, log_total = pieces
        masked, query_pair, key_pair, value_pair, bucketkeys, bucketqueries = pair_scores(
            pair_index
        )
        probability = jnp.exp(masked - log_total[..., None])
        grad_context_pair = lax.dynamic_slice_in_dim(
            grad_context, pair_index * pair_width, pair_width, 2
        ).reshape(row_count, window, 2, HEAD)
        grad_soft = matmul("rihe,rjhe->rhij", grad_context_pair, value_pair)
        grad_scores = probability * (
            grad_soft - jnp.sum(probability * grad_soft, axis=-1, keepdims=True)
        )
        grad_low = (grad_scores * score_scale).astype(jnp.bfloat16)
        grad_value = matmul("rhij,rihe->rjhe", probability.astype(jnp.bfloat16), grad_context_pair)
        grad_near = unskew_rows(grad_low, window - 1, span)
        grad_far = unskew_rows(jnp.swapaxes(grad_low, 2, 3), length - 1, span)
        grad_query = matmul("rhij,rjhe->rihe", grad_low, key_pair) + matmul(
            "rhid,dhe->rihe", grad_near, bucketkeys
        )
        grad_key = matmul("rhij,rihe->rjhe", grad_low, query_pair) + matmul(
            "rhjd,dhe->rjhe", grad_far, bucketqueries
        )
        grad_bkeys = matmul("rhid,rihe->dhe", grad_near, query_pair)
        grad_bqueries = matmul("rhjd,rjhe->dhe", grad_far, key_pair)
        return (
            grad_query.reshape(row_count, window, pair_width),
            grad_key.reshape(row_count, length, pair_width),
            grad_value.reshape(row_count, length, pair_width),
            grad_bkeys.reshape(span, pair_width),
            grad_bqueries.reshape(span, pair_width),
        )

    query_parts, key_parts, value_parts, bkey_parts, bquery_parts = lax.map(
        attend_back, (jnp.arange(pair_count, dtype=jnp.int32), log_totals)
    )
    grad_query_all = jnp.moveaxis(query_parts, 0, 2).reshape(token_count, model_width)
    grad_key_all = jnp.moveaxis(key_parts, 0, 2).reshape(row_count, length, model_width)
    grad_value_all = jnp.moveaxis(value_parts, 0, 2).reshape(row_count, length, model_width)
    near_grads = jnp.moveaxis(bkey_parts, 0, 1).reshape(span, model_width)
    far_grads = jnp.moveaxis(bquery_parts, 0, 1).reshape(span, model_width)
    grad_bucket_keys = lax.dynamic_update_slice_in_dim(
        jnp.zeros((distances, model_width), jnp.float32), near_grads, near_start, 0
    )
    grad_bucket_queries = lax.dynamic_update_slice_in_dim(
        jnp.zeros((distances, model_width), jnp.float32), far_grads, window_start, 0
    )
    key_grads, value_grads = (
        lax.psum_scatter(
            grad_key_all.astype(jnp.bfloat16), "seq", scatter_dimension=1, tiled=True
        ).astype(jnp.float32),
        lax.psum_scatter(
            grad_value_all.astype(jnp.bfloat16), "seq", scatter_dimension=1, tiled=True
        ).astype(jnp.float32),
    )
    query_low = grad_query_all.astype(jnp.bfloat16)
    key_low = key_grads.reshape(token_count, model_width).astype(jnp.bfloat16)
    value_low = value_grads.reshape(token_count, model_width).astype(jnp.bfloat16)
    grad_key_rel = jax.ops.segment_sum(grad_bucket_keys, reversed_buckets, num_segments=table_rows)
    grad_query_rel = jax.ops.segment_sum(
        grad_bucket_queries, reversed_buckets, num_segments=table_rows
    )
    query_token_part = matmul("td,te->de", tokens, query_low)
    query_bias_token = jnp.sum(query_low.astype(jnp.float32), axis=0)
    key_token_part = matmul("td,te->de", tokens, key_low)
    value_weight_part = matmul("td,te->de", tokens, value_low)
    value_bias_part = jnp.sum(value_low.astype(jnp.float32), axis=0)
    grad_input = (
        grad_sum1
        + matmul("te,de->td", query_low, query_back)
        + matmul("te,de->td", key_low, key_back)
        + matmul("te,de->td", value_low, value_back)
    )
    input_grad = grad_input.astype(jnp.bfloat16).reshape(row_count, window, model_width)
    key_rel_total, query_rel_total = lax.psum((grad_key_rel, grad_query_rel), ("fsdp", "seq"))
    attention_grads = (
        lax.psum_scatter(query_token_part, ("fsdp", "seq"), scatter_dimension=0, tiled=True),
        lax.psum_scatter(query_bias_token, ("fsdp", "seq"), scatter_dimension=0, tiled=True),
        lax.psum_scatter(key_token_part, ("fsdp", "seq"), scatter_dimension=0, tiled=True),
        lax.psum_scatter(value_weight_part, ("fsdp", "seq"), scatter_dimension=0, tiled=True),
        lax.psum_scatter(value_bias_part, ("fsdp", "seq"), scatter_dimension=0, tiled=True),
        lax.psum_scatter(output_weight_part, ("fsdp", "seq"), scatter_dimension=0, tiled=True),
        lax.psum_scatter(output_bias_part, ("fsdp", "seq"), scatter_dimension=0, tiled=True),
        lax.psum_scatter(grad_gain1, ("fsdp", "seq"), scatter_dimension=0, tiled=True),
        lax.psum_scatter(grad_shift1, ("fsdp", "seq"), scatter_dimension=0, tiled=True),
    )
    shard_rows = query_weight.shape[0]
    shard_start = lax.axis_index(("fsdp", "seq")) * shard_rows
    table_shard = relative_table.astype(jnp.float32)
    query_weight_grad = attention_grads[0] + precise("pd,pe->de", table_shard, query_rel_total)
    key_weight_grad = attention_grads[2] + precise("pd,pe->de", table_shard, key_rel_total)
    query_bias_grad = attention_grads[1] + jnp.sum(
        lax.dynamic_slice_in_dim(query_rel_total, shard_start, shard_rows, 1), axis=0
    )
    relative_table_grad = precise(
        "pe,de->pd", query_rel_total, query_weight.astype(jnp.float32)
    ) + precise("pe,de->pd", key_rel_total, key_weight.astype(jnp.float32))
    return (
        result,
        input_grad,
        query_weight_grad,
        query_bias_grad,
        key_weight_grad,
        attention_grads[3],
        attention_grads[4],
        attention_grads[5],
        attention_grads[6],
        attention_grads[7],
        attention_grads[8],
        feed_grads[0],
        feed_grads[1],
        feed_grads[2],
        feed_grads[3],
        feed_grads[4],
        feed_grads[5],
        relative_table_grad,
        correct_count,
    )


MESH = pl.DeviceIdType.MESH
F32 = jnp.float32
BF16 = jnp.bfloat16


def dot(left, right, left_dim=1, right_dim=0):
    return lax.dot_general(
        left, right, (((left_dim,), (right_dim,)), ((), ())), preferred_element_type=F32
    )


def low(value):
    return value.astype(BF16)


class Route:
    def __init__(self):
        chip = lax.axis_index("fsdp")
        self.core = lax.axis_index("seq")
        self.other = 1 - self.core
        self.chip = chip
        self.x = chip % 2
        self.y = (chip // 2) % 2
        self.z = chip // 4
        self.plane = chip % 4
        self.plane_x = self.plane + 1 - 2 * self.x
        self.plane_y = self.plane + 2 - 4 * self.y
        self.pair = self.z + 1 - 2 * (self.z % 2)
        self.near = (self.z, (self.z + 2) % LINE)
        self.far = (self.pair, (self.pair + 2) % LINE)
        self.partner = (chip, self.other)
        self.at_x = (self.z * 4 + self.plane_x, self.core)
        self.at_y = (self.z * 4 + self.plane_y, self.core)

    def at_line(self, line):
        return (line * 4 + self.plane, self.core)

    def ahead(self, step):
        return (self.z + step) % LINE

    def behind(self, step):
        return (self.z + LINE - step) % LINE


def remote(source, target, send_sem, recv_sem, device):
    return pltpu.make_async_remote_copy(
        source, target, send_sem, recv_sem, device_id=device, device_id_type=MESH
    )


class Gather:
    def __init__(self, route, arrays, send, recv):
        self.r, self.arrays, self.send, self.recv = route, arrays, send, recv

    def copies(self, kind, line):
        r = self.r
        for i, array in enumerate(self.arrays):
            by_x = i == 1
            plane, device = (
                (r.plane, r.at_line((r.z + 1) % LINE)),
                (r.plane, r.at_line((r.z + LINE - 1) % LINE)),
                (r.plane, r.at_x),
                (r.plane, r.at_y),
                (r.plane_y, r.at_x) if by_x else (r.plane_x, r.at_y),
                (3 - r.plane, r.at_line(r.pair)),
            )[kind]
            block = array.at[line, plane]
            yield remote(
                block, block, self.send.at[i, kind, line], self.recv.at[i, kind, line], device
            )

    def begin(self, kind, line):
        for copy in self.copies(kind, line):
            copy.start()

    def got(self, kind, line):
        for copy in self.copies(kind, line):
            copy.wait_recv()

    def sides(self, line):
        self.begin(2, line)
        self.begin(3, line)

    def got_sides(self, line):
        self.got(2, line)
        self.got(3, line)

    def up(self, line):
        @pl.when(self.r.z < LINE - 1)
        def _():
            self.begin(0, line)

    def down(self, line):
        @pl.when(self.r.z > 0)
        def _():
            self.begin(1, line)

    def start_line(self):
        self.up(self.r.z)
        self.down(self.r.z)

    def start_sides(self):
        self.sides(self.r.z)

    def round(self, step):
        r = self.r

        @pl.when(r.z >= step)
        def _():
            self.got(0, r.z - step)
            self.up(r.z - step)
            self.sides(r.z - step)

        @pl.when(r.z + step < LINE)
        def _():
            self.got(1, r.z + step)
            self.down(r.z + step)
            self.sides(r.z + step)

    def corner(self, which):
        line = self.r.near[which]
        self.got_sides(line)
        self.begin(4, line)

    def hand(self, which):
        line = self.r.near[which]
        self.got(4, line)
        self.begin(5, line)

    def finish(self):
        for line in self.r.far:
            self.got_sides(line)
            self.got(5, line)

    def drained(self, kind, line):
        for copy in self.copies(kind, line):
            copy.wait_send()

    def sent(self):
        r = self.r
        for line in range(LINE):

            @pl.when((r.z < LINE - 1) & (r.z >= line))
            def _():
                self.drained(0, line)

            @pl.when((r.z > 0) & (r.z <= line))
            def _():
                self.drained(1, line)

            self.drained(2, line)
            self.drained(3, line)
        for line in r.near:
            self.drained(4, line)
            self.drained(5, line)


class Scatter:
    def __init__(self, route, arrays, rooms, send, recv):
        self.r, self.arrays, self.rooms = route, arrays, rooms
        self.send, self.recv = send, recv

    def across(self, i):
        return self.r.plane_y if i == 0 else self.r.plane_x

    def copy(self, i, kind, line):
        r = self.r
        near, across = (r.at_x, r.at_y) if i == 0 else (r.at_y, r.at_x)
        near_plane = r.plane_x if i == 0 else r.plane_y
        plane, room, device = (
            (3 - r.plane, line // 2, r.at_line(r.pair)),
            (near_plane, line, near),
            (3 - r.plane, line // 2, near),
            (self.across(i), line, across),
            (r.plane, r.z, r.at_line(line)),
        )[kind]
        return remote(
            self.arrays[i].at[line, plane],
            self.rooms[i][kind].at[room],
            self.send.at[i, kind, line],
            self.recv.at[i, kind, r.z if kind == 4 else line],
            device,
        )

    def got_along(self, i, line):
        r = self.r
        remote(
            self.arrays[i].at[line, r.plane],
            self.rooms[i][4].at[line],
            self.send.at[i, 4, line],
            self.recv.at[i, 4, line],
            r.at_line(line),
        ).wait_recv()

    def begin_far(self, i, line):
        for kind in (0, 1, 3):
            self.copy(i, kind, line).start()

    def begin_near(self, i, line):
        self.copy(i, 1, line).start()

    def begin(self, i):
        for line in self.r.far:
            self.begin_far(i, line)
        for line in self.r.near[::-1]:
            self.begin_near(i, line)

    def merge(self, i, line, plane, *came):
        at = self.arrays[i].at[line, plane]
        value = at[...].astype(F32)
        for kind, room in came:
            value = value + self.rooms[i][kind][room].astype(F32)
        at[...] = low(value)

    def corners(self, i):
        for line in self.r.near[::-1]:
            self.copy(i, 0, line).wait_recv()
            self.merge(i, line, 3 - self.r.plane, (0, line // 2))
            self.copy(i, 2, line).start()

    def turn(self, i):
        for line in self.r.near[::-1]:
            self.copy(i, 2, line).wait_recv()
            self.merge(i, line, self.across(i), (2, line // 2))
            self.copy(i, 3, line).start()

    def along(self, i, line):
        self.copy(i, 1, line).wait_recv()
        self.copy(i, 3, line).wait_recv()
        self.merge(i, line, self.r.plane, (1, line), (3, line))
        self.copy(i, 4, line).start()

    def along_far(self, i):
        for line in self.r.far:
            self.along(i, line)

    def along_near(self, i):
        self.along(i, self.r.near[1])

    def total(self, i):
        r = self.r
        self.copy(i, 1, r.z).wait_recv()
        self.copy(i, 3, r.z).wait_recv()
        rooms = self.rooms[i]
        value = self.arrays[i][r.z, r.plane].astype(F32)
        value = value + rooms[1][r.z].astype(F32) + rooms[3][r.z].astype(F32)
        for line in r.far + r.near[1:]:
            self.got_along(i, line)
            value = value + rooms[4][line].astype(F32)
        return value

    def sent(self):
        r = self.r
        for i in (0, 1):
            for line in range(LINE):
                self.copy(i, 1, line).wait_send()
                self.copy(i, 3, line).wait_send()
            for line in r.far:
                self.copy(i, 0, line).wait_send()
                self.copy(i, 4, line).wait_send()
            for line in r.near:
                self.copy(i, 2, line).wait_send()
            self.copy(i, 4, r.near[1]).wait_send()


def loop(count, body):
    def step(index, carry):
        body(index)
        return carry

    lax.fori_loop(0, count, step, 0)


def aligned(index, size):
    return pl.ds(pl.multiple_of(index * size, size), size)


def erf_parts(value):
    tail = lax.erf(value * np.float32(0.5**0.5))
    half = 0.5 * (1.0 + tail)
    density = jnp.exp(value * value * -0.5) * np.float32((2.0 * np.pi) ** -0.5)
    return value * half, half + value * density


def norm(values, gain, shift):
    average = jnp.mean(values, axis=-1, keepdims=True)
    centred = values - average
    variance = jnp.mean(centred * centred, axis=-1, keepdims=True)
    inverse = lax.rsqrt(variance + EPSILON)
    normed = centred * inverse
    return normed * gain + shift, normed, inverse


def norm_pull(upstream, normed, inverse, gain):
    scaled_up = upstream * gain
    first_mean = jnp.mean(scaled_up, axis=-1, keepdims=True)
    second_mean = jnp.mean(scaled_up * normed, axis=-1, keepdims=True)
    return inverse * (scaled_up - first_mean - normed * second_mean)


def layer_kernel(names, *refs):
    b = dict(zip(names, refs))
    at = type("Refs", (), b)
    r = Route()
    core, other = r.core, r.other
    own_rows = aligned(core, 256)
    other_rows = aligned(other, 256)
    score_scale = np.float32((3.0 * HEAD) ** (-0.5))

    barrier = pltpu.get_barrier_semaphore()
    friends = [r.partner, r.at_x, r.at_y] + [r.at_line(r.ahead(k)) for k in range(1, LINE)]
    for device in friends:
        pl.semaphore_signal(barrier, inc=1, device_id=device, device_id_type=MESH)

    waiting = []

    def swap(slot, source, target):
        copy = remote(source, target, at.swap_send.at[slot], at.swap_recv.at[slot], r.partner)
        copy.start()
        waiting.append(copy)
        return copy

    gather_one = Gather(r, (at.gat_a, at.gat_b, at.gat_s), at.ga_send, at.ga_recv)
    gather_two = Gather(r, (at.gat_1, at.gat_2), at.gf_send, at.gf_recv)

    at.sums[...] = jnp.zeros_like(at.sums)
    at.small_wide[...] = jnp.zeros_like(at.small_wide)
    small_rows = (
        at.query_b, at.value_b, at.output_b, at.gain_1, at.shift_1, at.outer_b, at.gain_2, at.shift_2,
        at.inner_b,
    )
    for index, row in enumerate(small_rows):
        at.small_wide[index : index + 1, 0 : row.shape[1]] = row[...].astype(F32)
    at.small[...] = low(at.small_wide[...])
    right = (at.predicted[...] == at.labels[...]).astype(F32)
    at.sums[10:11, :] = jnp.broadcast_to(jnp.sum(right, axis=1, keepdims=True), (1, 768))
    pl.semaphore_wait(barrier, len(friends))

    half = aligned(other, 384)
    arrive = [
        swap(0, at.key_w.at[:, half], at.come_a.at[:, pl.ds(0, 384)]),
        swap(1, at.value_w.at[:, half], at.come_a.at[:, pl.ds(384, 384)]),
        swap(2, at.query_w.at[:, half], at.come_b.at[:, pl.ds(0, 384)]),
        swap(3, at.output_w.at[:, half], at.come_b.at[:, pl.ds(384, 384)]),
        swap(4, at.table_t.at[:, aligned(other, 256)], at.come_b.at[:, pl.ds(768, 256)]),
        swap(5, at.small, at.come_s),
    ]
    come_x = swap(7, at.hidden, at.x_all.at[own_rows])
    place_x = pltpu.make_async_copy(at.hidden, at.x_all.at[own_rows], at.here.at[0])
    place_x.start()
    place_2 = pltpu.make_async_copy(at.outer_w, at.gat_2.at[r.z, r.plane], at.here.at[1])
    place_2.start()
    for copy in arrive:
        copy.wait_recv()

    def stack(mine, came):
        mine, came = mine.astype(F32), came.astype(F32)
        upper = jnp.where(core == 0, mine, came)
        lower = jnp.where(core == 0, came, mine)
        return low(jnp.concatenate([upper, lower], axis=0))

    mine_half = aligned(core, 384)
    at.gat_a[r.z, r.plane, :, 0:384] = stack(at.key_w[:, mine_half], at.come_a[:, 0:384])
    at.gat_a[r.z, r.plane, :, 384:768] = stack(at.value_w[:, mine_half], at.come_a[:, 384:768])
    at.gat_b[r.z, r.plane, :, 0:384] = stack(at.query_w[:, mine_half], at.come_b[:, 0:384])
    at.gat_b[r.z, r.plane, :, 384:768] = stack(at.output_w[:, mine_half], at.come_b[:, 384:768])
    at.gat_b[r.z, r.plane, :, 768:1024] = stack(
        at.table_t[:, aligned(core, 256)], at.come_b[:, 768:1024]
    )
    at.gat_s[r.z, r.plane, core] = at.small[...]
    at.gat_s[r.z, r.plane, other] = at.come_s[...]
    gather_one.start_line()
    gather_one.start_sides()
    for chip in range(4 * LINE):
        for which in range(2):
            device = 2 * chip + which
            at.inner_pair[which, :, 96 * chip : 96 * chip + 96] = at.inner_w[
                :, 96 * device : 96 * device + 96
            ]
    come_inner = swap(6, at.inner_pair.at[other], at.come_1)
    come_inner.wait_recv()
    at.gat_1[r.z, r.plane] = stack(at.inner_pair[core], at.come_1[...])
    place_2.wait()
    place_x.wait()
    come_x.wait_recv()
    at.x_turned[...] = at.x_all[...].T
    wide_i = lax.broadcasted_iota(jnp.int32, (512, 512), 0)
    wide_j = lax.broadcasted_iota(jnp.int32, (512, 512), 1)
    used = low((at.buckets[0:1, 256:768] == wide_i).astype(F32))
    at.one_hot[...] = low(dot(used, low((wide_i + wide_j == 511).astype(F32))))
    segment_wide = jnp.broadcast_to(at.segments[...].astype(F32), (128, 512))
    at.segment_row[...] = segment_wide[0:8]
    at.segment_col[...] = segment_wide.T
    flip_i = lax.broadcasted_iota(jnp.int32, (128, 128), 0)
    flip_j = lax.broadcasted_iota(jnp.int32, (128, 128), 1)
    at.flip[...] = low((flip_i + flip_j == 127).astype(F32))
    for table in (at.near_rows, at.far_rows):
        table[0:256, :] = jnp.zeros((256, 384), BF16)
        table[768:1024, :] = jnp.zeros((256, 384), BF16)
    gather_one.round(1)
    gather_one.corner(0)
    gather_one.round(2)
    gather_one.hand(0)
    gather_one.round(3)
    gather_one.corner(1)
    gather_two.start_sides()
    gather_one.hand(1)
    gather_two.start_line()
    gather_one.finish()

    out_mine = at.gat_b.at[:, :, :, pl.ds(384, 384)]
    table_mine = at.gat_b.at[:, :, :, pl.ds(768, 256)]
    come_table = swap(8, table_mine, at.table_all.at[core])
    come_out = swap(9, out_mine, at.out_all.at[core])
    place_table = pltpu.make_async_copy(table_mine, at.table_all.at[core], at.here.at[0])
    place_table.start()
    place_out = pltpu.make_async_copy(out_mine, at.out_all.at[core], at.here.at[1])
    place_out.start()

    for line in range(LINE):
        for plane in range(4):
            chip = line * 4 + plane
            for which in range(2):
                device = 2 * chip + which
                tile = at.gat_s[line, plane, which].astype(F32)
                at.vectors[:, 24 * device : 24 * device + 24] = tile[0:8, 0:24]
            tile = at.gat_s[line, plane, core].astype(F32)
            at.inner_bias[0:1, 96 * chip : 96 * chip + 96] = tile[8:9, 0:96]

    def rows(value):
        return value.reshape(768, value.shape[-1])

    vector_half = aligned(core, 384)
    query_bias = at.vectors[0:1, vector_half]
    value_bias = at.vectors[1:2, vector_half]
    at.kvq[:, 0:384] = low(dot(at.x_all[...], rows(at.gat_a[:, :, :, 0:384])))
    at.kvq[:, 384:768] = low(dot(at.x_all[...], rows(at.gat_a[:, :, :, 384:768])) + value_bias)
    at.kvq[:, 768:1152] = low(dot(at.x_all[...], rows(at.gat_b[:, :, :, 0:384])) + query_bias)
    place_table.wait()
    come_table.wait_recv()
    for part in range(2):
        piece = pl.ds(256 * part, 256)
        table = rows(at.table_all[part])
        at.key_rel[piece, :] = low(dot(table, rows(at.gat_a[:, :, :, 0:384]), 0, 0))
        at.query_rel[piece, :] = low(dot(table, rows(at.gat_b[:, :, :, 0:384]), 0, 0) + query_bias)
    at.near_rows[256:768, :] = low(dot(at.one_hot[...], at.key_rel[...], 0, 0))
    at.far_rows[256:768, :] = low(dot(at.one_hot[...], at.query_rel[...], 0, 0))

    gather_two.round(1)
    gather_two.corner(0)

    lanes = lax.broadcasted_iota(jnp.int32, (1, 128), 1) // HEAD
    no_score = np.float32(NEGATIVE)

    def forward_head(head):
        pair = aligned(head // 2, 128)
        key_lanes = pl.ds(pl.multiple_of((head // 2) * 128, 128), 128)
        value_lanes = pl.ds(pl.multiple_of(384 + (head // 2) * 128, 128), 128)
        query_lanes = pl.ds(pl.multiple_of(768 + (head // 2) * 128, 128), 128)
        mine = lanes == head % 2
        only = low(mine.astype(F32))
        keys = at.kvq[:, key_lanes]
        values = at.kvq[:, value_lanes]
        for block in range(4):
            piece = pl.ds(128 * block, 128)
            shifted = dot(
                at.kvq[piece, key_lanes] * only, at.far_rows[pl.ds(384 - 128 * block, 640), pair], 1, 1
            )
            at.far_scores[piece, :] = pltpu.roll(shifted, 0, 1, stride=1, stride_axis=0)[:, 128:640]
        for block in range(4):
            piece = pl.ds(128 * block, 128)
            queries = at.kvq[piece, query_lanes] * only
            shifted = dot(queries, at.near_rows[pl.ds(384 - 128 * block, 640), pair], 1, 1)
            summed = (
                dot(queries, keys, 1, 1)
                + pltpu.roll(shifted, 0, 1, stride=1, stride_axis=0)[:, 128:640]
                + at.far_scores[:, piece].T
            )
            masked = jnp.where(
                at.segment_col[piece, 0:1] == at.segment_row[0:1, :], summed * score_scale, no_score
            )
            highest = jnp.max(masked, axis=-1, keepdims=True)
            expsum = jnp.exp(masked - highest)
            soft = expsum / jnp.sum(expsum, axis=-1, keepdims=True)
            at.soft[head, piece, :] = soft
            context = dot(low(soft), values)
            here = at.context.at[core, piece, pair]
            here[...] = low(jnp.where(mine, context, here[...].astype(F32)))

    def forward_pair(index):
        def forward(which):
            head = 2 * index + which
            forward_head(head)
            for after, move in (
                (1, lambda: gather_two.round(2)),
                (3, lambda: gather_two.hand(0)),
                (4, lambda: gather_two.round(3)),
            ):
                pl.when(head == after)(move)

        loop(2, forward)
        remote(
            at.context.at[core, :, aligned(index, 128)],
            at.context.at[core, :, aligned(index, 128)],
            at.context_send.at[index],
            at.context_recv.at[index],
            r.partner,
        ).start()

    loop(3, forward_pair)
    place_out.wait()
    come_out.wait_recv()
    for index in range(3):
        remote(
            at.context.at[other, :, pl.ds(128 * index, 128)],
            at.context.at[other, :, pl.ds(128 * index, 128)],
            at.context_send.at[index],
            at.context_recv.at[index],
            r.partner,
        ).wait_recv()

    def vector(index):
        return at.vectors[index : index + 1, :]

    for part in range(2):
        piece = pl.ds(384 * part, 384)
        weight = rows(at.out_all[part])
        at.wide[:, piece] = dot(at.context[0, own_rows, :], weight[0:384]) + dot(
            at.context[1, own_rows, :], weight[384:768]
        )

    def first_norm(index):
        piece = aligned(index, 64)
        token_rows = pl.ds(pl.multiple_of(core * 256 + index * 64, 64), 64)
        residual = at.x_all[token_rows, :].astype(F32) + at.wide[piece, :] + vector(2)
        out, normed, inverse = norm(residual, vector(3), vector(4))
        at.first_out[piece, :] = out
        at.first_normed[piece, :] = normed
        at.first_inverse[piece, :] = jnp.broadcast_to(inverse, (64, 128))
        at.first_low[token_rows, :] = low(out)

    loop(4, first_norm)
    come_first = swap(10, at.first_low.at[own_rows], at.first_low.at[own_rows])
    gather_two.corner(1)
    come_first.wait_recv()
    at.first_turned[...] = at.first_low[...].T
    gather_two.hand(1)
    gather_two.finish()

    def inner_units(index):
        piece = aligned(index, 256)
        pre = dot(at.first_low[...], rows(at.gat_1[:, :, :, piece])) + at.inner_bias[0:1, piece]
        value, slope = erf_parts(pre)
        at.active[:, piece] = low(value)
        at.slope[:, piece] = slope

    loop(6, inner_units)

    def outer_half(rows_at, out):
        for part in range(3):
            piece = pl.ds(256 * part, 256)
            out[:, piece] = dot(
                at.active[rows_at, :], at.gat_2[:, :, :, piece].reshape(1536, 256)
            )

    outer_half(other_rows, at.part_send)
    come_outer = swap(11, at.part_send, at.part_recv)
    outer_half(own_rows, at.wide)
    come_outer.wait_recv()

    def second_norm(index):
        piece = aligned(index, 64)
        token_rows = pl.ds(pl.multiple_of(core * 256 + index * 64, 64), 64)
        total = at.first_out[piece, :] + at.wide[piece, :] + at.part_recv[piece, :] + vector(5)
        out, normed, inverse = norm(total, vector(6), vector(7))
        at.result[piece, :] = low(out)
        upstream = at.cotangent[piece, :].astype(F32)
        grad = norm_pull(upstream, normed, inverse, vector(6))
        at.grad_sum[piece, :] = grad
        rounded = low(grad)
        at.grad_outer[token_rows, :] = rounded
        at.sums[5:6, :] += jnp.sum(rounded.astype(F32), axis=0, keepdims=True)
        at.sums[6:7, :] += jnp.sum(upstream * normed, axis=0, keepdims=True)
        at.sums[7:8, :] += jnp.sum(upstream, axis=0, keepdims=True)

    loop(4, second_norm)
    come_grad = swap(12, at.grad_outer.at[own_rows], at.grad_outer.at[own_rows])

    def scatter(arrays, tags, send, recv):
        rooms = [[b[kind + tag] for kind in ROOMS] for tag in tags]
        return Scatter(r, arrays, rooms, send, recv)

    scatter_two = scatter((at.grad_1, at.grad_2), ("1", "2"), at.sf_send, at.sf_recv)
    scatter_a = scatter((at.grad_o, at.grad_p.at[0]), ("o", "p0"), at.sa_send, at.sa_recv)
    scatter_b = scatter((at.grad_p.at[1], at.grad_p.at[2]), ("p1", "p2"), at.sb_send, at.sb_recv)
    scatter_c = scatter((at.grad_t.at[0], at.grad_t.at[1]), ("t0", "t1"), at.sc_send, at.sc_recv)
    come_grad.wait_recv()

    def line_of(index):
        half = index // 2
        start = r.pair * (1 - half) + r.z * half
        return (start + 2 * ((index + 1) // 2 % 2)) % LINE

    def send_lines(i, index, line):
        pl.when(index < 2)(lambda: scatter_two.begin_far(i, line))
        pl.when(index >= 2)(lambda: scatter_two.begin_near(i, line))

    def outer_weight(index):
        line = line_of(index)
        grad = dot(at.active[:, aligned(line, 384)], at.grad_outer[...], 0, 0)
        at.grad_2[line] = low(grad).reshape(4, 96, 768)
        send_lines(1, index, line)

    loop(4, outer_weight)

    def inner_grad(index):
        units = aligned(index, 384)
        grad = low(dot(at.grad_outer[...], at.gat_2[index].reshape(384, 768), 1, 1))
        pre = low(grad.astype(F32) * at.slope[:, units])
        at.grad_pre[:, units] = pre
        at.bias_inner[0:1, units] = jnp.sum(pre.astype(F32), axis=0, keepdims=True)

    loop(4, inner_grad)

    def inner_weight(index):
        line = line_of(index)
        grad = dot(at.first_turned[aligned(line, 192), :], at.grad_pre[...])
        at.grad_1[line] = low(grad).reshape(4, 48, 1536)
        send_lines(0, index, line)

    loop(4, inner_weight)
    at.sums[8:9, :] = at.bias_inner[0:1, 0:768]
    at.sums[9:10, :] = at.bias_inner[0:1, 768:1536]

    def first_half(rows_at, out):
        for part in range(2):
            weight = at.gat_1[2 * part : 2 * part + 2].reshape(384, 1536)
            out[:, 384 * part : 384 * part + 384] = dot(at.grad_pre[rows_at, :], weight, 1, 1)

    first_half(other_rows, at.part_send2)
    come_grad_first = swap(13, at.part_send2, at.part_recv2)
    first_half(own_rows, at.wide)
    come_grad_first.wait_recv()

    def first_norm_back(index):
        piece = aligned(index, 64)
        token_rows = pl.ds(pl.multiple_of(core * 256 + index * 64, 64), 64)
        upstream = at.wide[piece, :] + at.part_recv2[piece, :] + at.grad_sum[piece, :]
        normed = at.first_normed[piece, :]
        grad = norm_pull(upstream, normed, at.first_inverse[piece, 0:1], vector(3))
        at.grad_sum[piece, :] = grad
        rounded = low(grad)
        at.grad_att[token_rows, :] = rounded
        at.sums[2:3, :] += jnp.sum(rounded.astype(F32), axis=0, keepdims=True)
        at.sums[3:4, :] += jnp.sum(upstream * normed, axis=0, keepdims=True)
        at.sums[4:5, :] += jnp.sum(upstream, axis=0, keepdims=True)

    loop(4, first_norm_back)
    come_att = swap(14, at.grad_att.at[own_rows], at.grad_att.at[own_rows])
    come_att.wait_recv()
    scatter_two.corners(1)
    out_rows = pl.ds(pl.multiple_of(2 * core, 2), 2)
    weight_0 = at.out_all[0, out_rows].reshape(384, 384)
    weight_1 = at.out_all[1, out_rows].reshape(384, 384)
    at.grad_context[...] = low(
        dot(at.grad_att[:, 0:384], weight_0, 1, 1) + dot(at.grad_att[:, 384:768], weight_1, 1, 1)
    )
    for part in range(2):
        grad = dot(at.context[part], at.grad_att[:, aligned(core, 384)], 0, 0)
        at.grad_o[2 * part : 2 * part + 2] = low(grad).reshape(2, 4, 48, 384)

    at.near_grad[...] = jnp.zeros_like(at.near_grad)
    at.far_grad[...] = jnp.zeros_like(at.far_grad)
    room = jnp.zeros((128, 128), BF16)

    def spread(flipped):
        return pltpu.roll(jnp.concatenate([flipped, room], axis=1), 1, 1, stride=1, stride_axis=0)

    def backward_head(head):
        pair = aligned(head // 2, 128)
        key_lanes = pl.ds(pl.multiple_of((head // 2) * 128, 128), 128)
        value_lanes = pl.ds(pl.multiple_of(384 + (head // 2) * 128, 128), 128)
        query_lanes = pl.ds(pl.multiple_of(768 + (head // 2) * 128, 128), 128)
        mine = lanes == head % 2
        only = low(mine.astype(F32))
        flip = at.flip[...]
        keys = at.kvq[:, key_lanes]
        queries = at.kvq[:, query_lanes]
        values = at.kvq[:, value_lanes]

        def merge(here, value):
            here[...] = low(jnp.where(mine, value, here[...].astype(F32)))

        for block in range(4):
            piece = pl.ds(128 * block, 128)
            window = pl.ds(384 - 128 * block, 640)
            soft = at.soft[head, piece, :]
            grad_soft = dot(at.grad_context[piece, pair] * only, values, 1, 1)
            inner = jnp.sum(soft * grad_soft, axis=-1, keepdims=True)
            grad_low = low(soft * (grad_soft - inner) * score_scale)
            at.grad_low[piece, :] = grad_low
            flipped = low(dot(flip, grad_low))
            near = spread(flipped)
            grad = low(dot(flipped, keys) + dot(near, at.near_rows[window, pair]))
            merge(at.grad_kvq.at[piece, query_lanes], dot(flip, grad))
            back = low(dot(flip, at.kvq[piece, query_lanes] * only))
            at.near_grad[window, pair] += dot(near, back, 0, 0)
        grad_context = at.grad_context[:, pair]
        for block in range(4):
            piece = pl.ds(128 * block, 128)
            window = pl.ds(384 - 128 * block, 640)
            flipped = low(dot(flip, at.grad_low[:, piece], 1, 1))
            far = spread(flipped)
            grad = low(dot(flipped, queries) + dot(far, at.far_rows[window, pair]))
            merge(at.grad_kvq.at[piece, key_lanes], dot(flip, grad))
            back = low(dot(flip, at.kvq[piece, key_lanes] * only))
            at.far_grad[window, pair] += dot(far, back, 0, 0)
            weights = low(at.soft[head, :, piece])
            merge(at.grad_kvq.at[piece, value_lanes], dot(weights, grad_context, 0, 0))

    def shape_weight(value):
        return low(value).reshape(LINE, 4, 48, value.shape[-1])

    def weights_pair(index):
        pair = aligned(index, 128)
        at.key_rel[:, pair] = low(dot(at.one_hot[...], low(at.near_grad[256:768, pair])))
        at.query_rel[:, pair] = low(dot(at.one_hot[...], low(at.far_grad[256:768, pair])))
        for place, rel in enumerate((at.key_rel, None, at.query_rel)):
            lanes_at = pl.ds(pl.multiple_of(384 * place + index * 128, 128), 128)
            grad = dot(at.x_turned[...], at.grad_kvq[:, lanes_at])
            if rel is not None:
                for part in range(2):
                    grad = grad + dot(rows(at.table_all[part]), rel[256 * part : 256 * part + 256, pair])
            at.grad_p[index, :, :, :, 128 * place : 128 * place + 128] = shape_weight(grad)

    def at_step(step, when, *moves):
        @pl.when(step == when)
        def _():
            for move in moves:
                move()

    def backward_pair(index):
        def backward(which):
            head = 2 * index + which
            backward_head(head)
            at_step(head, 0, lambda: scatter_two.corners(0))
            at_step(
                head, 2, lambda: scatter_two.along_far(1), lambda: scatter_two.along_far(0)
            )
            at_step(head, 3, lambda: scatter_two.turn(1))
            at_step(head, 4, lambda: scatter_two.turn(0), lambda: scatter_a.corners(0))

        loop(2, backward)
        weights_pair(index)
        at_step(index, 0, lambda: scatter_a.begin(0), lambda: scatter_a.begin(1))
        at_step(index, 1, lambda: scatter_b.begin(0))
        at_step(index, 2, lambda: scatter_b.begin(1))

    loop(3, backward_pair)

    def table_half(which):
        piece = aligned(which, 256)
        return dot(rows(at.gat_b[:, :, :, 0:384]), at.query_rel[piece, :], 1, 1) + dot(
            rows(at.gat_a[:, :, :, 0:384]), at.key_rel[piece, :], 1, 1
        )

    at.table_send[...] = shape_weight(table_half(other))
    come_part = swap(15, at.table_send, at.table_recv)
    own_table = table_half(core)
    scatter_two.along_near(1)
    come_part.wait_recv()
    own_table = own_table + rows(at.table_recv[...]).astype(F32)
    for part in range(2):
        at.grad_t[part] = shape_weight(own_table[:, 128 * part : 128 * part + 128])
        scatter_c.begin(part)
    scatter_two.along_near(0)
    scatter_a.corners(1)
    scatter_b.corners(0)
    scatter_a.turn(0)

    at.sums[0:1, vector_half] = jnp.sum(
        at.grad_kvq[:, 768:1152].astype(F32), axis=0, keepdims=True
    ) + jnp.sum(at.far_grad[256:768, :], axis=0, keepdims=True)
    at.sums[1:2, vector_half] = jnp.sum(
        at.grad_kvq[:, 384:768].astype(F32), axis=0, keepdims=True
    )

    def exchange(stage, source, device):
        return remote(
            source, at.sums_come.at[stage], at.sums_send.at[stage], at.sums_recv.at[stage], device
        )

    stage_copies = [exchange(0, at.sums, r.partner)]
    stage_copies[0].start()

    def input_half(rows_at, out):
        for part in range(2):
            weight_a = at.gat_a[2 * part : 2 * part + 2].reshape(384, 768)
            weight_b = at.gat_b[2 * part : 2 * part + 2, :, :, 0:384].reshape(384, 384)
            out[:, 384 * part : 384 * part + 384] = dot(
                at.grad_kvq[rows_at, 0:768], weight_a, 1, 1
            ) + dot(at.grad_kvq[rows_at, 768:1152], weight_b, 1, 1)

    come_outer.wait_send()
    input_half(other_rows, at.part_send)
    come_input = swap(16, at.part_send, at.part_recv)

    stage_copies[0].wait_recv()
    lines = lax.broadcasted_iota(jnp.int32, (16, 1), 0)
    shared = jnp.where((lines == 8) | (lines == 9), 0.0, at.sums_come[0])
    at.sums_step[0] = at.sums[...] + shared
    stage_copies.append(exchange(1, at.sums_step.at[0], r.at_x))
    stage_copies[1].start()
    scatter_b.corners(1)
    scatter_a.along_far(0)
    scatter_a.turn(1)
    scatter_b.turn(0)
    input_half(own_rows, at.wide)
    for part in range(2):
        scatter_c.corners(part)
    scatter_a.along_far(1)
    scatter_b.along_far(0)
    scatter_b.turn(1)
    stage_copies[1].wait_recv()
    at.sums_step[1] = at.sums_step[0] + at.sums_come[1]
    stage_copies.append(exchange(2, at.sums_step.at[1], r.at_y))
    stage_copies[2].start()
    come_input.wait_recv()
    at.input_grad[...] = low(at.grad_sum[...] + at.wide[...] + at.part_recv[...])
    for part in range(2):
        scatter_a.along_near(part)
    for part in range(2):
        scatter_c.turn(part)
    scatter_b.along_near(0)
    scatter_b.along_far(1)
    for part in range(2):
        scatter_c.along_far(part)
    scatter_b.along_near(1)
    for part in range(2):
        scatter_c.along_near(part)
    stage_copies[2].wait_recv()
    at.sums_step[2] = at.sums_step[1] + at.sums_come[2]
    for step in range(1, LINE):
        copy = exchange(2 + step, at.sums_step.at[2], r.at_line(r.ahead(step)))
        copy.start()
        stage_copies.append(copy)

    at.d_outer[...] = scatter_two.total(1)
    at.give_1[...] = scatter_two.total(0).reshape(2, 24, 1536)
    swap(17, at.give_1.at[other], at.d_inner.at[core])
    at.d_inner[core] = at.give_1[core]
    at.give_o[...] = scatter_a.total(0).reshape(2, 24, 384)

    def give_pair(index, total):
        for place in range(3):
            start = 384 * place + 128 * index
            at.give_p[:, :, start : start + 128] = total[:, 128 * place : 128 * place + 128].reshape(
                2, 24, 128
            )

    give_pair(0, scatter_a.total(1))
    give_pair(1, scatter_b.total(0))
    give_pair(2, scatter_b.total(1))
    for part in range(2):
        at.give_t[:, :, 128 * part : 128 * part + 128] = scatter_c.total(part).reshape(2, 24, 128)
    for copy in stage_copies[3:]:
        copy.wait_recv()
    at.vector_grads[...] = (
        at.sums_step[2] + at.sums_come[3] + at.sums_come[4] + at.sums_come[5]
    )
    outs = (
        (at.give_p, 0, 384, at.d_key),
        (at.give_p, 384, 384, at.d_value),
        (at.give_p, 768, 384, at.d_query),
        (at.give_o, 0, 384, at.d_output),
        (at.give_t, 0, 256, at.d_table),
    )
    for slot, (give, start, width, out) in enumerate(outs):
        swap(18 + slot, give.at[other, :, pl.ds(start, width)], out.at[:, aligned(core, width)])
        out[:, aligned(core, width)] = give[core, :, start : start + width]
    for copy in waiting[17:]:
        copy.wait_recv()
    for copy in waiting:
        if copy is not come_outer:
            copy.wait_send()
    for copy in stage_copies:
        copy.wait_send()
    for index in range(3):
        remote(
            at.context.at[core, :, pl.ds(128 * index, 128)],
            at.context.at[core, :, pl.ds(128 * index, 128)],
            at.context_send.at[index],
            at.context_recv.at[index],
            r.partner,
        ).wait_send()
    for user in (gather_one, gather_two, scatter_two, scatter_a, scatter_b, scatter_c):
        user.sent()


def finish_kernel(names, *refs):
    at = type("Refs", (), dict(zip(names, refs)))
    chip, core = lax.axis_index("fsdp"), lax.axis_index("seq")
    at.result_out[...] = at.result[...]
    at.input_grad_out[...] = at.input_grad[...]
    at.query_w_out[...] = at.d_query[...]
    at.key_w_out[...] = at.d_key[...]
    at.value_w_out[...] = at.d_value[...]
    at.output_w_out[...] = at.d_output[...]
    at.table_out[...] = at.d_table[...]
    at.outer_w_out[...] = at.d_outer[...]
    for group in range(4 * LINE):
        for which in range(2):
            device = 2 * group + which
            at.inner_w_out[:, 96 * device : 96 * device + 96] = at.d_inner[
                which, :, 96 * group : 96 * group + 96
            ]
    sums = at.vector_grads[...]
    own = pltpu.roll(sums, (768 - 24 * (2 * chip + core)) % 768, 1)
    small_outs = (
        at.query_b_out, at.value_b_out, at.output_b_out, at.gain_1_out, at.shift_1_out,
        at.outer_b_out, at.gain_2_out, at.shift_2_out,
    )
    for index, out in enumerate(small_outs):
        out[...] = own[index : index + 1, 0:24]
    units = jnp.where(chip < 2 * LINE, sums[8:9], sums[9:10])
    units = jnp.broadcast_to(units, (8, 768))
    at.inner_b_out[...] = pltpu.roll(units, (768 - 96 * (chip % (2 * LINE))) % 768, 1)[0:1, 0:96]
    at.count_out[...] = sums[10:11, 0:1].astype(jnp.int32)


OUTPUTS = dict(
    result=((256, 768), BF16),
    input_grad=((256, 768), BF16),
    d_query=((24, 768), F32),
    d_key=((24, 768), F32),
    d_value=((24, 768), F32),
    d_output=((24, 768), F32),
    d_table=((24, 512), F32),
    d_inner=((2, 24, 1536), F32),
    d_outer=((96, 768), F32),
    vector_grads=((16, 768), F32),
)
FINALS = dict(
    result_out=((256, 768), BF16),
    input_grad_out=((256, 768), BF16),
    query_w_out=((24, 768), F32),
    key_w_out=((24, 768), F32),
    value_w_out=((24, 768), F32),
    output_w_out=((24, 768), F32),
    table_out=((24, 512), F32),
    inner_w_out=((24, 3072), F32),
    outer_w_out=((96, 768), F32),
    query_b_out=((1, 24), F32),
    value_b_out=((1, 24), F32),
    output_b_out=((1, 24), F32),
    gain_1_out=((1, 24), F32),
    shift_1_out=((1, 24), F32),
    outer_b_out=((1, 24), F32),
    gain_2_out=((1, 24), F32),
    shift_2_out=((1, 24), F32),
    inner_b_out=((1, 96), F32),
    count_out=((1, 1), jnp.int32),
)
LINE = 4
BLOCKS = (LINE, 4, 48)
SCRATCH = dict(
    small_wide=((16, 128), F32),
    small=((16, 128), BF16),
    inner_pair=((2, 24, 1536), BF16),
    segment_row=((8, 512), F32),
    segment_col=((512, 128), F32),
    come_a=((24, 768), BF16),
    come_b=((24, 1024), BF16),
    come_s=((16, 128), BF16),
    come_1=((24, 1536), BF16),
    gat_a=(BLOCKS + (768,), BF16),
    gat_b=(BLOCKS + (1024,), BF16),
    gat_s=((LINE, 4, 2, 16, 128), BF16),
    gat_1=(BLOCKS + (1536,), BF16),
    gat_2=((LINE, 4, 96, 768), BF16),
    x_all=((512, 768), BF16),
    x_turned=((768, 512), BF16),
    one_hot=((512, 512), BF16),
    flip=((128, 128), BF16),
    near_rows=((1024, 384), BF16),
    far_rows=((1024, 384), BF16),
    near_grad=((1024, 384), F32),
    far_grad=((1024, 384), F32),
    key_rel=((512, 384), BF16),
    query_rel=((512, 384), BF16),
    table_all=((2,) + BLOCKS + (256,), BF16),
    out_all=((2,) + BLOCKS + (384,), BF16),
    vectors=((8, 768), F32),
    inner_bias=((8, 1536), F32),
    bias_inner=((8, 1536), F32),
    kvq=((512, 1152), BF16),
    grad_kvq=((512, 1152), BF16),
    far_scores=((512, 512), F32),
    grad_low=((512, 512), BF16),
    soft=((6, 512, 512), F32),
    context=((2, 512, 384), BF16),
    grad_context=((512, 384), BF16),
    wide=((256, 768), F32),
    first_out=((256, 768), F32),
    first_normed=((256, 768), F32),
    first_inverse=((256, 128), F32),
    first_low=((512, 768), BF16),
    first_turned=((768, 512), BF16),
    active=((512, 1536), BF16),
    slope=((512, 1536), F32),
    grad_pre=((512, 1536), BF16),
    part_send=((256, 768), F32),
    part_recv=((256, 768), F32),
    part_send2=((256, 768), F32),
    part_recv2=((256, 768), F32),
    grad_sum=((256, 768), F32),
    grad_outer=((512, 768), BF16),
    grad_att=((512, 768), BF16),
    table_send=(BLOCKS + (256,), BF16),
    table_recv=(BLOCKS + (256,), BF16),
    sums=((16, 768), F32),
    sums_step=((3, 16, 768), F32),
    sums_come=((6, 16, 768), F32),
    grad_1=(BLOCKS + (1536,), BF16),
    grad_2=((LINE, 4, 96, 768), BF16),
    grad_o=(BLOCKS + (384,), BF16),
    grad_p=((3,) + BLOCKS + (384,), BF16),
    grad_t=((2,) + BLOCKS + (128,), BF16),
    give_1=((2, 24, 1536), F32),
    give_o=((2, 24, 384), F32),
    give_p=((2, 24, 1152), F32),
    give_t=((2, 24, 256), F32),
)
ROOMS = dict(pair_=2, first_=LINE, corner_=2, second_=LINE, line_=LINE)
BLOCK = {
    "1": (48, 1536), "2": (96, 768), "o": (48, 384), "p0": (48, 384), "p1": (48, 384),
    "p2": (48, 384), "t0": (48, 128), "t1": (48, 128),
}
for tag, block in BLOCK.items():
    for kind, count in ROOMS.items():
        SCRATCH[kind + tag] = ((count,) + block, BF16)
SEMAPHORES = dict(
    swap_send=(23,),
    swap_recv=(23,),
    here=(2,),
    context_send=(3,),
    context_recv=(3,),
    ga_send=(3, 6, LINE),
    ga_recv=(3, 6, LINE),
    gf_send=(2, 6, LINE),
    gf_recv=(2, 6, LINE),
    sf_send=(2, 5, LINE),
    sf_recv=(2, 5, LINE),
    sa_send=(2, 5, LINE),
    sa_recv=(2, 5, LINE),
    sb_send=(2, 5, LINE),
    sb_recv=(2, 5, LINE),
    sc_send=(2, 5, LINE),
    sc_recv=(2, 5, LINE),
    sums_send=(6,),
    sums_recv=(6,),
)


def block_shards(
    hidden_in,
    query_weight,
    query_bias,
    key_weight,
    value_weight,
    value_bias,
    output_weight,
    output_bias,
    first_gain,
    first_shift,
    inner_weight,
    inner_bias,
    outer_weight,
    outer_bias,
    second_gain,
    second_shift,
    relative_table,
    segments,
    buckets,
    predicted,
    labels,
    cotangent,
):
    inputs = dict(
        hidden=hidden_in[0],
        query_w=query_weight,
        key_w=key_weight,
        value_w=value_weight,
        output_w=output_weight,
        table_t=relative_table.T,
        inner_w=inner_weight,
        outer_w=outer_weight,
        query_b=query_bias[None],
        value_b=value_bias[None],
        output_b=output_bias[None],
        gain_1=first_gain[None],
        shift_1=first_shift[None],
        outer_b=outer_bias[None],
        gain_2=second_gain[None],
        shift_2=second_shift[None],
        inner_b=inner_bias[None],
        segments=segments,
        buckets=buckets[None],
        predicted=predicted,
        labels=labels,
        cotangent=cotangent[0],
    )
    names = tuple(inputs) + tuple(OUTPUTS) + tuple(SCRATCH) + tuple(SEMAPHORES)
    vmem = pl.BlockSpec(memory_space=pltpu.VMEM)
    outs = pl.pallas_call(
        partial(layer_kernel, names),
        name="layer",
        out_shape=tuple(jax.ShapeDtypeStruct(*out) for out in OUTPUTS.values()),
        in_specs=[vmem] * len(inputs),
        out_specs=(vmem,) * len(OUTPUTS),
        scratch_shapes=[pltpu.VMEM(*spec) for spec in SCRATCH.values()]
        + [pltpu.SemaphoreType.DMA(shape) for shape in SEMAPHORES.values()],
        compiler_params=pltpu.CompilerParams(
            collective_id=0, has_side_effects=True, vmem_limit_bytes=67043328
        ),
    )(*inputs.values())
    finals = pl.pallas_call(
        partial(finish_kernel, tuple(OUTPUTS) + tuple(FINALS)),
        name="finish",
        out_shape=tuple(jax.ShapeDtypeStruct(*out) for out in FINALS.values()),
        in_specs=[vmem] * len(OUTPUTS),
        out_specs=(vmem,) * len(FINALS),
    )(*outs)
    got = type("Outs", (), dict(zip(FINALS, finals)))
    return (
        got.result_out[None],
        got.input_grad_out[None],
        got.query_w_out,
        got.query_b_out[0],
        got.key_w_out,
        got.value_w_out,
        got.value_b_out[0],
        got.output_w_out,
        got.output_b_out[0],
        got.gain_1_out[0],
        got.shift_1_out[0],
        got.inner_w_out,
        got.inner_b_out[0],
        got.outer_w_out,
        got.outer_b_out[0],
        got.gain_2_out[0],
        got.shift_2_out[0],
        got.table_out.T,
        got.count_out[0, 0],
    )


def fits(mesh):
    return mesh.shape["fsdp"] == 4 * LINE and mesh.shape["seq"] == 2


def solution(mesh):
    return jax.shard_map(
        block_shards if fits(mesh) else shards,
        mesh=mesh,
        in_specs=(
            P("fsdp", "seq", None),
            P(("fsdp", "seq"), None),
            P(("fsdp", "seq")),
            P(("fsdp", "seq"), None),
            P(("fsdp", "seq"), None),
            P(("fsdp", "seq")),
            P(("fsdp", "seq"), None),
            P(("fsdp", "seq")),
            P(("fsdp", "seq")),
            P(("fsdp", "seq")),
            P(("fsdp", "seq"), None),
            P(("fsdp", "seq")),
            P(("fsdp", "seq"), None),
            P(("fsdp", "seq")),
            P(("fsdp", "seq")),
            P(("fsdp", "seq")),
            P(None, ("fsdp", "seq")),
            P("fsdp", None),
            P(),
            P("fsdp", "seq"),
            P("fsdp", "seq"),
            P("fsdp", "seq", None),
        ),
        out_specs=(
            P("fsdp", "seq", None),
            P("fsdp", "seq", None),
            P(("fsdp", "seq"), None),
            P(("fsdp", "seq")),
            P(("fsdp", "seq"), None),
            P(("fsdp", "seq"), None),
            P(("fsdp", "seq")),
            P(("fsdp", "seq"), None),
            P(("fsdp", "seq")),
            P(("fsdp", "seq")),
            P(("fsdp", "seq")),
            P(("fsdp", "seq"), None),
            P(("fsdp", "seq")),
            P(("fsdp", "seq"), None),
            P(("fsdp", "seq")),
            P(("fsdp", "seq")),
            P(("fsdp", "seq")),
            P(None, ("fsdp", "seq")),
            P(),
        ),
        check_vma=False,
    )
```

```python
from functools import partial

import jax
import jax.numpy as jnp
import numpy as np
from jax import lax
from jax.experimental import pallas as pl
from jax.experimental.pallas import tpu as pltpu
from jax.sharding import PartitionSpec as P

HEAD = 64


EPSILON = 1e-07
NEGATIVE = -1e30


def matmul(spec, left, right):
    return jnp.einsum(spec, left, right, preferred_element_type=jnp.float32)


def precise(spec, left, right):
    return jnp.einsum(spec, left, right, precision=lax.Precision.HIGHEST)


def skew_rows(scores_in, offset, columns):
    leading = scores_in.shape[:-2]
    row_count = scores_in.shape[-2]
    breadth = scores_in.shape[-1]
    flattened = scores_in.reshape(leading + (row_count * breadth,))
    flattened = jnp.concatenate(
        [flattened, jnp.zeros(leading + (2 * breadth,), scores_in.dtype)], axis=-1
    )
    selected = lax.dynamic_slice_in_dim(flattened, offset, row_count * (breadth - 1), len(leading))
    return selected.reshape(leading + (row_count, breadth - 1))[..., :columns]


def unskew_rows(values, offset, breadth):
    leading = values.shape[:-2]
    row_count = values.shape[-2]
    columns = values.shape[-1]
    padded = jnp.concatenate(
        [values, jnp.zeros(leading + (row_count, breadth - 1 - columns), values.dtype)], axis=-1
    )
    flattened = padded.reshape(leading + (row_count * (breadth - 1),))
    zero_room = jnp.zeros(leading + (row_count * breadth + 2 * breadth,), values.dtype)
    placed = lax.dynamic_update_slice_in_dim(zero_room, flattened, offset, len(leading))
    return placed[..., : row_count * breadth].reshape(leading + (row_count, breadth))


def layer_norm(values, gain, shift):
    average = jnp.mean(values, axis=-1, keepdims=True)
    centred = values - average
    variance = jnp.mean(centred * centred, axis=-1, keepdims=True)
    inverse = lax.rsqrt(variance + EPSILON)
    normed = centred * inverse
    return (normed * gain + shift, normed, inverse)


def norm_backward(upstream, normed, inverse, gain):
    scaled_up = upstream * gain
    first_mean = jnp.mean(scaled_up, axis=-1, keepdims=True)
    second_mean = jnp.mean(scaled_up * normed, axis=-1, keepdims=True)
    grad_in = inverse * (scaled_up - first_mean - normed * second_mean)
    return (grad_in, jnp.sum(upstream * normed, axis=0), jnp.sum(upstream, axis=0))


def shards(
    hidden_in,
    query_weight,
    query_bias,
    key_weight,
    value_weight,
    value_bias,
    output_weight,
    output_bias,
    first_gain,
    first_shift,
    inner_weight,
    inner_bias,
    outer_weight,
    outer_bias,
    second_gain,
    second_shift,
    relative_table,
    segments,
    buckets,
    predicted,
    labels,
    cotangent,
):
    row_count, window, model_width = hidden_in.shape
    length = segments.shape[1]
    distances = 2 * length - 1
    span = window + length - 1
    pair_width = 2 * HEAD
    pair_count = model_width // pair_width
    score_scale = (3.0 * HEAD) ** (-0.5)
    window_start = lax.axis_index("seq") * window
    near_start = length - window - window_start
    token_count = row_count * window
    attention_set = (
        lax.all_gather(query_weight, ("fsdp", "seq"), axis=0, tiled=True),
        lax.all_gather(query_bias, ("fsdp", "seq"), axis=0, tiled=True),
        lax.all_gather(key_weight, ("fsdp", "seq"), axis=0, tiled=True),
        lax.all_gather(value_weight, ("fsdp", "seq"), axis=0, tiled=True),
        lax.all_gather(value_bias, ("fsdp", "seq"), axis=0, tiled=True),
        lax.all_gather(output_weight, ("fsdp", "seq"), axis=0, tiled=True),
        lax.all_gather(output_bias, ("fsdp", "seq"), axis=0, tiled=True),
        lax.all_gather(first_gain, ("fsdp", "seq"), axis=0, tiled=True),
        lax.all_gather(first_shift, ("fsdp", "seq"), axis=0, tiled=True),
        lax.all_gather(relative_table, ("fsdp", "seq"), axis=1, tiled=True),
    )
    feed_set = (
        lax.all_gather(inner_weight, ("fsdp", "seq"), axis=0, tiled=True),
        lax.all_gather(inner_bias, ("fsdp", "seq"), axis=0, tiled=True),
        lax.all_gather(outer_weight, ("fsdp", "seq"), axis=0, tiled=True),
        lax.all_gather(outer_bias, ("fsdp", "seq"), axis=0, tiled=True),
        lax.all_gather(second_gain, ("fsdp", "seq"), axis=0, tiled=True),
        lax.all_gather(second_shift, ("fsdp", "seq"), axis=0, tiled=True),
    )
    (
        query_matrix,
        query_offset,
        key_matrix,
        value_matrix,
        value_offset,
        output_matrix,
        output_offset,
        gain_first,
        shift_first,
        table_full,
    ) = attention_set
    inner_matrix, inner_offset, outer_matrix, outer_offset, gain_second, shift_second = feed_set
    tokens = hidden_in.reshape(token_count, model_width)
    queries = (
        (matmul("td,de->te", tokens, query_matrix) + query_offset.astype(jnp.float32))
        .astype(jnp.bfloat16)
        .reshape(row_count, window, model_width)
    )
    keys_own = (
        matmul("td,de->te", tokens, key_matrix)
        .astype(jnp.bfloat16)
        .reshape(row_count, window, model_width)
    )
    values_own = (
        (matmul("td,de->te", tokens, value_matrix) + value_offset.astype(jnp.float32))
        .astype(jnp.bfloat16)
        .reshape(row_count, window, model_width)
    )
    keys_all, values_all = (
        lax.all_gather(keys_own, "seq", axis=1, tiled=True),
        lax.all_gather(values_own, "seq", axis=1, tiled=True),
    )
    key_rel = matmul("pd,de->pe", table_full, key_matrix).astype(jnp.bfloat16)
    query_rel = (
        matmul("pd,de->pe", table_full, query_matrix) + query_offset.astype(jnp.float32)
    ).astype(jnp.bfloat16)
    reversed_buckets = buckets[::-1]
    table_rows = table_full.shape[0]
    one_hot = (
        reversed_buckets[:, None] == jnp.arange(table_rows, dtype=jnp.int32)[None, :]
    ).astype(jnp.bfloat16)
    bucket_keys = matmul("dp,pe->de", one_hot, key_rel).astype(jnp.bfloat16)
    bucket_queries = matmul("dp,pe->de", one_hot, query_rel).astype(jnp.bfloat16)
    near_keys = lax.dynamic_slice_in_dim(bucket_keys, near_start, span, 0)
    far_queries = lax.dynamic_slice_in_dim(bucket_queries, window_start, span, 0)
    segment_own = lax.dynamic_slice_in_dim(segments, window_start, window, 1)
    same_doc = (segment_own[:, :, None] == segments[:, None, :])[:, None]

    def pair_scores(pair_index):
        column = pair_index * pair_width
        query_pair = lax.dynamic_slice_in_dim(queries, column, pair_width, 2).reshape(
            row_count, window, 2, HEAD
        )
        key_pair = lax.dynamic_slice_in_dim(keys_all, column, pair_width, 2).reshape(
            row_count, length, 2, HEAD
        )
        value_pair = lax.dynamic_slice_in_dim(values_all, column, pair_width, 2).reshape(
            row_count, length, 2, HEAD
        )
        bucketkeys = lax.dynamic_slice_in_dim(near_keys, column, pair_width, 1).reshape(
            span, 2, HEAD
        )
        bucketqueries = lax.dynamic_slice_in_dim(far_queries, column, pair_width, 1).reshape(
            span, 2, HEAD
        )
        content = matmul("rihe,rjhe->rhij", query_pair, key_pair)
        near_scores = matmul("rihe,dhe->rhid", query_pair, bucketkeys)
        far_scores = matmul("rjhe,dhe->rhjd", key_pair, bucketqueries)
        to_position = skew_rows(near_scores, window - 1, length)
        from_position = jnp.swapaxes(skew_rows(far_scores, length - 1, window), 2, 3)
        summed = content + to_position + from_position
        masked = jnp.where(same_doc, summed * score_scale, NEGATIVE)
        return (masked, query_pair, key_pair, value_pair, bucketkeys, bucketqueries)

    def attend_pair(pair_index):
        masked, query_pair, key_pair, value_pair, bucketkeys, bucketqueries = pair_scores(
            pair_index
        )
        highest = jnp.max(masked, axis=-1, keepdims=True)
        expsum = jnp.exp(masked - highest)
        totals = jnp.sum(expsum, axis=-1, keepdims=True)
        weights_soft = (expsum / totals).astype(jnp.bfloat16)
        context_pair = matmul("rhij,rjhe->rihe", weights_soft, value_pair).astype(jnp.bfloat16)
        return (
            context_pair.reshape(row_count, window, pair_width),
            (highest + jnp.log(totals))[..., 0],
        )

    context_parts, log_totals = lax.map(attend_pair, jnp.arange(pair_count, dtype=jnp.int32))
    context = jnp.moveaxis(context_parts, 0, 2).reshape(token_count, model_width)
    attention_out = matmul("te,ed->td", context, output_matrix) + output_offset.astype(jnp.float32)
    residual_one = tokens.astype(jnp.float32) + attention_out
    first_out, first_normed, first_inverse = layer_norm(
        residual_one, gain_first.astype(jnp.float32), shift_first.astype(jnp.float32)
    )
    first_low = first_out.astype(jnp.bfloat16)
    inner_pre = matmul("td,df->tf", first_low, inner_matrix) + inner_offset.astype(jnp.float32)
    activated = jax.nn.gelu(inner_pre, approximate=False).astype(jnp.bfloat16)
    outer_out = matmul("tf,fd->td", activated, outer_matrix) + outer_offset.astype(jnp.float32)
    final_out, final_normed, final_inverse = layer_norm(
        first_out + outer_out, gain_second.astype(jnp.float32), shift_second.astype(jnp.float32)
    )
    result = final_out.astype(jnp.bfloat16).reshape(row_count, window, model_width)
    correct_count = lax.psum(jnp.sum((predicted == labels).astype(jnp.int32)), ("fsdp", "seq"))
    regathered = attention_set + feed_set
    (
        query_back,
        query_offset_back,
        key_back,
        value_back,
        value_offset_back,
        output_back,
        output_offset_back,
        gain_first_back,
        shift_first_back,
        table_back,
        inner_back,
        inner_offset_back,
        outer_back,
        outer_offset_back,
        gain_second_back,
        shift_second_back,
    ) = regathered
    upstream = cotangent.reshape(token_count, model_width).astype(jnp.float32)
    grad_sum2, grad_gain2, grad_shift2 = norm_backward(
        upstream, final_normed, final_inverse, gain_second_back.astype(jnp.float32)
    )
    grad_outer = grad_sum2.astype(jnp.bfloat16)
    outer_bias_part = jnp.sum(grad_outer.astype(jnp.float32), axis=0)
    outer_weight_part = matmul("tf,td->fd", activated, grad_outer)
    grad_act = matmul("td,fd->tf", grad_outer, outer_back).astype(jnp.bfloat16)
    _, gelu_back = jax.vjp(partial(jax.nn.gelu, approximate=False), inner_pre)
    grad_inner = gelu_back(grad_act.astype(jnp.float32))[0].astype(jnp.bfloat16)
    inner_bias_part = jnp.sum(grad_inner.astype(jnp.float32), axis=0)
    inner_weight_part = matmul("td,tf->df", first_low, grad_inner)
    grad_first = matmul("tf,df->td", grad_inner, inner_back) + grad_sum2
    feed_grads = (
        lax.psum_scatter(inner_weight_part, ("fsdp", "seq"), scatter_dimension=0, tiled=True),
        lax.psum_scatter(inner_bias_part, ("fsdp", "seq"), scatter_dimension=0, tiled=True),
        lax.psum_scatter(outer_weight_part, ("fsdp", "seq"), scatter_dimension=0, tiled=True),
        lax.psum_scatter(outer_bias_part, ("fsdp", "seq"), scatter_dimension=0, tiled=True),
        lax.psum_scatter(grad_gain2, ("fsdp", "seq"), scatter_dimension=0, tiled=True),
        lax.psum_scatter(grad_shift2, ("fsdp", "seq"), scatter_dimension=0, tiled=True),
    )
    grad_sum1, grad_gain1, grad_shift1 = norm_backward(
        grad_first, first_normed, first_inverse, gain_first_back.astype(jnp.float32)
    )
    grad_attention = grad_sum1.astype(jnp.bfloat16)
    output_bias_part = jnp.sum(grad_attention.astype(jnp.float32), axis=0)
    output_weight_part = matmul("te,td->ed", context, grad_attention)
    grad_context = (
        matmul("td,ed->te", grad_attention, output_back)
        .astype(jnp.bfloat16)
        .reshape(row_count, window, model_width)
    )

    def attend_back(pieces):
        pair_index, log_total = pieces
        masked, query_pair, key_pair, value_pair, bucketkeys, bucketqueries = pair_scores(
            pair_index
        )
        probability = jnp.exp(masked - log_total[..., None])
        grad_context_pair = lax.dynamic_slice_in_dim(
            grad_context, pair_index * pair_width, pair_width, 2
        ).reshape(row_count, window, 2, HEAD)
        grad_soft = matmul("rihe,rjhe->rhij", grad_context_pair, value_pair)
        grad_scores = probability * (
            grad_soft - jnp.sum(probability * grad_soft, axis=-1, keepdims=True)
        )
        grad_low = (grad_scores * score_scale).astype(jnp.bfloat16)
        grad_value = matmul("rhij,rihe->rjhe", probability.astype(jnp.bfloat16), grad_context_pair)
        grad_near = unskew_rows(grad_low, window - 1, span)
        grad_far = unskew_rows(jnp.swapaxes(grad_low, 2, 3), length - 1, span)
        grad_query = matmul("rhij,rjhe->rihe", grad_low, key_pair) + matmul(
            "rhid,dhe->rihe", grad_near, bucketkeys
        )
        grad_key = matmul("rhij,rihe->rjhe", grad_low, query_pair) + matmul(
            "rhjd,dhe->rjhe", grad_far, bucketqueries
        )
        grad_bkeys = matmul("rhid,rihe->dhe", grad_near, query_pair)
        grad_bqueries = matmul("rhjd,rjhe->dhe", grad_far, key_pair)
        return (
            grad_query.reshape(row_count, window, pair_width),
            grad_key.reshape(row_count, length, pair_width),
            grad_value.reshape(row_count, length, pair_width),
            grad_bkeys.reshape(span, pair_width),
            grad_bqueries.reshape(span, pair_width),
        )

    query_parts, key_parts, value_parts, bkey_parts, bquery_parts = lax.map(
        attend_back, (jnp.arange(pair_count, dtype=jnp.int32), log_totals)
    )
    grad_query_all = jnp.moveaxis(query_parts, 0, 2).reshape(token_count, model_width)
    grad_key_all = jnp.moveaxis(key_parts, 0, 2).reshape(row_count, length, model_width)
    grad_value_all = jnp.moveaxis(value_parts, 0, 2).reshape(row_count, length, model_width)
    near_grads = jnp.moveaxis(bkey_parts, 0, 1).reshape(span, model_width)
    far_grads = jnp.moveaxis(bquery_parts, 0, 1).reshape(span, model_width)
    grad_bucket_keys = lax.dynamic_update_slice_in_dim(
        jnp.zeros((distances, model_width), jnp.float32), near_grads, near_start, 0
    )
    grad_bucket_queries = lax.dynamic_update_slice_in_dim(
        jnp.zeros((distances, model_width), jnp.float32), far_grads, window_start, 0
    )
    key_grads, value_grads = (
        lax.psum_scatter(
            grad_key_all.astype(jnp.bfloat16), "seq", scatter_dimension=1, tiled=True
        ).astype(jnp.float32),
        lax.psum_scatter(
            grad_value_all.astype(jnp.bfloat16), "seq", scatter_dimension=1, tiled=True
        ).astype(jnp.float32),
    )
    query_low = grad_query_all.astype(jnp.bfloat16)
    key_low = key_grads.reshape(token_count, model_width).astype(jnp.bfloat16)
    value_low = value_grads.reshape(token_count, model_width).astype(jnp.bfloat16)
    grad_key_rel = jax.ops.segment_sum(grad_bucket_keys, reversed_buckets, num_segments=table_rows)
    grad_query_rel = jax.ops.segment_sum(
        grad_bucket_queries, reversed_buckets, num_segments=table_rows
    )
    query_token_part = matmul("td,te->de", tokens, query_low)
    query_bias_token = jnp.sum(query_low.astype(jnp.float32), axis=0)
    key_token_part = matmul("td,te->de", tokens, key_low)
    value_weight_part = matmul("td,te->de", tokens, value_low)
    value_bias_part = jnp.sum(value_low.astype(jnp.float32), axis=0)
    grad_input = (
        grad_sum1
        + matmul("te,de->td", query_low, query_back)
        + matmul("te,de->td", key_low, key_back)
        + matmul("te,de->td", value_low, value_back)
    )
    input_grad = grad_input.astype(jnp.bfloat16).reshape(row_count, window, model_width)
    key_rel_total, query_rel_total = lax.psum((grad_key_rel, grad_query_rel), ("fsdp", "seq"))
    attention_grads = (
        lax.psum_scatter(query_token_part, ("fsdp", "seq"), scatter_dimension=0, tiled=True),
        lax.psum_scatter(query_bias_token, ("fsdp", "seq"), scatter_dimension=0, tiled=True),
        lax.psum_scatter(key_token_part, ("fsdp", "seq"), scatter_dimension=0, tiled=True),
        lax.psum_scatter(value_weight_part, ("fsdp", "seq"), scatter_dimension=0, tiled=True),
        lax.psum_scatter(value_bias_part, ("fsdp", "seq"), scatter_dimension=0, tiled=True),
        lax.psum_scatter(output_weight_part, ("fsdp", "seq"), scatter_dimension=0, tiled=True),
        lax.psum_scatter(output_bias_part, ("fsdp", "seq"), scatter_dimension=0, tiled=True),
        lax.psum_scatter(grad_gain1, ("fsdp", "seq"), scatter_dimension=0, tiled=True),
        lax.psum_scatter(grad_shift1, ("fsdp", "seq"), scatter_dimension=0, tiled=True),
    )
    shard_rows = query_weight.shape[0]
    shard_start = lax.axis_index(("fsdp", "seq")) * shard_rows
    table_shard = relative_table.astype(jnp.float32)
    query_weight_grad = attention_grads[0] + precise("pd,pe->de", table_shard, query_rel_total)
    key_weight_grad = attention_grads[2] + precise("pd,pe->de", table_shard, key_rel_total)
    query_bias_grad = attention_grads[1] + jnp.sum(
        lax.dynamic_slice_in_dim(query_rel_total, shard_start, shard_rows, 1), axis=0
    )
    relative_table_grad = precise(
        "pe,de->pd", query_rel_total, query_weight.astype(jnp.float32)
    ) + precise("pe,de->pd", key_rel_total, key_weight.astype(jnp.float32))
    return (
        result,
        input_grad,
        query_weight_grad,
        query_bias_grad,
        key_weight_grad,
        attention_grads[3],
        attention_grads[4],
        attention_grads[5],
        attention_grads[6],
        attention_grads[7],
        attention_grads[8],
        feed_grads[0],
        feed_grads[1],
        feed_grads[2],
        feed_grads[3],
        feed_grads[4],
        feed_grads[5],
        relative_table_grad,
        correct_count,
    )


MESH = pl.DeviceIdType.MESH
F32 = jnp.float32
BF16 = jnp.bfloat16


def dot(left, right, left_dim=1, right_dim=0):
    return lax.dot_general(
        left, right, (((left_dim,), (right_dim,)), ((), ())), preferred_element_type=F32
    )


def low(value):
    return value.astype(BF16)


class Route:
    def __init__(self):
        chip = lax.axis_index("fsdp")
        self.core = lax.axis_index("seq")
        self.other = 1 - self.core
        self.chip = chip
        self.x = chip % 2
        self.y = (chip // 2) % 2
        self.z = chip // 4
        self.plane = chip % 4
        self.plane_x = self.plane + 1 - 2 * self.x
        self.plane_y = self.plane + 2 - 4 * self.y
        self.pair = self.z + 1 - 2 * (self.z % 2)
        self.near = (self.z, (self.z + 2) % LINE)
        self.far = (self.pair, (self.pair + 2) % LINE)
        self.soon = 1 + self.z % 2
        self.late = 3 - 3 * (self.z % 2)
        self.partner = (chip, self.other)
        self.at_x = (self.z * 4 + self.plane_x, self.core)
        self.at_y = (self.z * 4 + self.plane_y, self.core)

    def at_line(self, line):
        return (line * 4 + self.plane, self.core)

    def ahead(self, step):
        return (self.z + step) % LINE

    def behind(self, step):
        return (self.z + LINE - step) % LINE


def remote(source, target, send_sem, recv_sem, device):
    return pltpu.make_async_remote_copy(
        source, target, send_sem, recv_sem, device_id=device, device_id_type=MESH
    )


class Gather:
    def __init__(self, route, arrays, send, recv):
        self.r, self.arrays, self.send, self.recv = route, arrays, send, recv

    def copies(self, kind, line):
        r = self.r
        for i, array in enumerate(self.arrays):
            by_x = i == 1
            plane, device = (
                (r.plane, r.at_line((r.z + 1) % LINE)),
                (r.plane, r.at_line((r.z + LINE - 1) % LINE)),
                (r.plane, r.at_x),
                (r.plane, r.at_y),
                (r.plane_y, r.at_x) if by_x else (r.plane_x, r.at_y),
                (3 - r.plane, r.at_line(r.pair)),
            )[kind]
            block = array.at[line, plane]
            yield remote(
                block, block, self.send.at[i, kind, line], self.recv.at[i, kind, line], device
            )

    def begin(self, kind, line):
        for copy in self.copies(kind, line):
            copy.start()

    def got(self, kind, line):
        for copy in self.copies(kind, line):
            copy.wait_recv()

    def sides(self, line):
        self.begin(2, line)
        self.begin(3, line)

    def got_sides(self, line):
        self.got(2, line)
        self.got(3, line)

    def up(self, line):
        @pl.when(self.r.z < LINE - 1)
        def _():
            self.begin(0, line)

    def down(self, line):
        @pl.when(self.r.z > 0)
        def _():
            self.begin(1, line)

    def start_line(self):
        self.up(self.r.z)
        self.down(self.r.z)

    def start_sides(self):
        self.sides(self.r.z)

    def round(self, step):
        r = self.r

        @pl.when(r.z >= step)
        def _():
            self.got(0, r.z - step)
            self.up(r.z - step)

        @pl.when(r.z + step < LINE)
        def _():
            self.got(1, r.z + step)
            self.down(r.z + step)

    def first(self):
        self.corner(0)
        self.round(1)
        self.sides(self.r.soon)

    def second(self):
        self.round(2)
        self.sides(self.r.near[1])
        self.hand(0)

    def third(self):
        self.round(3)
        self.corner(1)
        self.sides(self.r.late)

    def corner(self, which):
        line = self.r.near[which]
        self.got_sides(line)
        self.begin(4, line)

    def hand(self, which):
        line = self.r.near[which]
        self.got(4, line)
        self.begin(5, line)

    def finish(self):
        for line in self.r.far:
            self.got_sides(line)
            self.got(5, line)

    def drained(self, kind, line):
        for copy in self.copies(kind, line):
            copy.wait_send()

    def sent(self):
        r = self.r
        for line in range(LINE):

            @pl.when((r.z < LINE - 1) & (r.z >= line))
            def _():
                self.drained(0, line)

            @pl.when((r.z > 0) & (r.z <= line))
            def _():
                self.drained(1, line)

            self.drained(2, line)
            self.drained(3, line)
        for line in r.near:
            self.drained(4, line)
            self.drained(5, line)


class Scatter:
    def __init__(self, route, arrays, rooms, send, recv):
        self.r, self.arrays, self.rooms = route, arrays, rooms
        self.send, self.recv = send, recv

    def across(self, i):
        return self.r.plane_y if i == 0 else self.r.plane_x

    def copy(self, i, kind, line):
        r = self.r
        near, across = (r.at_x, r.at_y) if i == 0 else (r.at_y, r.at_x)
        near_plane = r.plane_x if i == 0 else r.plane_y
        plane, room, device = (
            (3 - r.plane, line // 2, r.at_line(r.pair)),
            (near_plane, line, near),
            (3 - r.plane, line // 2, near),
            (self.across(i), line, across),
            (r.plane, r.z, r.at_line(line)),
        )[kind]
        return remote(
            self.arrays[i].at[line, plane],
            self.rooms[i][kind].at[room],
            self.send.at[i, kind, line],
            self.recv.at[i, kind, r.z if kind == 4 else line],
            device,
        )

    def got_along(self, i, line):
        r = self.r
        remote(
            self.arrays[i].at[line, r.plane],
            self.rooms[i][4].at[line],
            self.send.at[i, 4, line],
            self.recv.at[i, 4, line],
            r.at_line(line),
        ).wait_recv()

    def begin_far(self, i, line):
        for kind in (0, 1, 3):
            self.copy(i, kind, line).start()

    def begin_near(self, i, line):
        self.copy(i, 1, line).start()

    def begin(self, i):
        for line in self.r.far:
            self.begin_far(i, line)
        for line in self.r.near[::-1]:
            self.begin_near(i, line)

    def merge(self, i, line, plane, *came):
        at = self.arrays[i].at[line, plane]
        value = at[...].astype(F32)
        for kind, room in came:
            value = value + self.rooms[i][kind][room].astype(F32)
        at[...] = low(value)

    def corners(self, i):
        for line in self.r.near[::-1]:
            self.copy(i, 0, line).wait_recv()
            self.merge(i, line, 3 - self.r.plane, (0, line // 2))
            self.copy(i, 2, line).start()

    def turn(self, i):
        for line in self.r.near[::-1]:
            self.copy(i, 2, line).wait_recv()
            self.merge(i, line, self.across(i), (2, line // 2))
            self.copy(i, 3, line).start()

    def along(self, i, line):
        self.copy(i, 1, line).wait_recv()
        self.copy(i, 3, line).wait_recv()
        self.merge(i, line, self.r.plane, (1, line), (3, line))
        self.copy(i, 4, line).start()

    def along_far(self, i):
        for line in self.r.far:
            self.along(i, line)

    def along_near(self, i):
        self.along(i, self.r.near[1])

    def total(self, i):
        r = self.r
        self.copy(i, 1, r.z).wait_recv()
        self.copy(i, 3, r.z).wait_recv()
        rooms = self.rooms[i]
        value = self.arrays[i][r.z, r.plane].astype(F32)
        value = value + rooms[1][r.z].astype(F32) + rooms[3][r.z].astype(F32)
        for line in r.far + r.near[1:]:
            self.got_along(i, line)
            value = value + rooms[4][line].astype(F32)
        return value

    def sent(self):
        r = self.r
        for i in (0, 1):
            for line in range(LINE):
                self.copy(i, 1, line).wait_send()
                self.copy(i, 3, line).wait_send()
            for line in r.far:
                self.copy(i, 0, line).wait_send()
                self.copy(i, 4, line).wait_send()
            for line in r.near:
                self.copy(i, 2, line).wait_send()
            self.copy(i, 4, r.near[1]).wait_send()


def loop(count, body):
    def step(index, carry):
        body(index)
        return carry

    lax.fori_loop(0, count, step, 0)


def aligned(index, size):
    return pl.ds(pl.multiple_of(index * size, size), size)


def erf_parts(value):
    tail = lax.erf(value * np.float32(0.5**0.5))
    half = 0.5 * (1.0 + tail)
    density = jnp.exp(value * value * -0.5) * np.float32((2.0 * np.pi) ** -0.5)
    return value * half, half + value * density


def norm(values, gain, shift):
    average = jnp.mean(values, axis=-1, keepdims=True)
    centred = values - average
    variance = jnp.mean(centred * centred, axis=-1, keepdims=True)
    inverse = lax.rsqrt(variance + EPSILON)
    normed = centred * inverse
    return normed * gain + shift, normed, inverse


def norm_pull(upstream, normed, inverse, gain):
    scaled_up = upstream * gain
    first_mean = jnp.mean(scaled_up, axis=-1, keepdims=True)
    second_mean = jnp.mean(scaled_up * normed, axis=-1, keepdims=True)
    return inverse * (scaled_up - first_mean - normed * second_mean)


def layer_kernel(names, *refs):
    b = dict(zip(names, refs))
    at = type("Refs", (), b)
    r = Route()
    core, other = r.core, r.other
    own_rows = aligned(core, 256)
    other_rows = aligned(other, 256)
    score_scale = np.float32((3.0 * HEAD) ** (-0.5))

    barrier = pltpu.get_barrier_semaphore()
    friends = [r.partner, r.at_x, r.at_y] + [r.at_line(r.ahead(k)) for k in range(1, LINE)]
    for device in friends:
        pl.semaphore_signal(barrier, inc=1, device_id=device, device_id_type=MESH)

    def give_rows(kind, index, array):
        piece = pl.ds(pl.multiple_of(core * 256 + index * 64, 64), 64)
        return remote(
            array.at[piece],
            array.at[piece],
            at.row_send.at[kind, index],
            at.row_recv.at[kind, index],
            r.partner,
        )

    def got_rows(kind, array):
        for index in range(4):
            give_rows(kind, index, array).wait_recv()

    waiting = []

    def swap(slot, source, target):
        copy = remote(source, target, at.swap_send.at[slot], at.swap_recv.at[slot], r.partner)
        copy.start()
        waiting.append(copy)
        return copy

    gather_one = Gather(r, (at.gat_a, at.gat_b, at.gat_s), at.ga_send, at.ga_recv)
    gather_two = Gather(r, (at.gat_1, at.gat_2), at.gf_send, at.gf_recv)

    at.sums[...] = jnp.zeros_like(at.sums)
    at.small_wide[...] = jnp.zeros_like(at.small_wide)
    small_rows = (
        at.query_b, at.value_b, at.output_b, at.gain_1, at.shift_1, at.outer_b, at.gain_2, at.shift_2,
        at.inner_b,
    )
    for index, row in enumerate(small_rows):
        at.small_wide[index : index + 1, 0 : row.shape[1]] = row[...].astype(F32)
    at.small[...] = low(at.small_wide[...])
    right = (at.predicted[...] == at.labels[...]).astype(F32)
    at.sums[10:11, :] = jnp.broadcast_to(jnp.sum(right, axis=1, keepdims=True), (1, 768))
    pl.semaphore_wait(barrier, len(friends))

    half = aligned(other, 384)
    arrive = [
        swap(0, at.key_w.at[:, half], at.come_a.at[:, pl.ds(0, 384)]),
        swap(1, at.value_w.at[:, half], at.come_a.at[:, pl.ds(384, 384)]),
        swap(2, at.query_w.at[:, half], at.come_b.at[:, pl.ds(0, 384)]),
        swap(3, at.output_w.at[:, half], at.come_b.at[:, pl.ds(384, 384)]),
        swap(4, at.table_t.at[:, aligned(other, 256)], at.come_b.at[:, pl.ds(768, 256)]),
        swap(5, at.small, at.come_s),
    ]
    come_x = swap(7, at.hidden, at.x_all.at[own_rows])
    place_x = pltpu.make_async_copy(at.hidden, at.x_all.at[own_rows], at.here.at[0])
    place_x.start()
    place_2 = pltpu.make_async_copy(at.outer_w, at.gat_2.at[r.z, r.plane], at.here.at[1])
    place_2.start()
    for copy in arrive:
        copy.wait_recv()

    def stack(mine, came):
        mine, came = mine.astype(F32), came.astype(F32)
        upper = jnp.where(core == 0, mine, came)
        lower = jnp.where(core == 0, came, mine)
        return low(jnp.concatenate([upper, lower], axis=0))

    mine_half = aligned(core, 384)
    at.gat_a[r.z, r.plane, :, 0:384] = stack(at.key_w[:, mine_half], at.come_a[:, 0:384])
    at.gat_a[r.z, r.plane, :, 384:768] = stack(at.value_w[:, mine_half], at.come_a[:, 384:768])
    at.gat_b[r.z, r.plane, :, 0:384] = stack(at.query_w[:, mine_half], at.come_b[:, 0:384])
    at.gat_b[r.z, r.plane, :, 384:768] = stack(at.output_w[:, mine_half], at.come_b[:, 384:768])
    at.gat_b[r.z, r.plane, :, 768:1024] = stack(
        at.table_t[:, aligned(core, 256)], at.come_b[:, 768:1024]
    )
    at.gat_s[r.z, r.plane, core] = at.small[...]
    at.gat_s[r.z, r.plane, other] = at.come_s[...]
    gather_one.start_line()
    gather_one.start_sides()
    for chip in range(4 * LINE):
        for which in range(2):
            device = 2 * chip + which
            at.inner_pair[which, :, 96 * chip : 96 * chip + 96] = at.inner_w[
                :, 96 * device : 96 * device + 96
            ]
    come_inner = swap(6, at.inner_pair.at[other], at.come_1)
    come_inner.wait_recv()
    at.gat_1[r.z, r.plane] = stack(at.inner_pair[core], at.come_1[...])
    place_2.wait()
    place_x.wait()
    come_x.wait_recv()
    at.x_turned[...] = at.x_all[...].T
    wide_i = lax.broadcasted_iota(jnp.int32, (512, 512), 0)
    wide_j = lax.broadcasted_iota(jnp.int32, (512, 512), 1)
    at.one_natural[...] = low((at.buckets[0:1, 256:768] == wide_i).astype(F32))
    at.one_hot[...] = low(dot(at.one_natural[...], low((wide_i + wide_j == 511).astype(F32))))
    segment_wide = jnp.broadcast_to(at.segments[...].astype(F32), (128, 512))
    at.segment_row[...] = segment_wide[0:8]
    at.segment_col[...] = segment_wide.T
    flip_i = lax.broadcasted_iota(jnp.int32, (128, 128), 0)
    flip_j = lax.broadcasted_iota(jnp.int32, (128, 128), 1)
    at.flip[...] = low((flip_i + flip_j == 127).astype(F32))
    for table in (at.near_rows, at.far_rows, at.far_natural):
        table[0:256, :] = jnp.zeros((256, 384), BF16)
        table[768:1024, :] = jnp.zeros((256, 384), BF16)
    gather_one.first()
    gather_one.second()
    gather_one.third()
    gather_two.start_sides()
    gather_one.hand(1)
    gather_two.start_line()
    gather_one.finish()

    out_mine = at.gat_b.at[:, :, :, pl.ds(384, 384)]
    table_mine = at.gat_b.at[:, :, :, pl.ds(768, 256)]
    come_table = swap(8, table_mine, at.table_all.at[core])
    come_out = swap(9, out_mine, at.out_all.at[core])
    place_table = pltpu.make_async_copy(table_mine, at.table_all.at[core], at.here.at[0])
    place_table.start()
    place_out = pltpu.make_async_copy(out_mine, at.out_all.at[core], at.here.at[1])
    place_out.start()

    for line in range(LINE):
        for plane in range(4):
            chip = line * 4 + plane
            for which in range(2):
                device = 2 * chip + which
                tile = at.gat_s[line, plane, which].astype(F32)
                at.vectors[:, 24 * device : 24 * device + 24] = tile[0:8, 0:24]
            tile = at.gat_s[line, plane, core].astype(F32)
            at.inner_bias[0:1, 96 * chip : 96 * chip + 96] = tile[8:9, 0:96]

    def rows(value):
        return value.reshape(768, value.shape[-1])

    vector_half = aligned(core, 384)
    query_bias = at.vectors[0:1, vector_half]
    value_bias = at.vectors[1:2, vector_half]
    at.kvq[:, 0:384] = low(dot(at.x_all[...], rows(at.gat_a[:, :, :, 0:384])))
    at.kvq[:, 384:768] = low(dot(at.x_all[...], rows(at.gat_a[:, :, :, 384:768])) + value_bias)
    at.kvq[:, 768:1152] = low(dot(at.x_all[...], rows(at.gat_b[:, :, :, 0:384])) + query_bias)
    gather_two.first()
    place_table.wait()
    come_table.wait_recv()
    for part in range(2):
        piece = pl.ds(256 * part, 256)
        table = rows(at.table_all[part])
        at.key_rel[piece, :] = low(dot(table, rows(at.gat_a[:, :, :, 0:384]), 0, 0))
        at.query_rel[piece, :] = low(dot(table, rows(at.gat_b[:, :, :, 0:384]), 0, 0) + query_bias)
    at.near_rows[256:768, :] = low(dot(at.one_hot[...], at.key_rel[...], 0, 0))
    at.far_rows[256:768, :] = low(dot(at.one_hot[...], at.query_rel[...], 0, 0))
    at.far_natural[256:768, :] = low(dot(at.one_natural[...], at.query_rel[...], 0, 0))

    lanes = lax.broadcasted_iota(jnp.int32, (1, 128), 1) // HEAD
    no_score = np.float32(NEGATIVE)

    def forward_head(head):
        pair = aligned(head // 2, 128)
        key_lanes = pl.ds(pl.multiple_of((head // 2) * 128, 128), 128)
        value_lanes = pl.ds(pl.multiple_of(384 + (head // 2) * 128, 128), 128)
        query_lanes = pl.ds(pl.multiple_of(768 + (head // 2) * 128, 128), 128)
        mine = lanes == head % 2
        only = low(mine.astype(F32))
        keys = at.kvq[:, key_lanes]
        values = at.kvq[:, value_lanes]
        for block in range(4):
            piece = pl.ds(128 * block, 128)
            shifted = dot(
                at.kvq[piece, key_lanes] * only, at.far_rows[pl.ds(384 - 128 * block, 640), pair], 1, 1
            )
            at.far_scores[piece, :] = pltpu.roll(shifted, 0, 1, stride=1, stride_axis=0)[:, 128:640]
        for block in range(4):
            piece = pl.ds(128 * block, 128)
            queries = at.kvq[piece, query_lanes] * only
            shifted = dot(queries, at.near_rows[pl.ds(384 - 128 * block, 640), pair], 1, 1)
            summed = (
                dot(queries, keys, 1, 1)
                + pltpu.roll(shifted, 0, 1, stride=1, stride_axis=0)[:, 128:640]
                + at.far_scores[:, piece].T
            )
            masked = jnp.where(
                at.segment_col[piece, 0:1] == at.segment_row[0:1, :], summed * score_scale, no_score
            )
            highest = jnp.max(masked, axis=-1, keepdims=True)
            expsum = jnp.exp(masked - highest)
            soft = expsum / jnp.sum(expsum, axis=-1, keepdims=True)
            rounded = low(soft)
            at.soft[head, piece, :] = low(dot(at.flip[...], rounded))
            context = dot(rounded, values)
            here = at.context.at[core, piece, pair]
            here[...] = low(jnp.where(mine, context, here[...].astype(F32)))

    def forward_pair(index):
        def forward(which):
            head = 2 * index + which
            forward_head(head)
            pl.when(head == 1)(gather_two.second)
            pl.when(head == 5)(gather_two.third)

        loop(2, forward)
        remote(
            at.context.at[core, :, aligned(index, 128)],
            at.context.at[core, :, aligned(index, 128)],
            at.context_send.at[index],
            at.context_recv.at[index],
            r.partner,
        ).start()

    loop(3, forward_pair)
    place_out.wait()
    come_out.wait_recv()
    for index in range(3):
        remote(
            at.context.at[other, :, pl.ds(128 * index, 128)],
            at.context.at[other, :, pl.ds(128 * index, 128)],
            at.context_send.at[index],
            at.context_recv.at[index],
            r.partner,
        ).wait_recv()

    def vector(index):
        return at.vectors[index : index + 1, :]

    for part in range(2):
        piece = pl.ds(384 * part, 384)
        weight = rows(at.out_all[part])
        at.wide[:, piece] = dot(at.context[0, own_rows, :], weight[0:384]) + dot(
            at.context[1, own_rows, :], weight[384:768]
        )

    def first_norm(index):
        piece = aligned(index, 64)
        token_rows = pl.ds(pl.multiple_of(core * 256 + index * 64, 64), 64)
        residual = at.x_all[token_rows, :].astype(F32) + at.wide[piece, :] + vector(2)
        out, normed, inverse = norm(residual, vector(3), vector(4))
        at.first_out[piece, :] = out
        at.first_normed[piece, :] = normed
        at.first_inverse[piece, :] = jnp.broadcast_to(inverse, (64, 128))
        at.first_low[token_rows, :] = low(out)
        give_rows(0, index, at.first_low).start()

    loop(4, first_norm)
    got_rows(0, at.first_low)
    at.first_turned[...] = at.first_low[...].T
    gather_two.hand(1)
    gather_two.finish()

    def inner_units(index):
        piece = aligned(index, 256)
        pre = dot(at.first_low[...], rows(at.gat_1[:, :, :, piece])) + at.inner_bias[0:1, piece]
        value, slope = erf_parts(pre)
        at.active[:, piece] = low(value)
        at.slope[:, piece] = slope

    loop(6, inner_units)

    def outer_part(rows_at, part):
        return dot(
            at.active[rows_at, :], at.gat_2[:, :, :, 256 * part : 256 * part + 256].reshape(1536, 256)
        )

    come_outer = []
    for part in range(3):
        piece = pl.ds(256 * part, 256)
        at.part_send[:, piece] = low(outer_part(other_rows, part))
        come_outer.append(swap((11, 23, 24)[part], at.part_send.at[:, piece], at.part_recv.at[:, piece]))
    for part in range(3):
        at.wide[:, 256 * part : 256 * part + 256] = outer_part(own_rows, part)
    for copy in come_outer:
        copy.wait_recv()

    def second_norm(index):
        piece = aligned(index, 64)
        token_rows = pl.ds(pl.multiple_of(core * 256 + index * 64, 64), 64)
        total = at.first_out[piece, :] + at.wide[piece, :] + at.part_recv[piece, :].astype(F32) + vector(5)
        out, normed, inverse = norm(total, vector(6), vector(7))
        at.result[piece, :] = low(out)
        upstream = at.cotangent[piece, :].astype(F32)
        grad = norm_pull(upstream, normed, inverse, vector(6))
        at.grad_sum[piece, :] = grad
        rounded = low(grad)
        at.grad_outer[token_rows, :] = rounded
        give_rows(1, index, at.grad_outer).start()
        at.sums[5:6, :] += jnp.sum(rounded.astype(F32), axis=0, keepdims=True)
        at.sums[6:7, :] += jnp.sum(upstream * normed, axis=0, keepdims=True)
        at.sums[7:8, :] += jnp.sum(upstream, axis=0, keepdims=True)

    loop(4, second_norm)

    def scatter(arrays, tags, send, recv):
        rooms = [[b[kind + tag] for kind in ROOMS] for tag in tags]
        return Scatter(r, arrays, rooms, send, recv)

    scatter_two = scatter((at.grad_1, at.grad_2), ("1", "2"), at.sf_send, at.sf_recv)
    scatter_a = scatter((at.grad_o, at.grad_p.at[0]), ("o", "p0"), at.sa_send, at.sa_recv)
    scatter_b = scatter((at.grad_p.at[1], at.grad_p.at[2]), ("p1", "p2"), at.sb_send, at.sb_recv)
    scatter_c = scatter((at.grad_t.at[0], at.grad_t.at[1]), ("t0", "t1"), at.sc_send, at.sc_recv)

    def inner_grad(rows_at):
        for part in range(4):
            units = pl.ds(384 * part, 384)
            grad = low(dot(at.grad_outer[rows_at, :], at.gat_2[part].reshape(384, 768), 1, 1))
            pre = low(grad.astype(F32) * at.slope[rows_at, units])
            at.grad_pre[rows_at, units] = pre
            at.bias_inner[0:1, units] += jnp.sum(pre.astype(F32), axis=0, keepdims=True)

    at.bias_inner[...] = jnp.zeros_like(at.bias_inner)
    inner_grad(own_rows)
    got_rows(1, at.grad_outer)

    def line_of(index):
        half = index // 2
        start = r.pair * (1 - half) + r.z * half
        return (start + 2 * ((index + 1) // 2 % 2)) % LINE

    def send_lines(i, index, line):
        pl.when(index < 2)(lambda: scatter_two.begin_far(i, line))
        pl.when(index >= 2)(lambda: scatter_two.begin_near(i, line))

    def outer_weight(index):
        line = line_of(index)
        grad = dot(at.active[:, aligned(line, 384)], at.grad_outer[...], 0, 0)
        at.grad_2[line] = low(grad).reshape(4, 96, 768)
        send_lines(1, index, line)

    loop(4, outer_weight)

    inner_grad(other_rows)
    at.sums[8:9, :] = at.bias_inner[0:1, 0:768]
    at.sums[9:10, :] = at.bias_inner[0:1, 768:1536]

    def first_part(rows_at, part):
        weight = at.gat_1[2 * part : 2 * part + 2].reshape(384, 1536)
        return dot(at.grad_pre[rows_at, :], weight, 1, 1)

    come_grad_first = []
    for part in range(2):
        piece = pl.ds(384 * part, 384)
        at.part_send2[:, piece] = low(first_part(other_rows, part))
        come_grad_first.append(
            swap((13, 25)[part], at.part_send2.at[:, piece], at.part_recv2.at[:, piece])
        )
    def inner_weight(index):
        line = line_of(index)
        grad = dot(at.first_turned[aligned(line, 192), :], at.grad_pre[...])
        at.grad_1[line] = low(grad).reshape(4, 48, 1536)
        send_lines(0, index, line)

    loop(4, inner_weight)
    for part in range(2):
        at.wide[:, 384 * part : 384 * part + 384] = first_part(own_rows, part)
    for copy in come_grad_first:
        copy.wait_recv()

    def first_norm_back(index):
        piece = aligned(index, 64)
        token_rows = pl.ds(pl.multiple_of(core * 256 + index * 64, 64), 64)
        upstream = at.wide[piece, :] + at.part_recv2[piece, :].astype(F32) + at.grad_sum[piece, :]
        normed = at.first_normed[piece, :]
        grad = norm_pull(upstream, normed, at.first_inverse[piece, 0:1], vector(3))
        at.grad_sum[piece, :] = grad
        rounded = low(grad)
        at.grad_att[token_rows, :] = rounded
        give_rows(2, index, at.grad_att).start()
        at.sums[2:3, :] += jnp.sum(rounded.astype(F32), axis=0, keepdims=True)
        at.sums[3:4, :] += jnp.sum(upstream * normed, axis=0, keepdims=True)
        at.sums[4:5, :] += jnp.sum(upstream, axis=0, keepdims=True)

    loop(4, first_norm_back)
    out_rows = pl.ds(pl.multiple_of(2 * core, 2), 2)

    def context_rows(rows_at):
        weight_0 = at.out_all[0, out_rows].reshape(384, 384)
        weight_1 = at.out_all[1, out_rows].reshape(384, 384)
        at.grad_context[rows_at, :] = low(
            dot(at.grad_att[rows_at, 0:384], weight_0, 1, 1)
            + dot(at.grad_att[rows_at, 384:768], weight_1, 1, 1)
        )

    context_rows(own_rows)
    got_rows(2, at.grad_att)
    context_rows(other_rows)
    scatter_two.corners(1)
    for part in range(2):
        grad = dot(at.context[part], at.grad_att[:, aligned(core, 384)], 0, 0)
        at.grad_o[2 * part : 2 * part + 2] = low(grad).reshape(2, 4, 48, 384)

    at.near_grad[...] = jnp.zeros_like(at.near_grad)
    at.far_grad[...] = jnp.zeros_like(at.far_grad)
    room = jnp.zeros((128, 128), BF16)

    def spread(value, start):
        wide = jnp.concatenate([value, room], axis=1)
        return pltpu.roll(wide, start, 1, stride=1, stride_axis=0)

    heads = [low((lanes == which).astype(F32)) for which in range(2)]

    def lanes_of(index, place):
        return pl.ds(pl.multiple_of(384 * place + index * 128, 128), 128)

    def masked(value):
        return [value * only for only in heads]

    def backward_queries(index):
        pair = aligned(index, 128)
        flip = at.flip[...]
        keys = masked(at.kvq[:, lanes_of(index, 0)])
        values = at.kvq[:, lanes_of(index, 1)]
        for block in range(4):
            piece = pl.ds(128 * block, 128)
            window = pl.ds(384 - 128 * block, 640)
            back = pl.ds(384 - 128 * block, 128)
            grad_context = low(dot(flip, at.grad_context[piece, pair]))
            query = low(dot(flip, at.kvq[piece, lanes_of(index, 2)]))
            at.turned_grad[piece, :] = grad_context
            at.turned_query[back, :] = query
            table = masked(at.near_rows[window, pair])
            near, grad = [], 0.0
            for which, context_only in enumerate(masked(grad_context)):
                soft = at.soft[2 * index + which, piece, :].astype(F32)
                grad_soft = dot(context_only, values, 1, 1)
                inner = jnp.sum(soft * grad_soft, axis=-1, keepdims=True)
                grad_low = low(soft * (grad_soft - inner) * score_scale)
                at.grad_low[which, back, :] = grad_low
                near.append(spread(grad_low, 1))
                grad = grad + dot(grad_low, keys[which]) + dot(near[which], table[which])
            at.grad_kvq[piece, lanes_of(index, 2)] = low(dot(flip, low(grad)))
            at.near_grad[window, pair] += dot(
                jnp.concatenate(near, axis=0), jnp.concatenate(masked(query), axis=0), 0, 0
            )

    def backward_keys(index):
        pair = aligned(index, 128)
        queries = masked(at.turned_query[...])
        contexts = masked(at.turned_grad[...])
        for block in range(4):
            piece = pl.ds(128 * block, 128)
            window = pl.ds(128 * block, 640)
            table = masked(at.far_natural[window, pair])
            far, grad, grad_value = [], 0.0, 0.0
            for which in range(2):
                turned = at.grad_low[which, :, piece].T
                far.append(spread(turned, 0))
                grad = grad + dot(turned, queries[which]) + dot(far[which], table[which])
                weights = at.soft[2 * index + which, :, piece]
                grad_value = grad_value + dot(weights, contexts[which], 0, 0)
            at.grad_kvq[piece, lanes_of(index, 0)] = low(grad)
            at.grad_kvq[piece, lanes_of(index, 1)] = low(grad_value)
            keys = masked(at.kvq[piece, lanes_of(index, 0)])
            at.far_grad[window, pair] += dot(
                jnp.concatenate(far, axis=0), jnp.concatenate(keys, axis=0), 0, 0
            )

    def shape_weight(value):
        return low(value).reshape(LINE, 4, 48, value.shape[-1])

    def rel_pair(index):
        pair = aligned(index, 128)
        at.key_rel[:, pair] = low(dot(at.one_hot[...], low(at.near_grad[256:768, pair])))
        at.query_rel[:, pair] = low(dot(at.one_natural[...], low(at.far_grad[256:768, pair])))

    def weights_pair(index):
        pair = aligned(index, 128)
        tokens = jnp.concatenate(
            [at.grad_kvq[:, lanes_of(index, place)] for place in (0, 2, 1)], axis=1
        )
        grad = dot(at.x_turned[...], tokens)
        rel = jnp.concatenate([at.key_rel[:, pair], at.query_rel[:, pair]], axis=1)
        table = dot(rows(at.table_all[0]), rel[0:256]) + dot(rows(at.table_all[1]), rel[256:512])
        at.grad_p[index, :, :, :, 0:256] = shape_weight(grad[:, 0:256] + table)
        at.grad_p[index, :, :, :, 256:384] = shape_weight(grad[:, 256:384])

    def table_half(which):
        piece = aligned(which, 256)
        return dot(rows(at.gat_b[:, :, :, 0:384]), at.query_rel[piece, :], 1, 1) + dot(
            rows(at.gat_a[:, :, :, 0:384]), at.key_rel[piece, :], 1, 1
        )

    def at_step(step, when, *moves):
        @pl.when(step == when)
        def _():
            for move in moves:
                move()

    def swap_table():
        return remote(
            at.table_send, at.table_recv, at.swap_send.at[15], at.swap_recv.at[15], r.partner
        )

    def send_table():
        at.table_send[...] = shape_weight(table_half(other))
        swap_table().start()

    def backward_pair(index):
        backward_queries(index)
        at_step(index, 0, lambda: scatter_two.corners(0))
        at_step(index, 1, lambda: scatter_two.along_far(1), lambda: scatter_two.along_far(0))
        at_step(index, 2, lambda: scatter_two.turn(0), lambda: scatter_a.corners(0))
        backward_keys(index)
        rel_pair(index)
        at_step(index, 2, send_table)
        weights_pair(index)
        at_step(index, 0, lambda: scatter_a.begin(0), lambda: scatter_a.begin(1))
        at_step(index, 1, lambda: scatter_b.begin(0), lambda: scatter_two.turn(1))
        at_step(index, 2, lambda: scatter_b.begin(1))

    loop(3, backward_pair)

    own_table = table_half(core)
    scatter_two.along_near(1)
    come_part = swap_table()
    waiting.append(come_part)
    come_part.wait_recv()
    own_table = own_table + rows(at.table_recv[...]).astype(F32)
    for part in range(2):
        at.grad_t[part] = shape_weight(own_table[:, 128 * part : 128 * part + 128])
        scatter_c.begin(part)
    scatter_two.along_near(0)
    scatter_a.corners(1)
    scatter_b.corners(0)
    scatter_a.turn(0)

    at.sums[0:1, vector_half] = jnp.sum(
        at.grad_kvq[:, 768:1152].astype(F32), axis=0, keepdims=True
    ) + jnp.sum(at.far_grad[256:768, :], axis=0, keepdims=True)
    at.sums[1:2, vector_half] = jnp.sum(
        at.grad_kvq[:, 384:768].astype(F32), axis=0, keepdims=True
    )

    def exchange(stage, source, device):
        return remote(
            source, at.sums_come.at[stage], at.sums_send.at[stage], at.sums_recv.at[stage], device
        )

    stage_copies = [exchange(0, at.sums, r.partner)]
    stage_copies[0].start()

    def input_part(rows_at, part):
        weight_a = at.gat_a[2 * part : 2 * part + 2].reshape(384, 768)
        weight_b = at.gat_b[2 * part : 2 * part + 2, :, :, 0:384].reshape(384, 384)
        return dot(at.grad_kvq[rows_at, 0:768], weight_a, 1, 1) + dot(
            at.grad_kvq[rows_at, 768:1152], weight_b, 1, 1
        )

    for copy in come_outer:
        copy.wait_send()
    come_input = []
    for part in range(2):
        piece = pl.ds(384 * part, 384)
        at.part_send[:, piece] = low(input_part(other_rows, part))
        come_input.append(swap((16, 26)[part], at.part_send.at[:, piece], at.part_recv.at[:, piece]))

    stage_copies[0].wait_recv()
    lines = lax.broadcasted_iota(jnp.int32, (16, 1), 0)
    shared = jnp.where((lines == 8) | (lines == 9), 0.0, at.sums_come[0])
    at.sums_step[0] = at.sums[...] + shared
    stage_copies.append(exchange(1, at.sums_step.at[0], r.at_x))
    stage_copies[1].start()
    scatter_b.corners(1)
    scatter_a.along_far(0)
    scatter_a.turn(1)
    scatter_b.turn(0)
    for part in range(2):
        at.wide[:, 384 * part : 384 * part + 384] = input_part(own_rows, part)
    for part in range(2):
        scatter_c.corners(part)
    scatter_a.along_far(1)
    scatter_b.along_far(0)
    scatter_b.turn(1)
    stage_copies[1].wait_recv()
    at.sums_step[1] = at.sums_step[0] + at.sums_come[1]
    stage_copies.append(exchange(2, at.sums_step.at[1], r.at_y))
    stage_copies[2].start()
    for copy in come_input:
        copy.wait_recv()
    at.input_grad[...] = low(at.grad_sum[...] + at.wide[...] + at.part_recv[...].astype(F32))
    for part in range(2):
        scatter_a.along_near(part)
    for part in range(2):
        scatter_c.turn(part)
    at.d_outer[...] = scatter_two.total(1)
    at.give_1[...] = scatter_two.total(0).reshape(2, 24, 1536)
    swap(17, at.give_1.at[other], at.d_inner.at[core])
    at.d_inner[core] = at.give_1[core]
    scatter_b.along_near(0)
    scatter_b.along_far(1)
    for part in range(2):
        scatter_c.along_far(part)
    scatter_b.along_near(1)
    for part in range(2):
        scatter_c.along_near(part)
    stage_copies[2].wait_recv()
    at.sums_step[2] = at.sums_step[1] + at.sums_come[2]
    for step in range(1, LINE):
        copy = exchange(2 + step, at.sums_step.at[2], r.at_line(r.ahead(step)))
        copy.start()
        stage_copies.append(copy)

    at.give_o[...] = scatter_a.total(0).reshape(2, 24, 384)

    def give_pair(index, total):
        for place in range(3):
            start = 384 * place + 128 * index
            at.give_p[:, :, start : start + 128] = total[:, 128 * place : 128 * place + 128].reshape(
                2, 24, 128
            )

    give_pair(0, scatter_a.total(1))
    give_pair(1, scatter_b.total(0))
    give_pair(2, scatter_b.total(1))
    for part in range(2):
        at.give_t[:, :, 128 * part : 128 * part + 128] = scatter_c.total(part).reshape(2, 24, 128)
    for copy in stage_copies[3:]:
        copy.wait_recv()
    at.vector_grads[...] = (
        at.sums_step[2] + at.sums_come[3] + at.sums_come[4] + at.sums_come[5]
    )
    outs = (
        (at.give_p, 0, 384, at.d_key),
        (at.give_p, 384, 384, at.d_query),
        (at.give_p, 768, 384, at.d_value),
        (at.give_o, 0, 384, at.d_output),
        (at.give_t, 0, 256, at.d_table),
    )
    for slot, (give, start, width, out) in enumerate(outs):
        swap(18 + slot, give.at[other, :, pl.ds(start, width)], out.at[:, aligned(core, width)])
        out[:, aligned(core, width)] = give[core, :, start : start + width]
    for copy in waiting[-6:]:
        copy.wait_recv()
    for copy in waiting:
        if all(copy is not early for early in come_outer):
            copy.wait_send()
    for copy in stage_copies:
        copy.wait_send()
    for kind, array in enumerate((at.first_low, at.grad_outer, at.grad_att)):
        for index in range(4):
            give_rows(kind, index, array).wait_send()
    for index in range(3):
        remote(
            at.context.at[core, :, pl.ds(128 * index, 128)],
            at.context.at[core, :, pl.ds(128 * index, 128)],
            at.context_send.at[index],
            at.context_recv.at[index],
            r.partner,
        ).wait_send()
    for user in (gather_one, gather_two, scatter_two, scatter_a, scatter_b, scatter_c):
        user.sent()


def finish_kernel(names, *refs):
    at = type("Refs", (), dict(zip(names, refs)))
    chip, core = lax.axis_index("fsdp"), lax.axis_index("seq")
    at.result_out[...] = at.result[...]
    at.input_grad_out[...] = at.input_grad[...]
    at.query_w_out[...] = at.d_query[...]
    at.key_w_out[...] = at.d_key[...]
    at.value_w_out[...] = at.d_value[...]
    at.output_w_out[...] = at.d_output[...]
    at.table_out[...] = at.d_table[...]
    at.outer_w_out[...] = at.d_outer[...]
    for group in range(4 * LINE):
        for which in range(2):
            device = 2 * group + which
            at.inner_w_out[:, 96 * device : 96 * device + 96] = at.d_inner[
                which, :, 96 * group : 96 * group + 96
            ]
    sums = at.vector_grads[...]
    own = pltpu.roll(sums, (768 - 24 * (2 * chip + core)) % 768, 1)
    small_outs = (
        at.query_b_out, at.value_b_out, at.output_b_out, at.gain_1_out, at.shift_1_out,
        at.outer_b_out, at.gain_2_out, at.shift_2_out,
    )
    for index, out in enumerate(small_outs):
        out[...] = own[index : index + 1, 0:24]
    units = jnp.where(chip < 2 * LINE, sums[8:9], sums[9:10])
    units = jnp.broadcast_to(units, (8, 768))
    at.inner_b_out[...] = pltpu.roll(units, (768 - 96 * (chip % (2 * LINE))) % 768, 1)[0:1, 0:96]
    at.count_out[...] = sums[10:11, 0:1].astype(jnp.int32)


OUTPUTS = dict(
    result=((256, 768), BF16),
    input_grad=((256, 768), BF16),
    d_query=((24, 768), F32),
    d_key=((24, 768), F32),
    d_value=((24, 768), F32),
    d_output=((24, 768), F32),
    d_table=((24, 512), F32),
    d_inner=((2, 24, 1536), F32),
    d_outer=((96, 768), F32),
    vector_grads=((16, 768), F32),
)
FINALS = dict(
    result_out=((256, 768), BF16),
    input_grad_out=((256, 768), BF16),
    query_w_out=((24, 768), F32),
    key_w_out=((24, 768), F32),
    value_w_out=((24, 768), F32),
    output_w_out=((24, 768), F32),
    table_out=((24, 512), F32),
    inner_w_out=((24, 3072), F32),
    outer_w_out=((96, 768), F32),
    query_b_out=((1, 24), F32),
    value_b_out=((1, 24), F32),
    output_b_out=((1, 24), F32),
    gain_1_out=((1, 24), F32),
    shift_1_out=((1, 24), F32),
    outer_b_out=((1, 24), F32),
    gain_2_out=((1, 24), F32),
    shift_2_out=((1, 24), F32),
    inner_b_out=((1, 96), F32),
    count_out=((1, 1), jnp.int32),
)
LINE = 4
BLOCKS = (LINE, 4, 48)
SCRATCH = dict(
    small_wide=((16, 128), F32),
    small=((16, 128), BF16),
    inner_pair=((2, 24, 1536), BF16),
    segment_row=((8, 512), F32),
    segment_col=((512, 128), F32),
    come_a=((24, 768), BF16),
    come_b=((24, 1024), BF16),
    come_s=((16, 128), BF16),
    come_1=((24, 1536), BF16),
    gat_a=(BLOCKS + (768,), BF16),
    gat_b=(BLOCKS + (1024,), BF16),
    gat_s=((LINE, 4, 2, 16, 128), BF16),
    gat_1=(BLOCKS + (1536,), BF16),
    gat_2=((LINE, 4, 96, 768), BF16),
    x_all=((512, 768), BF16),
    x_turned=((768, 512), BF16),
    one_hot=((512, 512), BF16),
    flip=((128, 128), BF16),
    near_rows=((1024, 384), BF16),
    far_rows=((1024, 384), BF16),
    far_natural=((1024, 384), BF16),
    one_natural=((512, 512), BF16),
    near_grad=((1024, 384), F32),
    far_grad=((1024, 384), F32),
    key_rel=((512, 384), BF16),
    query_rel=((512, 384), BF16),
    table_all=((2,) + BLOCKS + (256,), BF16),
    out_all=((2,) + BLOCKS + (384,), BF16),
    vectors=((8, 768), F32),
    inner_bias=((8, 1536), F32),
    bias_inner=((8, 1536), F32),
    kvq=((512, 1152), BF16),
    grad_kvq=((512, 1152), BF16),
    far_scores=((512, 512), F32),
    grad_low=((2, 512, 512), BF16),
    turned_query=((512, 128), BF16),
    turned_grad=((512, 128), BF16),
    soft=((6, 512, 512), BF16),
    context=((2, 512, 384), BF16),
    grad_context=((512, 384), BF16),
    wide=((256, 768), F32),
    first_out=((256, 768), F32),
    first_normed=((256, 768), F32),
    first_inverse=((256, 128), F32),
    first_low=((512, 768), BF16),
    first_turned=((768, 512), BF16),
    active=((512, 1536), BF16),
    slope=((512, 1536), F32),
    grad_pre=((512, 1536), BF16),
    part_send=((256, 768), BF16),
    part_recv=((256, 768), BF16),
    part_send2=((256, 768), BF16),
    part_recv2=((256, 768), BF16),
    grad_sum=((256, 768), F32),
    grad_outer=((512, 768), BF16),
    grad_att=((512, 768), BF16),
    table_send=(BLOCKS + (256,), BF16),
    table_recv=(BLOCKS + (256,), BF16),
    sums=((16, 768), F32),
    sums_step=((3, 16, 768), F32),
    sums_come=((6, 16, 768), F32),
    grad_1=(BLOCKS + (1536,), BF16),
    grad_2=((LINE, 4, 96, 768), BF16),
    grad_o=(BLOCKS + (384,), BF16),
    grad_p=((3,) + BLOCKS + (384,), BF16),
    grad_t=((2,) + BLOCKS + (128,), BF16),
    give_1=((2, 24, 1536), F32),
    give_o=((2, 24, 384), F32),
    give_p=((2, 24, 1152), F32),
    give_t=((2, 24, 256), F32),
)
ROOMS = dict(pair_=2, first_=LINE, corner_=2, second_=LINE, line_=LINE)
BLOCK = {
    "1": (48, 1536), "2": (96, 768), "o": (48, 384), "p0": (48, 384), "p1": (48, 384),
    "p2": (48, 384), "t0": (48, 128), "t1": (48, 128),
}
for tag, block in BLOCK.items():
    for kind, count in ROOMS.items():
        SCRATCH[kind + tag] = ((count,) + block, BF16)
SEMAPHORES = dict(
    swap_send=(27,),
    swap_recv=(27,),
    row_send=(3, 4),
    row_recv=(3, 4),
    here=(2,),
    context_send=(3,),
    context_recv=(3,),
    ga_send=(3, 6, LINE),
    ga_recv=(3, 6, LINE),
    gf_send=(2, 6, LINE),
    gf_recv=(2, 6, LINE),
    sf_send=(2, 5, LINE),
    sf_recv=(2, 5, LINE),
    sa_send=(2, 5, LINE),
    sa_recv=(2, 5, LINE),
    sb_send=(2, 5, LINE),
    sb_recv=(2, 5, LINE),
    sc_send=(2, 5, LINE),
    sc_recv=(2, 5, LINE),
    sums_send=(6,),
    sums_recv=(6,),
)


def block_shards(
    hidden_in,
    query_weight,
    query_bias,
    key_weight,
    value_weight,
    value_bias,
    output_weight,
    output_bias,
    first_gain,
    first_shift,
    inner_weight,
    inner_bias,
    outer_weight,
    outer_bias,
    second_gain,
    second_shift,
    relative_table,
    segments,
    buckets,
    predicted,
    labels,
    cotangent,
):
    inputs = dict(
        hidden=hidden_in[0],
        query_w=query_weight,
        key_w=key_weight,
        value_w=value_weight,
        output_w=output_weight,
        table_t=relative_table.T,
        inner_w=inner_weight,
        outer_w=outer_weight,
        query_b=query_bias[None],
        value_b=value_bias[None],
        output_b=output_bias[None],
        gain_1=first_gain[None],
        shift_1=first_shift[None],
        outer_b=outer_bias[None],
        gain_2=second_gain[None],
        shift_2=second_shift[None],
        inner_b=inner_bias[None],
        segments=segments,
        buckets=buckets[None],
        predicted=predicted,
        labels=labels,
        cotangent=cotangent[0],
    )
    names = tuple(inputs) + tuple(OUTPUTS) + tuple(SCRATCH) + tuple(SEMAPHORES)
    vmem = pl.BlockSpec(memory_space=pltpu.VMEM)
    outs = pl.pallas_call(
        partial(layer_kernel, names),
        name="layer",
        out_shape=tuple(jax.ShapeDtypeStruct(*out) for out in OUTPUTS.values()),
        in_specs=[vmem] * len(inputs),
        out_specs=(vmem,) * len(OUTPUTS),
        scratch_shapes=[pltpu.VMEM(*spec) for spec in SCRATCH.values()]
        + [pltpu.SemaphoreType.DMA(shape) for shape in SEMAPHORES.values()],
        compiler_params=pltpu.CompilerParams(
            collective_id=0, has_side_effects=True, vmem_limit_bytes=67043328
        ),
    )(*inputs.values())
    finals = pl.pallas_call(
        partial(finish_kernel, tuple(OUTPUTS) + tuple(FINALS)),
        name="finish",
        out_shape=tuple(jax.ShapeDtypeStruct(*out) for out in FINALS.values()),
        in_specs=[vmem] * len(OUTPUTS),
        out_specs=(vmem,) * len(FINALS),
    )(*outs)
    got = type("Outs", (), dict(zip(FINALS, finals)))
    return (
        got.result_out[None],
        got.input_grad_out[None],
        got.query_w_out,
        got.query_b_out[0],
        got.key_w_out,
        got.value_w_out,
        got.value_b_out[0],
        got.output_w_out,
        got.output_b_out[0],
        got.gain_1_out[0],
        got.shift_1_out[0],
        got.inner_w_out,
        got.inner_b_out[0],
        got.outer_w_out,
        got.outer_b_out[0],
        got.gain_2_out[0],
        got.shift_2_out[0],
        got.table_out.T,
        got.count_out[0, 0],
    )


def fits(mesh):
    return mesh.shape["fsdp"] == 4 * LINE and mesh.shape["seq"] == 2


def solution(mesh):
    return jax.shard_map(
        block_shards if fits(mesh) else shards,
        mesh=mesh,
        in_specs=(
            P("fsdp", "seq", None),
            P(("fsdp", "seq"), None),
            P(("fsdp", "seq")),
            P(("fsdp", "seq"), None),
            P(("fsdp", "seq"), None),
            P(("fsdp", "seq")),
            P(("fsdp", "seq"), None),
            P(("fsdp", "seq")),
            P(("fsdp", "seq")),
            P(("fsdp", "seq")),
            P(("fsdp", "seq"), None),
            P(("fsdp", "seq")),
            P(("fsdp", "seq"), None),
            P(("fsdp", "seq")),
            P(("fsdp", "seq")),
            P(("fsdp", "seq")),
            P(None, ("fsdp", "seq")),
            P("fsdp", None),
            P(),
            P("fsdp", "seq"),
            P("fsdp", "seq"),
            P("fsdp", "seq", None),
        ),
        out_specs=(
            P("fsdp", "seq", None),
            P("fsdp", "seq", None),
            P(("fsdp", "seq"), None),
            P(("fsdp", "seq")),
            P(("fsdp", "seq"), None),
            P(("fsdp", "seq"), None),
            P(("fsdp", "seq")),
            P(("fsdp", "seq"), None),
            P(("fsdp", "seq")),
            P(("fsdp", "seq")),
            P(("fsdp", "seq")),
            P(("fsdp", "seq"), None),
            P(("fsdp", "seq")),
            P(("fsdp", "seq"), None),
            P(("fsdp", "seq")),
            P(("fsdp", "seq")),
            P(("fsdp", "seq")),
            P(None, ("fsdp", "seq")),
            P(),
        ),
        check_vma=False,
    )
```

```python
from functools import partial

import jax
import jax.numpy as jnp
import numpy as np
from jax import lax
from jax.experimental import pallas as pl
from jax.experimental.pallas import tpu as pltpu
from jax.sharding import PartitionSpec as P

HEAD = 64


EPSILON = 1e-07
NEGATIVE = -1e30


def matmul(spec, left, right):
    return jnp.einsum(spec, left, right, preferred_element_type=jnp.float32)


def precise(spec, left, right):
    return jnp.einsum(spec, left, right, precision=lax.Precision.HIGHEST)


def skew_rows(scores_in, offset, columns):
    leading = scores_in.shape[:-2]
    row_count = scores_in.shape[-2]
    breadth = scores_in.shape[-1]
    flattened = scores_in.reshape(leading + (row_count * breadth,))
    flattened = jnp.concatenate(
        [flattened, jnp.zeros(leading + (2 * breadth,), scores_in.dtype)], axis=-1
    )
    selected = lax.dynamic_slice_in_dim(flattened, offset, row_count * (breadth - 1), len(leading))
    return selected.reshape(leading + (row_count, breadth - 1))[..., :columns]


def unskew_rows(values, offset, breadth):
    leading = values.shape[:-2]
    row_count = values.shape[-2]
    columns = values.shape[-1]
    padded = jnp.concatenate(
        [values, jnp.zeros(leading + (row_count, breadth - 1 - columns), values.dtype)], axis=-1
    )
    flattened = padded.reshape(leading + (row_count * (breadth - 1),))
    zero_room = jnp.zeros(leading + (row_count * breadth + 2 * breadth,), values.dtype)
    placed = lax.dynamic_update_slice_in_dim(zero_room, flattened, offset, len(leading))
    return placed[..., : row_count * breadth].reshape(leading + (row_count, breadth))


def layer_norm(values, gain, shift):
    average = jnp.mean(values, axis=-1, keepdims=True)
    centred = values - average
    variance = jnp.mean(centred * centred, axis=-1, keepdims=True)
    inverse = lax.rsqrt(variance + EPSILON)
    normed = centred * inverse
    return (normed * gain + shift, normed, inverse)


def norm_backward(upstream, normed, inverse, gain):
    scaled_up = upstream * gain
    first_mean = jnp.mean(scaled_up, axis=-1, keepdims=True)
    second_mean = jnp.mean(scaled_up * normed, axis=-1, keepdims=True)
    grad_in = inverse * (scaled_up - first_mean - normed * second_mean)
    return (grad_in, jnp.sum(upstream * normed, axis=0), jnp.sum(upstream, axis=0))


def shards(
    hidden_in,
    query_weight,
    query_bias,
    key_weight,
    value_weight,
    value_bias,
    output_weight,
    output_bias,
    first_gain,
    first_shift,
    inner_weight,
    inner_bias,
    outer_weight,
    outer_bias,
    second_gain,
    second_shift,
    relative_table,
    segments,
    buckets,
    predicted,
    labels,
    cotangent,
):
    row_count, window, model_width = hidden_in.shape
    length = segments.shape[1]
    distances = 2 * length - 1
    span = window + length - 1
    pair_width = 2 * HEAD
    pair_count = model_width // pair_width
    score_scale = (3.0 * HEAD) ** (-0.5)
    window_start = lax.axis_index("seq") * window
    near_start = length - window - window_start
    token_count = row_count * window
    attention_set = (
        lax.all_gather(query_weight, ("fsdp", "seq"), axis=0, tiled=True),
        lax.all_gather(query_bias, ("fsdp", "seq"), axis=0, tiled=True),
        lax.all_gather(key_weight, ("fsdp", "seq"), axis=0, tiled=True),
        lax.all_gather(value_weight, ("fsdp", "seq"), axis=0, tiled=True),
        lax.all_gather(value_bias, ("fsdp", "seq"), axis=0, tiled=True),
        lax.all_gather(output_weight, ("fsdp", "seq"), axis=0, tiled=True),
        lax.all_gather(output_bias, ("fsdp", "seq"), axis=0, tiled=True),
        lax.all_gather(first_gain, ("fsdp", "seq"), axis=0, tiled=True),
        lax.all_gather(first_shift, ("fsdp", "seq"), axis=0, tiled=True),
        lax.all_gather(relative_table, ("fsdp", "seq"), axis=1, tiled=True),
    )
    feed_set = (
        lax.all_gather(inner_weight, ("fsdp", "seq"), axis=0, tiled=True),
        lax.all_gather(inner_bias, ("fsdp", "seq"), axis=0, tiled=True),
        lax.all_gather(outer_weight, ("fsdp", "seq"), axis=0, tiled=True),
        lax.all_gather(outer_bias, ("fsdp", "seq"), axis=0, tiled=True),
        lax.all_gather(second_gain, ("fsdp", "seq"), axis=0, tiled=True),
        lax.all_gather(second_shift, ("fsdp", "seq"), axis=0, tiled=True),
    )
    (
        query_matrix,
        query_offset,
        key_matrix,
        value_matrix,
        value_offset,
        output_matrix,
        output_offset,
        gain_first,
        shift_first,
        table_full,
    ) = attention_set
    inner_matrix, inner_offset, outer_matrix, outer_offset, gain_second, shift_second = feed_set
    tokens = hidden_in.reshape(token_count, model_width)
    queries = (
        (matmul("td,de->te", tokens, query_matrix) + query_offset.astype(jnp.float32))
        .astype(jnp.bfloat16)
        .reshape(row_count, window, model_width)
    )
    keys_own = (
        matmul("td,de->te", tokens, key_matrix)
        .astype(jnp.bfloat16)
        .reshape(row_count, window, model_width)
    )
    values_own = (
        (matmul("td,de->te", tokens, value_matrix) + value_offset.astype(jnp.float32))
        .astype(jnp.bfloat16)
        .reshape(row_count, window, model_width)
    )
    keys_all, values_all = (
        lax.all_gather(keys_own, "seq", axis=1, tiled=True),
        lax.all_gather(values_own, "seq", axis=1, tiled=True),
    )
    key_rel = matmul("pd,de->pe", table_full, key_matrix).astype(jnp.bfloat16)
    query_rel = (
        matmul("pd,de->pe", table_full, query_matrix) + query_offset.astype(jnp.float32)
    ).astype(jnp.bfloat16)
    reversed_buckets = buckets[::-1]
    table_rows = table_full.shape[0]
    one_hot = (
        reversed_buckets[:, None] == jnp.arange(table_rows, dtype=jnp.int32)[None, :]
    ).astype(jnp.bfloat16)
    bucket_keys = matmul("dp,pe->de", one_hot, key_rel).astype(jnp.bfloat16)
    bucket_queries = matmul("dp,pe->de", one_hot, query_rel).astype(jnp.bfloat16)
    near_keys = lax.dynamic_slice_in_dim(bucket_keys, near_start, span, 0)
    far_queries = lax.dynamic_slice_in_dim(bucket_queries, window_start, span, 0)
    segment_own = lax.dynamic_slice_in_dim(segments, window_start, window, 1)
    same_doc = (segment_own[:, :, None] == segments[:, None, :])[:, None]

    def pair_scores(pair_index):
        column = pair_index * pair_width
        query_pair = lax.dynamic_slice_in_dim(queries, column, pair_width, 2).reshape(
            row_count, window, 2, HEAD
        )
        key_pair = lax.dynamic_slice_in_dim(keys_all, column, pair_width, 2).reshape(
            row_count, length, 2, HEAD
        )
        value_pair = lax.dynamic_slice_in_dim(values_all, column, pair_width, 2).reshape(
            row_count, length, 2, HEAD
        )
        bucketkeys = lax.dynamic_slice_in_dim(near_keys, column, pair_width, 1).reshape(
            span, 2, HEAD
        )
        bucketqueries = lax.dynamic_slice_in_dim(far_queries, column, pair_width, 1).reshape(
            span, 2, HEAD
        )
        content = matmul("rihe,rjhe->rhij", query_pair, key_pair)
        near_scores = matmul("rihe,dhe->rhid", query_pair, bucketkeys)
        far_scores = matmul("rjhe,dhe->rhjd", key_pair, bucketqueries)
        to_position = skew_rows(near_scores, window - 1, length)
        from_position = jnp.swapaxes(skew_rows(far_scores, length - 1, window), 2, 3)
        summed = content + to_position + from_position
        masked = jnp.where(same_doc, summed * score_scale, NEGATIVE)
        return (masked, query_pair, key_pair, value_pair, bucketkeys, bucketqueries)

    def attend_pair(pair_index):
        masked, query_pair, key_pair, value_pair, bucketkeys, bucketqueries = pair_scores(
            pair_index
        )
        highest = jnp.max(masked, axis=-1, keepdims=True)
        expsum = jnp.exp(masked - highest)
        totals = jnp.sum(expsum, axis=-1, keepdims=True)
        weights_soft = (expsum / totals).astype(jnp.bfloat16)
        context_pair = matmul("rhij,rjhe->rihe", weights_soft, value_pair).astype(jnp.bfloat16)
        return (
            context_pair.reshape(row_count, window, pair_width),
            (highest + jnp.log(totals))[..., 0],
        )

    context_parts, log_totals = lax.map(attend_pair, jnp.arange(pair_count, dtype=jnp.int32))
    context = jnp.moveaxis(context_parts, 0, 2).reshape(token_count, model_width)
    attention_out = matmul("te,ed->td", context, output_matrix) + output_offset.astype(jnp.float32)
    residual_one = tokens.astype(jnp.float32) + attention_out
    first_out, first_normed, first_inverse = layer_norm(
        residual_one, gain_first.astype(jnp.float32), shift_first.astype(jnp.float32)
    )
    first_low = first_out.astype(jnp.bfloat16)
    inner_pre = matmul("td,df->tf", first_low, inner_matrix) + inner_offset.astype(jnp.float32)
    activated = jax.nn.gelu(inner_pre, approximate=False).astype(jnp.bfloat16)
    outer_out = matmul("tf,fd->td", activated, outer_matrix) + outer_offset.astype(jnp.float32)
    final_out, final_normed, final_inverse = layer_norm(
        first_out + outer_out, gain_second.astype(jnp.float32), shift_second.astype(jnp.float32)
    )
    result = final_out.astype(jnp.bfloat16).reshape(row_count, window, model_width)
    correct_count = lax.psum(jnp.sum((predicted == labels).astype(jnp.int32)), ("fsdp", "seq"))
    regathered = attention_set + feed_set
    (
        query_back,
        query_offset_back,
        key_back,
        value_back,
        value_offset_back,
        output_back,
        output_offset_back,
        gain_first_back,
        shift_first_back,
        table_back,
        inner_back,
        inner_offset_back,
        outer_back,
        outer_offset_back,
        gain_second_back,
        shift_second_back,
    ) = regathered
    upstream = cotangent.reshape(token_count, model_width).astype(jnp.float32)
    grad_sum2, grad_gain2, grad_shift2 = norm_backward(
        upstream, final_normed, final_inverse, gain_second_back.astype(jnp.float32)
    )
    grad_outer = grad_sum2.astype(jnp.bfloat16)
    outer_bias_part = jnp.sum(grad_outer.astype(jnp.float32), axis=0)
    outer_weight_part = matmul("tf,td->fd", activated, grad_outer)
    grad_act = matmul("td,fd->tf", grad_outer, outer_back).astype(jnp.bfloat16)
    _, gelu_back = jax.vjp(partial(jax.nn.gelu, approximate=False), inner_pre)
    grad_inner = gelu_back(grad_act.astype(jnp.float32))[0].astype(jnp.bfloat16)
    inner_bias_part = jnp.sum(grad_inner.astype(jnp.float32), axis=0)
    inner_weight_part = matmul("td,tf->df", first_low, grad_inner)
    grad_first = matmul("tf,df->td", grad_inner, inner_back) + grad_sum2
    feed_grads = (
        lax.psum_scatter(inner_weight_part, ("fsdp", "seq"), scatter_dimension=0, tiled=True),
        lax.psum_scatter(inner_bias_part, ("fsdp", "seq"), scatter_dimension=0, tiled=True),
        lax.psum_scatter(outer_weight_part, ("fsdp", "seq"), scatter_dimension=0, tiled=True),
        lax.psum_scatter(outer_bias_part, ("fsdp", "seq"), scatter_dimension=0, tiled=True),
        lax.psum_scatter(grad_gain2, ("fsdp", "seq"), scatter_dimension=0, tiled=True),
        lax.psum_scatter(grad_shift2, ("fsdp", "seq"), scatter_dimension=0, tiled=True),
    )
    grad_sum1, grad_gain1, grad_shift1 = norm_backward(
        grad_first, first_normed, first_inverse, gain_first_back.astype(jnp.float32)
    )
    grad_attention = grad_sum1.astype(jnp.bfloat16)
    output_bias_part = jnp.sum(grad_attention.astype(jnp.float32), axis=0)
    output_weight_part = matmul("te,td->ed", context, grad_attention)
    grad_context = (
        matmul("td,ed->te", grad_attention, output_back)
        .astype(jnp.bfloat16)
        .reshape(row_count, window, model_width)
    )

    def attend_back(pieces):
        pair_index, log_total = pieces
        masked, query_pair, key_pair, value_pair, bucketkeys, bucketqueries = pair_scores(
            pair_index
        )
        probability = jnp.exp(masked - log_total[..., None])
        grad_context_pair = lax.dynamic_slice_in_dim(
            grad_context, pair_index * pair_width, pair_width, 2
        ).reshape(row_count, window, 2, HEAD)
        grad_soft = matmul("rihe,rjhe->rhij", grad_context_pair, value_pair)
        grad_scores = probability * (
            grad_soft - jnp.sum(probability * grad_soft, axis=-1, keepdims=True)
        )
        grad_low = (grad_scores * score_scale).astype(jnp.bfloat16)
        grad_value = matmul("rhij,rihe->rjhe", probability.astype(jnp.bfloat16), grad_context_pair)
        grad_near = unskew_rows(grad_low, window - 1, span)
        grad_far = unskew_rows(jnp.swapaxes(grad_low, 2, 3), length - 1, span)
        grad_query = matmul("rhij,rjhe->rihe", grad_low, key_pair) + matmul(
            "rhid,dhe->rihe", grad_near, bucketkeys
        )
        grad_key = matmul("rhij,rihe->rjhe", grad_low, query_pair) + matmul(
            "rhjd,dhe->rjhe", grad_far, bucketqueries
        )
        grad_bkeys = matmul("rhid,rihe->dhe", grad_near, query_pair)
        grad_bqueries = matmul("rhjd,rjhe->dhe", grad_far, key_pair)
        return (
            grad_query.reshape(row_count, window, pair_width),
            grad_key.reshape(row_count, length, pair_width),
            grad_value.reshape(row_count, length, pair_width),
            grad_bkeys.reshape(span, pair_width),
            grad_bqueries.reshape(span, pair_width),
        )

    query_parts, key_parts, value_parts, bkey_parts, bquery_parts = lax.map(
        attend_back, (jnp.arange(pair_count, dtype=jnp.int32), log_totals)
    )
    grad_query_all = jnp.moveaxis(query_parts, 0, 2).reshape(token_count, model_width)
    grad_key_all = jnp.moveaxis(key_parts, 0, 2).reshape(row_count, length, model_width)
    grad_value_all = jnp.moveaxis(value_parts, 0, 2).reshape(row_count, length, model_width)
    near_grads = jnp.moveaxis(bkey_parts, 0, 1).reshape(span, model_width)
    far_grads = jnp.moveaxis(bquery_parts, 0, 1).reshape(span, model_width)
    grad_bucket_keys = lax.dynamic_update_slice_in_dim(
        jnp.zeros((distances, model_width), jnp.float32), near_grads, near_start, 0
    )
    grad_bucket_queries = lax.dynamic_update_slice_in_dim(
        jnp.zeros((distances, model_width), jnp.float32), far_grads, window_start, 0
    )
    key_grads, value_grads = (
        lax.psum_scatter(
            grad_key_all.astype(jnp.bfloat16), "seq", scatter_dimension=1, tiled=True
        ).astype(jnp.float32),
        lax.psum_scatter(
            grad_value_all.astype(jnp.bfloat16), "seq", scatter_dimension=1, tiled=True
        ).astype(jnp.float32),
    )
    query_low = grad_query_all.astype(jnp.bfloat16)
    key_low = key_grads.reshape(token_count, model_width).astype(jnp.bfloat16)
    value_low = value_grads.reshape(token_count, model_width).astype(jnp.bfloat16)
    grad_key_rel = jax.ops.segment_sum(grad_bucket_keys, reversed_buckets, num_segments=table_rows)
    grad_query_rel = jax.ops.segment_sum(
        grad_bucket_queries, reversed_buckets, num_segments=table_rows
    )
    query_token_part = matmul("td,te->de", tokens, query_low)
    query_bias_token = jnp.sum(query_low.astype(jnp.float32), axis=0)
    key_token_part = matmul("td,te->de", tokens, key_low)
    value_weight_part = matmul("td,te->de", tokens, value_low)
    value_bias_part = jnp.sum(value_low.astype(jnp.float32), axis=0)
    grad_input = (
        grad_sum1
        + matmul("te,de->td", query_low, query_back)
        + matmul("te,de->td", key_low, key_back)
        + matmul("te,de->td", value_low, value_back)
    )
    input_grad = grad_input.astype(jnp.bfloat16).reshape(row_count, window, model_width)
    key_rel_total, query_rel_total = lax.psum((grad_key_rel, grad_query_rel), ("fsdp", "seq"))
    attention_grads = (
        lax.psum_scatter(query_token_part, ("fsdp", "seq"), scatter_dimension=0, tiled=True),
        lax.psum_scatter(query_bias_token, ("fsdp", "seq"), scatter_dimension=0, tiled=True),
        lax.psum_scatter(key_token_part, ("fsdp", "seq"), scatter_dimension=0, tiled=True),
        lax.psum_scatter(value_weight_part, ("fsdp", "seq"), scatter_dimension=0, tiled=True),
        lax.psum_scatter(value_bias_part, ("fsdp", "seq"), scatter_dimension=0, tiled=True),
        lax.psum_scatter(output_weight_part, ("fsdp", "seq"), scatter_dimension=0, tiled=True),
        lax.psum_scatter(output_bias_part, ("fsdp", "seq"), scatter_dimension=0, tiled=True),
        lax.psum_scatter(grad_gain1, ("fsdp", "seq"), scatter_dimension=0, tiled=True),
        lax.psum_scatter(grad_shift1, ("fsdp", "seq"), scatter_dimension=0, tiled=True),
    )
    shard_rows = query_weight.shape[0]
    shard_start = lax.axis_index(("fsdp", "seq")) * shard_rows
    table_shard = relative_table.astype(jnp.float32)
    query_weight_grad = attention_grads[0] + precise("pd,pe->de", table_shard, query_rel_total)
    key_weight_grad = attention_grads[2] + precise("pd,pe->de", table_shard, key_rel_total)
    query_bias_grad = attention_grads[1] + jnp.sum(
        lax.dynamic_slice_in_dim(query_rel_total, shard_start, shard_rows, 1), axis=0
    )
    relative_table_grad = precise(
        "pe,de->pd", query_rel_total, query_weight.astype(jnp.float32)
    ) + precise("pe,de->pd", key_rel_total, key_weight.astype(jnp.float32))
    return (
        result,
        input_grad,
        query_weight_grad,
        query_bias_grad,
        key_weight_grad,
        attention_grads[3],
        attention_grads[4],
        attention_grads[5],
        attention_grads[6],
        attention_grads[7],
        attention_grads[8],
        feed_grads[0],
        feed_grads[1],
        feed_grads[2],
        feed_grads[3],
        feed_grads[4],
        feed_grads[5],
        relative_table_grad,
        correct_count,
    )


MESH = pl.DeviceIdType.MESH
F32 = jnp.float32
BF16 = jnp.bfloat16


def dot(left, right, left_dim=1, right_dim=0):
    return lax.dot_general(
        left, right, (((left_dim,), (right_dim,)), ((), ())), preferred_element_type=F32
    )


def low(value):
    return value.astype(BF16)


class Route:
    def __init__(self):
        chip = lax.axis_index("fsdp")
        self.core = lax.axis_index("seq")
        self.other = 1 - self.core
        self.chip = chip
        self.x = chip % 2
        self.y = (chip // 2) % 2
        self.z = chip // 4
        self.plane = chip % 4
        self.plane_x = self.plane + 1 - 2 * self.x
        self.plane_y = self.plane + 2 - 4 * self.y
        self.pair = self.z + 1 - 2 * (self.z % 2)
        self.near = (self.z, (self.z + 2) % LINE)
        self.far = (self.pair, (self.pair + 2) % LINE)
        self.soon = 1 + self.z % 2
        self.late = 3 - 3 * (self.z % 2)
        self.partner = (chip, self.other)
        self.at_x = (self.z * 4 + self.plane_x, self.core)
        self.at_y = (self.z * 4 + self.plane_y, self.core)

    def at_line(self, line):
        return (line * 4 + self.plane, self.core)

    def ahead(self, step):
        return (self.z + step) % LINE

    def behind(self, step):
        return (self.z + LINE - step) % LINE


def remote(source, target, send_sem, recv_sem, device):
    return pltpu.make_async_remote_copy(
        source, target, send_sem, recv_sem, device_id=device, device_id_type=MESH
    )


class Gather:
    def __init__(self, route, arrays, send, recv):
        self.r, self.arrays, self.send, self.recv = route, arrays, send, recv

    def copies(self, kind, line):
        r = self.r
        for i, array in enumerate(self.arrays):
            by_x = i == 1
            plane, device = (
                (r.plane, r.at_line((r.z + 1) % LINE)),
                (r.plane, r.at_line((r.z + LINE - 1) % LINE)),
                (r.plane, r.at_x),
                (r.plane, r.at_y),
                (r.plane_y, r.at_x) if by_x else (r.plane_x, r.at_y),
                (3 - r.plane, r.at_line(r.pair)),
            )[kind]
            block = array.at[line, plane]
            yield remote(
                block, block, self.send.at[i, kind, line], self.recv.at[i, kind, line], device
            )

    def begin(self, kind, line):
        for copy in self.copies(kind, line):
            copy.start()

    def got(self, kind, line):
        for copy in self.copies(kind, line):
            copy.wait_recv()

    def sides(self, line):
        self.begin(2, line)
        self.begin(3, line)

    def got_sides(self, line):
        self.got(2, line)
        self.got(3, line)

    def up(self, line):
        @pl.when(self.r.z < LINE - 1)
        def _():
            self.begin(0, line)

    def down(self, line):
        @pl.when(self.r.z > 0)
        def _():
            self.begin(1, line)

    def start_line(self):
        self.up(self.r.z)
        self.down(self.r.z)

    def start_sides(self):
        self.sides(self.r.z)

    def round(self, step):
        r = self.r

        @pl.when(r.z >= step)
        def _():
            self.got(0, r.z - step)
            self.up(r.z - step)

        @pl.when(r.z + step < LINE)
        def _():
            self.got(1, r.z + step)
            self.down(r.z + step)

    def first(self):
        self.corner(0)
        self.round(1)
        self.sides(self.r.soon)

    def second(self):
        self.round(2)
        self.sides(self.r.near[1])
        self.hand(0)

    def third(self):
        self.round(3)
        self.corner(1)
        self.sides(self.r.late)

    def corner(self, which):
        line = self.r.near[which]
        self.got_sides(line)
        self.begin(4, line)

    def hand(self, which):
        line = self.r.near[which]
        self.got(4, line)
        self.begin(5, line)

    def finish(self):
        for line in self.r.far:
            self.got_sides(line)
            self.got(5, line)

    def drained(self, kind, line):
        for copy in self.copies(kind, line):
            copy.wait_send()

    def sent(self):
        r = self.r
        for line in range(LINE):

            @pl.when((r.z < LINE - 1) & (r.z >= line))
            def _():
                self.drained(0, line)

            @pl.when((r.z > 0) & (r.z <= line))
            def _():
                self.drained(1, line)

            self.drained(2, line)
            self.drained(3, line)
        for line in r.near:
            self.drained(4, line)
            self.drained(5, line)


class Scatter:
    def __init__(self, route, arrays, rooms, send, recv):
        self.r, self.arrays, self.rooms = route, arrays, rooms
        self.send, self.recv = send, recv

    def across(self, i):
        return self.r.plane_y if i == 0 else self.r.plane_x

    def copy(self, i, kind, line):
        r = self.r
        near, across = (r.at_x, r.at_y) if i == 0 else (r.at_y, r.at_x)
        near_plane = r.plane_x if i == 0 else r.plane_y
        plane, room, device = (
            (3 - r.plane, line // 2, r.at_line(r.pair)),
            (near_plane, line, near),
            (3 - r.plane, line // 2, near),
            (self.across(i), line, across),
            (r.plane, r.z, r.at_line(line)),
        )[kind]
        return remote(
            self.arrays[i].at[line, plane],
            self.rooms[i][kind].at[room],
            self.send.at[i, kind, line],
            self.recv.at[i, kind, r.z if kind == 4 else line],
            device,
        )

    def got_along(self, i, line):
        r = self.r
        remote(
            self.arrays[i].at[line, r.plane],
            self.rooms[i][4].at[line],
            self.send.at[i, 4, line],
            self.recv.at[i, 4, line],
            r.at_line(line),
        ).wait_recv()

    def begin_far(self, i, line):
        for kind in (0, 1, 3):
            self.copy(i, kind, line).start()

    def begin_near(self, i, line):
        self.copy(i, 1, line).start()

    def begin(self, i):
        for line in self.r.far:
            self.begin_far(i, line)
        for line in self.r.near[::-1]:
            self.begin_near(i, line)

    def merge(self, i, line, plane, *came):
        at = self.arrays[i].at[line, plane]
        value = at[...].astype(F32)
        for kind, room in came:
            value = value + self.rooms[i][kind][room].astype(F32)
        at[...] = low(value)

    def corners(self, i):
        for line in self.r.near[::-1]:
            self.copy(i, 0, line).wait_recv()
            self.merge(i, line, 3 - self.r.plane, (0, line // 2))
            self.copy(i, 2, line).start()

    def turn(self, i):
        for line in self.r.near[::-1]:
            self.copy(i, 2, line).wait_recv()
            self.merge(i, line, self.across(i), (2, line // 2))
            self.copy(i, 3, line).start()

    def along(self, i, line):
        self.copy(i, 1, line).wait_recv()
        self.copy(i, 3, line).wait_recv()
        self.merge(i, line, self.r.plane, (1, line), (3, line))
        self.copy(i, 4, line).start()

    def along_far(self, i):
        for line in self.r.far:
            self.along(i, line)

    def along_near(self, i):
        self.along(i, self.r.near[1])

    def total(self, i):
        r = self.r
        self.copy(i, 1, r.z).wait_recv()
        self.copy(i, 3, r.z).wait_recv()
        rooms = self.rooms[i]
        value = self.arrays[i][r.z, r.plane].astype(F32)
        value = value + rooms[1][r.z].astype(F32) + rooms[3][r.z].astype(F32)
        for line in r.far + r.near[1:]:
            self.got_along(i, line)
            value = value + rooms[4][line].astype(F32)
        return value

    def sent(self):
        r = self.r
        for i in (0, 1):
            for line in range(LINE):
                self.copy(i, 1, line).wait_send()
                self.copy(i, 3, line).wait_send()
            for line in r.far:
                self.copy(i, 0, line).wait_send()
                self.copy(i, 4, line).wait_send()
            for line in r.near:
                self.copy(i, 2, line).wait_send()
            self.copy(i, 4, r.near[1]).wait_send()


def loop(count, body):
    def step(index, carry):
        body(index)
        return carry

    lax.fori_loop(0, count, step, 0)


def aligned(index, size):
    return pl.ds(pl.multiple_of(index * size, size), size)


def erf_parts(value):
    tail = lax.erf(value * np.float32(0.5**0.5))
    half = 0.5 * (1.0 + tail)
    density = jnp.exp(value * value * -0.5) * np.float32((2.0 * np.pi) ** -0.5)
    return value * half, half + value * density


def norm(values, gain, shift):
    average = jnp.mean(values, axis=-1, keepdims=True)
    centred = values - average
    variance = jnp.mean(centred * centred, axis=-1, keepdims=True)
    inverse = lax.rsqrt(variance + EPSILON)
    normed = centred * inverse
    return normed * gain + shift, normed, inverse


def norm_pull(upstream, normed, inverse, gain):
    scaled_up = upstream * gain
    first_mean = jnp.mean(scaled_up, axis=-1, keepdims=True)
    second_mean = jnp.mean(scaled_up * normed, axis=-1, keepdims=True)
    return inverse * (scaled_up - first_mean - normed * second_mean)


def layer_kernel(names, *refs):
    b = dict(zip(names, refs))
    at = type("Refs", (), b)
    r = Route()
    core, other = r.core, r.other
    own_rows = aligned(core, 256)
    other_rows = aligned(other, 256)
    score_scale = np.float32((3.0 * HEAD) ** (-0.5))

    barrier = pltpu.get_barrier_semaphore()
    friends = [r.partner, r.at_x, r.at_y] + [r.at_line(r.ahead(k)) for k in range(1, LINE)]
    for device in friends:
        pl.semaphore_signal(barrier, inc=1, device_id=device, device_id_type=MESH)

    def give_rows(kind, index, array):
        piece = pl.ds(pl.multiple_of(core * 256 + index * 64, 64), 64)
        return remote(
            array.at[piece],
            array.at[piece],
            at.row_send.at[kind, index],
            at.row_recv.at[kind, index],
            r.partner,
        )

    def got_rows(kind, array):
        for index in range(4):
            give_rows(kind, index, array).wait_recv()

    waiting = []

    def swap(slot, source, target):
        copy = remote(source, target, at.swap_send.at[slot], at.swap_recv.at[slot], r.partner)
        copy.start()
        waiting.append(copy)
        return copy

    gather_one = Gather(r, (at.gat_a, at.gat_b, at.gat_s), at.ga_send, at.ga_recv)
    gather_two = Gather(r, (at.gat_1, at.gat_2), at.gf_send, at.gf_recv)

    at.sums[...] = jnp.zeros_like(at.sums)
    at.small_wide[...] = jnp.zeros_like(at.small_wide)
    small_rows = (
        at.query_b, at.value_b, at.output_b, at.gain_1, at.shift_1, at.outer_b, at.gain_2, at.shift_2,
        at.inner_b,
    )
    for index, row in enumerate(small_rows):
        at.small_wide[index : index + 1, 0 : row.shape[1]] = row[...].astype(F32)
    at.small[...] = low(at.small_wide[...])
    right = (at.predicted[...] == at.labels[...]).astype(F32)
    at.sums[10:11, :] = jnp.broadcast_to(jnp.sum(right, axis=1, keepdims=True), (1, 768))
    pl.semaphore_wait(barrier, len(friends))

    half = aligned(other, 384)
    arrive = [
        swap(0, at.key_w.at[:, half], at.come_a.at[:, pl.ds(0, 384)]),
        swap(1, at.value_w.at[:, half], at.come_a.at[:, pl.ds(384, 384)]),
        swap(2, at.query_w.at[:, half], at.come_b.at[:, pl.ds(0, 384)]),
        swap(3, at.output_w.at[:, half], at.come_b.at[:, pl.ds(384, 384)]),
        swap(4, at.table_t.at[:, aligned(other, 256)], at.come_b.at[:, pl.ds(768, 256)]),
        swap(5, at.small, at.come_s),
    ]
    come_x = swap(7, at.hidden, at.x_all.at[own_rows])
    place_x = pltpu.make_async_copy(at.hidden, at.x_all.at[own_rows], at.here.at[0])
    place_x.start()
    place_2 = pltpu.make_async_copy(at.outer_w, at.gat_2.at[r.z, r.plane], at.here.at[1])
    place_2.start()
    for copy in arrive:
        copy.wait_recv()

    def stack(mine, came):
        mine, came = mine.astype(F32), came.astype(F32)
        upper = jnp.where(core == 0, mine, came)
        lower = jnp.where(core == 0, came, mine)
        return low(jnp.concatenate([upper, lower], axis=0))

    mine_half = aligned(core, 384)
    at.gat_a[r.z, r.plane, :, 0:384] = stack(at.key_w[:, mine_half], at.come_a[:, 0:384])
    at.gat_a[r.z, r.plane, :, 384:768] = stack(at.value_w[:, mine_half], at.come_a[:, 384:768])
    at.gat_b[r.z, r.plane, :, 0:384] = stack(at.query_w[:, mine_half], at.come_b[:, 0:384])
    at.gat_b[r.z, r.plane, :, 384:768] = stack(at.output_w[:, mine_half], at.come_b[:, 384:768])
    at.gat_b[r.z, r.plane, :, 768:1024] = stack(
        at.table_t[:, aligned(core, 256)], at.come_b[:, 768:1024]
    )
    at.gat_s[r.z, r.plane, core] = at.small[...]
    at.gat_s[r.z, r.plane, other] = at.come_s[...]
    gather_one.start_line()
    gather_one.start_sides()
    for chip in range(4 * LINE):
        for which in range(2):
            device = 2 * chip + which
            at.inner_pair[which, :, 96 * chip : 96 * chip + 96] = at.inner_w[
                :, 96 * device : 96 * device + 96
            ]
    come_inner = swap(6, at.inner_pair.at[other], at.come_1)
    come_inner.wait_recv()
    at.gat_1[r.z, r.plane] = stack(at.inner_pair[core], at.come_1[...])
    place_2.wait()
    place_x.wait()
    come_x.wait_recv()
    at.x_turned[...] = at.x_all[...].T
    wide_i = lax.broadcasted_iota(jnp.int32, (512, 512), 0)
    wide_j = lax.broadcasted_iota(jnp.int32, (512, 512), 1)
    at.one_natural[...] = low((at.buckets[0:1, 256:768] == wide_i).astype(F32))
    at.one_hot[...] = low(dot(at.one_natural[...], low((wide_i + wide_j == 511).astype(F32))))
    segment_wide = jnp.broadcast_to(at.segments[...].astype(F32), (128, 512))
    at.segment_row[...] = segment_wide[0:8]
    at.segment_col[...] = segment_wide.T
    flip_i = lax.broadcasted_iota(jnp.int32, (128, 128), 0)
    flip_j = lax.broadcasted_iota(jnp.int32, (128, 128), 1)
    at.flip[...] = low((flip_i + flip_j == 127).astype(F32))
    for table in (at.near_rows, at.far_rows, at.far_natural):
        table[0:256, :] = jnp.zeros((256, 384), BF16)
        table[768:1024, :] = jnp.zeros((256, 384), BF16)
    gather_one.first()
    gather_one.second()
    gather_one.third()
    gather_two.start_sides()
    gather_one.hand(1)
    gather_two.start_line()
    gather_one.finish()

    out_mine = at.gat_b.at[:, :, :, pl.ds(384, 384)]
    table_mine = at.gat_b.at[:, :, :, pl.ds(768, 256)]
    come_table = swap(8, table_mine, at.table_all.at[core])
    come_out = swap(9, out_mine, at.out_all.at[core])
    place_table = pltpu.make_async_copy(table_mine, at.table_all.at[core], at.here.at[0])
    place_table.start()
    place_out = pltpu.make_async_copy(out_mine, at.out_all.at[core], at.here.at[1])
    place_out.start()

    for line in range(LINE):
        for plane in range(4):
            chip = line * 4 + plane
            for which in range(2):
                device = 2 * chip + which
                tile = at.gat_s[line, plane, which].astype(F32)
                at.vectors[:, 24 * device : 24 * device + 24] = tile[0:8, 0:24]
            tile = at.gat_s[line, plane, core].astype(F32)
            at.inner_bias[0:1, 96 * chip : 96 * chip + 96] = tile[8:9, 0:96]

    def rows(value):
        return value.reshape(768, value.shape[-1])

    vector_half = aligned(core, 384)
    query_bias = at.vectors[0:1, vector_half]
    value_bias = at.vectors[1:2, vector_half]
    at.kvq[:, 0:384] = low(dot(at.x_all[...], rows(at.gat_a[:, :, :, 0:384])))
    at.kvq[:, 384:768] = low(dot(at.x_all[...], rows(at.gat_a[:, :, :, 384:768])) + value_bias)
    at.kvq[:, 768:1152] = low(dot(at.x_all[...], rows(at.gat_b[:, :, :, 0:384])) + query_bias)
    gather_two.first()
    place_table.wait()
    come_table.wait_recv()
    for part in range(2):
        piece = pl.ds(256 * part, 256)
        table = rows(at.table_all[part])
        at.key_rel[piece, :] = low(dot(table, rows(at.gat_a[:, :, :, 0:384]), 0, 0))
        at.query_rel[piece, :] = low(dot(table, rows(at.gat_b[:, :, :, 0:384]), 0, 0) + query_bias)
    at.near_rows[256:768, :] = low(dot(at.one_hot[...], at.key_rel[...], 0, 0))
    at.far_rows[256:768, :] = low(dot(at.one_hot[...], at.query_rel[...], 0, 0))
    at.far_natural[256:768, :] = low(dot(at.one_natural[...], at.query_rel[...], 0, 0))

    lanes = lax.broadcasted_iota(jnp.int32, (1, 128), 1) // HEAD
    no_score = np.float32(NEGATIVE)

    def forward_head(head):
        pair = aligned(head // 2, 128)
        key_lanes = pl.ds(pl.multiple_of((head // 2) * 128, 128), 128)
        value_lanes = pl.ds(pl.multiple_of(384 + (head // 2) * 128, 128), 128)
        query_lanes = pl.ds(pl.multiple_of(768 + (head // 2) * 128, 128), 128)
        mine = lanes == head % 2
        only = low(mine.astype(F32))
        keys = at.kvq[:, key_lanes]
        values = at.kvq[:, value_lanes]
        for block in range(4):
            piece = pl.ds(128 * block, 128)
            shifted = dot(
                at.kvq[piece, key_lanes] * only, at.far_rows[pl.ds(384 - 128 * block, 640), pair], 1, 1
            )
            at.far_scores[piece, :] = pltpu.roll(shifted, 0, 1, stride=1, stride_axis=0)[:, 128:640]
        for block in range(4):
            piece = pl.ds(128 * block, 128)
            queries = at.kvq[piece, query_lanes] * only
            shifted = dot(queries, at.near_rows[pl.ds(384 - 128 * block, 640), pair], 1, 1)
            summed = (
                dot(queries, keys, 1, 1)
                + pltpu.roll(shifted, 0, 1, stride=1, stride_axis=0)[:, 128:640]
                + at.far_scores[:, piece].T
            )
            masked = jnp.where(
                at.segment_col[piece, 0:1] == at.segment_row[0:1, :], summed * score_scale, no_score
            )
            highest = jnp.max(masked, axis=-1, keepdims=True)
            expsum = jnp.exp(masked - highest)
            soft = expsum / jnp.sum(expsum, axis=-1, keepdims=True)
            rounded = low(soft)
            at.soft[head, piece, :] = low(dot(at.flip[...], rounded))
            context = dot(rounded, values)
            here = at.context.at[core, piece, pair]
            here[...] = low(jnp.where(mine, context, here[...].astype(F32)))

    def forward_pair(index):
        def forward(which):
            head = 2 * index + which
            forward_head(head)
            pl.when(head == 1)(gather_two.second)
            pl.when(head == 5)(gather_two.third)

        loop(2, forward)
        remote(
            at.context.at[core, :, aligned(index, 128)],
            at.context.at[core, :, aligned(index, 128)],
            at.context_send.at[index],
            at.context_recv.at[index],
            r.partner,
        ).start()

    loop(3, forward_pair)
    place_out.wait()
    come_out.wait_recv()
    for index in range(3):
        remote(
            at.context.at[other, :, pl.ds(128 * index, 128)],
            at.context.at[other, :, pl.ds(128 * index, 128)],
            at.context_send.at[index],
            at.context_recv.at[index],
            r.partner,
        ).wait_recv()

    def vector(index):
        return at.vectors[index : index + 1, :]

    for part in range(2):
        piece = pl.ds(384 * part, 384)
        weight = rows(at.out_all[part])
        at.wide[:, piece] = dot(at.context[0, own_rows, :], weight[0:384]) + dot(
            at.context[1, own_rows, :], weight[384:768]
        )

    def first_norm(index):
        piece = aligned(index, 64)
        token_rows = pl.ds(pl.multiple_of(core * 256 + index * 64, 64), 64)
        residual = at.x_all[token_rows, :].astype(F32) + at.wide[piece, :] + vector(2)
        out, normed, inverse = norm(residual, vector(3), vector(4))
        at.first_out[piece, :] = out
        at.first_normed[piece, :] = normed
        at.first_inverse[piece, :] = jnp.broadcast_to(inverse, (64, 128))
        at.first_low[token_rows, :] = low(out)
        give_rows(0, index, at.first_low).start()

    loop(4, first_norm)
    got_rows(0, at.first_low)
    at.first_turned[...] = at.first_low[...].T
    gather_two.hand(1)
    gather_two.finish()

    def inner_units(index):
        piece = aligned(index, 256)
        pre = dot(at.first_low[...], rows(at.gat_1[:, :, :, piece])) + at.inner_bias[0:1, piece]
        value, slope = erf_parts(pre)
        at.active[:, piece] = low(value)
        at.slope[:, piece] = slope

    loop(6, inner_units)

    def outer_part(rows_at, part):
        return dot(
            at.active[rows_at, :], at.gat_2[:, :, :, 256 * part : 256 * part + 256].reshape(1536, 256)
        )

    come_outer = []
    for part in range(3):
        piece = pl.ds(256 * part, 256)
        at.part_send[:, piece] = low(outer_part(other_rows, part))
        come_outer.append(swap((11, 23, 24)[part], at.part_send.at[:, piece], at.part_recv.at[:, piece]))
    for part in range(3):
        at.wide[:, 256 * part : 256 * part + 256] = outer_part(own_rows, part)
    for copy in come_outer:
        copy.wait_recv()

    def second_norm(index):
        piece = aligned(index, 64)
        token_rows = pl.ds(pl.multiple_of(core * 256 + index * 64, 64), 64)
        total = at.first_out[piece, :] + at.wide[piece, :] + at.part_recv[piece, :].astype(F32) + vector(5)
        out, normed, inverse = norm(total, vector(6), vector(7))
        at.result[piece, :] = low(out)
        upstream = at.cotangent[piece, :].astype(F32)
        grad = norm_pull(upstream, normed, inverse, vector(6))
        at.grad_sum[piece, :] = grad
        rounded = low(grad)
        at.grad_outer[token_rows, :] = rounded
        give_rows(1, index, at.grad_outer).start()
        at.sums[5:6, :] += jnp.sum(rounded.astype(F32), axis=0, keepdims=True)
        at.sums[6:7, :] += jnp.sum(upstream * normed, axis=0, keepdims=True)
        at.sums[7:8, :] += jnp.sum(upstream, axis=0, keepdims=True)

    loop(4, second_norm)

    def scatter(arrays, tags, send, recv):
        rooms = [[b[kind + tag] for kind in ROOMS] for tag in tags]
        return Scatter(r, arrays, rooms, send, recv)

    scatter_two = scatter((at.grad_1, at.grad_2), ("1", "2"), at.sf_send, at.sf_recv)
    scatter_a = scatter((at.grad_o, at.grad_p.at[0]), ("o", "p0"), at.sa_send, at.sa_recv)
    scatter_b = scatter((at.grad_p.at[1], at.grad_p.at[2]), ("p1", "p2"), at.sb_send, at.sb_recv)
    scatter_c = scatter((at.grad_t.at[0], at.grad_t.at[1]), ("t0", "t1"), at.sc_send, at.sc_recv)

    def inner_grad(rows_at):
        for part in range(4):
            units = pl.ds(384 * part, 384)
            grad = low(dot(at.grad_outer[rows_at, :], at.gat_2[part].reshape(384, 768), 1, 1))
            pre = low(grad.astype(F32) * at.slope[rows_at, units])
            at.grad_pre[rows_at, units] = pre
            at.bias_inner[0:1, units] += jnp.sum(pre.astype(F32), axis=0, keepdims=True)

    at.bias_inner[...] = jnp.zeros_like(at.bias_inner)
    inner_grad(own_rows)
    got_rows(1, at.grad_outer)

    def line_of(index):
        half = index // 2
        start = r.pair * (1 - half) + r.z * half
        return (start + 2 * ((index + 1) // 2 % 2)) % LINE

    def send_lines(i, index, line):
        pl.when(index < 2)(lambda: scatter_two.begin_far(i, line))
        pl.when(index >= 2)(lambda: scatter_two.begin_near(i, line))

    def outer_weight(index):
        line = line_of(index)
        grad = dot(at.active[:, aligned(line, 384)], at.grad_outer[...], 0, 0)
        at.grad_2[line] = low(grad).reshape(4, 96, 768)
        send_lines(1, index, line)

    loop(4, outer_weight)

    inner_grad(other_rows)
    at.sums[8:9, :] = at.bias_inner[0:1, 0:768]
    at.sums[9:10, :] = at.bias_inner[0:1, 768:1536]

    def first_part(rows_at, part):
        weight = at.gat_1[2 * part : 2 * part + 2].reshape(384, 1536)
        return dot(at.grad_pre[rows_at, :], weight, 1, 1)

    come_grad_first = []
    for part in range(2):
        piece = pl.ds(384 * part, 384)
        at.part_send2[:, piece] = low(first_part(other_rows, part))
        come_grad_first.append(
            swap((13, 25)[part], at.part_send2.at[:, piece], at.part_recv2.at[:, piece])
        )
    def inner_weight(index):
        line = line_of(index)
        grad = dot(at.first_turned[aligned(line, 192), :], at.grad_pre[...])
        at.grad_1[line] = low(grad).reshape(4, 48, 1536)
        send_lines(0, index, line)

    loop(4, inner_weight)
    for part in range(2):
        at.wide[:, 384 * part : 384 * part + 384] = first_part(own_rows, part)
    for copy in come_grad_first:
        copy.wait_recv()

    def first_norm_back(index):
        piece = aligned(index, 64)
        token_rows = pl.ds(pl.multiple_of(core * 256 + index * 64, 64), 64)
        upstream = at.wide[piece, :] + at.part_recv2[piece, :].astype(F32) + at.grad_sum[piece, :]
        normed = at.first_normed[piece, :]
        grad = norm_pull(upstream, normed, at.first_inverse[piece, 0:1], vector(3))
        at.grad_sum[piece, :] = grad
        rounded = low(grad)
        at.grad_att[token_rows, :] = rounded
        give_rows(2, index, at.grad_att).start()
        at.sums[2:3, :] += jnp.sum(rounded.astype(F32), axis=0, keepdims=True)
        at.sums[3:4, :] += jnp.sum(upstream * normed, axis=0, keepdims=True)
        at.sums[4:5, :] += jnp.sum(upstream, axis=0, keepdims=True)

    loop(4, first_norm_back)
    out_rows = pl.ds(pl.multiple_of(2 * core, 2), 2)

    def context_rows(rows_at):
        weight_0 = at.out_all[0, out_rows].reshape(384, 384)
        weight_1 = at.out_all[1, out_rows].reshape(384, 384)
        at.grad_context[rows_at, :] = low(
            dot(at.grad_att[rows_at, 0:384], weight_0, 1, 1)
            + dot(at.grad_att[rows_at, 384:768], weight_1, 1, 1)
        )

    context_rows(own_rows)
    got_rows(2, at.grad_att)
    context_rows(other_rows)
    scatter_two.corners(1)
    scatter_two.along_far(1)
    for part in range(2):
        grad = dot(at.context[part], at.grad_att[:, aligned(core, 384)], 0, 0)
        at.grad_o[2 * part : 2 * part + 2] = low(grad).reshape(2, 4, 48, 384)

    at.near_grad[...] = jnp.zeros_like(at.near_grad)
    at.far_grad[...] = jnp.zeros_like(at.far_grad)
    room = jnp.zeros((128, 128), BF16)

    def spread(value, start):
        wide = jnp.concatenate([value, room], axis=1)
        return pltpu.roll(wide, start, 1, stride=1, stride_axis=0)

    heads = [low((lanes == which).astype(F32)) for which in range(2)]

    def lanes_of(index, place):
        return pl.ds(pl.multiple_of(384 * place + index * 128, 128), 128)

    def masked(value):
        return [value * only for only in heads]

    def backward_queries(index):
        pair = aligned(index, 128)
        flip = at.flip[...]
        keys = masked(at.kvq[:, lanes_of(index, 0)])
        values = at.kvq[:, lanes_of(index, 1)]
        for block in range(4):
            piece = pl.ds(128 * block, 128)
            window = pl.ds(384 - 128 * block, 640)
            back = pl.ds(384 - 128 * block, 128)
            grad_context = low(dot(flip, at.grad_context[piece, pair]))
            query = low(dot(flip, at.kvq[piece, lanes_of(index, 2)]))
            at.turned_grad[piece, :] = grad_context
            at.turned_query[back, :] = query
            table = masked(at.near_rows[window, pair])
            near, grad = [], 0.0
            for which, context_only in enumerate(masked(grad_context)):
                soft = at.soft[2 * index + which, piece, :].astype(F32)
                grad_soft = dot(context_only, values, 1, 1)
                inner = jnp.sum(soft * grad_soft, axis=-1, keepdims=True)
                grad_low = low(soft * (grad_soft - inner) * score_scale)
                at.grad_low[which, back, :] = grad_low
                near.append(spread(grad_low, 1))
                grad = grad + dot(grad_low, keys[which]) + dot(near[which], table[which])
            at.grad_kvq[piece, lanes_of(index, 2)] = low(dot(flip, low(grad)))
            at.near_grad[window, pair] += dot(
                jnp.concatenate(near, axis=0), jnp.concatenate(masked(query), axis=0), 0, 0
            )

    def backward_keys(index):
        pair = aligned(index, 128)
        queries = masked(at.turned_query[...])
        contexts = masked(at.turned_grad[...])
        for block in range(4):
            piece = pl.ds(128 * block, 128)
            window = pl.ds(128 * block, 640)
            table = masked(at.far_natural[window, pair])
            far, grad, grad_value = [], 0.0, 0.0
            for which in range(2):
                turned = at.grad_low[which, :, piece].T
                far.append(spread(turned, 0))
                grad = grad + dot(turned, queries[which]) + dot(far[which], table[which])
                weights = at.soft[2 * index + which, :, piece]
                grad_value = grad_value + dot(weights, contexts[which], 0, 0)
            at.grad_kvq[piece, lanes_of(index, 0)] = low(grad)
            at.grad_kvq[piece, lanes_of(index, 1)] = low(grad_value)
            keys = masked(at.kvq[piece, lanes_of(index, 0)])
            at.far_grad[window, pair] += dot(
                jnp.concatenate(far, axis=0), jnp.concatenate(keys, axis=0), 0, 0
            )

    def shape_weight(value):
        return low(value).reshape(LINE, 4, 48, value.shape[-1])

    def rel_pair(index):
        pair = aligned(index, 128)
        at.key_rel[:, pair] = low(dot(at.one_hot[...], low(at.near_grad[256:768, pair])))
        at.query_rel[:, pair] = low(dot(at.one_natural[...], low(at.far_grad[256:768, pair])))

    def weights_pair(index):
        pair = aligned(index, 128)
        tokens = jnp.concatenate(
            [at.grad_kvq[:, lanes_of(index, place)] for place in (0, 2, 1)], axis=1
        )
        grad = dot(at.x_turned[...], tokens)
        rel = jnp.concatenate([at.key_rel[:, pair], at.query_rel[:, pair]], axis=1)
        table = dot(rows(at.table_all[0]), rel[0:256]) + dot(rows(at.table_all[1]), rel[256:512])
        at.grad_p[index, :, :, :, 0:256] = shape_weight(grad[:, 0:256] + table)
        at.grad_p[index, :, :, :, 256:384] = shape_weight(grad[:, 256:384])

    def table_half(which):
        piece = aligned(which, 256)
        return dot(rows(at.gat_b[:, :, :, 0:384]), at.query_rel[piece, :], 1, 1) + dot(
            rows(at.gat_a[:, :, :, 0:384]), at.key_rel[piece, :], 1, 1
        )

    def at_step(step, when, *moves):
        @pl.when(step == when)
        def _():
            for move in moves:
                move()

    def swap_table():
        return remote(
            at.table_send, at.table_recv, at.swap_send.at[15], at.swap_recv.at[15], r.partner
        )

    def send_table():
        at.table_send[...] = shape_weight(table_half(other))
        swap_table().start()

    def backward_pair(index):
        backward_queries(index)
        at_step(index, 2, lambda: scatter_two.turn(0), lambda: scatter_two.turn(1))
        backward_keys(index)
        at_step(index, 0, lambda: scatter_two.corners(0))
        at_step(index, 1, lambda: scatter_a.corners(0), lambda: scatter_two.along_far(0))
        at_step(index, 2, lambda: scatter_a.along_far(0))
        rel_pair(index)
        at_step(index, 2, send_table)
        weights_pair(index)
        at_step(index, 0, lambda: scatter_a.begin(0), lambda: scatter_a.begin(1))
        at_step(index, 1, lambda: scatter_b.begin(0), lambda: scatter_a.corners(1))
        at_step(index, 2, lambda: scatter_b.begin(1))

    loop(3, backward_pair)
    scatter_b.corners(0)
    scatter_a.along_far(1)

    own_table = table_half(core)
    come_part = swap_table()
    waiting.append(come_part)
    come_part.wait_recv()
    own_table = own_table + rows(at.table_recv[...]).astype(F32)
    for part in range(2):
        at.grad_t[part] = shape_weight(own_table[:, 128 * part : 128 * part + 128])
        scatter_c.begin(part)
    scatter_a.turn(0)

    at.sums[0:1, vector_half] = jnp.sum(
        at.grad_kvq[:, 768:1152].astype(F32), axis=0, keepdims=True
    ) + jnp.sum(at.far_grad[256:768, :], axis=0, keepdims=True)
    at.sums[1:2, vector_half] = jnp.sum(
        at.grad_kvq[:, 384:768].astype(F32), axis=0, keepdims=True
    )

    def exchange(stage, source, device):
        return remote(
            source, at.sums_come.at[stage], at.sums_send.at[stage], at.sums_recv.at[stage], device
        )

    stage_copies = [exchange(0, at.sums, r.partner)]
    stage_copies[0].start()

    def input_part(rows_at, part):
        weight_a = at.gat_a[2 * part : 2 * part + 2].reshape(384, 768)
        weight_b = at.gat_b[2 * part : 2 * part + 2, :, :, 0:384].reshape(384, 384)
        return dot(at.grad_kvq[rows_at, 0:768], weight_a, 1, 1) + dot(
            at.grad_kvq[rows_at, 768:1152], weight_b, 1, 1
        )

    for copy in come_outer:
        copy.wait_send()
    come_input = []
    for part in range(2):
        piece = pl.ds(384 * part, 384)
        at.part_send[:, piece] = low(input_part(other_rows, part))
        come_input.append(swap((16, 26)[part], at.part_send.at[:, piece], at.part_recv.at[:, piece]))

    stage_copies[0].wait_recv()
    lines = lax.broadcasted_iota(jnp.int32, (16, 1), 0)
    shared = jnp.where((lines == 8) | (lines == 9), 0.0, at.sums_come[0])
    at.sums_step[0] = at.sums[...] + shared
    stage_copies.append(exchange(1, at.sums_step.at[0], r.at_x))
    stage_copies[1].start()
    scatter_b.corners(1)
    scatter_a.turn(1)
    scatter_b.along_far(0)
    for part in range(2):
        at.wide[:, 384 * part : 384 * part + 384] = input_part(own_rows, part)
    for copy in come_input:
        copy.wait_recv()
    at.input_grad[...] = low(at.grad_sum[...] + at.wide[...] + at.part_recv[...].astype(F32))
    for part in range(2):
        scatter_c.corners(part)
    for part in range(2):
        scatter_two.along_near(part)
    stage_copies[1].wait_recv()
    at.sums_step[1] = at.sums_step[0] + at.sums_come[1]
    stage_copies.append(exchange(2, at.sums_step.at[1], r.at_y))
    stage_copies[2].start()
    at.give_1[...] = scatter_two.total(0).reshape(2, 24, 1536)
    swap(17, at.give_1.at[other], at.d_inner.at[core])
    at.d_inner[core] = at.give_1[core]
    scatter_b.along_far(1)
    at.d_outer[...] = scatter_two.total(1)
    scatter_b.turn(0)
    scatter_c.along_far(0)
    scatter_a.along_near(0)
    scatter_c.along_far(1)
    scatter_a.along_near(1)
    stage_copies[2].wait_recv()
    at.sums_step[2] = at.sums_step[1] + at.sums_come[2]
    for step in range(1, LINE):
        copy = exchange(2 + step, at.sums_step.at[2], r.at_line(r.ahead(step)))
        copy.start()
        stage_copies.append(copy)

    def give(slot, source, start, width, out):
        swap(slot, source.at[other, :, pl.ds(start, width)], out.at[:, aligned(core, width)])
        out[:, aligned(core, width)] = source[core, :, start : start + width]

    def give_pair(index, total):
        for place in range(3):
            start = 384 * place + 128 * index
            at.give_p[:, :, start : start + 128] = total[:, 128 * place : 128 * place + 128].reshape(
                2, 24, 128
            )

    at.give_o[...] = scatter_a.total(0).reshape(2, 24, 384)
    give(21, at.give_o, 0, 384, at.d_output)
    scatter_b.turn(1)
    for part in range(2):
        scatter_c.turn(part)
    give_pair(0, scatter_a.total(1))
    for user in (scatter_b, scatter_c):
        for part in range(2):
            user.along_near(part)
    give_pair(1, scatter_b.total(0))
    give_pair(2, scatter_b.total(1))
    give(18, at.give_p, 0, 384, at.d_key)
    give(19, at.give_p, 384, 384, at.d_query)
    give(20, at.give_p, 768, 384, at.d_value)
    for part in range(2):
        at.give_t[:, :, 128 * part : 128 * part + 128] = scatter_c.total(part).reshape(2, 24, 128)
    give(22, at.give_t, 0, 256, at.d_table)
    for copy in stage_copies[3:]:
        copy.wait_recv()
    at.vector_grads[...] = (
        at.sums_step[2] + at.sums_come[3] + at.sums_come[4] + at.sums_come[5]
    )
    for copy in waiting[-6:]:
        copy.wait_recv()
    for copy in waiting:
        if all(copy is not early for early in come_outer):
            copy.wait_send()
    for copy in stage_copies:
        copy.wait_send()
    for kind, array in enumerate((at.first_low, at.grad_outer, at.grad_att)):
        for index in range(4):
            give_rows(kind, index, array).wait_send()
    for index in range(3):
        remote(
            at.context.at[core, :, pl.ds(128 * index, 128)],
            at.context.at[core, :, pl.ds(128 * index, 128)],
            at.context_send.at[index],
            at.context_recv.at[index],
            r.partner,
        ).wait_send()
    for user in (gather_one, gather_two, scatter_two, scatter_a, scatter_b, scatter_c):
        user.sent()


def finish_kernel(names, *refs):
    at = type("Refs", (), dict(zip(names, refs)))
    chip, core = lax.axis_index("fsdp"), lax.axis_index("seq")
    at.result_out[...] = at.result[...]
    at.input_grad_out[...] = at.input_grad[...]
    at.query_w_out[...] = at.d_query[...]
    at.key_w_out[...] = at.d_key[...]
    at.value_w_out[...] = at.d_value[...]
    at.output_w_out[...] = at.d_output[...]
    at.table_out[...] = at.d_table[...]
    at.outer_w_out[...] = at.d_outer[...]
    for group in range(4 * LINE):
        for which in range(2):
            device = 2 * group + which
            at.inner_w_out[:, 96 * device : 96 * device + 96] = at.d_inner[
                which, :, 96 * group : 96 * group + 96
            ]
    sums = at.vector_grads[...]
    own = pltpu.roll(sums, (768 - 24 * (2 * chip + core)) % 768, 1)
    small_outs = (
        at.query_b_out, at.value_b_out, at.output_b_out, at.gain_1_out, at.shift_1_out,
        at.outer_b_out, at.gain_2_out, at.shift_2_out,
    )
    for index, out in enumerate(small_outs):
        out[...] = own[index : index + 1, 0:24]
    units = jnp.where(chip < 2 * LINE, sums[8:9], sums[9:10])
    units = jnp.broadcast_to(units, (8, 768))
    at.inner_b_out[...] = pltpu.roll(units, (768 - 96 * (chip % (2 * LINE))) % 768, 1)[0:1, 0:96]
    at.count_out[...] = sums[10:11, 0:1].astype(jnp.int32)


OUTPUTS = dict(
    result=((256, 768), BF16),
    input_grad=((256, 768), BF16),
    d_query=((24, 768), F32),
    d_key=((24, 768), F32),
    d_value=((24, 768), F32),
    d_output=((24, 768), F32),
    d_table=((24, 512), F32),
    d_inner=((2, 24, 1536), F32),
    d_outer=((96, 768), F32),
    vector_grads=((16, 768), F32),
)
FINALS = dict(
    result_out=((256, 768), BF16),
    input_grad_out=((256, 768), BF16),
    query_w_out=((24, 768), F32),
    key_w_out=((24, 768), F32),
    value_w_out=((24, 768), F32),
    output_w_out=((24, 768), F32),
    table_out=((24, 512), F32),
    inner_w_out=((24, 3072), F32),
    outer_w_out=((96, 768), F32),
    query_b_out=((1, 24), F32),
    value_b_out=((1, 24), F32),
    output_b_out=((1, 24), F32),
    gain_1_out=((1, 24), F32),
    shift_1_out=((1, 24), F32),
    outer_b_out=((1, 24), F32),
    gain_2_out=((1, 24), F32),
    shift_2_out=((1, 24), F32),
    inner_b_out=((1, 96), F32),
    count_out=((1, 1), jnp.int32),
)
LINE = 4
BLOCKS = (LINE, 4, 48)
SCRATCH = dict(
    small_wide=((16, 128), F32),
    small=((16, 128), BF16),
    inner_pair=((2, 24, 1536), BF16),
    segment_row=((8, 512), F32),
    segment_col=((512, 128), F32),
    come_a=((24, 768), BF16),
    come_b=((24, 1024), BF16),
    come_s=((16, 128), BF16),
    come_1=((24, 1536), BF16),
    gat_a=(BLOCKS + (768,), BF16),
    gat_b=(BLOCKS + (1024,), BF16),
    gat_s=((LINE, 4, 2, 16, 128), BF16),
    gat_1=(BLOCKS + (1536,), BF16),
    gat_2=((LINE, 4, 96, 768), BF16),
    x_all=((512, 768), BF16),
    x_turned=((768, 512), BF16),
    one_hot=((512, 512), BF16),
    flip=((128, 128), BF16),
    near_rows=((1024, 384), BF16),
    far_rows=((1024, 384), BF16),
    far_natural=((1024, 384), BF16),
    one_natural=((512, 512), BF16),
    near_grad=((1024, 384), F32),
    far_grad=((1024, 384), F32),
    key_rel=((512, 384), BF16),
    query_rel=((512, 384), BF16),
    table_all=((2,) + BLOCKS + (256,), BF16),
    out_all=((2,) + BLOCKS + (384,), BF16),
    vectors=((8, 768), F32),
    inner_bias=((8, 1536), F32),
    bias_inner=((8, 1536), F32),
    kvq=((512, 1152), BF16),
    grad_kvq=((512, 1152), BF16),
    far_scores=((512, 512), F32),
    grad_low=((2, 512, 512), BF16),
    turned_query=((512, 128), BF16),
    turned_grad=((512, 128), BF16),
    soft=((6, 512, 512), BF16),
    context=((2, 512, 384), BF16),
    grad_context=((512, 384), BF16),
    wide=((256, 768), F32),
    first_out=((256, 768), F32),
    first_normed=((256, 768), F32),
    first_inverse=((256, 128), F32),
    first_low=((512, 768), BF16),
    first_turned=((768, 512), BF16),
    active=((512, 1536), BF16),
    slope=((512, 1536), F32),
    grad_pre=((512, 1536), BF16),
    part_send=((256, 768), BF16),
    part_recv=((256, 768), BF16),
    part_send2=((256, 768), BF16),
    part_recv2=((256, 768), BF16),
    grad_sum=((256, 768), F32),
    grad_outer=((512, 768), BF16),
    grad_att=((512, 768), BF16),
    table_send=(BLOCKS + (256,), BF16),
    table_recv=(BLOCKS + (256,), BF16),
    sums=((16, 768), F32),
    sums_step=((3, 16, 768), F32),
    sums_come=((6, 16, 768), F32),
    grad_1=(BLOCKS + (1536,), BF16),
    grad_2=((LINE, 4, 96, 768), BF16),
    grad_o=(BLOCKS + (384,), BF16),
    grad_p=((3,) + BLOCKS + (384,), BF16),
    grad_t=((2,) + BLOCKS + (128,), BF16),
    give_1=((2, 24, 1536), F32),
    give_o=((2, 24, 384), F32),
    give_p=((2, 24, 1152), F32),
    give_t=((2, 24, 256), F32),
)
ROOMS = dict(pair_=2, first_=LINE, corner_=2, second_=LINE, line_=LINE)
BLOCK = {
    "1": (48, 1536), "2": (96, 768), "o": (48, 384), "p0": (48, 384), "p1": (48, 384),
    "p2": (48, 384), "t0": (48, 128), "t1": (48, 128),
}
for tag, block in BLOCK.items():
    for kind, count in ROOMS.items():
        SCRATCH[kind + tag] = ((count,) + block, BF16)
SEMAPHORES = dict(
    swap_send=(27,),
    swap_recv=(27,),
    row_send=(3, 4),
    row_recv=(3, 4),
    here=(2,),
    context_send=(3,),
    context_recv=(3,),
    ga_send=(3, 6, LINE),
    ga_recv=(3, 6, LINE),
    gf_send=(2, 6, LINE),
    gf_recv=(2, 6, LINE),
    sf_send=(2, 5, LINE),
    sf_recv=(2, 5, LINE),
    sa_send=(2, 5, LINE),
    sa_recv=(2, 5, LINE),
    sb_send=(2, 5, LINE),
    sb_recv=(2, 5, LINE),
    sc_send=(2, 5, LINE),
    sc_recv=(2, 5, LINE),
    sums_send=(6,),
    sums_recv=(6,),
)


def block_shards(
    hidden_in,
    query_weight,
    query_bias,
    key_weight,
    value_weight,
    value_bias,
    output_weight,
    output_bias,
    first_gain,
    first_shift,
    inner_weight,
    inner_bias,
    outer_weight,
    outer_bias,
    second_gain,
    second_shift,
    relative_table,
    segments,
    buckets,
    predicted,
    labels,
    cotangent,
):
    inputs = dict(
        hidden=hidden_in[0],
        query_w=query_weight,
        key_w=key_weight,
        value_w=value_weight,
        output_w=output_weight,
        table_t=relative_table.T,
        inner_w=inner_weight,
        outer_w=outer_weight,
        query_b=query_bias[None],
        value_b=value_bias[None],
        output_b=output_bias[None],
        gain_1=first_gain[None],
        shift_1=first_shift[None],
        outer_b=outer_bias[None],
        gain_2=second_gain[None],
        shift_2=second_shift[None],
        inner_b=inner_bias[None],
        segments=segments,
        buckets=buckets[None],
        predicted=predicted,
        labels=labels,
        cotangent=cotangent[0],
    )
    names = tuple(inputs) + tuple(OUTPUTS) + tuple(SCRATCH) + tuple(SEMAPHORES)
    vmem = pl.BlockSpec(memory_space=pltpu.VMEM)
    outs = pl.pallas_call(
        partial(layer_kernel, names),
        name="layer",
        out_shape=tuple(jax.ShapeDtypeStruct(*out) for out in OUTPUTS.values()),
        in_specs=[vmem] * len(inputs),
        out_specs=(vmem,) * len(OUTPUTS),
        scratch_shapes=[pltpu.VMEM(*spec) for spec in SCRATCH.values()]
        + [pltpu.SemaphoreType.DMA(shape) for shape in SEMAPHORES.values()],
        compiler_params=pltpu.CompilerParams(
            collective_id=0, has_side_effects=True, vmem_limit_bytes=67043328
        ),
    )(*inputs.values())
    finals = pl.pallas_call(
        partial(finish_kernel, tuple(OUTPUTS) + tuple(FINALS)),
        name="finish",
        out_shape=tuple(jax.ShapeDtypeStruct(*out) for out in FINALS.values()),
        in_specs=[vmem] * len(OUTPUTS),
        out_specs=(vmem,) * len(FINALS),
    )(*outs)
    got = type("Outs", (), dict(zip(FINALS, finals)))
    return (
        got.result_out[None],
        got.input_grad_out[None],
        got.query_w_out,
        got.query_b_out[0],
        got.key_w_out,
        got.value_w_out,
        got.value_b_out[0],
        got.output_w_out,
        got.output_b_out[0],
        got.gain_1_out[0],
        got.shift_1_out[0],
        got.inner_w_out,
        got.inner_b_out[0],
        got.outer_w_out,
        got.outer_b_out[0],
        got.gain_2_out[0],
        got.shift_2_out[0],
        got.table_out.T,
        got.count_out[0, 0],
    )


def fits(mesh):
    return mesh.shape["fsdp"] == 4 * LINE and mesh.shape["seq"] == 2


def solution(mesh):
    return jax.shard_map(
        block_shards if fits(mesh) else shards,
        mesh=mesh,
        in_specs=(
            P("fsdp", "seq", None),
            P(("fsdp", "seq"), None),
            P(("fsdp", "seq")),
            P(("fsdp", "seq"), None),
            P(("fsdp", "seq"), None),
            P(("fsdp", "seq")),
            P(("fsdp", "seq"), None),
            P(("fsdp", "seq")),
            P(("fsdp", "seq")),
            P(("fsdp", "seq")),
            P(("fsdp", "seq"), None),
            P(("fsdp", "seq")),
            P(("fsdp", "seq"), None),
            P(("fsdp", "seq")),
            P(("fsdp", "seq")),
            P(("fsdp", "seq")),
            P(None, ("fsdp", "seq")),
            P("fsdp", None),
            P(),
            P("fsdp", "seq"),
            P("fsdp", "seq"),
            P("fsdp", "seq", None),
        ),
        out_specs=(
            P("fsdp", "seq", None),
            P("fsdp", "seq", None),
            P(("fsdp", "seq"), None),
            P(("fsdp", "seq")),
            P(("fsdp", "seq"), None),
            P(("fsdp", "seq"), None),
            P(("fsdp", "seq")),
            P(("fsdp", "seq"), None),
            P(("fsdp", "seq")),
            P(("fsdp", "seq")),
            P(("fsdp", "seq")),
            P(("fsdp", "seq"), None),
            P(("fsdp", "seq")),
            P(("fsdp", "seq"), None),
            P(("fsdp", "seq")),
            P(("fsdp", "seq")),
            P(("fsdp", "seq")),
            P(None, ("fsdp", "seq")),
            P(),
        ),
        check_vma=False,
    )
```

```python
from functools import partial

import jax
import jax.numpy as jnp
import numpy as np
from jax import lax
from jax.experimental import pallas as pl
from jax.experimental.pallas import tpu as pltpu
from jax.sharding import PartitionSpec as P

HEAD = 64


EPSILON = 1e-07
NEGATIVE = -1e30


def matmul(spec, left, right):
    return jnp.einsum(spec, left, right, preferred_element_type=jnp.float32)


def precise(spec, left, right):
    return jnp.einsum(spec, left, right, precision=lax.Precision.HIGHEST)


def skew_rows(scores_in, offset, columns):
    leading = scores_in.shape[:-2]
    row_count = scores_in.shape[-2]
    breadth = scores_in.shape[-1]
    flattened = scores_in.reshape(leading + (row_count * breadth,))
    flattened = jnp.concatenate(
        [flattened, jnp.zeros(leading + (2 * breadth,), scores_in.dtype)], axis=-1
    )
    selected = lax.dynamic_slice_in_dim(flattened, offset, row_count * (breadth - 1), len(leading))
    return selected.reshape(leading + (row_count, breadth - 1))[..., :columns]


def unskew_rows(values, offset, breadth):
    leading = values.shape[:-2]
    row_count = values.shape[-2]
    columns = values.shape[-1]
    padded = jnp.concatenate(
        [values, jnp.zeros(leading + (row_count, breadth - 1 - columns), values.dtype)], axis=-1
    )
    flattened = padded.reshape(leading + (row_count * (breadth - 1),))
    zero_room = jnp.zeros(leading + (row_count * breadth + 2 * breadth,), values.dtype)
    placed = lax.dynamic_update_slice_in_dim(zero_room, flattened, offset, len(leading))
    return placed[..., : row_count * breadth].reshape(leading + (row_count, breadth))


def layer_norm(values, gain, shift):
    average = jnp.mean(values, axis=-1, keepdims=True)
    centred = values - average
    variance = jnp.mean(centred * centred, axis=-1, keepdims=True)
    inverse = lax.rsqrt(variance + EPSILON)
    normed = centred * inverse
    return (normed * gain + shift, normed, inverse)


def norm_backward(upstream, normed, inverse, gain):
    scaled_up = upstream * gain
    first_mean = jnp.mean(scaled_up, axis=-1, keepdims=True)
    second_mean = jnp.mean(scaled_up * normed, axis=-1, keepdims=True)
    grad_in = inverse * (scaled_up - first_mean - normed * second_mean)
    return (grad_in, jnp.sum(upstream * normed, axis=0), jnp.sum(upstream, axis=0))


def shards(
    hidden_in,
    query_weight,
    query_bias,
    key_weight,
    value_weight,
    value_bias,
    output_weight,
    output_bias,
    first_gain,
    first_shift,
    inner_weight,
    inner_bias,
    outer_weight,
    outer_bias,
    second_gain,
    second_shift,
    relative_table,
    segments,
    buckets,
    predicted,
    labels,
    cotangent,
):
    row_count, window, model_width = hidden_in.shape
    length = segments.shape[1]
    distances = 2 * length - 1
    span = window + length - 1
    pair_width = 2 * HEAD
    pair_count = model_width // pair_width
    score_scale = (3.0 * HEAD) ** (-0.5)
    window_start = lax.axis_index("seq") * window
    near_start = length - window - window_start
    token_count = row_count * window
    attention_set = (
        lax.all_gather(query_weight, ("fsdp", "seq"), axis=0, tiled=True),
        lax.all_gather(query_bias, ("fsdp", "seq"), axis=0, tiled=True),
        lax.all_gather(key_weight, ("fsdp", "seq"), axis=0, tiled=True),
        lax.all_gather(value_weight, ("fsdp", "seq"), axis=0, tiled=True),
        lax.all_gather(value_bias, ("fsdp", "seq"), axis=0, tiled=True),
        lax.all_gather(output_weight, ("fsdp", "seq"), axis=0, tiled=True),
        lax.all_gather(output_bias, ("fsdp", "seq"), axis=0, tiled=True),
        lax.all_gather(first_gain, ("fsdp", "seq"), axis=0, tiled=True),
        lax.all_gather(first_shift, ("fsdp", "seq"), axis=0, tiled=True),
        lax.all_gather(relative_table, ("fsdp", "seq"), axis=1, tiled=True),
    )
    feed_set = (
        lax.all_gather(inner_weight, ("fsdp", "seq"), axis=0, tiled=True),
        lax.all_gather(inner_bias, ("fsdp", "seq"), axis=0, tiled=True),
        lax.all_gather(outer_weight, ("fsdp", "seq"), axis=0, tiled=True),
        lax.all_gather(outer_bias, ("fsdp", "seq"), axis=0, tiled=True),
        lax.all_gather(second_gain, ("fsdp", "seq"), axis=0, tiled=True),
        lax.all_gather(second_shift, ("fsdp", "seq"), axis=0, tiled=True),
    )
    (
        query_matrix,
        query_offset,
        key_matrix,
        value_matrix,
        value_offset,
        output_matrix,
        output_offset,
        gain_first,
        shift_first,
        table_full,
    ) = attention_set
    inner_matrix, inner_offset, outer_matrix, outer_offset, gain_second, shift_second = feed_set
    tokens = hidden_in.reshape(token_count, model_width)
    queries = (
        (matmul("td,de->te", tokens, query_matrix) + query_offset.astype(jnp.float32))
        .astype(jnp.bfloat16)
        .reshape(row_count, window, model_width)
    )
    keys_own = (
        matmul("td,de->te", tokens, key_matrix)
        .astype(jnp.bfloat16)
        .reshape(row_count, window, model_width)
    )
    values_own = (
        (matmul("td,de->te", tokens, value_matrix) + value_offset.astype(jnp.float32))
        .astype(jnp.bfloat16)
        .reshape(row_count, window, model_width)
    )
    keys_all, values_all = (
        lax.all_gather(keys_own, "seq", axis=1, tiled=True),
        lax.all_gather(values_own, "seq", axis=1, tiled=True),
    )
    key_rel = matmul("pd,de->pe", table_full, key_matrix).astype(jnp.bfloat16)
    query_rel = (
        matmul("pd,de->pe", table_full, query_matrix) + query_offset.astype(jnp.float32)
    ).astype(jnp.bfloat16)
    reversed_buckets = buckets[::-1]
    table_rows = table_full.shape[0]
    one_hot = (
        reversed_buckets[:, None] == jnp.arange(table_rows, dtype=jnp.int32)[None, :]
    ).astype(jnp.bfloat16)
    bucket_keys = matmul("dp,pe->de", one_hot, key_rel).astype(jnp.bfloat16)
    bucket_queries = matmul("dp,pe->de", one_hot, query_rel).astype(jnp.bfloat16)
    near_keys = lax.dynamic_slice_in_dim(bucket_keys, near_start, span, 0)
    far_queries = lax.dynamic_slice_in_dim(bucket_queries, window_start, span, 0)
    segment_own = lax.dynamic_slice_in_dim(segments, window_start, window, 1)
    same_doc = (segment_own[:, :, None] == segments[:, None, :])[:, None]

    def pair_scores(pair_index):
        column = pair_index * pair_width
        query_pair = lax.dynamic_slice_in_dim(queries, column, pair_width, 2).reshape(
            row_count, window, 2, HEAD
        )
        key_pair = lax.dynamic_slice_in_dim(keys_all, column, pair_width, 2).reshape(
            row_count, length, 2, HEAD
        )
        value_pair = lax.dynamic_slice_in_dim(values_all, column, pair_width, 2).reshape(
            row_count, length, 2, HEAD
        )
        bucketkeys = lax.dynamic_slice_in_dim(near_keys, column, pair_width, 1).reshape(
            span, 2, HEAD
        )
        bucketqueries = lax.dynamic_slice_in_dim(far_queries, column, pair_width, 1).reshape(
            span, 2, HEAD
        )
        content = matmul("rihe,rjhe->rhij", query_pair, key_pair)
        near_scores = matmul("rihe,dhe->rhid", query_pair, bucketkeys)
        far_scores = matmul("rjhe,dhe->rhjd", key_pair, bucketqueries)
        to_position = skew_rows(near_scores, window - 1, length)
        from_position = jnp.swapaxes(skew_rows(far_scores, length - 1, window), 2, 3)
        summed = content + to_position + from_position
        masked = jnp.where(same_doc, summed * score_scale, NEGATIVE)
        return (masked, query_pair, key_pair, value_pair, bucketkeys, bucketqueries)

    def attend_pair(pair_index):
        masked, query_pair, key_pair, value_pair, bucketkeys, bucketqueries = pair_scores(
            pair_index
        )
        highest = jnp.max(masked, axis=-1, keepdims=True)
        expsum = jnp.exp(masked - highest)
        totals = jnp.sum(expsum, axis=-1, keepdims=True)
        weights_soft = (expsum / totals).astype(jnp.bfloat16)
        context_pair = matmul("rhij,rjhe->rihe", weights_soft, value_pair).astype(jnp.bfloat16)
        return (
            context_pair.reshape(row_count, window, pair_width),
            (highest + jnp.log(totals))[..., 0],
        )

    context_parts, log_totals = lax.map(attend_pair, jnp.arange(pair_count, dtype=jnp.int32))
    context = jnp.moveaxis(context_parts, 0, 2).reshape(token_count, model_width)
    attention_out = matmul("te,ed->td", context, output_matrix) + output_offset.astype(jnp.float32)
    residual_one = tokens.astype(jnp.float32) + attention_out
    first_out, first_normed, first_inverse = layer_norm(
        residual_one, gain_first.astype(jnp.float32), shift_first.astype(jnp.float32)
    )
    first_low = first_out.astype(jnp.bfloat16)
    inner_pre = matmul("td,df->tf", first_low, inner_matrix) + inner_offset.astype(jnp.float32)
    activated = jax.nn.gelu(inner_pre, approximate=False).astype(jnp.bfloat16)
    outer_out = matmul("tf,fd->td", activated, outer_matrix) + outer_offset.astype(jnp.float32)
    final_out, final_normed, final_inverse = layer_norm(
        first_out + outer_out, gain_second.astype(jnp.float32), shift_second.astype(jnp.float32)
    )
    result = final_out.astype(jnp.bfloat16).reshape(row_count, window, model_width)
    correct_count = lax.psum(jnp.sum((predicted == labels).astype(jnp.int32)), ("fsdp", "seq"))
    regathered = attention_set + feed_set
    (
        query_back,
        query_offset_back,
        key_back,
        value_back,
        value_offset_back,
        output_back,
        output_offset_back,
        gain_first_back,
        shift_first_back,
        table_back,
        inner_back,
        inner_offset_back,
        outer_back,
        outer_offset_back,
        gain_second_back,
        shift_second_back,
    ) = regathered
    upstream = cotangent.reshape(token_count, model_width).astype(jnp.float32)
    grad_sum2, grad_gain2, grad_shift2 = norm_backward(
        upstream, final_normed, final_inverse, gain_second_back.astype(jnp.float32)
    )
    grad_outer = grad_sum2.astype(jnp.bfloat16)
    outer_bias_part = jnp.sum(grad_outer.astype(jnp.float32), axis=0)
    outer_weight_part = matmul("tf,td->fd", activated, grad_outer)
    grad_act = matmul("td,fd->tf", grad_outer, outer_back).astype(jnp.bfloat16)
    _, gelu_back = jax.vjp(partial(jax.nn.gelu, approximate=False), inner_pre)
    grad_inner = gelu_back(grad_act.astype(jnp.float32))[0].astype(jnp.bfloat16)
    inner_bias_part = jnp.sum(grad_inner.astype(jnp.float32), axis=0)
    inner_weight_part = matmul("td,tf->df", first_low, grad_inner)
    grad_first = matmul("tf,df->td", grad_inner, inner_back) + grad_sum2
    feed_grads = (
        lax.psum_scatter(inner_weight_part, ("fsdp", "seq"), scatter_dimension=0, tiled=True),
        lax.psum_scatter(inner_bias_part, ("fsdp", "seq"), scatter_dimension=0, tiled=True),
        lax.psum_scatter(outer_weight_part, ("fsdp", "seq"), scatter_dimension=0, tiled=True),
        lax.psum_scatter(outer_bias_part, ("fsdp", "seq"), scatter_dimension=0, tiled=True),
        lax.psum_scatter(grad_gain2, ("fsdp", "seq"), scatter_dimension=0, tiled=True),
        lax.psum_scatter(grad_shift2, ("fsdp", "seq"), scatter_dimension=0, tiled=True),
    )
    grad_sum1, grad_gain1, grad_shift1 = norm_backward(
        grad_first, first_normed, first_inverse, gain_first_back.astype(jnp.float32)
    )
    grad_attention = grad_sum1.astype(jnp.bfloat16)
    output_bias_part = jnp.sum(grad_attention.astype(jnp.float32), axis=0)
    output_weight_part = matmul("te,td->ed", context, grad_attention)
    grad_context = (
        matmul("td,ed->te", grad_attention, output_back)
        .astype(jnp.bfloat16)
        .reshape(row_count, window, model_width)
    )

    def attend_back(pieces):
        pair_index, log_total = pieces
        masked, query_pair, key_pair, value_pair, bucketkeys, bucketqueries = pair_scores(
            pair_index
        )
        probability = jnp.exp(masked - log_total[..., None])
        grad_context_pair = lax.dynamic_slice_in_dim(
            grad_context, pair_index * pair_width, pair_width, 2
        ).reshape(row_count, window, 2, HEAD)
        grad_soft = matmul("rihe,rjhe->rhij", grad_context_pair, value_pair)
        grad_scores = probability * (
            grad_soft - jnp.sum(probability * grad_soft, axis=-1, keepdims=True)
        )
        grad_low = (grad_scores * score_scale).astype(jnp.bfloat16)
        grad_value = matmul("rhij,rihe->rjhe", probability.astype(jnp.bfloat16), grad_context_pair)
        grad_near = unskew_rows(grad_low, window - 1, span)
        grad_far = unskew_rows(jnp.swapaxes(grad_low, 2, 3), length - 1, span)
        grad_query = matmul("rhij,rjhe->rihe", grad_low, key_pair) + matmul(
            "rhid,dhe->rihe", grad_near, bucketkeys
        )
        grad_key = matmul("rhij,rihe->rjhe", grad_low, query_pair) + matmul(
            "rhjd,dhe->rjhe", grad_far, bucketqueries
        )
        grad_bkeys = matmul("rhid,rihe->dhe", grad_near, query_pair)
        grad_bqueries = matmul("rhjd,rjhe->dhe", grad_far, key_pair)
        return (
            grad_query.reshape(row_count, window, pair_width),
            grad_key.reshape(row_count, length, pair_width),
            grad_value.reshape(row_count, length, pair_width),
            grad_bkeys.reshape(span, pair_width),
            grad_bqueries.reshape(span, pair_width),
        )

    query_parts, key_parts, value_parts, bkey_parts, bquery_parts = lax.map(
        attend_back, (jnp.arange(pair_count, dtype=jnp.int32), log_totals)
    )
    grad_query_all = jnp.moveaxis(query_parts, 0, 2).reshape(token_count, model_width)
    grad_key_all = jnp.moveaxis(key_parts, 0, 2).reshape(row_count, length, model_width)
    grad_value_all = jnp.moveaxis(value_parts, 0, 2).reshape(row_count, length, model_width)
    near_grads = jnp.moveaxis(bkey_parts, 0, 1).reshape(span, model_width)
    far_grads = jnp.moveaxis(bquery_parts, 0, 1).reshape(span, model_width)
    grad_bucket_keys = lax.dynamic_update_slice_in_dim(
        jnp.zeros((distances, model_width), jnp.float32), near_grads, near_start, 0
    )
    grad_bucket_queries = lax.dynamic_update_slice_in_dim(
        jnp.zeros((distances, model_width), jnp.float32), far_grads, window_start, 0
    )
    key_grads, value_grads = (
        lax.psum_scatter(
            grad_key_all.astype(jnp.bfloat16), "seq", scatter_dimension=1, tiled=True
        ).astype(jnp.float32),
        lax.psum_scatter(
            grad_value_all.astype(jnp.bfloat16), "seq", scatter_dimension=1, tiled=True
        ).astype(jnp.float32),
    )
    query_low = grad_query_all.astype(jnp.bfloat16)
    key_low = key_grads.reshape(token_count, model_width).astype(jnp.bfloat16)
    value_low = value_grads.reshape(token_count, model_width).astype(jnp.bfloat16)
    grad_key_rel = jax.ops.segment_sum(grad_bucket_keys, reversed_buckets, num_segments=table_rows)
    grad_query_rel = jax.ops.segment_sum(
        grad_bucket_queries, reversed_buckets, num_segments=table_rows
    )
    query_token_part = matmul("td,te->de", tokens, query_low)
    query_bias_token = jnp.sum(query_low.astype(jnp.float32), axis=0)
    key_token_part = matmul("td,te->de", tokens, key_low)
    value_weight_part = matmul("td,te->de", tokens, value_low)
    value_bias_part = jnp.sum(value_low.astype(jnp.float32), axis=0)
    grad_input = (
        grad_sum1
        + matmul("te,de->td", query_low, query_back)
        + matmul("te,de->td", key_low, key_back)
        + matmul("te,de->td", value_low, value_back)
    )
    input_grad = grad_input.astype(jnp.bfloat16).reshape(row_count, window, model_width)
    key_rel_total, query_rel_total = lax.psum((grad_key_rel, grad_query_rel), ("fsdp", "seq"))
    attention_grads = (
        lax.psum_scatter(query_token_part, ("fsdp", "seq"), scatter_dimension=0, tiled=True),
        lax.psum_scatter(query_bias_token, ("fsdp", "seq"), scatter_dimension=0, tiled=True),
        lax.psum_scatter(key_token_part, ("fsdp", "seq"), scatter_dimension=0, tiled=True),
        lax.psum_scatter(value_weight_part, ("fsdp", "seq"), scatter_dimension=0, tiled=True),
        lax.psum_scatter(value_bias_part, ("fsdp", "seq"), scatter_dimension=0, tiled=True),
        lax.psum_scatter(output_weight_part, ("fsdp", "seq"), scatter_dimension=0, tiled=True),
        lax.psum_scatter(output_bias_part, ("fsdp", "seq"), scatter_dimension=0, tiled=True),
        lax.psum_scatter(grad_gain1, ("fsdp", "seq"), scatter_dimension=0, tiled=True),
        lax.psum_scatter(grad_shift1, ("fsdp", "seq"), scatter_dimension=0, tiled=True),
    )
    shard_rows = query_weight.shape[0]
    shard_start = lax.axis_index(("fsdp", "seq")) * shard_rows
    table_shard = relative_table.astype(jnp.float32)
    query_weight_grad = attention_grads[0] + precise("pd,pe->de", table_shard, query_rel_total)
    key_weight_grad = attention_grads[2] + precise("pd,pe->de", table_shard, key_rel_total)
    query_bias_grad = attention_grads[1] + jnp.sum(
        lax.dynamic_slice_in_dim(query_rel_total, shard_start, shard_rows, 1), axis=0
    )
    relative_table_grad = precise(
        "pe,de->pd", query_rel_total, query_weight.astype(jnp.float32)
    ) + precise("pe,de->pd", key_rel_total, key_weight.astype(jnp.float32))
    return (
        result,
        input_grad,
        query_weight_grad,
        query_bias_grad,
        key_weight_grad,
        attention_grads[3],
        attention_grads[4],
        attention_grads[5],
        attention_grads[6],
        attention_grads[7],
        attention_grads[8],
        feed_grads[0],
        feed_grads[1],
        feed_grads[2],
        feed_grads[3],
        feed_grads[4],
        feed_grads[5],
        relative_table_grad,
        correct_count,
    )


MESH = pl.DeviceIdType.MESH
F32 = jnp.float32
BF16 = jnp.bfloat16


def dot(left, right, left_dim=1, right_dim=0):
    return lax.dot_general(
        left, right, (((left_dim,), (right_dim,)), ((), ())), preferred_element_type=F32
    )


def low(value):
    return value.astype(BF16)


class Route:
    def __init__(self):
        chip = lax.axis_index("fsdp")
        self.core = lax.axis_index("seq")
        self.other = 1 - self.core
        self.chip = chip
        self.x = chip % 2
        self.y = (chip // 2) % 2
        self.z = chip // 4
        self.plane = chip % 4
        self.plane_x = self.plane + 1 - 2 * self.x
        self.plane_y = self.plane + 2 - 4 * self.y
        self.pair = self.z + 1 - 2 * (self.z % 2)
        self.near = (self.z, (self.z + 2) % LINE)
        self.far = (self.pair, (self.pair + 2) % LINE)
        self.soon = 1 + self.z % 2
        self.late = 3 - 3 * (self.z % 2)
        self.partner = (chip, self.other)
        self.at_x = (self.z * 4 + self.plane_x, self.core)
        self.at_y = (self.z * 4 + self.plane_y, self.core)

    def at_line(self, line):
        return (line * 4 + self.plane, self.core)

    def ahead(self, step):
        return (self.z + step) % LINE

    def behind(self, step):
        return (self.z + LINE - step) % LINE


def remote(source, target, send_sem, recv_sem, device):
    return pltpu.make_async_remote_copy(
        source, target, send_sem, recv_sem, device_id=device, device_id_type=MESH
    )


class Gather:
    def __init__(self, route, arrays, send, recv):
        self.r, self.arrays, self.send, self.recv = route, arrays, send, recv

    def copies(self, kind, line):
        r = self.r
        for i, array in enumerate(self.arrays):
            by_x = i == 1
            plane, device = (
                (r.plane, r.at_line((r.z + 1) % LINE)),
                (r.plane, r.at_line((r.z + LINE - 1) % LINE)),
                (r.plane, r.at_x),
                (r.plane, r.at_y),
                (r.plane_y, r.at_x) if by_x else (r.plane_x, r.at_y),
                (3 - r.plane, r.at_line(r.pair)),
            )[kind]
            block = array.at[line, plane]
            yield remote(
                block, block, self.send.at[i, kind, line], self.recv.at[i, kind, line], device
            )

    def begin(self, kind, line):
        for copy in self.copies(kind, line):
            copy.start()

    def got(self, kind, line):
        for copy in self.copies(kind, line):
            copy.wait_recv()

    def sides(self, line):
        self.begin(2, line)
        self.begin(3, line)

    def got_sides(self, line):
        self.got(2, line)
        self.got(3, line)

    def up(self, line):
        @pl.when(self.r.z < LINE - 1)
        def _():
            self.begin(0, line)

    def down(self, line):
        @pl.when(self.r.z > 0)
        def _():
            self.begin(1, line)

    def start_line(self):
        self.up(self.r.z)
        self.down(self.r.z)

    def start_sides(self):
        self.sides(self.r.z)

    def round(self, step):
        r = self.r

        @pl.when(r.z >= step)
        def _():
            self.got(0, r.z - step)
            self.up(r.z - step)

        @pl.when(r.z + step < LINE)
        def _():
            self.got(1, r.z + step)
            self.down(r.z + step)

    def first(self):
        self.corner(0)
        self.round(1)
        self.sides(self.r.soon)

    def second(self):
        self.round(2)
        self.sides(self.r.near[1])
        self.hand(0)

    def third(self):
        self.round(3)
        self.corner(1)
        self.sides(self.r.late)

    def corner(self, which):
        line = self.r.near[which]
        self.got_sides(line)
        self.begin(4, line)

    def hand(self, which):
        line = self.r.near[which]
        self.got(4, line)
        self.begin(5, line)

    def finish(self):
        for line in self.r.far:
            self.got_sides(line)
            self.got(5, line)

    def drained(self, kind, line):
        for copy in self.copies(kind, line):
            copy.wait_send()

    def sent(self):
        r = self.r
        for line in range(LINE):

            @pl.when((r.z < LINE - 1) & (r.z >= line))
            def _():
                self.drained(0, line)

            @pl.when((r.z > 0) & (r.z <= line))
            def _():
                self.drained(1, line)

            self.drained(2, line)
            self.drained(3, line)
        for line in r.near:
            self.drained(4, line)
            self.drained(5, line)


class Scatter:
    def __init__(self, route, arrays, rooms, send, recv):
        self.r, self.arrays, self.rooms = route, arrays, rooms
        self.send, self.recv = send, recv

    def across(self, i):
        return self.r.plane_y if i == 0 else self.r.plane_x

    def copy(self, i, kind, line):
        r = self.r
        near, across = (r.at_x, r.at_y) if i == 0 else (r.at_y, r.at_x)
        near_plane = r.plane_x if i == 0 else r.plane_y
        plane, room, device = (
            (3 - r.plane, line // 2, r.at_line(r.pair)),
            (near_plane, line, near),
            (3 - r.plane, line // 2, near),
            (self.across(i), line, across),
            (r.plane, r.z, r.at_line(line)),
        )[kind]
        return remote(
            self.arrays[i].at[line, plane],
            self.rooms[i][kind].at[room],
            self.send.at[i, kind, line],
            self.recv.at[i, kind, r.z if kind == 4 else line],
            device,
        )

    def got_along(self, i, line):
        r = self.r
        remote(
            self.arrays[i].at[line, r.plane],
            self.rooms[i][4].at[line],
            self.send.at[i, 4, line],
            self.recv.at[i, 4, line],
            r.at_line(line),
        ).wait_recv()

    def begin_far(self, i, line):
        for kind in (0, 1, 3):
            self.copy(i, kind, line).start()

    def begin_near(self, i, line):
        self.copy(i, 1, line).start()

    def begin(self, i):
        for line in self.r.far:
            self.begin_far(i, line)
        for line in self.r.near[::-1]:
            self.begin_near(i, line)

    def merge(self, i, line, plane, *came):
        at = self.arrays[i].at[line, plane]
        value = at[...].astype(F32)
        for kind, room in came:
            value = value + self.rooms[i][kind][room].astype(F32)
        at[...] = low(value)

    def corners(self, i):
        for line in self.r.near[::-1]:
            self.copy(i, 0, line).wait_recv()
            self.merge(i, line, 3 - self.r.plane, (0, line // 2))
            self.copy(i, 2, line).start()

    def turn(self, i):
        for line in self.r.near[::-1]:
            self.copy(i, 2, line).wait_recv()
            self.merge(i, line, self.across(i), (2, line // 2))
            self.copy(i, 3, line).start()

    def along(self, i, line):
        self.copy(i, 1, line).wait_recv()
        self.copy(i, 3, line).wait_recv()
        self.merge(i, line, self.r.plane, (1, line), (3, line))
        self.copy(i, 4, line).start()

    def along_far(self, i):
        for line in self.r.far:
            self.along(i, line)

    def along_near(self, i):
        self.along(i, self.r.near[1])

    def total(self, i):
        r = self.r
        self.copy(i, 1, r.z).wait_recv()
        self.copy(i, 3, r.z).wait_recv()
        rooms = self.rooms[i]
        value = self.arrays[i][r.z, r.plane].astype(F32)
        value = value + rooms[1][r.z].astype(F32) + rooms[3][r.z].astype(F32)
        for line in r.far + r.near[1:]:
            self.got_along(i, line)
            value = value + rooms[4][line].astype(F32)
        return value

    def sent(self):
        r = self.r
        for i in (0, 1):
            for line in range(LINE):
                self.copy(i, 1, line).wait_send()
                self.copy(i, 3, line).wait_send()
            for line in r.far:
                self.copy(i, 0, line).wait_send()
                self.copy(i, 4, line).wait_send()
            for line in r.near:
                self.copy(i, 2, line).wait_send()
            self.copy(i, 4, r.near[1]).wait_send()


def loop(count, body):
    def step(index, carry):
        body(index)
        return carry

    lax.fori_loop(0, count, step, 0)


def aligned(index, size):
    return pl.ds(pl.multiple_of(index * size, size), size)


def erf_parts(value):
    tail = lax.erf(value * np.float32(0.5**0.5))
    half = 0.5 * (1.0 + tail)
    density = jnp.exp(value * value * -0.5) * np.float32((2.0 * np.pi) ** -0.5)
    return value * half, half + value * density


def norm(values, gain, shift):
    average = jnp.mean(values, axis=-1, keepdims=True)
    centred = values - average
    variance = jnp.mean(centred * centred, axis=-1, keepdims=True)
    inverse = lax.rsqrt(variance + EPSILON)
    normed = centred * inverse
    return normed * gain + shift, normed, inverse


def norm_pull(upstream, normed, inverse, gain):
    scaled_up = upstream * gain
    first_mean = jnp.mean(scaled_up, axis=-1, keepdims=True)
    second_mean = jnp.mean(scaled_up * normed, axis=-1, keepdims=True)
    return inverse * (scaled_up - first_mean - normed * second_mean)


def layer_kernel(names, *refs):
    b = dict(zip(names, refs))
    at = type("Refs", (), b)
    r = Route()
    core, other = r.core, r.other
    own_rows = aligned(core, 256)
    other_rows = aligned(other, 256)
    score_scale = np.float32((3.0 * HEAD) ** (-0.5))

    barrier = pltpu.get_barrier_semaphore()
    friends = [r.partner, r.at_x, r.at_y] + [r.at_line(r.ahead(k)) for k in range(1, LINE)]
    for device in friends:
        pl.semaphore_signal(barrier, inc=1, device_id=device, device_id_type=MESH)

    def give_rows(kind, index, array):
        piece = pl.ds(pl.multiple_of(core * 256 + index * 64, 64), 64)
        return remote(
            array.at[piece],
            array.at[piece],
            at.row_send.at[kind, index],
            at.row_recv.at[kind, index],
            r.partner,
        )

    def got_rows(kind, array):
        for index in range(4):
            give_rows(kind, index, array).wait_recv()

    waiting = []

    def swap(slot, source, target):
        copy = remote(source, target, at.swap_send.at[slot], at.swap_recv.at[slot], r.partner)
        copy.start()
        waiting.append(copy)
        return copy

    gather_one = Gather(r, (at.gat_a, at.gat_b, at.gat_s), at.ga_send, at.ga_recv)
    def halves(array):
        width = array.shape[-1] // 2
        return [array.at[:, :, :, pl.ds(width * part, width)] for part in range(2)]

    gather_two = Gather(r, halves(at.gat_1), at.gf_send, at.gf_recv)
    gather_three = Gather(r, halves(at.gat_2), at.gg_send, at.gg_recv)

    at.sums[...] = jnp.zeros_like(at.sums)
    at.small_wide[...] = jnp.zeros_like(at.small_wide)
    small_rows = (
        at.query_b, at.value_b, at.output_b, at.gain_1, at.shift_1, at.outer_b, at.gain_2, at.shift_2,
        at.inner_b,
    )
    for index, row in enumerate(small_rows):
        at.small_wide[index : index + 1, 0 : row.shape[1]] = row[...].astype(F32)
    at.small[...] = low(at.small_wide[...])
    right = (at.predicted[...] == at.labels[...]).astype(F32)
    at.sums[10:11, :] = jnp.broadcast_to(jnp.sum(right, axis=1, keepdims=True), (1, 768))
    pl.semaphore_wait(barrier, len(friends))

    half = aligned(other, 384)
    arrive = [
        swap(0, at.key_w.at[:, half], at.come_a.at[:, pl.ds(0, 384)]),
        swap(1, at.value_w.at[:, half], at.come_a.at[:, pl.ds(384, 384)]),
        swap(2, at.query_w.at[:, half], at.come_b.at[:, pl.ds(0, 384)]),
        swap(3, at.output_w.at[:, half], at.come_b.at[:, pl.ds(384, 384)]),
        swap(4, at.table_t.at[:, aligned(other, 256)], at.come_b.at[:, pl.ds(768, 256)]),
        swap(5, at.small, at.come_s),
    ]
    come_x = swap(7, at.hidden, at.x_all.at[own_rows])
    place_x = pltpu.make_async_copy(at.hidden, at.x_all.at[own_rows], at.here.at[0])
    place_x.start()
    place_2 = pltpu.make_async_copy(at.outer_w, at.gat_2.at[r.z, r.plane], at.here.at[1])
    place_2.start()
    for copy in arrive:
        copy.wait_recv()

    def stack(mine, came):
        mine, came = mine.astype(F32), came.astype(F32)
        upper = jnp.where(core == 0, mine, came)
        lower = jnp.where(core == 0, came, mine)
        return low(jnp.concatenate([upper, lower], axis=0))

    mine_half = aligned(core, 384)
    at.gat_a[r.z, r.plane, :, 0:384] = stack(at.key_w[:, mine_half], at.come_a[:, 0:384])
    at.gat_a[r.z, r.plane, :, 384:768] = stack(at.value_w[:, mine_half], at.come_a[:, 384:768])
    at.gat_b[r.z, r.plane, :, 0:384] = stack(at.query_w[:, mine_half], at.come_b[:, 0:384])
    at.gat_b[r.z, r.plane, :, 384:768] = stack(at.output_w[:, mine_half], at.come_b[:, 384:768])
    at.gat_b[r.z, r.plane, :, 768:1024] = stack(
        at.table_t[:, aligned(core, 256)], at.come_b[:, 768:1024]
    )
    at.gat_s[r.z, r.plane, core] = at.small[...]
    at.gat_s[r.z, r.plane, other] = at.come_s[...]
    gather_one.start_line()
    gather_one.start_sides()
    for chip in range(4 * LINE):
        for which in range(2):
            device = 2 * chip + which
            at.inner_pair[which, :, 96 * chip : 96 * chip + 96] = at.inner_w[
                :, 96 * device : 96 * device + 96
            ]
    come_inner = swap(6, at.inner_pair.at[other], at.come_1)
    come_inner.wait_recv()
    at.gat_1[r.z, r.plane] = stack(at.inner_pair[core], at.come_1[...])
    place_2.wait()
    place_x.wait()
    come_x.wait_recv()
    at.x_turned[...] = at.x_all[...].T
    wide_i = lax.broadcasted_iota(jnp.int32, (512, 512), 0)
    wide_j = lax.broadcasted_iota(jnp.int32, (512, 512), 1)
    at.one_natural[...] = low((at.buckets[0:1, 256:768] == wide_i).astype(F32))
    at.one_hot[...] = low(dot(at.one_natural[...], low((wide_i + wide_j == 511).astype(F32))))
    segment_wide = jnp.broadcast_to(at.segments[...].astype(F32), (128, 512))
    at.segment_row[...] = segment_wide[0:8]
    at.segment_col[...] = segment_wide.T
    flip_i = lax.broadcasted_iota(jnp.int32, (128, 128), 0)
    flip_j = lax.broadcasted_iota(jnp.int32, (128, 128), 1)
    at.flip[...] = low((flip_i + flip_j == 127).astype(F32))
    for table in (at.near_rows, at.far_rows, at.far_natural):
        table[0:256, :] = jnp.zeros((256, 384), BF16)
        table[768:1024, :] = jnp.zeros((256, 384), BF16)
    gather_one.first()
    gather_one.second()
    gather_one.third()
    gather_two.start_sides()
    gather_three.start_sides()
    gather_one.hand(1)
    gather_two.start_line()
    gather_three.start_line()
    gather_one.finish()

    out_mine = at.gat_b.at[:, :, :, pl.ds(384, 384)]
    table_mine = at.gat_b.at[:, :, :, pl.ds(768, 256)]
    come_table = swap(8, table_mine, at.table_all.at[core])
    come_out = swap(9, out_mine, at.out_all.at[core])
    place_table = pltpu.make_async_copy(table_mine, at.table_all.at[core], at.here.at[0])
    place_table.start()
    place_out = pltpu.make_async_copy(out_mine, at.out_all.at[core], at.here.at[1])
    place_out.start()

    for line in range(LINE):
        for plane in range(4):
            chip = line * 4 + plane
            for which in range(2):
                device = 2 * chip + which
                tile = at.gat_s[line, plane, which].astype(F32)
                at.vectors[:, 24 * device : 24 * device + 24] = tile[0:8, 0:24]
            tile = at.gat_s[line, plane, core].astype(F32)
            at.inner_bias[0:1, 96 * chip : 96 * chip + 96] = tile[8:9, 0:96]

    def rows(value):
        return value.reshape(768, value.shape[-1])

    vector_half = aligned(core, 384)
    query_bias = at.vectors[0:1, vector_half]
    value_bias = at.vectors[1:2, vector_half]
    at.kvq[:, 0:384] = low(dot(at.x_all[...], rows(at.gat_a[:, :, :, 0:384])))
    at.kvq[:, 384:768] = low(dot(at.x_all[...], rows(at.gat_a[:, :, :, 384:768])) + value_bias)
    at.kvq[:, 768:1152] = low(dot(at.x_all[...], rows(at.gat_b[:, :, :, 0:384])) + query_bias)
    gather_two.first()
    place_table.wait()
    come_table.wait_recv()
    for part in range(2):
        piece = pl.ds(256 * part, 256)
        table = rows(at.table_all[part])
        at.key_rel[piece, :] = low(dot(table, rows(at.gat_a[:, :, :, 0:384]), 0, 0))
        at.query_rel[piece, :] = low(dot(table, rows(at.gat_b[:, :, :, 0:384]), 0, 0) + query_bias)
    at.near_rows[256:768, :] = low(dot(at.one_hot[...], at.key_rel[...], 0, 0))
    at.far_rows[256:768, :] = low(dot(at.one_hot[...], at.query_rel[...], 0, 0))
    at.far_natural[256:768, :] = low(dot(at.one_natural[...], at.query_rel[...], 0, 0))

    gather_three.first()

    lanes = lax.broadcasted_iota(jnp.int32, (1, 128), 1) // HEAD
    no_score = np.float32(NEGATIVE)

    def forward_head(head):
        pair = aligned(head // 2, 128)
        key_lanes = pl.ds(pl.multiple_of((head // 2) * 128, 128), 128)
        value_lanes = pl.ds(pl.multiple_of(384 + (head // 2) * 128, 128), 128)
        query_lanes = pl.ds(pl.multiple_of(768 + (head // 2) * 128, 128), 128)
        mine = lanes == head % 2
        only = low(mine.astype(F32))
        keys = at.kvq[:, key_lanes]
        values = at.kvq[:, value_lanes]
        for block in range(4):
            piece = pl.ds(128 * block, 128)
            shifted = dot(
                at.kvq[piece, key_lanes] * only, at.far_rows[pl.ds(384 - 128 * block, 640), pair], 1, 1
            )
            at.far_scores[piece, :] = pltpu.roll(shifted, 0, 1, stride=1, stride_axis=0)[:, 128:640]
        for block in range(4):
            piece = pl.ds(128 * block, 128)
            queries = at.kvq[piece, query_lanes] * only
            shifted = dot(queries, at.near_rows[pl.ds(384 - 128 * block, 640), pair], 1, 1)
            summed = (
                dot(queries, keys, 1, 1)
                + pltpu.roll(shifted, 0, 1, stride=1, stride_axis=0)[:, 128:640]
                + at.far_scores[:, piece].T
            )
            masked = jnp.where(
                at.segment_col[piece, 0:1] == at.segment_row[0:1, :], summed * score_scale, no_score
            )
            highest = jnp.max(masked, axis=-1, keepdims=True)
            expsum = jnp.exp(masked - highest)
            soft = expsum / jnp.sum(expsum, axis=-1, keepdims=True)
            rounded = low(soft)
            at.soft[head, piece, :] = low(dot(at.flip[...], rounded))
            context = dot(rounded, values)
            here = at.context.at[core, piece, pair]
            here[...] = low(jnp.where(mine, context, here[...].astype(F32)))

    def forward_pair(index):
        def forward(which):
            head = 2 * index + which
            forward_head(head)
            pl.when(head == 1)(gather_two.second)
            pl.when(head == 2)(gather_three.second)
            pl.when(head == 4)(gather_two.third)
            pl.when(head == 5)(gather_three.third)

        loop(2, forward)
        remote(
            at.context.at[core, :, aligned(index, 128)],
            at.context.at[core, :, aligned(index, 128)],
            at.context_send.at[index],
            at.context_recv.at[index],
            r.partner,
        ).start()

    loop(3, forward_pair)
    place_out.wait()
    come_out.wait_recv()
    for index in range(3):
        remote(
            at.context.at[other, :, pl.ds(128 * index, 128)],
            at.context.at[other, :, pl.ds(128 * index, 128)],
            at.context_send.at[index],
            at.context_recv.at[index],
            r.partner,
        ).wait_recv()

    def vector(index):
        return at.vectors[index : index + 1, :]

    for part in range(2):
        piece = pl.ds(384 * part, 384)
        weight = rows(at.out_all[part])
        at.wide[:, piece] = dot(at.context[0, own_rows, :], weight[0:384]) + dot(
            at.context[1, own_rows, :], weight[384:768]
        )

    def first_norm(index):
        piece = aligned(index, 64)
        token_rows = pl.ds(pl.multiple_of(core * 256 + index * 64, 64), 64)
        residual = at.x_all[token_rows, :].astype(F32) + at.wide[piece, :] + vector(2)
        out, normed, inverse = norm(residual, vector(3), vector(4))
        at.first_out[piece, :] = out
        at.first_normed[piece, :] = normed
        at.first_inverse[piece, :] = jnp.broadcast_to(inverse, (64, 128))
        at.first_low[token_rows, :] = low(out)
        give_rows(0, index, at.first_low).start()

    loop(4, first_norm)
    gather_two.hand(1)
    got_rows(0, at.first_low)
    at.first_turned[...] = at.first_low[...].T
    gather_two.finish()
    gather_three.hand(1)

    def inner_units(index):
        piece = aligned(index, 256)
        pre = dot(at.first_low[...], rows(at.gat_1[:, :, :, piece])) + at.inner_bias[0:1, piece]
        value, slope = erf_parts(pre)
        at.active[:, piece] = low(value)
        at.slope[:, piece] = slope

    loop(6, inner_units)
    gather_three.finish()

    def outer_part(rows_at, part):
        return dot(
            at.active[rows_at, :], at.gat_2[:, :, :, 256 * part : 256 * part + 256].reshape(1536, 256)
        )

    come_outer = []
    for part in range(3):
        piece = pl.ds(256 * part, 256)
        at.part_send[:, piece] = low(outer_part(other_rows, part))
        come_outer.append(swap((11, 23, 24)[part], at.part_send.at[:, piece], at.part_recv.at[:, piece]))
    for part in range(3):
        at.wide[:, 256 * part : 256 * part + 256] = outer_part(own_rows, part)
    for copy in come_outer:
        copy.wait_recv()

    def second_norm(index):
        piece = aligned(index, 64)
        token_rows = pl.ds(pl.multiple_of(core * 256 + index * 64, 64), 64)
        total = at.first_out[piece, :] + at.wide[piece, :] + at.part_recv[piece, :].astype(F32) + vector(5)
        out, normed, inverse = norm(total, vector(6), vector(7))
        at.result[piece, :] = low(out)
        upstream = at.cotangent[piece, :].astype(F32)
        grad = norm_pull(upstream, normed, inverse, vector(6))
        at.grad_sum[piece, :] = grad
        rounded = low(grad)
        at.grad_outer[token_rows, :] = rounded
        give_rows(1, index, at.grad_outer).start()
        at.sums[5:6, :] += jnp.sum(rounded.astype(F32), axis=0, keepdims=True)
        at.sums[6:7, :] += jnp.sum(upstream * normed, axis=0, keepdims=True)
        at.sums[7:8, :] += jnp.sum(upstream, axis=0, keepdims=True)

    loop(4, second_norm)

    def scatter(arrays, tags, send, recv):
        rooms = [[b[kind + tag] for kind in ROOMS] for tag in tags]
        return Scatter(r, arrays, rooms, send, recv)

    scatter_two = scatter((at.grad_1, at.grad_2), ("1", "2"), at.sf_send, at.sf_recv)
    scatter_a = scatter((at.grad_o, at.grad_p.at[0]), ("o", "p0"), at.sa_send, at.sa_recv)
    scatter_b = scatter((at.grad_p.at[1], at.grad_p.at[2]), ("p1", "p2"), at.sb_send, at.sb_recv)
    scatter_c = scatter((at.grad_t.at[0], at.grad_t.at[1]), ("t0", "t1"), at.sc_send, at.sc_recv)

    def inner_grad(rows_at):
        for part in range(4):
            units = pl.ds(384 * part, 384)
            grad = low(dot(at.grad_outer[rows_at, :], at.gat_2[part].reshape(384, 768), 1, 1))
            pre = low(grad.astype(F32) * at.slope[rows_at, units])
            at.grad_pre[rows_at, units] = pre
            at.bias_inner[0:1, units] += jnp.sum(pre.astype(F32), axis=0, keepdims=True)

    at.bias_inner[...] = jnp.zeros_like(at.bias_inner)
    inner_grad(own_rows)
    got_rows(1, at.grad_outer)

    def line_of(index):
        half = index // 2
        start = r.pair * (1 - half) + r.z * half
        return (start + 2 * ((index + 1) // 2 % 2)) % LINE

    def send_lines(i, index, line):
        pl.when(index < 2)(lambda: scatter_two.begin_far(i, line))
        pl.when(index >= 2)(lambda: scatter_two.begin_near(i, line))

    def outer_weight(index):
        line = line_of(index)
        grad = dot(at.active[:, aligned(line, 384)], at.grad_outer[...], 0, 0)
        at.grad_2[line] = low(grad).reshape(4, 96, 768)
        send_lines(1, index, line)

    loop(4, outer_weight)

    inner_grad(other_rows)
    at.sums[8:9, :] = at.bias_inner[0:1, 0:768]
    at.sums[9:10, :] = at.bias_inner[0:1, 768:1536]

    def first_part(rows_at, part):
        weight = at.gat_1[2 * part : 2 * part + 2].reshape(384, 1536)
        return dot(at.grad_pre[rows_at, :], weight, 1, 1)

    come_grad_first = []
    for part in range(2):
        piece = pl.ds(384 * part, 384)
        at.part_send2[:, piece] = low(first_part(other_rows, part))
        come_grad_first.append(
            swap((13, 25)[part], at.part_send2.at[:, piece], at.part_recv2.at[:, piece])
        )
    def inner_weight(index):
        line = line_of(index)
        grad = dot(at.first_turned[aligned(line, 192), :], at.grad_pre[...])
        at.grad_1[line] = low(grad).reshape(4, 48, 1536)
        send_lines(0, index, line)

    loop(4, inner_weight)
    for part in range(2):
        at.wide[:, 384 * part : 384 * part + 384] = first_part(own_rows, part)
    for copy in come_grad_first:
        copy.wait_recv()

    def first_norm_back(index):
        piece = aligned(index, 64)
        token_rows = pl.ds(pl.multiple_of(core * 256 + index * 64, 64), 64)
        upstream = at.wide[piece, :] + at.part_recv2[piece, :].astype(F32) + at.grad_sum[piece, :]
        normed = at.first_normed[piece, :]
        grad = norm_pull(upstream, normed, at.first_inverse[piece, 0:1], vector(3))
        at.grad_sum[piece, :] = grad
        rounded = low(grad)
        at.grad_att[token_rows, :] = rounded
        give_rows(2, index, at.grad_att).start()
        at.sums[2:3, :] += jnp.sum(rounded.astype(F32), axis=0, keepdims=True)
        at.sums[3:4, :] += jnp.sum(upstream * normed, axis=0, keepdims=True)
        at.sums[4:5, :] += jnp.sum(upstream, axis=0, keepdims=True)

    loop(4, first_norm_back)
    out_rows = pl.ds(pl.multiple_of(2 * core, 2), 2)

    def context_rows(rows_at):
        weight_0 = at.out_all[0, out_rows].reshape(384, 384)
        weight_1 = at.out_all[1, out_rows].reshape(384, 384)
        at.grad_context[rows_at, :] = low(
            dot(at.grad_att[rows_at, 0:384], weight_0, 1, 1)
            + dot(at.grad_att[rows_at, 384:768], weight_1, 1, 1)
        )

    context_rows(own_rows)
    got_rows(2, at.grad_att)
    context_rows(other_rows)
    scatter_two.corners(1)
    scatter_two.along_far(1)
    for part in range(2):
        grad = dot(at.context[part], at.grad_att[:, aligned(core, 384)], 0, 0)
        at.grad_o[2 * part : 2 * part + 2] = low(grad).reshape(2, 4, 48, 384)

    at.near_grad[...] = jnp.zeros_like(at.near_grad)
    at.far_grad[...] = jnp.zeros_like(at.far_grad)
    room = jnp.zeros((128, 128), BF16)

    def spread(value, start):
        wide = jnp.concatenate([value, room], axis=1)
        return pltpu.roll(wide, start, 1, stride=1, stride_axis=0)

    heads = [low((lanes == which).astype(F32)) for which in range(2)]

    def lanes_of(index, place):
        return pl.ds(pl.multiple_of(384 * place + index * 128, 128), 128)

    def masked(value):
        return [value * only for only in heads]

    def backward_queries(index):
        pair = aligned(index, 128)
        flip = at.flip[...]
        keys = masked(at.kvq[:, lanes_of(index, 0)])
        values = at.kvq[:, lanes_of(index, 1)]
        for block in range(4):
            piece = pl.ds(128 * block, 128)
            window = pl.ds(384 - 128 * block, 640)
            back = pl.ds(384 - 128 * block, 128)
            grad_context = low(dot(flip, at.grad_context[piece, pair]))
            query = low(dot(flip, at.kvq[piece, lanes_of(index, 2)]))
            at.turned_grad[piece, :] = grad_context
            at.turned_query[back, :] = query
            table = masked(at.near_rows[window, pair])
            near, grad = [], 0.0
            for which, context_only in enumerate(masked(grad_context)):
                soft = at.soft[2 * index + which, piece, :].astype(F32)
                grad_soft = dot(context_only, values, 1, 1)
                inner = jnp.sum(soft * grad_soft, axis=-1, keepdims=True)
                grad_low = low(soft * (grad_soft - inner) * score_scale)
                at.grad_low[which, back, :] = grad_low
                near.append(spread(grad_low, 1))
                grad = grad + dot(grad_low, keys[which]) + dot(near[which], table[which])
            at.grad_kvq[piece, lanes_of(index, 2)] = low(dot(flip, low(grad)))
            at.near_grad[window, pair] += dot(
                jnp.concatenate(near, axis=0), jnp.concatenate(masked(query), axis=0), 0, 0
            )

    def backward_keys(index):
        pair = aligned(index, 128)
        queries = masked(at.turned_query[...])
        contexts = masked(at.turned_grad[...])
        for block in range(4):
            piece = pl.ds(128 * block, 128)
            window = pl.ds(128 * block, 640)
            table = masked(at.far_natural[window, pair])
            far, grad, grad_value = [], 0.0, 0.0
            for which in range(2):
                turned = at.grad_low[which, :, piece].T
                far.append(spread(turned, 0))
                grad = grad + dot(turned, queries[which]) + dot(far[which], table[which])
                weights = at.soft[2 * index + which, :, piece]
                grad_value = grad_value + dot(weights, contexts[which], 0, 0)
            at.grad_kvq[piece, lanes_of(index, 0)] = low(grad)
            at.grad_kvq[piece, lanes_of(index, 1)] = low(grad_value)
            keys = masked(at.kvq[piece, lanes_of(index, 0)])
            at.far_grad[window, pair] += dot(
                jnp.concatenate(far, axis=0), jnp.concatenate(keys, axis=0), 0, 0
            )

    def shape_weight(value):
        return low(value).reshape(LINE, 4, 48, value.shape[-1])

    def rel_pair(index):
        pair = aligned(index, 128)
        at.key_rel[:, pair] = low(dot(at.one_hot[...], low(at.near_grad[256:768, pair])))
        at.query_rel[:, pair] = low(dot(at.one_natural[...], low(at.far_grad[256:768, pair])))

    def weights_pair(index):
        pair = aligned(index, 128)
        tokens = jnp.concatenate(
            [at.grad_kvq[:, lanes_of(index, place)] for place in (0, 2, 1)], axis=1
        )
        grad = dot(at.x_turned[...], tokens)
        rel = jnp.concatenate([at.key_rel[:, pair], at.query_rel[:, pair]], axis=1)
        table = dot(rows(at.table_all[0]), rel[0:256]) + dot(rows(at.table_all[1]), rel[256:512])
        at.grad_p[index, :, :, :, 0:256] = shape_weight(grad[:, 0:256] + table)
        at.grad_p[index, :, :, :, 256:384] = shape_weight(grad[:, 256:384])

    def table_half(which):
        piece = aligned(which, 256)
        return dot(rows(at.gat_b[:, :, :, 0:384]), at.query_rel[piece, :], 1, 1) + dot(
            rows(at.gat_a[:, :, :, 0:384]), at.key_rel[piece, :], 1, 1
        )

    def at_step(step, when, *moves):
        @pl.when(step == when)
        def _():
            for move in moves:
                move()

    def swap_table():
        return remote(
            at.table_send, at.table_recv, at.swap_send.at[15], at.swap_recv.at[15], r.partner
        )

    def send_table():
        at.table_send[...] = shape_weight(table_half(other))
        swap_table().start()

    def backward_pair(index):
        backward_queries(index)
        at_step(index, 2, lambda: scatter_two.turn(0), lambda: scatter_two.turn(1))
        backward_keys(index)
        at_step(index, 0, lambda: scatter_two.corners(0))
        at_step(index, 1, lambda: scatter_a.corners(0), lambda: scatter_two.along_far(0))
        at_step(index, 2, lambda: scatter_a.along_far(0))
        rel_pair(index)
        at_step(index, 2, send_table)
        weights_pair(index)
        at_step(index, 0, lambda: scatter_a.begin(0), lambda: scatter_a.begin(1))
        at_step(index, 1, lambda: scatter_b.begin(0), lambda: scatter_a.corners(1))
        at_step(index, 2, lambda: scatter_b.begin(1))

    loop(3, backward_pair)
    scatter_b.corners(0)
    scatter_a.along_far(1)

    own_table = table_half(core)
    come_part = swap_table()
    waiting.append(come_part)
    come_part.wait_recv()
    own_table = own_table + rows(at.table_recv[...]).astype(F32)
    for part in range(2):
        at.grad_t[part] = shape_weight(own_table[:, 128 * part : 128 * part + 128])
        scatter_c.begin(part)
    scatter_a.turn(0)

    at.sums[0:1, vector_half] = jnp.sum(
        at.grad_kvq[:, 768:1152].astype(F32), axis=0, keepdims=True
    ) + jnp.sum(at.far_grad[256:768, :], axis=0, keepdims=True)
    at.sums[1:2, vector_half] = jnp.sum(
        at.grad_kvq[:, 384:768].astype(F32), axis=0, keepdims=True
    )

    def exchange(stage, source, device):
        return remote(
            source, at.sums_come.at[stage], at.sums_send.at[stage], at.sums_recv.at[stage], device
        )

    stage_copies = [exchange(0, at.sums, r.partner)]
    stage_copies[0].start()

    def input_part(rows_at, part):
        weight_a = at.gat_a[2 * part : 2 * part + 2].reshape(384, 768)
        weight_b = at.gat_b[2 * part : 2 * part + 2, :, :, 0:384].reshape(384, 384)
        return dot(at.grad_kvq[rows_at, 0:768], weight_a, 1, 1) + dot(
            at.grad_kvq[rows_at, 768:1152], weight_b, 1, 1
        )

    for copy in come_outer:
        copy.wait_send()
    come_input = []
    for part in range(2):
        piece = pl.ds(384 * part, 384)
        at.part_send[:, piece] = low(input_part(other_rows, part))
        come_input.append(swap((16, 26)[part], at.part_send.at[:, piece], at.part_recv.at[:, piece]))

    stage_copies[0].wait_recv()
    lines = lax.broadcasted_iota(jnp.int32, (16, 1), 0)
    shared = jnp.where((lines == 8) | (lines == 9), 0.0, at.sums_come[0])
    at.sums_step[0] = at.sums[...] + shared
    stage_copies.append(exchange(1, at.sums_step.at[0], r.at_x))
    stage_copies[1].start()
    scatter_b.corners(1)
    scatter_a.turn(1)
    scatter_b.along_far(0)
    for part in range(2):
        at.wide[:, 384 * part : 384 * part + 384] = input_part(own_rows, part)
    for copy in come_input:
        copy.wait_recv()
    at.input_grad[...] = low(at.grad_sum[...] + at.wide[...] + at.part_recv[...].astype(F32))
    for part in range(2):
        scatter_c.corners(part)
    for part in range(2):
        scatter_two.along_near(part)
    stage_copies[1].wait_recv()
    at.sums_step[1] = at.sums_step[0] + at.sums_come[1]
    stage_copies.append(exchange(2, at.sums_step.at[1], r.at_y))
    stage_copies[2].start()
    at.give_1[...] = scatter_two.total(0).reshape(2, 24, 1536)
    swap(17, at.give_1.at[other], at.d_inner.at[core])
    at.d_inner[core] = at.give_1[core]
    scatter_b.along_far(1)
    at.d_outer[...] = scatter_two.total(1)
    scatter_b.turn(0)
    scatter_c.along_far(0)
    scatter_a.along_near(0)
    scatter_c.along_far(1)
    scatter_a.along_near(1)
    stage_copies[2].wait_recv()
    at.sums_step[2] = at.sums_step[1] + at.sums_come[2]
    for step in range(1, LINE):
        copy = exchange(2 + step, at.sums_step.at[2], r.at_line(r.ahead(step)))
        copy.start()
        stage_copies.append(copy)

    def give(slot, source, start, width, out):
        swap(slot, source.at[other, :, pl.ds(start, width)], out.at[:, aligned(core, width)])
        out[:, aligned(core, width)] = source[core, :, start : start + width]

    def give_pair(index, total):
        for place in range(3):
            start = 384 * place + 128 * index
            at.give_p[:, :, start : start + 128] = total[:, 128 * place : 128 * place + 128].reshape(
                2, 24, 128
            )

    at.give_o[...] = scatter_a.total(0).reshape(2, 24, 384)
    give(21, at.give_o, 0, 384, at.d_output)
    scatter_b.turn(1)
    for part in range(2):
        scatter_c.turn(part)
    give_pair(0, scatter_a.total(1))
    for user in (scatter_b, scatter_c):
        for part in range(2):
            user.along_near(part)
    give_pair(1, scatter_b.total(0))
    give_pair(2, scatter_b.total(1))
    give(18, at.give_p, 0, 384, at.d_key)
    give(19, at.give_p, 384, 384, at.d_query)
    give(20, at.give_p, 768, 384, at.d_value)
    for part in range(2):
        at.give_t[:, :, 128 * part : 128 * part + 128] = scatter_c.total(part).reshape(2, 24, 128)
    give(22, at.give_t, 0, 256, at.d_table)
    for copy in stage_copies[3:]:
        copy.wait_recv()
    at.vector_grads[...] = (
        at.sums_step[2] + at.sums_come[3] + at.sums_come[4] + at.sums_come[5]
    )
    for copy in waiting[-6:]:
        copy.wait_recv()
    for copy in waiting:
        if all(copy is not early for early in come_outer):
            copy.wait_send()
    for copy in stage_copies:
        copy.wait_send()
    for kind, array in enumerate((at.first_low, at.grad_outer, at.grad_att)):
        for index in range(4):
            give_rows(kind, index, array).wait_send()
    for index in range(3):
        remote(
            at.context.at[core, :, pl.ds(128 * index, 128)],
            at.context.at[core, :, pl.ds(128 * index, 128)],
            at.context_send.at[index],
            at.context_recv.at[index],
            r.partner,
        ).wait_send()
    for user in (gather_one, gather_two, gather_three, scatter_two, scatter_a, scatter_b, scatter_c):
        user.sent()


def finish_kernel(names, *refs):
    at = type("Refs", (), dict(zip(names, refs)))
    chip, core = lax.axis_index("fsdp"), lax.axis_index("seq")
    at.result_out[...] = at.result[...]
    at.input_grad_out[...] = at.input_grad[...]
    at.query_w_out[...] = at.d_query[...]
    at.key_w_out[...] = at.d_key[...]
    at.value_w_out[...] = at.d_value[...]
    at.output_w_out[...] = at.d_output[...]
    at.table_out[...] = at.d_table[...]
    at.outer_w_out[...] = at.d_outer[...]
    for group in range(4 * LINE):
        for which in range(2):
            device = 2 * group + which
            at.inner_w_out[:, 96 * device : 96 * device + 96] = at.d_inner[
                which, :, 96 * group : 96 * group + 96
            ]
    sums = at.vector_grads[...]
    own = pltpu.roll(sums, (768 - 24 * (2 * chip + core)) % 768, 1)
    small_outs = (
        at.query_b_out, at.value_b_out, at.output_b_out, at.gain_1_out, at.shift_1_out,
        at.outer_b_out, at.gain_2_out, at.shift_2_out,
    )
    for index, out in enumerate(small_outs):
        out[...] = own[index : index + 1, 0:24]
    units = jnp.where(chip < 2 * LINE, sums[8:9], sums[9:10])
    units = jnp.broadcast_to(units, (8, 768))
    at.inner_b_out[...] = pltpu.roll(units, (768 - 96 * (chip % (2 * LINE))) % 768, 1)[0:1, 0:96]
    at.count_out[...] = sums[10:11, 0:1].astype(jnp.int32)


OUTPUTS = dict(
    result=((256, 768), BF16),
    input_grad=((256, 768), BF16),
    d_query=((24, 768), F32),
    d_key=((24, 768), F32),
    d_value=((24, 768), F32),
    d_output=((24, 768), F32),
    d_table=((24, 512), F32),
    d_inner=((2, 24, 1536), F32),
    d_outer=((96, 768), F32),
    vector_grads=((16, 768), F32),
)
FINALS = dict(
    result_out=((256, 768), BF16),
    input_grad_out=((256, 768), BF16),
    query_w_out=((24, 768), F32),
    key_w_out=((24, 768), F32),
    value_w_out=((24, 768), F32),
    output_w_out=((24, 768), F32),
    table_out=((24, 512), F32),
    inner_w_out=((24, 3072), F32),
    outer_w_out=((96, 768), F32),
    query_b_out=((1, 24), F32),
    value_b_out=((1, 24), F32),
    output_b_out=((1, 24), F32),
    gain_1_out=((1, 24), F32),
    shift_1_out=((1, 24), F32),
    outer_b_out=((1, 24), F32),
    gain_2_out=((1, 24), F32),
    shift_2_out=((1, 24), F32),
    inner_b_out=((1, 96), F32),
    count_out=((1, 1), jnp.int32),
)
LINE = 4
BLOCKS = (LINE, 4, 48)
SCRATCH = dict(
    small_wide=((16, 128), F32),
    small=((16, 128), BF16),
    inner_pair=((2, 24, 1536), BF16),
    segment_row=((8, 512), F32),
    segment_col=((512, 128), F32),
    come_a=((24, 768), BF16),
    come_b=((24, 1024), BF16),
    come_s=((16, 128), BF16),
    come_1=((24, 1536), BF16),
    gat_a=(BLOCKS + (768,), BF16),
    gat_b=(BLOCKS + (1024,), BF16),
    gat_s=((LINE, 4, 2, 16, 128), BF16),
    gat_1=(BLOCKS + (1536,), BF16),
    gat_2=((LINE, 4, 96, 768), BF16),
    x_all=((512, 768), BF16),
    x_turned=((768, 512), BF16),
    one_hot=((512, 512), BF16),
    flip=((128, 128), BF16),
    near_rows=((1024, 384), BF16),
    far_rows=((1024, 384), BF16),
    far_natural=((1024, 384), BF16),
    one_natural=((512, 512), BF16),
    near_grad=((1024, 384), F32),
    far_grad=((1024, 384), F32),
    key_rel=((512, 384), BF16),
    query_rel=((512, 384), BF16),
    table_all=((2,) + BLOCKS + (256,), BF16),
    out_all=((2,) + BLOCKS + (384,), BF16),
    vectors=((8, 768), F32),
    inner_bias=((8, 1536), F32),
    bias_inner=((8, 1536), F32),
    kvq=((512, 1152), BF16),
    grad_kvq=((512, 1152), BF16),
    far_scores=((512, 512), F32),
    grad_low=((2, 512, 512), BF16),
    turned_query=((512, 128), BF16),
    turned_grad=((512, 128), BF16),
    soft=((6, 512, 512), BF16),
    context=((2, 512, 384), BF16),
    grad_context=((512, 384), BF16),
    wide=((256, 768), F32),
    first_out=((256, 768), F32),
    first_normed=((256, 768), F32),
    first_inverse=((256, 128), F32),
    first_low=((512, 768), BF16),
    first_turned=((768, 512), BF16),
    active=((512, 1536), BF16),
    slope=((512, 1536), F32),
    grad_pre=((512, 1536), BF16),
    part_send=((256, 768), BF16),
    part_recv=((256, 768), BF16),
    part_send2=((256, 768), BF16),
    part_recv2=((256, 768), BF16),
    grad_sum=((256, 768), F32),
    grad_outer=((512, 768), BF16),
    grad_att=((512, 768), BF16),
    table_send=(BLOCKS + (256,), BF16),
    table_recv=(BLOCKS + (256,), BF16),
    sums=((16, 768), F32),
    sums_step=((3, 16, 768), F32),
    sums_come=((6, 16, 768), F32),
    grad_1=(BLOCKS + (1536,), BF16),
    grad_2=((LINE, 4, 96, 768), BF16),
    grad_o=(BLOCKS + (384,), BF16),
    grad_p=((3,) + BLOCKS + (384,), BF16),
    grad_t=((2,) + BLOCKS + (128,), BF16),
    give_1=((2, 24, 1536), F32),
    give_o=((2, 24, 384), F32),
    give_p=((2, 24, 1152), F32),
    give_t=((2, 24, 256), F32),
)
ROOMS = dict(pair_=2, first_=LINE, corner_=2, second_=LINE, line_=LINE)
BLOCK = {
    "1": (48, 1536), "2": (96, 768), "o": (48, 384), "p0": (48, 384), "p1": (48, 384),
    "p2": (48, 384), "t0": (48, 128), "t1": (48, 128),
}
for tag, block in BLOCK.items():
    for kind, count in ROOMS.items():
        SCRATCH[kind + tag] = ((count,) + block, BF16)
SEMAPHORES = dict(
    swap_send=(27,),
    swap_recv=(27,),
    row_send=(3, 4),
    row_recv=(3, 4),
    here=(2,),
    context_send=(3,),
    context_recv=(3,),
    ga_send=(3, 6, LINE),
    ga_recv=(3, 6, LINE),
    gf_send=(2, 6, LINE),
    gf_recv=(2, 6, LINE),
    gg_send=(2, 6, LINE),
    gg_recv=(2, 6, LINE),
    sf_send=(2, 5, LINE),
    sf_recv=(2, 5, LINE),
    sa_send=(2, 5, LINE),
    sa_recv=(2, 5, LINE),
    sb_send=(2, 5, LINE),
    sb_recv=(2, 5, LINE),
    sc_send=(2, 5, LINE),
    sc_recv=(2, 5, LINE),
    sums_send=(6,),
    sums_recv=(6,),
)


def block_shards(
    hidden_in,
    query_weight,
    query_bias,
    key_weight,
    value_weight,
    value_bias,
    output_weight,
    output_bias,
    first_gain,
    first_shift,
    inner_weight,
    inner_bias,
    outer_weight,
    outer_bias,
    second_gain,
    second_shift,
    relative_table,
    segments,
    buckets,
    predicted,
    labels,
    cotangent,
):
    inputs = dict(
        hidden=hidden_in[0],
        query_w=query_weight,
        key_w=key_weight,
        value_w=value_weight,
        output_w=output_weight,
        table_t=relative_table.T,
        inner_w=inner_weight,
        outer_w=outer_weight,
        query_b=query_bias[None],
        value_b=value_bias[None],
        output_b=output_bias[None],
        gain_1=first_gain[None],
        shift_1=first_shift[None],
        outer_b=outer_bias[None],
        gain_2=second_gain[None],
        shift_2=second_shift[None],
        inner_b=inner_bias[None],
        segments=segments,
        buckets=buckets[None],
        predicted=predicted,
        labels=labels,
        cotangent=cotangent[0],
    )
    names = tuple(inputs) + tuple(OUTPUTS) + tuple(SCRATCH) + tuple(SEMAPHORES)
    vmem = pl.BlockSpec(memory_space=pltpu.VMEM)
    outs = pl.pallas_call(
        partial(layer_kernel, names),
        name="layer",
        out_shape=tuple(jax.ShapeDtypeStruct(*out) for out in OUTPUTS.values()),
        in_specs=[vmem] * len(inputs),
        out_specs=(vmem,) * len(OUTPUTS),
        scratch_shapes=[pltpu.VMEM(*spec) for spec in SCRATCH.values()]
        + [pltpu.SemaphoreType.DMA(shape) for shape in SEMAPHORES.values()],
        compiler_params=pltpu.CompilerParams(
            collective_id=0, has_side_effects=True, vmem_limit_bytes=67043328
        ),
    )(*inputs.values())
    finals = pl.pallas_call(
        partial(finish_kernel, tuple(OUTPUTS) + tuple(FINALS)),
        name="finish",
        out_shape=tuple(jax.ShapeDtypeStruct(*out) for out in FINALS.values()),
        in_specs=[vmem] * len(OUTPUTS),
        out_specs=(vmem,) * len(FINALS),
    )(*outs)
    got = type("Outs", (), dict(zip(FINALS, finals)))
    return (
        got.result_out[None],
        got.input_grad_out[None],
        got.query_w_out,
        got.query_b_out[0],
        got.key_w_out,
        got.value_w_out,
        got.value_b_out[0],
        got.output_w_out,
        got.output_b_out[0],
        got.gain_1_out[0],
        got.shift_1_out[0],
        got.inner_w_out,
        got.inner_b_out[0],
        got.outer_w_out,
        got.outer_b_out[0],
        got.gain_2_out[0],
        got.shift_2_out[0],
        got.table_out.T,
        got.count_out[0, 0],
    )


def fits(mesh):
    return mesh.shape["fsdp"] == 4 * LINE and mesh.shape["seq"] == 2


def solution(mesh):
    return jax.shard_map(
        block_shards if fits(mesh) else shards,
        mesh=mesh,
        in_specs=(
            P("fsdp", "seq", None),
            P(("fsdp", "seq"), None),
            P(("fsdp", "seq")),
            P(("fsdp", "seq"), None),
            P(("fsdp", "seq"), None),
            P(("fsdp", "seq")),
            P(("fsdp", "seq"), None),
            P(("fsdp", "seq")),
            P(("fsdp", "seq")),
            P(("fsdp", "seq")),
            P(("fsdp", "seq"), None),
            P(("fsdp", "seq")),
            P(("fsdp", "seq"), None),
            P(("fsdp", "seq")),
            P(("fsdp", "seq")),
            P(("fsdp", "seq")),
            P(None, ("fsdp", "seq")),
            P("fsdp", None),
            P(),
            P("fsdp", "seq"),
            P("fsdp", "seq"),
            P("fsdp", "seq", None),
        ),
        out_specs=(
            P("fsdp", "seq", None),
            P("fsdp", "seq", None),
            P(("fsdp", "seq"), None),
            P(("fsdp", "seq")),
            P(("fsdp", "seq"), None),
            P(("fsdp", "seq"), None),
            P(("fsdp", "seq")),
            P(("fsdp", "seq"), None),
            P(("fsdp", "seq")),
            P(("fsdp", "seq")),
            P(("fsdp", "seq")),
            P(("fsdp", "seq"), None),
            P(("fsdp", "seq")),
            P(("fsdp", "seq"), None),
            P(("fsdp", "seq")),
            P(("fsdp", "seq")),
            P(("fsdp", "seq")),
            P(None, ("fsdp", "seq")),
            P(),
        ),
        check_vma=False,
    )
```

```python
from functools import partial

import jax
import jax.numpy as jnp
import numpy as np
from jax import lax
from jax.experimental import pallas as pl
from jax.experimental.pallas import tpu as pltpu
from jax.sharding import PartitionSpec as P

HEAD = 64


EPSILON = 1e-07
NEGATIVE = -1e30


def matmul(spec, left, right):
    return jnp.einsum(spec, left, right, preferred_element_type=jnp.float32)


def precise(spec, left, right):
    return jnp.einsum(spec, left, right, precision=lax.Precision.HIGHEST)


def skew_rows(scores_in, offset, columns):
    leading = scores_in.shape[:-2]
    row_count = scores_in.shape[-2]
    breadth = scores_in.shape[-1]
    flattened = scores_in.reshape(leading + (row_count * breadth,))
    flattened = jnp.concatenate(
        [flattened, jnp.zeros(leading + (2 * breadth,), scores_in.dtype)], axis=-1
    )
    selected = lax.dynamic_slice_in_dim(flattened, offset, row_count * (breadth - 1), len(leading))
    return selected.reshape(leading + (row_count, breadth - 1))[..., :columns]


def unskew_rows(values, offset, breadth):
    leading = values.shape[:-2]
    row_count = values.shape[-2]
    columns = values.shape[-1]
    padded = jnp.concatenate(
        [values, jnp.zeros(leading + (row_count, breadth - 1 - columns), values.dtype)], axis=-1
    )
    flattened = padded.reshape(leading + (row_count * (breadth - 1),))
    zero_room = jnp.zeros(leading + (row_count * breadth + 2 * breadth,), values.dtype)
    placed = lax.dynamic_update_slice_in_dim(zero_room, flattened, offset, len(leading))
    return placed[..., : row_count * breadth].reshape(leading + (row_count, breadth))


def layer_norm(values, gain, shift):
    average = jnp.mean(values, axis=-1, keepdims=True)
    centred = values - average
    variance = jnp.mean(centred * centred, axis=-1, keepdims=True)
    inverse = lax.rsqrt(variance + EPSILON)
    normed = centred * inverse
    return (normed * gain + shift, normed, inverse)


def norm_backward(upstream, normed, inverse, gain):
    scaled_up = upstream * gain
    first_mean = jnp.mean(scaled_up, axis=-1, keepdims=True)
    second_mean = jnp.mean(scaled_up * normed, axis=-1, keepdims=True)
    grad_in = inverse * (scaled_up - first_mean - normed * second_mean)
    return (grad_in, jnp.sum(upstream * normed, axis=0), jnp.sum(upstream, axis=0))


def shards(
    hidden_in,
    query_weight,
    query_bias,
    key_weight,
    value_weight,
    value_bias,
    output_weight,
    output_bias,
    first_gain,
    first_shift,
    inner_weight,
    inner_bias,
    outer_weight,
    outer_bias,
    second_gain,
    second_shift,
    relative_table,
    segments,
    buckets,
    predicted,
    labels,
    cotangent,
):
    row_count, window, model_width = hidden_in.shape
    length = segments.shape[1]
    distances = 2 * length - 1
    span = window + length - 1
    pair_width = 2 * HEAD
    pair_count = model_width // pair_width
    score_scale = (3.0 * HEAD) ** (-0.5)
    window_start = lax.axis_index("seq") * window
    near_start = length - window - window_start
    token_count = row_count * window
    attention_set = (
        lax.all_gather(query_weight, ("fsdp", "seq"), axis=0, tiled=True),
        lax.all_gather(query_bias, ("fsdp", "seq"), axis=0, tiled=True),
        lax.all_gather(key_weight, ("fsdp", "seq"), axis=0, tiled=True),
        lax.all_gather(value_weight, ("fsdp", "seq"), axis=0, tiled=True),
        lax.all_gather(value_bias, ("fsdp", "seq"), axis=0, tiled=True),
        lax.all_gather(output_weight, ("fsdp", "seq"), axis=0, tiled=True),
        lax.all_gather(output_bias, ("fsdp", "seq"), axis=0, tiled=True),
        lax.all_gather(first_gain, ("fsdp", "seq"), axis=0, tiled=True),
        lax.all_gather(first_shift, ("fsdp", "seq"), axis=0, tiled=True),
        lax.all_gather(relative_table, ("fsdp", "seq"), axis=1, tiled=True),
    )
    feed_set = (
        lax.all_gather(inner_weight, ("fsdp", "seq"), axis=0, tiled=True),
        lax.all_gather(inner_bias, ("fsdp", "seq"), axis=0, tiled=True),
        lax.all_gather(outer_weight, ("fsdp", "seq"), axis=0, tiled=True),
        lax.all_gather(outer_bias, ("fsdp", "seq"), axis=0, tiled=True),
        lax.all_gather(second_gain, ("fsdp", "seq"), axis=0, tiled=True),
        lax.all_gather(second_shift, ("fsdp", "seq"), axis=0, tiled=True),
    )
    (
        query_matrix,
        query_offset,
        key_matrix,
        value_matrix,
        value_offset,
        output_matrix,
        output_offset,
        gain_first,
        shift_first,
        table_full,
    ) = attention_set
    inner_matrix, inner_offset, outer_matrix, outer_offset, gain_second, shift_second = feed_set
    tokens = hidden_in.reshape(token_count, model_width)
    queries = (
        (matmul("td,de->te", tokens, query_matrix) + query_offset.astype(jnp.float32))
        .astype(jnp.bfloat16)
        .reshape(row_count, window, model_width)
    )
    keys_own = (
        matmul("td,de->te", tokens, key_matrix)
        .astype(jnp.bfloat16)
        .reshape(row_count, window, model_width)
    )
    values_own = (
        (matmul("td,de->te", tokens, value_matrix) + value_offset.astype(jnp.float32))
        .astype(jnp.bfloat16)
        .reshape(row_count, window, model_width)
    )
    keys_all, values_all = (
        lax.all_gather(keys_own, "seq", axis=1, tiled=True),
        lax.all_gather(values_own, "seq", axis=1, tiled=True),
    )
    key_rel = matmul("pd,de->pe", table_full, key_matrix).astype(jnp.bfloat16)
    query_rel = (
        matmul("pd,de->pe", table_full, query_matrix) + query_offset.astype(jnp.float32)
    ).astype(jnp.bfloat16)
    reversed_buckets = buckets[::-1]
    table_rows = table_full.shape[0]
    one_hot = (
        reversed_buckets[:, None] == jnp.arange(table_rows, dtype=jnp.int32)[None, :]
    ).astype(jnp.bfloat16)
    bucket_keys = matmul("dp,pe->de", one_hot, key_rel).astype(jnp.bfloat16)
    bucket_queries = matmul("dp,pe->de", one_hot, query_rel).astype(jnp.bfloat16)
    near_keys = lax.dynamic_slice_in_dim(bucket_keys, near_start, span, 0)
    far_queries = lax.dynamic_slice_in_dim(bucket_queries, window_start, span, 0)
    segment_own = lax.dynamic_slice_in_dim(segments, window_start, window, 1)
    same_doc = (segment_own[:, :, None] == segments[:, None, :])[:, None]

    def pair_scores(pair_index):
        column = pair_index * pair_width
        query_pair = lax.dynamic_slice_in_dim(queries, column, pair_width, 2).reshape(
            row_count, window, 2, HEAD
        )
        key_pair = lax.dynamic_slice_in_dim(keys_all, column, pair_width, 2).reshape(
            row_count, length, 2, HEAD
        )
        value_pair = lax.dynamic_slice_in_dim(values_all, column, pair_width, 2).reshape(
            row_count, length, 2, HEAD
        )
        bucketkeys = lax.dynamic_slice_in_dim(near_keys, column, pair_width, 1).reshape(
            span, 2, HEAD
        )
        bucketqueries = lax.dynamic_slice_in_dim(far_queries, column, pair_width, 1).reshape(
            span, 2, HEAD
        )
        content = matmul("rihe,rjhe->rhij", query_pair, key_pair)
        near_scores = matmul("rihe,dhe->rhid", query_pair, bucketkeys)
        far_scores = matmul("rjhe,dhe->rhjd", key_pair, bucketqueries)
        to_position = skew_rows(near_scores, window - 1, length)
        from_position = jnp.swapaxes(skew_rows(far_scores, length - 1, window), 2, 3)
        summed = content + to_position + from_position
        masked = jnp.where(same_doc, summed * score_scale, NEGATIVE)
        return (masked, query_pair, key_pair, value_pair, bucketkeys, bucketqueries)

    def attend_pair(pair_index):
        masked, query_pair, key_pair, value_pair, bucketkeys, bucketqueries = pair_scores(
            pair_index
        )
        highest = jnp.max(masked, axis=-1, keepdims=True)
        expsum = jnp.exp(masked - highest)
        totals = jnp.sum(expsum, axis=-1, keepdims=True)
        weights_soft = (expsum / totals).astype(jnp.bfloat16)
        context_pair = matmul("rhij,rjhe->rihe", weights_soft, value_pair).astype(jnp.bfloat16)
        return (
            context_pair.reshape(row_count, window, pair_width),
            (highest + jnp.log(totals))[..., 0],
        )

    context_parts, log_totals = lax.map(attend_pair, jnp.arange(pair_count, dtype=jnp.int32))
    context = jnp.moveaxis(context_parts, 0, 2).reshape(token_count, model_width)
    attention_out = matmul("te,ed->td", context, output_matrix) + output_offset.astype(jnp.float32)
    residual_one = tokens.astype(jnp.float32) + attention_out
    first_out, first_normed, first_inverse = layer_norm(
        residual_one, gain_first.astype(jnp.float32), shift_first.astype(jnp.float32)
    )
    first_low = first_out.astype(jnp.bfloat16)
    inner_pre = matmul("td,df->tf", first_low, inner_matrix) + inner_offset.astype(jnp.float32)
    activated = jax.nn.gelu(inner_pre, approximate=False).astype(jnp.bfloat16)
    outer_out = matmul("tf,fd->td", activated, outer_matrix) + outer_offset.astype(jnp.float32)
    final_out, final_normed, final_inverse = layer_norm(
        first_out + outer_out, gain_second.astype(jnp.float32), shift_second.astype(jnp.float32)
    )
    result = final_out.astype(jnp.bfloat16).reshape(row_count, window, model_width)
    correct_count = lax.psum(jnp.sum((predicted == labels).astype(jnp.int32)), ("fsdp", "seq"))
    regathered = attention_set + feed_set
    (
        query_back,
        query_offset_back,
        key_back,
        value_back,
        value_offset_back,
        output_back,
        output_offset_back,
        gain_first_back,
        shift_first_back,
        table_back,
        inner_back,
        inner_offset_back,
        outer_back,
        outer_offset_back,
        gain_second_back,
        shift_second_back,
    ) = regathered
    upstream = cotangent.reshape(token_count, model_width).astype(jnp.float32)
    grad_sum2, grad_gain2, grad_shift2 = norm_backward(
        upstream, final_normed, final_inverse, gain_second_back.astype(jnp.float32)
    )
    grad_outer = grad_sum2.astype(jnp.bfloat16)
    outer_bias_part = jnp.sum(grad_outer.astype(jnp.float32), axis=0)
    outer_weight_part = matmul("tf,td->fd", activated, grad_outer)
    grad_act = matmul("td,fd->tf", grad_outer, outer_back).astype(jnp.bfloat16)
    _, gelu_back = jax.vjp(partial(jax.nn.gelu, approximate=False), inner_pre)
    grad_inner = gelu_back(grad_act.astype(jnp.float32))[0].astype(jnp.bfloat16)
    inner_bias_part = jnp.sum(grad_inner.astype(jnp.float32), axis=0)
    inner_weight_part = matmul("td,tf->df", first_low, grad_inner)
    grad_first = matmul("tf,df->td", grad_inner, inner_back) + grad_sum2
    feed_grads = (
        lax.psum_scatter(inner_weight_part, ("fsdp", "seq"), scatter_dimension=0, tiled=True),
        lax.psum_scatter(inner_bias_part, ("fsdp", "seq"), scatter_dimension=0, tiled=True),
        lax.psum_scatter(outer_weight_part, ("fsdp", "seq"), scatter_dimension=0, tiled=True),
        lax.psum_scatter(outer_bias_part, ("fsdp", "seq"), scatter_dimension=0, tiled=True),
        lax.psum_scatter(grad_gain2, ("fsdp", "seq"), scatter_dimension=0, tiled=True),
        lax.psum_scatter(grad_shift2, ("fsdp", "seq"), scatter_dimension=0, tiled=True),
    )
    grad_sum1, grad_gain1, grad_shift1 = norm_backward(
        grad_first, first_normed, first_inverse, gain_first_back.astype(jnp.float32)
    )
    grad_attention = grad_sum1.astype(jnp.bfloat16)
    output_bias_part = jnp.sum(grad_attention.astype(jnp.float32), axis=0)
    output_weight_part = matmul("te,td->ed", context, grad_attention)
    grad_context = (
        matmul("td,ed->te", grad_attention, output_back)
        .astype(jnp.bfloat16)
        .reshape(row_count, window, model_width)
    )

    def attend_back(pieces):
        pair_index, log_total = pieces
        masked, query_pair, key_pair, value_pair, bucketkeys, bucketqueries = pair_scores(
            pair_index
        )
        probability = jnp.exp(masked - log_total[..., None])
        grad_context_pair = lax.dynamic_slice_in_dim(
            grad_context, pair_index * pair_width, pair_width, 2
        ).reshape(row_count, window, 2, HEAD)
        grad_soft = matmul("rihe,rjhe->rhij", grad_context_pair, value_pair)
        grad_scores = probability * (
            grad_soft - jnp.sum(probability * grad_soft, axis=-1, keepdims=True)
        )
        grad_low = (grad_scores * score_scale).astype(jnp.bfloat16)
        grad_value = matmul("rhij,rihe->rjhe", probability.astype(jnp.bfloat16), grad_context_pair)
        grad_near = unskew_rows(grad_low, window - 1, span)
        grad_far = unskew_rows(jnp.swapaxes(grad_low, 2, 3), length - 1, span)
        grad_query = matmul("rhij,rjhe->rihe", grad_low, key_pair) + matmul(
            "rhid,dhe->rihe", grad_near, bucketkeys
        )
        grad_key = matmul("rhij,rihe->rjhe", grad_low, query_pair) + matmul(
            "rhjd,dhe->rjhe", grad_far, bucketqueries
        )
        grad_bkeys = matmul("rhid,rihe->dhe", grad_near, query_pair)
        grad_bqueries = matmul("rhjd,rjhe->dhe", grad_far, key_pair)
        return (
            grad_query.reshape(row_count, window, pair_width),
            grad_key.reshape(row_count, length, pair_width),
            grad_value.reshape(row_count, length, pair_width),
            grad_bkeys.reshape(span, pair_width),
            grad_bqueries.reshape(span, pair_width),
        )

    query_parts, key_parts, value_parts, bkey_parts, bquery_parts = lax.map(
        attend_back, (jnp.arange(pair_count, dtype=jnp.int32), log_totals)
    )
    grad_query_all = jnp.moveaxis(query_parts, 0, 2).reshape(token_count, model_width)
    grad_key_all = jnp.moveaxis(key_parts, 0, 2).reshape(row_count, length, model_width)
    grad_value_all = jnp.moveaxis(value_parts, 0, 2).reshape(row_count, length, model_width)
    near_grads = jnp.moveaxis(bkey_parts, 0, 1).reshape(span, model_width)
    far_grads = jnp.moveaxis(bquery_parts, 0, 1).reshape(span, model_width)
    grad_bucket_keys = lax.dynamic_update_slice_in_dim(
        jnp.zeros((distances, model_width), jnp.float32), near_grads, near_start, 0
    )
    grad_bucket_queries = lax.dynamic_update_slice_in_dim(
        jnp.zeros((distances, model_width), jnp.float32), far_grads, window_start, 0
    )
    key_grads, value_grads = (
        lax.psum_scatter(
            grad_key_all.astype(jnp.bfloat16), "seq", scatter_dimension=1, tiled=True
        ).astype(jnp.float32),
        lax.psum_scatter(
            grad_value_all.astype(jnp.bfloat16), "seq", scatter_dimension=1, tiled=True
        ).astype(jnp.float32),
    )
    query_low = grad_query_all.astype(jnp.bfloat16)
    key_low = key_grads.reshape(token_count, model_width).astype(jnp.bfloat16)
    value_low = value_grads.reshape(token_count, model_width).astype(jnp.bfloat16)
    grad_key_rel = jax.ops.segment_sum(grad_bucket_keys, reversed_buckets, num_segments=table_rows)
    grad_query_rel = jax.ops.segment_sum(
        grad_bucket_queries, reversed_buckets, num_segments=table_rows
    )
    query_token_part = matmul("td,te->de", tokens, query_low)
    query_bias_token = jnp.sum(query_low.astype(jnp.float32), axis=0)
    key_token_part = matmul("td,te->de", tokens, key_low)
    value_weight_part = matmul("td,te->de", tokens, value_low)
    value_bias_part = jnp.sum(value_low.astype(jnp.float32), axis=0)
    grad_input = (
        grad_sum1
        + matmul("te,de->td", query_low, query_back)
        + matmul("te,de->td", key_low, key_back)
        + matmul("te,de->td", value_low, value_back)
    )
    input_grad = grad_input.astype(jnp.bfloat16).reshape(row_count, window, model_width)
    key_rel_total, query_rel_total = lax.psum((grad_key_rel, grad_query_rel), ("fsdp", "seq"))
    attention_grads = (
        lax.psum_scatter(query_token_part, ("fsdp", "seq"), scatter_dimension=0, tiled=True),
        lax.psum_scatter(query_bias_token, ("fsdp", "seq"), scatter_dimension=0, tiled=True),
        lax.psum_scatter(key_token_part, ("fsdp", "seq"), scatter_dimension=0, tiled=True),
        lax.psum_scatter(value_weight_part, ("fsdp", "seq"), scatter_dimension=0, tiled=True),
        lax.psum_scatter(value_bias_part, ("fsdp", "seq"), scatter_dimension=0, tiled=True),
        lax.psum_scatter(output_weight_part, ("fsdp", "seq"), scatter_dimension=0, tiled=True),
        lax.psum_scatter(output_bias_part, ("fsdp", "seq"), scatter_dimension=0, tiled=True),
        lax.psum_scatter(grad_gain1, ("fsdp", "seq"), scatter_dimension=0, tiled=True),
        lax.psum_scatter(grad_shift1, ("fsdp", "seq"), scatter_dimension=0, tiled=True),
    )
    shard_rows = query_weight.shape[0]
    shard_start = lax.axis_index(("fsdp", "seq")) * shard_rows
    table_shard = relative_table.astype(jnp.float32)
    query_weight_grad = attention_grads[0] + precise("pd,pe->de", table_shard, query_rel_total)
    key_weight_grad = attention_grads[2] + precise("pd,pe->de", table_shard, key_rel_total)
    query_bias_grad = attention_grads[1] + jnp.sum(
        lax.dynamic_slice_in_dim(query_rel_total, shard_start, shard_rows, 1), axis=0
    )
    relative_table_grad = precise(
        "pe,de->pd", query_rel_total, query_weight.astype(jnp.float32)
    ) + precise("pe,de->pd", key_rel_total, key_weight.astype(jnp.float32))
    return (
        result,
        input_grad,
        query_weight_grad,
        query_bias_grad,
        key_weight_grad,
        attention_grads[3],
        attention_grads[4],
        attention_grads[5],
        attention_grads[6],
        attention_grads[7],
        attention_grads[8],
        feed_grads[0],
        feed_grads[1],
        feed_grads[2],
        feed_grads[3],
        feed_grads[4],
        feed_grads[5],
        relative_table_grad,
        correct_count,
    )


MESH = pl.DeviceIdType.MESH
F32 = jnp.float32
BF16 = jnp.bfloat16


def dot(left, right, left_dim=1, right_dim=0):
    return lax.dot_general(
        left, right, (((left_dim,), (right_dim,)), ((), ())), preferred_element_type=F32
    )


def low(value):
    return value.astype(BF16)


class Route:
    def __init__(self):
        chip = lax.axis_index("fsdp")
        self.core = lax.axis_index("seq")
        self.other = 1 - self.core
        self.chip = chip
        self.x = chip % 2
        self.y = (chip // 2) % 2
        self.z = chip // 4
        self.plane = chip % 4
        self.plane_x = self.plane + 1 - 2 * self.x
        self.plane_y = self.plane + 2 - 4 * self.y
        self.pair = self.z + 1 - 2 * (self.z % 2)
        self.near = (self.z, (self.z + 2) % LINE)
        self.far = (self.pair, (self.pair + 2) % LINE)
        self.soon = 1 + self.z % 2
        self.late = 3 - 3 * (self.z % 2)
        self.partner = (chip, self.other)
        self.at_x = (self.z * 4 + self.plane_x, self.core)
        self.at_y = (self.z * 4 + self.plane_y, self.core)

    def at_line(self, line):
        return (line * 4 + self.plane, self.core)

    def ahead(self, step):
        return (self.z + step) % LINE

    def behind(self, step):
        return (self.z + LINE - step) % LINE


def remote(source, target, send_sem, recv_sem, device):
    return pltpu.make_async_remote_copy(
        source, target, send_sem, recv_sem, device_id=device, device_id_type=MESH
    )


class Gather:
    def __init__(self, route, arrays, send, recv):
        self.r, self.arrays, self.send, self.recv = route, arrays, send, recv

    def copies(self, kind, line):
        r = self.r
        for i, array in enumerate(self.arrays):
            by_x = i == 1
            plane, device = (
                (r.plane, r.at_line((r.z + 1) % LINE)),
                (r.plane, r.at_line((r.z + LINE - 1) % LINE)),
                (r.plane, r.at_x),
                (r.plane, r.at_y),
                (r.plane_y, r.at_x) if by_x else (r.plane_x, r.at_y),
                (3 - r.plane, r.at_line(r.pair)),
            )[kind]
            block = array.at[line, plane]
            yield remote(
                block, block, self.send.at[i, kind, line], self.recv.at[i, kind, line], device
            )

    def begin(self, kind, line):
        for copy in self.copies(kind, line):
            copy.start()

    def got(self, kind, line):
        for copy in self.copies(kind, line):
            copy.wait_recv()

    def sides(self, line):
        self.begin(2, line)
        self.begin(3, line)

    def got_sides(self, line):
        self.got(2, line)
        self.got(3, line)

    def up(self, line):
        @pl.when(self.r.z < LINE - 1)
        def _():
            self.begin(0, line)

    def down(self, line):
        @pl.when(self.r.z > 0)
        def _():
            self.begin(1, line)

    def start_line(self):
        self.up(self.r.z)
        self.down(self.r.z)

    def start_sides(self):
        self.sides(self.r.z)

    def round(self, step):
        r = self.r

        @pl.when(r.z >= step)
        def _():
            self.got(0, r.z - step)
            self.up(r.z - step)

        @pl.when(r.z + step < LINE)
        def _():
            self.got(1, r.z + step)
            self.down(r.z + step)

    def first(self):
        self.corner(0)
        self.round(1)
        self.sides(self.r.soon)

    def second(self):
        self.round(2)
        self.sides(self.r.near[1])
        self.hand(0)

    def third(self):
        self.round(3)
        self.corner(1)
        self.sides(self.r.late)

    def corner(self, which):
        line = self.r.near[which]
        self.got_sides(line)
        self.begin(4, line)

    def hand(self, which):
        line = self.r.near[which]
        self.got(4, line)
        self.begin(5, line)

    def finish(self):
        for line in self.r.far:
            self.got_sides(line)
            self.got(5, line)

    def drained(self, kind, line):
        for copy in self.copies(kind, line):
            copy.wait_send()

    def sent(self):
        r = self.r
        for line in range(LINE):

            @pl.when((r.z < LINE - 1) & (r.z >= line))
            def _():
                self.drained(0, line)

            @pl.when((r.z > 0) & (r.z <= line))
            def _():
                self.drained(1, line)

            self.drained(2, line)
            self.drained(3, line)
        for line in r.near:
            self.drained(4, line)
            self.drained(5, line)


class Scatter:
    def __init__(self, route, arrays, rooms, send, recv):
        self.r, self.arrays, self.rooms = route, arrays, rooms
        self.send, self.recv = send, recv

    def across(self, i):
        return self.r.plane_y if i == 0 else self.r.plane_x

    def copy(self, i, kind, line):
        r = self.r
        near, across = (r.at_x, r.at_y) if i == 0 else (r.at_y, r.at_x)
        near_plane = r.plane_x if i == 0 else r.plane_y
        plane, room, device = (
            (3 - r.plane, line // 2, r.at_line(r.pair)),
            (near_plane, line, near),
            (3 - r.plane, line // 2, near),
            (self.across(i), line, across),
            (r.plane, r.z, r.at_line(line)),
        )[kind]
        return remote(
            self.arrays[i].at[line, plane],
            self.rooms[i][kind].at[room],
            self.send.at[i, kind, line],
            self.recv.at[i, kind, r.z if kind == 4 else line],
            device,
        )

    def got_along(self, i, line):
        r = self.r
        remote(
            self.arrays[i].at[line, r.plane],
            self.rooms[i][4].at[line],
            self.send.at[i, 4, line],
            self.recv.at[i, 4, line],
            r.at_line(line),
        ).wait_recv()

    def begin_far(self, i, line):
        for kind in (0, 1, 3):
            self.copy(i, kind, line).start()

    def begin_near(self, i, line):
        self.copy(i, 1, line).start()

    def begin(self, i):
        for line in self.r.far:
            self.begin_far(i, line)
        for line in self.r.near[::-1]:
            self.begin_near(i, line)

    def merge(self, i, line, plane, *came):
        at = self.arrays[i].at[line, plane]
        value = at[...].astype(F32)
        for kind, room in came:
            value = value + self.rooms[i][kind][room].astype(F32)
        at[...] = low(value)

    def corners(self, i):
        for line in self.r.near[::-1]:
            self.copy(i, 0, line).wait_recv()
            self.merge(i, line, 3 - self.r.plane, (0, line // 2))
            self.copy(i, 2, line).start()

    def turn(self, i):
        for line in self.r.near[::-1]:
            self.copy(i, 2, line).wait_recv()
            self.merge(i, line, self.across(i), (2, line // 2))
            self.copy(i, 3, line).start()

    def along(self, i, line):
        self.copy(i, 1, line).wait_recv()
        self.copy(i, 3, line).wait_recv()
        self.merge(i, line, self.r.plane, (1, line), (3, line))
        self.copy(i, 4, line).start()

    def along_far(self, i):
        for line in self.r.far:
            self.along(i, line)

    def along_near(self, i):
        self.along(i, self.r.near[1])

    def total(self, i):
        r = self.r
        self.copy(i, 1, r.z).wait_recv()
        self.copy(i, 3, r.z).wait_recv()
        rooms = self.rooms[i]
        value = self.arrays[i][r.z, r.plane].astype(F32)
        value = value + rooms[1][r.z].astype(F32) + rooms[3][r.z].astype(F32)
        for line in r.far + r.near[1:]:
            self.got_along(i, line)
            value = value + rooms[4][line].astype(F32)
        return value

    def sent(self):
        r = self.r
        for i in (0, 1):
            for line in range(LINE):
                self.copy(i, 1, line).wait_send()
                self.copy(i, 3, line).wait_send()
            for line in r.far:
                self.copy(i, 0, line).wait_send()
                self.copy(i, 4, line).wait_send()
            for line in r.near:
                self.copy(i, 2, line).wait_send()
            self.copy(i, 4, r.near[1]).wait_send()


def loop(count, body):
    def step(index, carry):
        body(index)
        return carry

    lax.fori_loop(0, count, step, 0)


def aligned(index, size):
    return pl.ds(pl.multiple_of(index * size, size), size)


def erf_parts(value):
    tail = lax.erf(value * np.float32(0.5**0.5))
    half = 0.5 * (1.0 + tail)
    density = jnp.exp(value * value * -0.5) * np.float32((2.0 * np.pi) ** -0.5)
    return value * half, half + value * density


def norm(values, gain, shift):
    average = jnp.mean(values, axis=-1, keepdims=True)
    centred = values - average
    variance = jnp.mean(centred * centred, axis=-1, keepdims=True)
    inverse = lax.rsqrt(variance + EPSILON)
    normed = centred * inverse
    return normed * gain + shift, normed, inverse


def norm_pull(upstream, normed, inverse, gain):
    scaled_up = upstream * gain
    first_mean = jnp.mean(scaled_up, axis=-1, keepdims=True)
    second_mean = jnp.mean(scaled_up * normed, axis=-1, keepdims=True)
    return inverse * (scaled_up - first_mean - normed * second_mean)


def layer_kernel(names, *refs):
    b = dict(zip(names, refs))
    at = type("Refs", (), b)
    r = Route()
    core, other = r.core, r.other
    own_rows = aligned(core, 256)
    other_rows = aligned(other, 256)
    score_scale = np.float32((3.0 * HEAD) ** (-0.5))

    barrier = pltpu.get_barrier_semaphore()
    friends = [r.partner, r.at_x, r.at_y] + [r.at_line(r.ahead(k)) for k in range(1, LINE)]
    for device in friends:
        pl.semaphore_signal(barrier, inc=1, device_id=device, device_id_type=MESH)

    def give_rows(kind, index, array):
        piece = pl.ds(pl.multiple_of(core * 256 + index * 64, 64), 64)
        return remote(
            array.at[piece],
            array.at[piece],
            at.row_send.at[kind, index],
            at.row_recv.at[kind, index],
            r.partner,
        )

    def got_rows(kind, array):
        for index in range(4):
            give_rows(kind, index, array).wait_recv()

    waiting = []

    def swap(slot, source, target):
        copy = remote(source, target, at.swap_send.at[slot], at.swap_recv.at[slot], r.partner)
        copy.start()
        waiting.append(copy)
        return copy

    gather_one = Gather(r, (at.gat_a, at.gat_b, at.gat_s), at.ga_send, at.ga_recv)
    def halves(array):
        width = array.shape[-1] // 2
        return [array.at[:, :, :, pl.ds(width * part, width)] for part in range(2)]

    gather_two = Gather(r, halves(at.gat_1), at.gf_send, at.gf_recv)
    gather_three = Gather(r, halves(at.gat_2), at.gg_send, at.gg_recv)

    at.sums[...] = jnp.zeros_like(at.sums)
    at.small_wide[...] = jnp.zeros_like(at.small_wide)
    small_rows = (
        at.query_b, at.value_b, at.output_b, at.gain_1, at.shift_1, at.outer_b, at.gain_2, at.shift_2,
        at.inner_b,
    )
    for index, row in enumerate(small_rows):
        at.small_wide[index : index + 1, 0 : row.shape[1]] = row[...].astype(F32)
    at.small[...] = low(at.small_wide[...])
    right = (at.predicted[...] == at.labels[...]).astype(F32)
    at.sums[10:11, :] = jnp.broadcast_to(jnp.sum(right, axis=1, keepdims=True), (1, 768))
    pl.semaphore_wait(barrier, len(friends))

    half = aligned(other, 384)
    arrive = [
        swap(0, at.key_w.at[:, half], at.come_a.at[:, pl.ds(0, 384)]),
        swap(1, at.value_w.at[:, half], at.come_a.at[:, pl.ds(384, 384)]),
        swap(2, at.query_w.at[:, half], at.come_b.at[:, pl.ds(0, 384)]),
        swap(3, at.output_w.at[:, half], at.come_b.at[:, pl.ds(384, 384)]),
        swap(4, at.table_t.at[:, aligned(other, 256)], at.come_b.at[:, pl.ds(768, 256)]),
        swap(5, at.small, at.come_s),
    ]
    come_x = swap(7, at.hidden, at.x_all.at[own_rows])
    place_x = pltpu.make_async_copy(at.hidden, at.x_all.at[own_rows], at.here.at[0])
    place_x.start()
    place_2 = pltpu.make_async_copy(at.outer_w, at.gat_2.at[r.z, r.plane], at.here.at[1])
    place_2.start()
    for copy in arrive:
        copy.wait_recv()

    def stack(mine, came):
        mine, came = mine.astype(F32), came.astype(F32)
        upper = jnp.where(core == 0, mine, came)
        lower = jnp.where(core == 0, came, mine)
        return low(jnp.concatenate([upper, lower], axis=0))

    mine_half = aligned(core, 384)
    at.gat_a[r.z, r.plane, :, 0:384] = stack(at.key_w[:, mine_half], at.come_a[:, 0:384])
    at.gat_a[r.z, r.plane, :, 384:768] = stack(at.value_w[:, mine_half], at.come_a[:, 384:768])
    at.gat_b[r.z, r.plane, :, 0:384] = stack(at.query_w[:, mine_half], at.come_b[:, 0:384])
    at.gat_b[r.z, r.plane, :, 384:768] = stack(at.output_w[:, mine_half], at.come_b[:, 384:768])
    at.gat_b[r.z, r.plane, :, 768:1024] = stack(
        at.table_t[:, aligned(core, 256)], at.come_b[:, 768:1024]
    )
    at.gat_s[r.z, r.plane, core] = at.small[...]
    at.gat_s[r.z, r.plane, other] = at.come_s[...]
    gather_one.start_line()
    gather_one.start_sides()
    for chip in range(4 * LINE):
        for which in range(2):
            device = 2 * chip + which
            at.inner_pair[which, :, 96 * chip : 96 * chip + 96] = at.inner_w[
                :, 96 * device : 96 * device + 96
            ]
    come_inner = swap(6, at.inner_pair.at[other], at.come_1)
    come_inner.wait_recv()
    at.gat_1[r.z, r.plane] = stack(at.inner_pair[core], at.come_1[...])
    place_2.wait()
    place_x.wait()
    come_x.wait_recv()
    at.x_turned[...] = at.x_all[...].T
    wide_i = lax.broadcasted_iota(jnp.int32, (512, 512), 0)
    wide_j = lax.broadcasted_iota(jnp.int32, (512, 512), 1)
    at.one_natural[...] = low((at.buckets[0:1, 256:768] == wide_i).astype(F32))
    at.one_hot[...] = low(dot(at.one_natural[...], low((wide_i + wide_j == 511).astype(F32))))
    segment_wide = jnp.broadcast_to(at.segments[...].astype(F32), (128, 512))
    at.segment_row[...] = segment_wide[0:8]
    at.segment_col[...] = segment_wide.T
    flip_i = lax.broadcasted_iota(jnp.int32, (128, 128), 0)
    flip_j = lax.broadcasted_iota(jnp.int32, (128, 128), 1)
    at.flip[...] = low((flip_i + flip_j == 127).astype(F32))
    for table in (at.near_rows, at.far_rows, at.far_natural):
        table[0:256, :] = jnp.zeros((256, 384), BF16)
        table[768:1024, :] = jnp.zeros((256, 384), BF16)
    at.near_grad[...] = jnp.zeros_like(at.near_grad)
    at.far_grad[...] = jnp.zeros_like(at.far_grad)
    gather_one.first()
    gather_one.second()
    gather_one.third()
    gather_two.start_sides()
    gather_three.start_sides()
    gather_one.hand(1)
    gather_two.start_line()
    gather_three.start_line()
    gather_one.finish()

    out_mine = at.gat_b.at[:, :, :, pl.ds(384, 384)]
    table_mine = at.gat_b.at[:, :, :, pl.ds(768, 256)]
    come_table = swap(8, table_mine, at.table_all.at[core])
    come_out = swap(9, out_mine, at.out_all.at[core])
    place_table = pltpu.make_async_copy(table_mine, at.table_all.at[core], at.here.at[0])
    place_table.start()
    place_out = pltpu.make_async_copy(out_mine, at.out_all.at[core], at.here.at[1])
    place_out.start()

    for line in range(LINE):
        for plane in range(4):
            chip = line * 4 + plane
            for which in range(2):
                device = 2 * chip + which
                tile = at.gat_s[line, plane, which].astype(F32)
                at.vectors[:, 24 * device : 24 * device + 24] = tile[0:8, 0:24]
            tile = at.gat_s[line, plane, core].astype(F32)
            at.inner_bias[0:1, 96 * chip : 96 * chip + 96] = tile[8:9, 0:96]

    def rows(value):
        return value.reshape(768, value.shape[-1])

    vector_half = aligned(core, 384)
    query_bias = at.vectors[0:1, vector_half]
    value_bias = at.vectors[1:2, vector_half]
    at.kvq[:, 0:384] = low(dot(at.x_all[...], rows(at.gat_a[:, :, :, 0:384])))
    at.kvq[:, 384:768] = low(dot(at.x_all[...], rows(at.gat_a[:, :, :, 384:768])) + value_bias)
    at.kvq[:, 768:1152] = low(dot(at.x_all[...], rows(at.gat_b[:, :, :, 0:384])) + query_bias)
    gather_two.first()
    place_table.wait()
    come_table.wait_recv()
    for part in range(2):
        piece = pl.ds(256 * part, 256)
        table = rows(at.table_all[part])
        at.key_rel[piece, :] = low(dot(table, rows(at.gat_a[:, :, :, 0:384]), 0, 0))
        at.query_rel[piece, :] = low(dot(table, rows(at.gat_b[:, :, :, 0:384]), 0, 0) + query_bias)
    at.near_rows[256:768, :] = low(dot(at.one_hot[...], at.key_rel[...], 0, 0))
    at.far_rows[256:768, :] = low(dot(at.one_hot[...], at.query_rel[...], 0, 0))
    at.far_natural[256:768, :] = low(dot(at.one_natural[...], at.query_rel[...], 0, 0))

    gather_three.first()

    lanes = lax.broadcasted_iota(jnp.int32, (1, 128), 1) // HEAD
    no_score = np.float32(NEGATIVE)

    def forward_head(head):
        pair = aligned(head // 2, 128)
        key_lanes = pl.ds(pl.multiple_of((head // 2) * 128, 128), 128)
        value_lanes = pl.ds(pl.multiple_of(384 + (head // 2) * 128, 128), 128)
        query_lanes = pl.ds(pl.multiple_of(768 + (head // 2) * 128, 128), 128)
        mine = lanes == head % 2
        only = low(mine.astype(F32))
        keys = at.kvq[:, key_lanes]
        values = at.kvq[:, value_lanes]
        for block in range(4):
            piece = pl.ds(128 * block, 128)
            shifted = dot(
                at.kvq[piece, key_lanes] * only, at.far_rows[pl.ds(384 - 128 * block, 640), pair], 1, 1
            )
            at.far_scores[piece, :] = pltpu.roll(shifted, 0, 1, stride=1, stride_axis=0)[:, 128:640]
        for block in range(4):
            piece = pl.ds(128 * block, 128)
            queries = at.kvq[piece, query_lanes] * only
            shifted = dot(queries, at.near_rows[pl.ds(384 - 128 * block, 640), pair], 1, 1)
            summed = (
                dot(queries, keys, 1, 1)
                + pltpu.roll(shifted, 0, 1, stride=1, stride_axis=0)[:, 128:640]
                + at.far_scores[:, piece].T
            )
            masked = jnp.where(
                at.segment_col[piece, 0:1] == at.segment_row[0:1, :], summed * score_scale, no_score
            )
            highest = jnp.max(masked, axis=-1, keepdims=True)
            expsum = jnp.exp(masked - highest)
            soft = expsum / jnp.sum(expsum, axis=-1, keepdims=True)
            rounded = low(soft)
            at.soft[head, piece, :] = low(dot(at.flip[...], rounded))
            context = dot(rounded, values)
            here = at.context.at[core, piece, pair]
            here[...] = low(jnp.where(mine, context, here[...].astype(F32)))

    def forward_pair(index):
        def forward(which):
            head = 2 * index + which
            forward_head(head)
            pl.when(head == 1)(gather_two.second)
            pl.when(head == 2)(gather_three.second)
            pl.when(head == 4)(gather_two.third)
            pl.when(head == 5)(gather_three.third)

        loop(2, forward)
        remote(
            at.context.at[core, :, aligned(index, 128)],
            at.context.at[core, :, aligned(index, 128)],
            at.context_send.at[index],
            at.context_recv.at[index],
            r.partner,
        ).start()

    loop(3, forward_pair)
    place_out.wait()
    come_out.wait_recv()
    for index in range(3):
        remote(
            at.context.at[other, :, pl.ds(128 * index, 128)],
            at.context.at[other, :, pl.ds(128 * index, 128)],
            at.context_send.at[index],
            at.context_recv.at[index],
            r.partner,
        ).wait_recv()

    def vector(index):
        return at.vectors[index : index + 1, :]

    for part in range(2):
        piece = pl.ds(384 * part, 384)
        weight = rows(at.out_all[part])
        at.wide[:, piece] = dot(at.context[0, own_rows, :], weight[0:384]) + dot(
            at.context[1, own_rows, :], weight[384:768]
        )

    def first_norm(index):
        piece = aligned(index, 64)
        token_rows = pl.ds(pl.multiple_of(core * 256 + index * 64, 64), 64)
        residual = at.x_all[token_rows, :].astype(F32) + at.wide[piece, :] + vector(2)
        out, normed, inverse = norm(residual, vector(3), vector(4))
        at.first_out[piece, :] = out
        at.first_normed[piece, :] = normed
        at.first_inverse[piece, :] = jnp.broadcast_to(inverse, (64, 128))
        at.first_low[token_rows, :] = low(out)
        give_rows(0, index, at.first_low).start()

    loop(4, first_norm)
    gather_two.hand(1)
    got_rows(0, at.first_low)
    at.first_turned[...] = at.first_low[...].T
    gather_two.finish()
    gather_three.hand(1)

    def inner_units(index):
        piece = aligned(index, 256)
        pre = dot(at.first_low[...], rows(at.gat_1[:, :, :, piece])) + at.inner_bias[0:1, piece]
        value, slope = erf_parts(pre)
        at.active[:, piece] = low(value)
        at.slope[:, piece] = slope

    loop(6, inner_units)
    gather_three.finish()

    def outer_part(rows_at, part):
        return dot(
            at.active[rows_at, :], at.gat_2[:, :, :, 256 * part : 256 * part + 256].reshape(1536, 256)
        )

    come_outer = []
    for part in range(3):
        piece = pl.ds(256 * part, 256)
        at.part_send[:, piece] = low(outer_part(other_rows, part))
        come_outer.append(swap((11, 23, 24)[part], at.part_send.at[:, piece], at.part_recv.at[:, piece]))
    for part in range(3):
        at.wide[:, 256 * part : 256 * part + 256] = outer_part(own_rows, part)
    for copy in come_outer:
        copy.wait_recv()

    def second_norm(index):
        piece = aligned(index, 64)
        token_rows = pl.ds(pl.multiple_of(core * 256 + index * 64, 64), 64)
        total = at.first_out[piece, :] + at.wide[piece, :] + at.part_recv[piece, :].astype(F32) + vector(5)
        out, normed, inverse = norm(total, vector(6), vector(7))
        at.result[piece, :] = low(out)
        upstream = at.cotangent[piece, :].astype(F32)
        grad = norm_pull(upstream, normed, inverse, vector(6))
        at.grad_sum[piece, :] = grad
        rounded = low(grad)
        at.grad_outer[token_rows, :] = rounded
        give_rows(1, index, at.grad_outer).start()
        at.sums[5:6, :] += jnp.sum(rounded.astype(F32), axis=0, keepdims=True)
        at.sums[6:7, :] += jnp.sum(upstream * normed, axis=0, keepdims=True)
        at.sums[7:8, :] += jnp.sum(upstream, axis=0, keepdims=True)

    loop(4, second_norm)

    def scatter(arrays, tags, send, recv):
        rooms = [[b[kind + tag] for kind in ROOMS] for tag in tags]
        return Scatter(r, arrays, rooms, send, recv)

    scatter_two = scatter((at.grad_1, at.grad_2), ("1", "2"), at.sf_send, at.sf_recv)
    scatter_a = scatter((at.grad_o, at.grad_p.at[0]), ("o", "p0"), at.sa_send, at.sa_recv)
    scatter_b = scatter((at.grad_p.at[1], at.grad_p.at[2]), ("p1", "p2"), at.sb_send, at.sb_recv)
    scatter_c = scatter((at.grad_t.at[0], at.grad_t.at[1]), ("t0", "t1"), at.sc_send, at.sc_recv)

    def inner_grad(rows_at):
        for part in range(4):
            units = pl.ds(384 * part, 384)
            grad = low(dot(at.grad_outer[rows_at, :], at.gat_2[part].reshape(384, 768), 1, 1))
            pre = low(grad.astype(F32) * at.slope[rows_at, units])
            at.grad_pre[rows_at, units] = pre
            at.bias_inner[0:1, units] += jnp.sum(pre.astype(F32), axis=0, keepdims=True)

    at.bias_inner[...] = jnp.zeros_like(at.bias_inner)
    inner_grad(own_rows)
    got_rows(1, at.grad_outer)

    def line_of(index):
        half = index // 2
        start = r.pair * (1 - half) + r.z * half
        return (start + 2 * ((index + 1) // 2 % 2)) % LINE

    def send_lines(i, index, line):
        pl.when(index < 2)(lambda: scatter_two.begin_far(i, line))
        pl.when(index >= 2)(lambda: scatter_two.begin_near(i, line))

    def outer_weight(index):
        line = line_of(index)
        grad = dot(at.active[:, aligned(line, 384)], at.grad_outer[...], 0, 0)
        at.grad_2[line] = low(grad).reshape(4, 96, 768)
        send_lines(1, index, line)

    loop(4, outer_weight)

    inner_grad(other_rows)
    at.sums[8:9, :] = at.bias_inner[0:1, 0:768]
    at.sums[9:10, :] = at.bias_inner[0:1, 768:1536]

    def first_part(rows_at, part):
        weight = at.gat_1[2 * part : 2 * part + 2].reshape(384, 1536)
        return dot(at.grad_pre[rows_at, :], weight, 1, 1)

    come_grad_first = []
    for part in range(2):
        piece = pl.ds(384 * part, 384)
        at.part_send2[:, piece] = low(first_part(other_rows, part))
        come_grad_first.append(
            swap((13, 25)[part], at.part_send2.at[:, piece], at.part_recv2.at[:, piece])
        )
    def inner_weight(index):
        line = line_of(index)
        grad = dot(at.first_turned[aligned(line, 192), :], at.grad_pre[...])
        at.grad_1[line] = low(grad).reshape(4, 48, 1536)
        send_lines(0, index, line)

    loop(4, inner_weight)
    for part in range(2):
        at.wide[:, 384 * part : 384 * part + 384] = first_part(own_rows, part)
    for copy in come_grad_first:
        copy.wait_recv()

    def first_norm_back(index):
        piece = aligned(index, 64)
        token_rows = pl.ds(pl.multiple_of(core * 256 + index * 64, 64), 64)
        upstream = at.wide[piece, :] + at.part_recv2[piece, :].astype(F32) + at.grad_sum[piece, :]
        normed = at.first_normed[piece, :]
        grad = norm_pull(upstream, normed, at.first_inverse[piece, 0:1], vector(3))
        at.grad_sum[piece, :] = grad
        rounded = low(grad)
        at.grad_att[token_rows, :] = rounded
        give_rows(2, index, at.grad_att).start()
        at.sums[2:3, :] += jnp.sum(rounded.astype(F32), axis=0, keepdims=True)
        at.sums[3:4, :] += jnp.sum(upstream * normed, axis=0, keepdims=True)
        at.sums[4:5, :] += jnp.sum(upstream, axis=0, keepdims=True)

    loop(4, first_norm_back)
    out_rows = pl.ds(pl.multiple_of(2 * core, 2), 2)

    def context_rows(rows_at):
        weight_0 = at.out_all[0, out_rows].reshape(384, 384)
        weight_1 = at.out_all[1, out_rows].reshape(384, 384)
        at.grad_context[rows_at, :] = low(
            dot(at.grad_att[rows_at, 0:384], weight_0, 1, 1)
            + dot(at.grad_att[rows_at, 384:768], weight_1, 1, 1)
        )

    context_rows(own_rows)
    got_rows(2, at.grad_att)
    context_rows(other_rows)
    scatter_two.corners(1)
    scatter_two.along_far(1)
    for part in range(2):
        grad = dot(at.context[part], at.grad_att[:, aligned(core, 384)], 0, 0)
        at.grad_o[2 * part : 2 * part + 2] = low(grad).reshape(2, 4, 48, 384)

    room = jnp.zeros((128, 128), BF16)

    def spread(value, start):
        wide = jnp.concatenate([value, room], axis=1)
        return pltpu.roll(wide, start, 1, stride=1, stride_axis=0)

    heads = [low((lanes == which).astype(F32)) for which in range(2)]

    def lanes_of(index, place):
        return pl.ds(pl.multiple_of(384 * place + index * 128, 128), 128)

    def masked(value):
        return [value * only for only in heads]

    def backward_queries(index):
        pair = aligned(index, 128)
        flip = at.flip[...]
        keys = masked(at.kvq[:, lanes_of(index, 0)])
        values = at.kvq[:, lanes_of(index, 1)]
        for block in range(4):
            piece = pl.ds(128 * block, 128)
            window = pl.ds(384 - 128 * block, 640)
            back = pl.ds(384 - 128 * block, 128)
            grad_context = low(dot(flip, at.grad_context[piece, pair]))
            query = low(dot(flip, at.kvq[piece, lanes_of(index, 2)]))
            at.turned_grad[piece, :] = grad_context
            at.turned_query[back, :] = query
            table = masked(at.near_rows[window, pair])
            near, grad = [], 0.0
            for which, context_only in enumerate(masked(grad_context)):
                soft = at.soft[2 * index + which, piece, :].astype(F32)
                grad_soft = dot(context_only, values, 1, 1)
                inner = jnp.sum(soft * grad_soft, axis=-1, keepdims=True)
                grad_low = low(soft * (grad_soft - inner) * score_scale)
                at.grad_low[which, back, :] = grad_low
                near.append(spread(grad_low, 1))
                grad = grad + dot(grad_low, keys[which]) + dot(near[which], table[which])
            at.grad_kvq[piece, lanes_of(index, 2)] = low(dot(flip, low(grad)))
            at.near_grad[window, pair] += dot(
                jnp.concatenate(near, axis=0), jnp.concatenate(masked(query), axis=0), 0, 0
            )

    def backward_keys(index):
        pair = aligned(index, 128)
        queries = masked(at.turned_query[...])
        contexts = masked(at.turned_grad[...])
        for block in range(4):
            piece = pl.ds(128 * block, 128)
            window = pl.ds(128 * block, 640)
            table = masked(at.far_natural[window, pair])
            far, grad, grad_value = [], 0.0, 0.0
            for which in range(2):
                turned = at.grad_low[which, :, piece].T
                far.append(spread(turned, 0))
                grad = grad + dot(turned, queries[which]) + dot(far[which], table[which])
                weights = at.soft[2 * index + which, :, piece]
                grad_value = grad_value + dot(weights, contexts[which], 0, 0)
            at.grad_kvq[piece, lanes_of(index, 0)] = low(grad)
            at.grad_kvq[piece, lanes_of(index, 1)] = low(grad_value)
            keys = masked(at.kvq[piece, lanes_of(index, 0)])
            at.far_grad[window, pair] += dot(
                jnp.concatenate(far, axis=0), jnp.concatenate(keys, axis=0), 0, 0
            )

    def shape_weight(value):
        return low(value).reshape(LINE, 4, 48, value.shape[-1])

    def rel_pair(index):
        pair = aligned(index, 128)
        at.key_rel[:, pair] = low(dot(at.one_hot[...], low(at.near_grad[256:768, pair])))
        at.query_rel[:, pair] = low(dot(at.one_natural[...], low(at.far_grad[256:768, pair])))

    def weights_pair(index):
        pair = aligned(index, 128)
        tokens = jnp.concatenate(
            [at.grad_kvq[:, lanes_of(index, place)] for place in (0, 2, 1)], axis=1
        )
        grad = dot(at.x_turned[...], tokens)
        rel = jnp.concatenate([at.key_rel[:, pair], at.query_rel[:, pair]], axis=1)
        table = dot(rows(at.table_all[0]), rel[0:256]) + dot(rows(at.table_all[1]), rel[256:512])
        at.grad_p[index, :, :, :, 0:256] = shape_weight(grad[:, 0:256] + table)
        at.grad_p[index, :, :, :, 256:384] = shape_weight(grad[:, 256:384])

    def table_half(which):
        piece = aligned(which, 256)
        return dot(rows(at.gat_b[:, :, :, 0:384]), at.query_rel[piece, :], 1, 1) + dot(
            rows(at.gat_a[:, :, :, 0:384]), at.key_rel[piece, :], 1, 1
        )

    def at_step(step, when, *moves):
        @pl.when(step == when)
        def _():
            for move in moves:
                move()

    def swap_table():
        return remote(
            at.table_send, at.table_recv, at.swap_send.at[15], at.swap_recv.at[15], r.partner
        )

    def send_table():
        at.table_send[...] = shape_weight(table_half(other))
        swap_table().start()

    def backward_pair(index):
        backward_queries(index)
        at_step(index, 2, lambda: scatter_two.turn(0), lambda: scatter_two.turn(1))
        backward_keys(index)
        at_step(index, 0, lambda: scatter_two.corners(0))
        at_step(index, 1, lambda: scatter_a.corners(0), lambda: scatter_two.along_far(0))
        at_step(index, 2, lambda: scatter_a.along_far(0))
        rel_pair(index)
        at_step(index, 2, send_table)
        weights_pair(index)
        at_step(index, 0, lambda: scatter_a.begin(0), lambda: scatter_a.begin(1))
        at_step(index, 1, lambda: scatter_b.begin(0), lambda: scatter_a.corners(1))
        at_step(index, 2, lambda: scatter_b.begin(1))

    loop(3, backward_pair)
    scatter_b.corners(0)
    scatter_a.along_far(1)

    own_table = table_half(core)
    come_part = swap_table()
    waiting.append(come_part)
    come_part.wait_recv()
    own_table = own_table + rows(at.table_recv[...]).astype(F32)
    for part in range(2):
        at.grad_t[part] = shape_weight(own_table[:, 128 * part : 128 * part + 128])
        scatter_c.begin(part)
    scatter_a.turn(0)

    at.sums[0:1, vector_half] = jnp.sum(
        at.grad_kvq[:, 768:1152].astype(F32), axis=0, keepdims=True
    ) + jnp.sum(at.far_grad[256:768, :], axis=0, keepdims=True)
    at.sums[1:2, vector_half] = jnp.sum(
        at.grad_kvq[:, 384:768].astype(F32), axis=0, keepdims=True
    )

    def exchange(stage, source, device):
        return remote(
            source, at.sums_come.at[stage], at.sums_send.at[stage], at.sums_recv.at[stage], device
        )

    stage_copies = [exchange(0, at.sums, r.partner)]
    stage_copies[0].start()

    def input_part(rows_at, part):
        weight_a = at.gat_a[2 * part : 2 * part + 2].reshape(384, 768)
        weight_b = at.gat_b[2 * part : 2 * part + 2, :, :, 0:384].reshape(384, 384)
        return dot(at.grad_kvq[rows_at, 0:768], weight_a, 1, 1) + dot(
            at.grad_kvq[rows_at, 768:1152], weight_b, 1, 1
        )

    for copy in come_outer:
        copy.wait_send()
    come_input = []
    for part in range(2):
        piece = pl.ds(384 * part, 384)
        at.part_send[:, piece] = low(input_part(other_rows, part))
        come_input.append(swap((16, 26)[part], at.part_send.at[:, piece], at.part_recv.at[:, piece]))

    stage_copies[0].wait_recv()
    lines = lax.broadcasted_iota(jnp.int32, (16, 1), 0)
    shared = jnp.where((lines == 8) | (lines == 9), 0.0, at.sums_come[0])
    at.sums_step[0] = at.sums[...] + shared
    stage_copies.append(exchange(1, at.sums_step.at[0], r.at_x))
    stage_copies[1].start()
    scatter_b.corners(1)
    scatter_a.turn(1)
    scatter_b.along_far(0)
    for part in range(2):
        at.wide[:, 384 * part : 384 * part + 384] = input_part(own_rows, part)
    for copy in come_input:
        copy.wait_recv()
    at.input_grad[...] = low(at.grad_sum[...] + at.wide[...] + at.part_recv[...].astype(F32))
    for part in range(2):
        scatter_c.corners(part)
    for part in range(2):
        scatter_two.along_near(part)
    stage_copies[1].wait_recv()
    at.sums_step[1] = at.sums_step[0] + at.sums_come[1]
    stage_copies.append(exchange(2, at.sums_step.at[1], r.at_y))
    stage_copies[2].start()
    at.give_1[...] = scatter_two.total(0).reshape(2, 24, 1536)
    swap(17, at.give_1.at[other], at.d_inner.at[core])
    at.d_inner[core] = at.give_1[core]
    scatter_b.along_far(1)
    at.d_outer[...] = scatter_two.total(1)
    scatter_b.turn(0)
    scatter_c.along_far(0)
    scatter_a.along_near(0)
    scatter_c.along_far(1)
    scatter_a.along_near(1)
    stage_copies[2].wait_recv()
    at.sums_step[2] = at.sums_step[1] + at.sums_come[2]
    for step in range(1, LINE):
        copy = exchange(2 + step, at.sums_step.at[2], r.at_line(r.ahead(step)))
        copy.start()
        stage_copies.append(copy)

    def give(slot, source, start, width, out):
        swap(slot, source.at[other, :, pl.ds(start, width)], out.at[:, aligned(core, width)])
        out[:, aligned(core, width)] = source[core, :, start : start + width]

    def give_pair(index, total):
        for place in range(3):
            start = 384 * place + 128 * index
            at.give_p[:, :, start : start + 128] = total[:, 128 * place : 128 * place + 128].reshape(
                2, 24, 128
            )

    at.give_o[...] = scatter_a.total(0).reshape(2, 24, 384)
    give(21, at.give_o, 0, 384, at.d_output)
    scatter_b.turn(1)
    for part in range(2):
        scatter_c.turn(part)
    give_pair(0, scatter_a.total(1))
    for user in (scatter_b, scatter_c):
        for part in range(2):
            user.along_near(part)
    give_pair(1, scatter_b.total(0))
    give_pair(2, scatter_b.total(1))
    give(18, at.give_p, 0, 384, at.d_key)
    give(19, at.give_p, 384, 384, at.d_query)
    give(20, at.give_p, 768, 384, at.d_value)
    for part in range(2):
        at.give_t[:, :, 128 * part : 128 * part + 128] = scatter_c.total(part).reshape(2, 24, 128)
    give(22, at.give_t, 0, 256, at.d_table)
    for copy in stage_copies[3:]:
        copy.wait_recv()
    at.vector_grads[...] = (
        at.sums_step[2] + at.sums_come[3] + at.sums_come[4] + at.sums_come[5]
    )
    for copy in waiting[-6:]:
        copy.wait_recv()
    for copy in waiting:
        if all(copy is not early for early in come_outer):
            copy.wait_send()
    for copy in stage_copies:
        copy.wait_send()
    for kind, array in enumerate((at.first_low, at.grad_outer, at.grad_att)):
        for index in range(4):
            give_rows(kind, index, array).wait_send()
    for index in range(3):
        remote(
            at.context.at[core, :, pl.ds(128 * index, 128)],
            at.context.at[core, :, pl.ds(128 * index, 128)],
            at.context_send.at[index],
            at.context_recv.at[index],
            r.partner,
        ).wait_send()
    for user in (gather_one, gather_two, gather_three, scatter_two, scatter_a, scatter_b, scatter_c):
        user.sent()


def finish_kernel(names, *refs):
    at = type("Refs", (), dict(zip(names, refs)))
    chip, core = lax.axis_index("fsdp"), lax.axis_index("seq")
    at.result_out[...] = at.result[...]
    at.input_grad_out[...] = at.input_grad[...]
    at.query_w_out[...] = at.d_query[...]
    at.key_w_out[...] = at.d_key[...]
    at.value_w_out[...] = at.d_value[...]
    at.output_w_out[...] = at.d_output[...]
    at.table_out[...] = at.d_table[...]
    at.outer_w_out[...] = at.d_outer[...]
    for group in range(4 * LINE):
        for which in range(2):
            device = 2 * group + which
            at.inner_w_out[:, 96 * device : 96 * device + 96] = at.d_inner[
                which, :, 96 * group : 96 * group + 96
            ]
    sums = at.vector_grads[...]
    own = pltpu.roll(sums, (768 - 24 * (2 * chip + core)) % 768, 1)
    small_outs = (
        at.query_b_out, at.value_b_out, at.output_b_out, at.gain_1_out, at.shift_1_out,
        at.outer_b_out, at.gain_2_out, at.shift_2_out,
    )
    for index, out in enumerate(small_outs):
        out[...] = own[index : index + 1, 0:24]
    units = jnp.where(chip < 2 * LINE, sums[8:9], sums[9:10])
    units = jnp.broadcast_to(units, (8, 768))
    at.inner_b_out[...] = pltpu.roll(units, (768 - 96 * (chip % (2 * LINE))) % 768, 1)[0:1, 0:96]
    at.count_out[...] = sums[10:11, 0:1].astype(jnp.int32)


OUTPUTS = dict(
    result=((256, 768), BF16),
    input_grad=((256, 768), BF16),
    d_query=((24, 768), F32),
    d_key=((24, 768), F32),
    d_value=((24, 768), F32),
    d_output=((24, 768), F32),
    d_table=((24, 512), F32),
    d_inner=((2, 24, 1536), F32),
    d_outer=((96, 768), F32),
    vector_grads=((16, 768), F32),
)
FINALS = dict(
    result_out=((256, 768), BF16),
    input_grad_out=((256, 768), BF16),
    query_w_out=((24, 768), F32),
    key_w_out=((24, 768), F32),
    value_w_out=((24, 768), F32),
    output_w_out=((24, 768), F32),
    table_out=((24, 512), F32),
    inner_w_out=((24, 3072), F32),
    outer_w_out=((96, 768), F32),
    query_b_out=((1, 24), F32),
    value_b_out=((1, 24), F32),
    output_b_out=((1, 24), F32),
    gain_1_out=((1, 24), F32),
    shift_1_out=((1, 24), F32),
    outer_b_out=((1, 24), F32),
    gain_2_out=((1, 24), F32),
    shift_2_out=((1, 24), F32),
    inner_b_out=((1, 96), F32),
    count_out=((1, 1), jnp.int32),
)
LINE = 4
BLOCKS = (LINE, 4, 48)
SCRATCH = dict(
    small_wide=((16, 128), F32),
    small=((16, 128), BF16),
    inner_pair=((2, 24, 1536), BF16),
    segment_row=((8, 512), F32),
    segment_col=((512, 128), F32),
    come_a=((24, 768), BF16),
    come_b=((24, 1024), BF16),
    come_s=((16, 128), BF16),
    come_1=((24, 1536), BF16),
    gat_a=(BLOCKS + (768,), BF16),
    gat_b=(BLOCKS + (1024,), BF16),
    gat_s=((LINE, 4, 2, 16, 128), BF16),
    gat_1=(BLOCKS + (1536,), BF16),
    gat_2=((LINE, 4, 96, 768), BF16),
    x_all=((512, 768), BF16),
    x_turned=((768, 512), BF16),
    one_hot=((512, 512), BF16),
    flip=((128, 128), BF16),
    near_rows=((1024, 384), BF16),
    far_rows=((1024, 384), BF16),
    far_natural=((1024, 384), BF16),
    one_natural=((512, 512), BF16),
    near_grad=((1024, 384), F32),
    far_grad=((1024, 384), F32),
    key_rel=((512, 384), BF16),
    query_rel=((512, 384), BF16),
    table_all=((2,) + BLOCKS + (256,), BF16),
    out_all=((2,) + BLOCKS + (384,), BF16),
    vectors=((8, 768), F32),
    inner_bias=((8, 1536), F32),
    bias_inner=((8, 1536), F32),
    kvq=((512, 1152), BF16),
    grad_kvq=((512, 1152), BF16),
    far_scores=((512, 512), F32),
    grad_low=((2, 512, 512), BF16),
    turned_query=((512, 128), BF16),
    turned_grad=((512, 128), BF16),
    soft=((6, 512, 512), BF16),
    context=((2, 512, 384), BF16),
    grad_context=((512, 384), BF16),
    wide=((256, 768), F32),
    first_out=((256, 768), F32),
    first_normed=((256, 768), F32),
    first_inverse=((256, 128), F32),
    first_low=((512, 768), BF16),
    first_turned=((768, 512), BF16),
    active=((512, 1536), BF16),
    slope=((512, 1536), F32),
    grad_pre=((512, 1536), BF16),
    part_send=((256, 768), BF16),
    part_recv=((256, 768), BF16),
    part_send2=((256, 768), BF16),
    part_recv2=((256, 768), BF16),
    grad_sum=((256, 768), F32),
    grad_outer=((512, 768), BF16),
    grad_att=((512, 768), BF16),
    table_send=(BLOCKS + (256,), BF16),
    table_recv=(BLOCKS + (256,), BF16),
    sums=((16, 768), F32),
    sums_step=((3, 16, 768), F32),
    sums_come=((6, 16, 768), F32),
    grad_1=(BLOCKS + (1536,), BF16),
    grad_2=((LINE, 4, 96, 768), BF16),
    grad_o=(BLOCKS + (384,), BF16),
    grad_p=((3,) + BLOCKS + (384,), BF16),
    grad_t=((2,) + BLOCKS + (128,), BF16),
    give_1=((2, 24, 1536), F32),
    give_o=((2, 24, 384), F32),
    give_p=((2, 24, 1152), F32),
    give_t=((2, 24, 256), F32),
)
ROOMS = dict(pair_=2, first_=LINE, corner_=2, second_=LINE, line_=LINE)
BLOCK = {
    "1": (48, 1536), "2": (96, 768), "o": (48, 384), "p0": (48, 384), "p1": (48, 384),
    "p2": (48, 384), "t0": (48, 128), "t1": (48, 128),
}
for tag, block in BLOCK.items():
    for kind, count in ROOMS.items():
        SCRATCH[kind + tag] = ((count,) + block, BF16)
SEMAPHORES = dict(
    swap_send=(27,),
    swap_recv=(27,),
    row_send=(3, 4),
    row_recv=(3, 4),
    here=(2,),
    context_send=(3,),
    context_recv=(3,),
    ga_send=(3, 6, LINE),
    ga_recv=(3, 6, LINE),
    gf_send=(2, 6, LINE),
    gf_recv=(2, 6, LINE),
    gg_send=(2, 6, LINE),
    gg_recv=(2, 6, LINE),
    sf_send=(2, 5, LINE),
    sf_recv=(2, 5, LINE),
    sa_send=(2, 5, LINE),
    sa_recv=(2, 5, LINE),
    sb_send=(2, 5, LINE),
    sb_recv=(2, 5, LINE),
    sc_send=(2, 5, LINE),
    sc_recv=(2, 5, LINE),
    sums_send=(6,),
    sums_recv=(6,),
)


def block_shards(
    hidden_in,
    query_weight,
    query_bias,
    key_weight,
    value_weight,
    value_bias,
    output_weight,
    output_bias,
    first_gain,
    first_shift,
    inner_weight,
    inner_bias,
    outer_weight,
    outer_bias,
    second_gain,
    second_shift,
    relative_table,
    segments,
    buckets,
    predicted,
    labels,
    cotangent,
):
    inputs = dict(
        hidden=hidden_in[0],
        query_w=query_weight,
        key_w=key_weight,
        value_w=value_weight,
        output_w=output_weight,
        table_t=relative_table.T,
        inner_w=inner_weight,
        outer_w=outer_weight,
        query_b=query_bias[None],
        value_b=value_bias[None],
        output_b=output_bias[None],
        gain_1=first_gain[None],
        shift_1=first_shift[None],
        outer_b=outer_bias[None],
        gain_2=second_gain[None],
        shift_2=second_shift[None],
        inner_b=inner_bias[None],
        segments=segments,
        buckets=buckets[None],
        predicted=predicted,
        labels=labels,
        cotangent=cotangent[0],
    )
    names = tuple(inputs) + tuple(OUTPUTS) + tuple(SCRATCH) + tuple(SEMAPHORES)
    vmem = pl.BlockSpec(memory_space=pltpu.VMEM)
    outs = pl.pallas_call(
        partial(layer_kernel, names),
        name="layer",
        out_shape=tuple(jax.ShapeDtypeStruct(*out) for out in OUTPUTS.values()),
        in_specs=[vmem] * len(inputs),
        out_specs=(vmem,) * len(OUTPUTS),
        scratch_shapes=[pltpu.VMEM(*spec) for spec in SCRATCH.values()]
        + [pltpu.SemaphoreType.DMA(shape) for shape in SEMAPHORES.values()],
        compiler_params=pltpu.CompilerParams(
            collective_id=0, has_side_effects=True, vmem_limit_bytes=67043328
        ),
    )(*inputs.values())
    finals = pl.pallas_call(
        partial(finish_kernel, tuple(OUTPUTS) + tuple(FINALS)),
        name="finish",
        out_shape=tuple(jax.ShapeDtypeStruct(*out) for out in FINALS.values()),
        in_specs=[vmem] * len(OUTPUTS),
        out_specs=(vmem,) * len(FINALS),
    )(*outs)
    got = type("Outs", (), dict(zip(FINALS, finals)))
    return (
        got.result_out[None],
        got.input_grad_out[None],
        got.query_w_out,
        got.query_b_out[0],
        got.key_w_out,
        got.value_w_out,
        got.value_b_out[0],
        got.output_w_out,
        got.output_b_out[0],
        got.gain_1_out[0],
        got.shift_1_out[0],
        got.inner_w_out,
        got.inner_b_out[0],
        got.outer_w_out,
        got.outer_b_out[0],
        got.gain_2_out[0],
        got.shift_2_out[0],
        got.table_out.T,
        got.count_out[0, 0],
    )


def fits(mesh):
    return mesh.shape["fsdp"] == 4 * LINE and mesh.shape["seq"] == 2


def solution(mesh):
    return jax.shard_map(
        block_shards if fits(mesh) else shards,
        mesh=mesh,
        in_specs=(
            P("fsdp", "seq", None),
            P(("fsdp", "seq"), None),
            P(("fsdp", "seq")),
            P(("fsdp", "seq"), None),
            P(("fsdp", "seq"), None),
            P(("fsdp", "seq")),
            P(("fsdp", "seq"), None),
            P(("fsdp", "seq")),
            P(("fsdp", "seq")),
            P(("fsdp", "seq")),
            P(("fsdp", "seq"), None),
            P(("fsdp", "seq")),
            P(("fsdp", "seq"), None),
            P(("fsdp", "seq")),
            P(("fsdp", "seq")),
            P(("fsdp", "seq")),
            P(None, ("fsdp", "seq")),
            P("fsdp", None),
            P(),
            P("fsdp", "seq"),
            P("fsdp", "seq"),
            P("fsdp", "seq", None),
        ),
        out_specs=(
            P("fsdp", "seq", None),
            P("fsdp", "seq", None),
            P(("fsdp", "seq"), None),
            P(("fsdp", "seq")),
            P(("fsdp", "seq"), None),
            P(("fsdp", "seq"), None),
            P(("fsdp", "seq")),
            P(("fsdp", "seq"), None),
            P(("fsdp", "seq")),
            P(("fsdp", "seq")),
            P(("fsdp", "seq")),
            P(("fsdp", "seq"), None),
            P(("fsdp", "seq")),
            P(("fsdp", "seq"), None),
            P(("fsdp", "seq")),
            P(("fsdp", "seq")),
            P(("fsdp", "seq")),
            P(None, ("fsdp", "seq")),
            P(),
        ),
        check_vma=False,
    )
```
